32 devices in a mesh: group: 16 (over z, x, core), fsdp: 2 (over y).
Axes of the slice: x: 2, y: 2, z: 4, core: 2. Of those that a mesh axis runs over, the one named last changes fastest.
Arguments:
- inputs: bfloat16 [32, 1024, 1152], P('group', 'fsdp'), may hold values from -6 to 6
- segments: int32 [32, 1024], P('group'), may hold values from 0 to 3, never falling along the last dimension, each value on 1 to 768 neighbouring positions
- out_grad: bfloat16 [32, 1024, 1152], P('group', 'fsdp'), may hold values from -6 to 6
- attention_gain: bfloat16 [1152], P('fsdp'), may hold values from 0.5 to 1.5
- query_weight: bfloat16 [1152, 1152], P('fsdp'), may hold values from -0.1875 to 0.1875
- key_weight: bfloat16 [1152, 384], P('fsdp'), may hold values from -0.1875 to 0.1875
- value_weight: bfloat16 [1152, 384], P('fsdp'), may hold values from -0.1875 to 0.1875
- output_weight: bfloat16 [1152, 1152], P('fsdp'), may hold values from -1 to 1
- feedforward_gain: bfloat16 [1152], P('fsdp'), may hold values from 0.5 to 1.5
- gate_weight: bfloat16 [1152, 3072], P('fsdp'), may hold values from -0.1875 to 0.1875
- up_weight: bfloat16 [1152, 3072], P('fsdp'), may hold values from -0.1875 to 0.1875
- down_weight: bfloat16 [3072, 1152], P('fsdp'), may hold values from -0.109375 to 0.109375
Outputs:
- output: bfloat16 [32, 1024, 1152], P('group', 'fsdp')
- input_grad: bfloat16 [32, 1024, 1152], P('group', 'fsdp')
- attention_gain_grad: float32 [1152], P('fsdp')
- query_weight_grad: float32 [1152, 1152], P('fsdp')
- key_weight_grad: float32 [1152, 384], P('fsdp')
- value_weight_grad: float32 [1152, 384], P('fsdp')
- output_weight_grad: float32 [1152, 1152], P('fsdp')
- feedforward_gain_grad: float32 [1152], P('fsdp')
- gate_weight_grad: float32 [1152, 3072], P('fsdp')
- up_weight_grad: float32 [1152, 3072], P('fsdp')
- down_weight_grad: float32 [3072, 1152], P('fsdp')
The draws below stay inside these ranges and needn't reach their ends.
All inputs are finite; a program needn't handle non-finite values.
Results may differ from the reference program's by a relative error of at most 0.015.
Values may be sent and summed in bfloat16 or wider, within the bound.
A program may use at most 448 MiB of HBM per device.

```python
import math
import jax
import jax.numpy as jnp
import numpy as np
from jax import lax

D = 1152
HEADS = 18
KV_HEADS = 6
HEAD = 64
FF = 3072
LEN = 1024
QD = 1152
KVD = 384
SEQUENCES = 32


def shard_levels(stream_key, shape, shards, low, top_value):
    factor_of, own = 1.0, jax.random.fold_in(stream_key, 6)
    for position, blocks in shards:
        draws = jnp.exp(jax.random.uniform(jax.random.fold_in(own, position), (blocks,), jnp.float32, low / len(shards), top_value / len(shards)))
        factor_of = factor_of * jnp.repeat(draws, shape[position] // blocks).reshape([-1 if axis == position else 1 for axis in range(len(shape))])
    return factor_of


def profile(number_of, total, most, skew):
    weights = [(1 << 20) // math.isqrt(grade ** skew) + 1 for grade in range(2, number_of + 1)]
    rest, given = total - most - (number_of - 1), [1] * (number_of - 1)
    while rest > 0:
        movable = [i for i in range(number_of - 1) if given[i] < most]
        mass, left = sum([weights[i] for i in movable]), rest
        for i in movable:
            addition = min(most - given[i], max(1, left * weights[i] // mass), rest)
            given[i] = given[i] + addition
            rest = rest - addition
    return np.array([most] + given)


def ragged_sizes(rng, number_of, total, limit, slope):
    if number_of == 2:
        one = jax.random.randint(rng, (), max(1, total - limit), min(limit, total - 1) + 1)
        return jnp.stack([one, total - one])
    tallies = jnp.asarray(profile(number_of, total, limit, slope), jnp.int32)
    couples = (number_of - 1) // 2
    source_of, taker = tallies[1:1 + 2 * couples:2], tallies[2:2 + 2 * couples:2]
    room = jnp.minimum(source_of - 1, limit - taker)
    shifted = jax.random.randint(jax.random.fold_in(rng, 1), (couples,), 0, 1 << 20) % (room + 1)
    tallies = tallies.at[1:1 + 2 * couples:2].set(source_of - shifted).at[2:2 + 2 * couples:2].set(taker + shifted)
    return tallies[jax.random.permutation(jax.random.fold_in(rng, 2), number_of)]


def noise(rng, dims, scale, reach, shards=(), kind=jnp.bfloat16):
    array = jax.random.normal(rng, dims, jnp.float32) * scale
    if len(shards) > 0:
        array = shard_levels(rng, dims, shards, -0.22, 0.18) * array
    return jnp.clip(array, min=-reach, max=reach).astype(kind)


def setup_inputs(seed: int = 0) -> dict:
    key_of = jax.random.split(jax.random.key(seed), 13)
    return {
        "inputs": noise(key_of[0], (SEQUENCES, LEN, D), 1.0, 6.0, ((0, 16), (1, 2))),
        "segments": jax.vmap(lambda own: jnp.searchsorted(jnp.cumsum(ragged_sizes(own, 4, LEN, 3 * LEN // 4, 2)), jnp.arange(LEN), side="right"))(jax.random.split(key_of[1], SEQUENCES)).reshape((SEQUENCES, LEN)).astype(jnp.int32),
        "out_grad": noise(key_of[2], (SEQUENCES, LEN, D), 1.0, 6.0, ((0, 16), (1, 2))),
        "attention_gain": jnp.clip(1.0 + 0.1 * jax.random.normal(key_of[3], (D,), jnp.float32), 0.5, 1.5).astype(jnp.bfloat16),
        "query_weight": noise(key_of[4], (D, QD), D ** -0.5, 0.1875, ((0, 2),)),
        "key_weight": noise(key_of[5], (D, KVD), D ** -0.5, 0.1875, ((0, 2),)),
        "value_weight": noise(key_of[6], (D, KVD), D ** -0.5, 0.1875, ((0, 2),)),
        "output_weight": noise(key_of[7], (QD, D), (max(QD // 32, 1)) ** -0.5, 1.0, ((0, 2),)),
        "feedforward_gain": jnp.clip(1.0 + 0.1 * jax.random.normal(key_of[8], (D,), jnp.float32), 0.5, 1.5).astype(jnp.bfloat16),
        "gate_weight": noise(key_of[9], (D, FF), D ** -0.5, 0.1875, ((0, 2),)),
        "up_weight": noise(key_of[10], (D, FF), D ** -0.5, 0.1875, ((0, 2),)),
        "down_weight": noise(key_of[11], (FF, D), FF ** -0.5, 0.109375, ((0, 2),)),
    }


epsilon = 1e-05
rope_base = 10000.0

@jax.custom_vjp
def low(v):
    return lax.optimization_barrier(v.astype(jnp.bfloat16)).astype(jnp.float32)

@jax.custom_vjp
def low_back(v):
    return v

def low_keep(v):
    return (low(v), None)

def low_pass(kept, grad):
    return (grad,)

def back_keep(v):
    return (v, None)

def back_low(kept, grad):
    return (low(grad),)
low.defvjp(low_keep, low_pass)
low_back.defvjp(back_keep, back_low)

def matmul_high(left, right):
    return jnp.dot(left, right, precision=lax.Precision.HIGHEST)

def rms_norm(values, gain):
    return values * lax.rsqrt(lax.optimization_barrier(jnp.mean(values * values, axis=-1, keepdims=True)) + epsilon) * gain

def rotary_tables(positions, width):
    half_width = width // 2
    freqs = jnp.exp(jnp.arange(half_width, dtype=jnp.float32) * (-2.0 * math.log(rope_base) / width))
    angles = positions[:, None] * freqs[None, :]
    return (jnp.cos(angles), jnp.sin(angles))

def rotate(values, cosines, sines):
    half_width = values.shape[-1] // 2
    first = values[..., :half_width]
    second = values[..., half_width:]
    return jnp.concatenate([first * cosines - second * sines, second * cosines + first * sines], axis=-1)

def layer(tokens, params, allowed, cosines, sines):
    gain_attention, full_query, full_key, full_value, full_output, gain_feed, full_gate, full_up, full_down = params
    length = tokens.shape[0]
    normed_a = low(rms_norm(tokens, gain_attention))
    query_lin = low_back(matmul_high(normed_a, full_query)).reshape(length, KV_HEADS, HEADS // KV_HEADS, HEAD)
    queries = low(rotate(query_lin, cosines[:, None, None, :], sines[:, None, None, :]))
    key_lin = low_back(matmul_high(normed_a, full_key)).reshape(length, KV_HEADS, HEAD)
    key_rows = low(rotate(key_lin, cosines[:, None, :], sines[:, None, :]))
    value_rows = low(low_back(matmul_high(normed_a, full_value))).reshape(length, KV_HEADS, HEAD)
    scores = low_back(jnp.einsum('qhgd,khd->hgqk', queries, key_rows, precision=lax.Precision.HIGHEST)) * HEAD ** (-0.5)
    scores = jnp.where(allowed, scores, -1e+30)
    attention = jax.nn.softmax(scores, axis=-1)
    mixed = jnp.einsum('hgqk,khd->qhgd', low(attention), value_rows, precision=lax.Precision.HIGHEST)
    mixed = low(low_back(mixed.reshape(length, HEADS * HEAD)))
    residual = tokens + low_back(matmul_high(mixed, full_output))
    normed_f = low(rms_norm(residual, gain_feed))
    gate_sum = low_back(matmul_high(normed_f, full_gate))
    up_sum = low_back(matmul_high(normed_f, full_up))
    hidden = low(jax.nn.silu(gate_sum) * up_sum)
    return residual + low_back(matmul_high(hidden, full_down))

def reference(inputs, segments, out_grad, attention_gain, query_weight, key_weight, value_weight, output_weight, feedforward_gain, gate_weight, up_weight, down_weight):
    params = tuple((weight.astype(jnp.float32) for weight in (attention_gain, query_weight, key_weight, value_weight, output_weight, feedforward_gain, gate_weight, up_weight, down_weight)))
    places = jnp.arange(LEN, dtype=jnp.int32)
    cosines, sines = rotary_tables(places.astype(jnp.float32), HEAD)
    causal = places[:, None] >= places[None, :]

    def one_sequence(totals, sequence):
        tokens, segment_row, cotangent = sequence
        allowed = causal & (segment_row[:, None] == segment_row[None, :])

        def forward(values, weights):
            return layer(values, weights, allowed, cosines, sines)
        result, pullback = jax.vjp(forward, tokens.astype(jnp.float32), params)
        token_grad, weight_grads = pullback(cotangent.astype(jnp.float32))
        totals = tuple((left + right for left, right in zip(totals, weight_grads)))
        return (totals, (result.astype(jnp.bfloat16), token_grad.astype(jnp.bfloat16)))
    initial = tuple((jnp.zeros(weight.shape, jnp.float32) for weight in params))
    totals, (outputs, input_grads) = lax.scan(one_sequence, initial, (inputs, segments, out_grad))
    return (outputs, input_grads, totals[0], totals[1], totals[2], totals[3], totals[4], totals[5], totals[6], totals[7], totals[8])
```

```python
import functools
import math

import jax
import jax.numpy as jnp
from jax import lax
from jax.experimental import pallas as pl
from jax.experimental.pallas import tpu as pltpu
from jax.sharding import PartitionSpec as P

HEADS = 18
KV_HEADS = 6
HEAD = 64
epsilon = 1e-05
rope_base = 10000.0
BLOCK = 256
WIDE = 128
VMEM_MOST = 66 * 1024 * 1024 - 3 * 1024 * 1024


def mm(left, right):
    return jnp.dot(left, right, preferred_element_type=jnp.float32)


def mm_nt(left, right):
    return lax.dot_general(
        left, right, (((1,), (1,)), ((), ())), preferred_element_type=jnp.float32
    )


def mm_tn(left, right):
    return lax.dot_general(
        left, right, (((0,), (0,)), ((), ())), preferred_element_type=jnp.float32
    )


def low(values):
    return values.astype(jnp.bfloat16)


def lanes_below(rows, period, limit):
    lane = lax.broadcasted_iota(jnp.int32, (rows, WIDE), 1)
    return lane % period < limit


def swap_halves(tile):
    ahead = pltpu.roll(tile, WIDE - HEAD // 2, 1)
    behind = pltpu.roll(tile, HEAD // 2, 1)
    return jnp.where(lanes_below(tile.shape[0], HEAD, HEAD // 2), ahead, behind)


def rope_tables(length):
    half_width = HEAD // 2
    freqs = jnp.exp(
        jnp.arange(half_width, dtype=jnp.float32) * (-2.0 * math.log(rope_base) / HEAD)
    )
    angles = jnp.arange(length, dtype=jnp.float32)[:, None] * freqs[None, :]
    cosines, sines = jnp.cos(angles), jnp.sin(angles)
    return (
        jnp.concatenate([cosines] * 4, axis=1),
        jnp.concatenate([-sines, sines] * 2, axis=1),
    )


def project_body(x_ref, gain_ref, w_ref, cos_ref, sin_ref, normed_ref, qkv_ref):
    values = x_ref[...].astype(jnp.float32)
    inverse = lax.rsqrt(jnp.mean(values * values, axis=-1, keepdims=True) + epsilon)
    normed = low(values * inverse * gain_ref[...])
    normed_ref[...] = normed
    cosines, sines = cos_ref[...], sin_ref[...]
    width = qkv_ref.shape[1]
    q_width, k_width = HEADS * HEAD, KV_HEADS * HEAD
    step = 384
    for at in range(0, width, step):
        wide = mm(normed, w_ref[:, at : at + step])
        for part in range(0, step, WIDE):
            tile = wide[:, part : part + WIDE]
            if at + part < q_width + k_width:
                tile = tile * cosines + swap_halves(tile) * sines
            if at + part < q_width:
                tile = tile * HEAD ** (-0.5)
            qkv_ref[:, at + part : at + part + WIDE] = low(tile)


def project(x, gain, w, cosines, sines):
    length, width = x.shape
    out = w.shape[1]
    rows = pl.BlockSpec((BLOCK, width), lambda i: (i, 0))
    table = pl.BlockSpec((BLOCK, WIDE), lambda i: (i, 0))
    return pl.pallas_call(
        project_body,
        grid=(length // BLOCK,),
        in_specs=[
            rows,
            pl.BlockSpec((1, width), lambda i: (0, 0)),
            pl.BlockSpec((width, out), lambda i: (0, 0), pipeline_mode=pl.Buffered(1)),
            table,
            table,
        ],
        out_specs=[rows, pl.BlockSpec((BLOCK, out), lambda i: (i, 0))],
        out_shape=[
            jax.ShapeDtypeStruct((length, width), jnp.bfloat16),
            jax.ShapeDtypeStruct((length, out), jnp.bfloat16),
        ],
        cost_estimate=pl.CostEstimate(
            flops=2 * length * width * out,
            bytes_accessed=2 * (2 * length * width + length * out + width * out),
            transcendentals=0,
        ),
        name="project",
    )(x, gain, w, cosines, sines)


def place_heads(tile, variants_ref):
    wide = tile.astype(jnp.float32)
    turned = pltpu.roll(wide, HEAD, 1)
    low_lanes = lanes_below(tile.shape[0], WIDE, HEAD)
    variants_ref[0] = low(jnp.where(low_lanes, wide, 0.0))
    variants_ref[1] = low(jnp.where(low_lanes, 0.0, turned))
    variants_ref[2] = low(jnp.where(low_lanes, turned, 0.0))
    variants_ref[3] = low(jnp.where(low_lanes, 0.0, wide))


def allowed_block(seg_k, seg_q, diagonal):
    same = seg_k == seg_q
    if diagonal:
        rows = lax.broadcasted_iota(jnp.int32, same.shape, 0)
        lanes = lax.broadcasted_iota(jnp.int32, same.shape, 1)
        same = same & (rows <= lanes)
    return same


def attend_body(q_ref, k_ref, v_ref, seg_col_ref, seg_row_ref, mixed_ref, lse_ref, ks, vt, acc, stats):
    block = pl.program_id(1)

    @pl.when(block == 0)
    def _():
        place_heads(k_ref[...], ks)
        vt[...] = low(v_ref[...].astype(jnp.float32).T)

    acc[...] = jnp.zeros_like(acc)
    stats[0] = jnp.full((8, BLOCK), -1e30, jnp.float32)
    stats[1] = jnp.zeros((8, BLOCK), jnp.float32)
    seg_q = seg_row_ref[...]

    def step(j, diagonal):
        rows = pl.ds(pl.multiple_of(j * BLOCK, BLOCK), BLOCK)
        seg_k = seg_col_ref[rows, :]
        allowed = allowed_block(seg_k, seg_q, diagonal)
        for head in range(6):
            part, side, kv = head // 2, head % 2, head // 3
            q_tile = q_ref[:, part * WIDE : (part + 1) * WIDE]
            scores = mm_nt(ks[kv * 2 + side, rows, :], q_tile)
            scores = jnp.where(allowed, scores, -1e30)
            before = stats[0, head : head + 1, :]
            highest = jnp.maximum(before, jnp.max(scores, axis=0, keepdims=True))
            shrink = jnp.exp(before - highest)
            chances = jnp.exp(scores - highest)
            stats[0, head : head + 1, :] = highest
            stats[1, head : head + 1, :] = stats[1, head : head + 1, :] * shrink + jnp.sum(
                chances, axis=0, keepdims=True
            )
            values = vt[kv * HEAD : (kv + 1) * HEAD, rows]
            at = head * HEAD
            acc[at : at + HEAD, :] = acc[at : at + HEAD, :] * shrink + mm(values, low(chances))

    @pl.loop(0, block)
    def _(j):
        step(j, False)

    step(block, True)
    total = stats[1]
    for part in range(3):
        at = part * WIDE
        both = jnp.concatenate(
            [
                acc[at : at + HEAD, :] / total[2 * part : 2 * part + 1, :],
                acc[at + HEAD : at + WIDE, :] / total[2 * part + 1 : 2 * part + 2, :],
            ],
            axis=0,
        )
        mixed_ref[:, at : at + WIDE] = low(both.T)
    lse_ref[0] = stats[0] + jnp.log(jnp.maximum(total, 1e-30))


def attend(qkv, seg_col, seg_row):
    length = qkv.shape[0]
    pairs = KV_HEADS // 2
    q_tiles = HEADS * HEAD // WIDE
    return pl.pallas_call(
        attend_body,
        grid=(pairs, length // BLOCK),
        in_specs=[
            pl.BlockSpec((BLOCK, 3 * WIDE), lambda b, i: (i, b)),
            pl.BlockSpec((length, WIDE), lambda b, i: (0, q_tiles + b)),
            pl.BlockSpec((length, WIDE), lambda b, i: (0, q_tiles + pairs + b)),
            pl.BlockSpec((length, 1), lambda b, i: (0, 0)),
            pl.BlockSpec((1, BLOCK), lambda b, i: (0, i)),
        ],
        out_specs=[
            pl.BlockSpec((BLOCK, 3 * WIDE), lambda b, i: (i, b)),
            pl.BlockSpec((1, 8, BLOCK), lambda b, i: (b, 0, i)),
        ],
        out_shape=[
            jax.ShapeDtypeStruct((length, HEADS * HEAD), jnp.bfloat16),
            jax.ShapeDtypeStruct((pairs, 8, length), jnp.float32),
        ],
        scratch_shapes=[
            pltpu.VMEM((4, length, WIDE), jnp.bfloat16),
            pltpu.VMEM((WIDE, length), jnp.bfloat16),
            pltpu.VMEM((6 * HEAD, BLOCK), jnp.float32),
            pltpu.VMEM((2, 8, BLOCK), jnp.float32),
        ],
        cost_estimate=pl.CostEstimate(
            flops=16 * length * length * HEADS * HEAD // 2,
            bytes_accessed=6 * length * HEADS * HEAD,
            transcendentals=HEADS * length * length // 2,
        ),
        name="attend",
    )(qkv, qkv, qkv, seg_col, seg_row)


def attend_back_body(
    q_ref, k_ref, v_ref, grad_ref, mixed_ref, lse_ref, seg_col_ref, seg_row_ref, cos_ref, sin_ref,
    dq_ref, dk_ref, dv_ref, ks, vs, kt, k_acc, v_acc, q_acc, sides, delta
):
    block = pl.program_id(1)
    length = k_ref.shape[0]

    @pl.when(block == 0)
    def _():
        place_heads(k_ref[...], ks)
        place_heads(v_ref[...], vs)
        kt[...] = low(k_ref[...].astype(jnp.float32).T)
        k_acc[...] = jnp.zeros_like(k_acc)
        v_acc[...] = jnp.zeros_like(v_acc)

    q_acc[...] = jnp.zeros_like(q_acc)
    seg_q = seg_row_ref[...]
    low_lanes = lanes_below(BLOCK, WIDE, HEAD)
    zero = jnp.zeros((BLOCK, WIDE), jnp.bfloat16)
    for part in range(3):
        at = part * WIDE
        tile, grad = q_ref[:, at : at + WIDE], grad_ref[:, at : at + WIDE]
        sides[0, part, 0:BLOCK, :] = jnp.where(low_lanes, tile, zero)
        sides[0, part, BLOCK : 2 * BLOCK, :] = jnp.where(low_lanes, zero, tile)
        sides[1, part, 0:BLOCK, :] = jnp.where(low_lanes, grad, zero)
        sides[1, part, BLOCK : 2 * BLOCK, :] = jnp.where(low_lanes, zero, grad)
        product = (grad.astype(jnp.float32) * mixed_ref[:, at : at + WIDE].astype(jnp.float32)).T
        delta[2 * part : 2 * part + 1, :] = jnp.sum(product[:HEAD], axis=0, keepdims=True)
        delta[2 * part + 1 : 2 * part + 2, :] = jnp.sum(product[HEAD:], axis=0, keepdims=True)

    def step(j, diagonal):
        rows = pl.ds(pl.multiple_of(j * BLOCK, BLOCK), BLOCK)
        allowed = allowed_block(seg_col_ref[rows, :], seg_q, diagonal)
        for part in range(3):
            at = part * WIDE
            q_tile, grad_tile = q_ref[:, at : at + WIDE], grad_ref[:, at : at + WIDE]
            chances_pair, score_pair = [], []
            for side in range(2):
                head = 2 * part + side
                kv = head // 3
                scores = mm_nt(ks[kv * 2 + side, rows, :], q_tile)
                scores = jnp.where(allowed, scores, -1e30)
                chances = jnp.exp(scores - lse_ref[0, head : head + 1, :])
                onto = mm_nt(vs[kv * 2 + side, rows, :], grad_tile)
                score_grad = low(chances * (onto - delta[head : head + 1, :]))
                chances_pair.append(low(chances))
                score_pair.append(score_grad)
                to = head * HEAD
                q_acc[to : to + HEAD, :] += mm(kt[kv * HEAD : (kv + 1) * HEAD, rows], score_grad)
            v_acc[part, rows, :] += mm(jnp.concatenate(chances_pair, axis=1), sides[1, part])
            k_acc[part, rows, :] += mm(jnp.concatenate(score_pair, axis=1), sides[0, part])

    @pl.loop(0, block)
    def _(j):
        step(j, False)

    step(block, True)
    here = pl.ds(pl.multiple_of(block * BLOCK, BLOCK), BLOCK)
    for part in range(3):
        at = part * WIDE
        tile = q_acc[at : at + WIDE, :].T * HEAD ** (-0.5)
        tile = tile * cos_ref[here, :] - swap_halves(tile) * sin_ref[here, :]
        dq_ref[:, at : at + WIDE] = low(tile)

    @pl.when(block == length // BLOCK - 1)
    def _():
        for j in range(0, length, BLOCK):
            rows = slice(j, j + BLOCK)

            def gather(acc):
                first, middle, last = acc[0, rows, :], acc[1, rows, :], acc[2, rows, :]
                return middle + jnp.where(
                    low_lanes, first + pltpu.roll(first, HEAD, 1), last + pltpu.roll(last, HEAD, 1)
                )

            tile = gather(k_acc)
            tile = tile * cos_ref[rows, :] - swap_halves(tile) * sin_ref[rows, :]
            dk_ref[rows, :] = low(tile)
            dv_ref[rows, :] = low(gather(v_acc))


def attend_back(qkv, mixed_grad, mixed, lse, seg_col, seg_row, cosines, sines):
    length = qkv.shape[0]
    pairs = KV_HEADS // 2
    q_tiles = HEADS * HEAD // WIDE
    q_block = pl.BlockSpec((BLOCK, 3 * WIDE), lambda b, i: (i, b))
    kv_block = pl.BlockSpec((length, WIDE), lambda b, i: (0, b))
    table = pl.BlockSpec((length, WIDE), lambda b, i: (0, 0), pipeline_mode=pl.Buffered(1))
    return pl.pallas_call(
        attend_back_body,
        grid=(pairs, length // BLOCK),
        in_specs=[
            q_block,
            pl.BlockSpec((length, WIDE), lambda b, i: (0, q_tiles + b)),
            pl.BlockSpec((length, WIDE), lambda b, i: (0, q_tiles + pairs + b)),
            q_block,
            q_block,
            pl.BlockSpec((1, 8, BLOCK), lambda b, i: (b, 0, i)),
            pl.BlockSpec((length, 1), lambda b, i: (0, 0)),
            pl.BlockSpec((1, BLOCK), lambda b, i: (0, i)),
            table,
            table,
        ],
        out_specs=[q_block, kv_block, kv_block],
        out_shape=[
            jax.ShapeDtypeStruct((length, HEADS * HEAD), jnp.bfloat16),
            jax.ShapeDtypeStruct((length, KV_HEADS * HEAD), jnp.bfloat16),
            jax.ShapeDtypeStruct((length, KV_HEADS * HEAD), jnp.bfloat16),
        ],
        scratch_shapes=[
            pltpu.VMEM((4, length, WIDE), jnp.bfloat16),
            pltpu.VMEM((4, length, WIDE), jnp.bfloat16),
            pltpu.VMEM((WIDE, length), jnp.bfloat16),
            pltpu.VMEM((3, length, WIDE), jnp.float32),
            pltpu.VMEM((3, length, WIDE), jnp.float32),
            pltpu.VMEM((6 * HEAD, BLOCK), jnp.float32),
            pltpu.VMEM((2, 3, 2 * BLOCK, WIDE), jnp.bfloat16),
            pltpu.VMEM((8, BLOCK), jnp.float32),
        ],
        cost_estimate=pl.CostEstimate(
            flops=40 * length * length * HEADS * HEAD // 2,
            bytes_accessed=12 * length * HEADS * HEAD,
            transcendentals=HEADS * length * length // 2,
        ),
        name="attend_back",
    )(qkv, qkv, qkv, mixed_grad, mixed, lse, seg_col, seg_row, cosines, sines)


def feed_body(which_ref, normed_ref, turned_ref, c_ref, gate_ref, up_ref, down_ref,
              out_ref, back_ref, gate_grad_ref, up_grad_ref, down_grad_ref,
              hidden_t, gate_low, up_low):
    first = pl.program_id(0) == 0
    length, width = normed_ref.shape

    @pl.when(first)
    def _():
        out_ref[...] = jnp.zeros_like(out_ref)
        back_ref[...] = jnp.zeros_like(back_ref)

    for at in range(0, length, BLOCK):
        rows = slice(at, at + BLOCK)
        normed = normed_ref[rows, :]
        gate_sum = mm(normed, gate_ref[...])
        up_sum = mm(normed, up_ref[...])
        hidden_grad = mm_nt(c_ref[rows, :], down_ref[...])
        sigmoid = jax.nn.sigmoid(gate_sum)
        activated = gate_sum * sigmoid
        hidden = low(activated * up_sum)
        gate_grad = low(hidden_grad * up_sum * (sigmoid + activated * (1.0 - sigmoid)))
        up_grad = low(hidden_grad * activated)
        hidden_t[:, rows] = hidden.T
        gate_low[rows, :] = gate_grad
        up_low[rows, :] = up_grad
        out_ref[rows, :] += mm(hidden, down_ref[...])
        back_ref[rows, :] += mm_nt(gate_grad, gate_ref[...]) + mm_nt(up_grad, up_ref[...])
    step = 384
    for at in range(0, width, step):
        rows = slice(at, at + step)
        gate_grad_ref[rows, :] = low(mm(turned_ref[rows, :], gate_low[...]))
        up_grad_ref[rows, :] = low(mm(turned_ref[rows, :], up_low[...]))
        down_grad_ref[:, rows] = low(mm(hidden_t[...], c_ref[:, rows]))


def feed(which, normed, turned, c, gate, up, down):
    length, width = normed.shape
    wide = gate.shape[1] // 4
    whole = pl.BlockSpec((length, width), lambda t, w: (0, 0), pipeline_mode=pl.Buffered(1))
    columns = pl.BlockSpec((width, wide), lambda t, w: (0, w[0] + 2 * t))
    rows = pl.BlockSpec((wide, width), lambda t, w: (w[0] + 2 * t, 0))
    total = pl.BlockSpec((length, width), lambda t, w: (0, 0), pipeline_mode=pl.Buffered(1))
    columns_out = pl.BlockSpec((width, wide), lambda t, w: (0, t))
    return pl.pallas_call(
        feed_body,
        grid_spec=pltpu.PrefetchScalarGridSpec(
            num_scalar_prefetch=1,
            grid=(2,),
            in_specs=[
                whole,
                pl.BlockSpec((width, length), lambda t, w: (0, 0), pipeline_mode=pl.Buffered(1)),
                whole,
                columns,
                columns,
                rows,
            ],
            out_specs=[
                total,
                total,
                columns_out,
                columns_out,
                pl.BlockSpec((wide, width), lambda t, w: (t, 0)),
            ],
            scratch_shapes=[
                pltpu.VMEM((wide, length), jnp.bfloat16),
                pltpu.VMEM((length, wide), jnp.bfloat16),
                pltpu.VMEM((length, wide), jnp.bfloat16),
            ],
        ),
        out_shape=[
            jax.ShapeDtypeStruct((length, width), jnp.float32),
            jax.ShapeDtypeStruct((length, width), jnp.float32),
            jax.ShapeDtypeStruct((width, 2 * wide), jnp.bfloat16),
            jax.ShapeDtypeStruct((width, 2 * wide), jnp.bfloat16),
            jax.ShapeDtypeStruct((2 * wide, width), jnp.bfloat16),
        ],
        compiler_params=pltpu.CompilerParams(vmem_limit_bytes=VMEM_MOST),
        cost_estimate=pl.CostEstimate(
            flops=18 * length * width * wide * 2,
            bytes_accessed=12 * width * wide * 2 + 16 * length * width,
            transcendentals=length * wide * 2,
        ),
        name="feed",
    )(which, normed, turned, c, gate, up, down)


def shortened(array):
    return jax.tree.map(lambda a: a.astype(jnp.bfloat16) if a.dtype == jnp.float32 else a, array)


def product(left, right):
    return jnp.dot(left, right, preferred_element_type=jnp.float32)


def product_tn(left, right):
    return lax.dot_general(
        left, right, (((0,), (0,)), ((), ())), preferred_element_type=jnp.float32
    )


def product_nt(left, right):
    return lax.dot_general(
        left, right, (((1,), (1,)), ((), ())), preferred_element_type=jnp.float32
    )


def rotary_tables(positions, width):
    half_width = width // 2
    freqs = jnp.exp(
        jnp.arange(half_width, dtype=jnp.float32) * (-2.0 * math.log(rope_base) / width)
    )
    angles = positions[:, None] * freqs[None, :]
    return (jnp.cos(angles), jnp.sin(angles))


def rotate(values, cosines, sines):
    half_width = values.shape[-1] // 2
    first = values[..., :half_width]
    second = values[..., half_width:]
    return jnp.concatenate(
        [first * cosines - second * sines, second * cosines + first * sines], axis=-1
    )


def unrotate(values, cosines, sines):
    half_width = values.shape[-1] // 2
    first = values[..., :half_width]
    second = values[..., half_width:]
    return jnp.concatenate(
        [first * cosines + second * sines, second * cosines - first * sines], axis=-1
    )


def norm_back(grad_rows, gain, scaled, inverse):
    weighted = grad_rows * gain
    return inverse * (weighted - scaled * jnp.mean(weighted * scaled, axis=-1, keepdims=True))


def plain_local(
    inputs,
    segments,
    out_grad,
    attention_gain,
    query_weight,
    key_weight,
    value_weight,
    output_weight,
    feedforward_gain,
    gate_weight,
    up_weight,
    down_weight,
):
    gathered = (
        lax.all_gather(attention_gain, "fsdp", axis=0, tiled=True),
        lax.all_gather(query_weight, "fsdp", axis=0, tiled=True),
        lax.all_gather(key_weight, "fsdp", axis=0, tiled=True),
        lax.all_gather(value_weight, "fsdp", axis=0, tiled=True),
        lax.all_gather(output_weight, "fsdp", axis=0, tiled=True),
        lax.all_gather(feedforward_gain, "fsdp", axis=0, tiled=True),
        lax.all_gather(gate_weight, "fsdp", axis=0, tiled=True),
        lax.all_gather(up_weight, "fsdp", axis=0, tiled=True),
        lax.all_gather(down_weight, "fsdp", axis=0, tiled=True),
    )
    full_query, full_key, full_value, full_output = (
        gathered[1],
        gathered[2],
        gathered[3],
        gathered[4],
    )
    full_gate, full_up, full_down = (gathered[6], gathered[7], gathered[8])
    gain_attention = gathered[0].astype(jnp.float32)
    gain_feed = gathered[5].astype(jnp.float32)
    span = inputs.shape[1]
    length = segments.shape[1]
    groups_q = HEADS // KV_HEADS
    key_width = KV_HEADS * HEAD
    start = lax.axis_index("fsdp") * span
    query_pos = start + jnp.arange(span, dtype=jnp.int32)
    key_pos = jnp.arange(length, dtype=jnp.int32)
    cosines, sines = rotary_tables(query_pos.astype(jnp.float32), HEAD)
    cos_four, sin_four = (cosines[:, None, None, :], sines[:, None, None, :])
    cos_three, sin_three = (cosines[:, None, :], sines[:, None, :])
    causal = query_pos[:, None] >= key_pos[None, :]
    scale = HEAD ** (-0.5)

    def micro_step(totals, sequence):
        tokens, segment_row, cotangent = sequence
        own_segment = lax.dynamic_slice_in_dim(segment_row, start, span)
        allowed = causal & (own_segment[:, None] == segment_row[None, :])
        values = tokens.astype(jnp.float32)
        inverse_a = lax.rsqrt(jnp.mean(values * values, axis=-1, keepdims=True) + epsilon)
        scaled_a = values * inverse_a
        normed_a = (scaled_a * gain_attention).astype(jnp.bfloat16)
        query_lin = product(normed_a, full_query).reshape(span, KV_HEADS, groups_q, HEAD)
        queries = rotate(query_lin, cos_four, sin_four).astype(jnp.bfloat16)
        key_lin = product(normed_a, full_key).reshape(span, KV_HEADS, HEAD)
        key_rows = (
            rotate(key_lin, cos_three, sin_three).astype(jnp.bfloat16).reshape(span, key_width)
        )
        value_rows = product(normed_a, full_value).astype(jnp.bfloat16)
        all_keys, all_values = (
            lax.all_gather(key_rows, "fsdp", axis=0, tiled=True),
            lax.all_gather(value_rows, "fsdp", axis=0, tiled=True),
        )
        all_keys = all_keys.reshape(length, KV_HEADS, HEAD)
        all_values = all_values.reshape(length, KV_HEADS, HEAD)
        scores = (
            jnp.einsum("qhgd,khd->hgqk", queries, all_keys, preferred_element_type=jnp.float32)
            * scale
        )
        scores = jnp.where(allowed, scores, -1e30)
        highest = jnp.max(scores, axis=-1, keepdims=True)
        expo_scores = jnp.exp(scores - highest)
        attention = expo_scores / jnp.sum(expo_scores, axis=-1, keepdims=True)
        attention_low = attention.astype(jnp.bfloat16)
        mixed = jnp.einsum(
            "hgqk,khd->qhgd", attention_low, all_values, preferred_element_type=jnp.float32
        )
        mixed = mixed.reshape(span, HEADS * HEAD).astype(jnp.bfloat16)
        residual = values + product(mixed, full_output)
        inverse_f = lax.rsqrt(jnp.mean(residual * residual, axis=-1, keepdims=True) + epsilon)
        scaled_f = residual * inverse_f
        normed_f = (scaled_f * gain_feed).astype(jnp.bfloat16)
        gate_sum = product(normed_f, full_gate)
        up_sum = product(normed_f, full_up)
        sigmoid_gate = jax.nn.sigmoid(gate_sum)
        activated = gate_sum * sigmoid_gate
        hidden = (activated * up_sum).astype(jnp.bfloat16)
        result = (residual + product(hidden, full_down)).astype(jnp.bfloat16)
        down_wgrad = product_tn(hidden, cotangent)
        hidden_grad = product_nt(cotangent, full_down)
        gate_grad = (
            hidden_grad * up_sum * sigmoid_gate * (1.0 + gate_sum * (1.0 - sigmoid_gate))
        ).astype(jnp.bfloat16)
        up_grad = (hidden_grad * activated).astype(jnp.bfloat16)
        gate_wgrad = product_tn(normed_f, gate_grad)
        up_wgrad = product_tn(normed_f, up_grad)
        normed_f_grad = product_nt(gate_grad, full_gate) + product_nt(up_grad, full_up)
        feed_gain_grad = jnp.sum(normed_f_grad * scaled_f, axis=0)
        residual_grad = cotangent.astype(jnp.float32) + norm_back(
            normed_f_grad, gain_feed, scaled_f, inverse_f
        )
        residual_low = residual_grad.astype(jnp.bfloat16)
        output_wgrad = product_tn(mixed, residual_low)
        mixed_grad = (
            product_nt(residual_low, full_output)
            .astype(jnp.bfloat16)
            .reshape(span, KV_HEADS, groups_q, HEAD)
        )
        attention_grad = jnp.einsum(
            "qhgd,khd->hgqk", mixed_grad, all_values, preferred_element_type=jnp.float32
        )
        row_totals = jnp.sum(attention * attention_grad, axis=-1, keepdims=True)
        score_grad = (attention * (attention_grad - row_totals) * scale).astype(jnp.bfloat16)
        value_grads = jnp.einsum(
            "hgqk,qhgd->khd", attention_low, mixed_grad, preferred_element_type=jnp.float32
        ).reshape(length, key_width)
        key_grads = jnp.einsum(
            "hgqk,qhgd->khd", score_grad, queries, preferred_element_type=jnp.float32
        ).reshape(length, key_width)
        query_grad = jnp.einsum(
            "hgqk,khd->qhgd", score_grad, all_keys, preferred_element_type=jnp.float32
        )
        key_back, value_back = (
            lax.psum_scatter(key_grads, "fsdp", scatter_dimension=0, tiled=True),
            lax.psum_scatter(value_grads, "fsdp", scatter_dimension=0, tiled=True),
        )
        query_low = (
            unrotate(query_grad, cos_four, sin_four)
            .reshape(span, HEADS * HEAD)
            .astype(jnp.bfloat16)
        )
        key_low = (
            unrotate(key_back.reshape(span, KV_HEADS, HEAD), cos_three, sin_three)
            .reshape(span, key_width)
            .astype(jnp.bfloat16)
        )
        value_low = value_back.astype(jnp.bfloat16)
        query_wgrad = product_tn(normed_a, query_low)
        key_wgrad = product_tn(normed_a, key_low)
        value_wgrad = product_tn(normed_a, value_low)
        normed_a_grad = (
            product_nt(query_low, full_query)
            + product_nt(key_low, full_key)
            + product_nt(value_low, full_value)
        )
        attention_gain_term = jnp.sum(normed_a_grad * scaled_a, axis=0)
        token_grad = (
            residual_grad + norm_back(normed_a_grad, gain_attention, scaled_a, inverse_a)
        ).astype(jnp.bfloat16)
        terms = (
            attention_gain_term,
            query_wgrad,
            key_wgrad,
            value_wgrad,
            output_wgrad,
            feed_gain_grad,
            gate_wgrad,
            up_wgrad,
            down_wgrad,
        )
        totals = tuple((left + right for left, right in zip(totals, terms)))
        return (totals, (result, token_grad))

    initial = tuple((jnp.zeros(weight.shape, jnp.float32) for weight in gathered))
    totals, (outputs, input_grads) = lax.scan(micro_step, initial, (inputs, segments, out_grad))
    shards = jax.tree.map(
        lambda part: part.astype(jnp.float32),
        lax.psum_scatter(shortened(totals), "fsdp", scatter_dimension=0, tiled=True),
    )
    summed = lax.psum(shards, "group")
    return (
        outputs,
        input_grads,
        summed[0],
        summed[1],
        summed[2],
        summed[3],
        summed[4],
        summed[5],
        summed[6],
        summed[7],
        summed[8],
    )


class Places:
    def __init__(self, group_size):
        self.group = lax.axis_index("group")
        self.y = lax.axis_index("fsdp")
        self.size = group_size
        self.masks = {"core": 1, "x": 2, "zlo": 4, "zhi": 8}

    def bit(self, name):
        if name == "y":
            return self.y
        return (self.group // self.masks[name]) % 2

    def swap(self, array, name):
        if name == "y":
            return lax.ppermute(array, "fsdp", [(0, 1), (1, 0)])
        mask = self.masks[name]
        return lax.ppermute(array, "group", [(i, i ^ mask) for i in range(self.size)])


def part_of(array, axis, bit):
    size = array.shape[axis] // 2
    return lax.dynamic_slice_in_dim(array, bit * size, size, axis)


def add_up(terms):
    total = terms[0].astype(jnp.float32)
    for term in terms[1:]:
        total = total + term.astype(jnp.float32)
    return low(total)


def in_order(bit, own, other, axis):
    return jnp.where(
        bit == 0,
        jnp.concatenate([own, other], axis=axis),
        jnp.concatenate([other, own], axis=axis),
    )


def reduce_down(places, terms, stages):
    for name, axis in stages:
        bit = places.bit(name)
        sent = add_up([part_of(term, axis, 1 - bit) for term in terms])
        terms = [part_of(term, axis, bit) for term in terms] + [places.swap(sent, name)]
    return add_up(terms)


def gather_up(places, piece, stages):
    for name, axis in stages:
        piece = in_order(places.bit(name), piece, places.swap(piece, name), axis)
    return piece


def gather_rows(places, shard):
    rows = shard.shape[0]
    quarter = rows // 4
    core, x = places.bit("core"), places.bit("x")
    mine = x * 2 + core
    first = places.swap(lax.dynamic_slice_in_dim(shard, mine * quarter, quarter, 0), "y")
    second = places.swap(first, "x")
    third = places.swap(first, "core")
    fourth = places.swap(second, "core")
    here = places.y * rows
    there = (1 - places.y) * rows
    full = jnp.zeros((2 * rows, shard.shape[1]), shard.dtype)
    full = lax.dynamic_update_slice_in_dim(full, shard, here, 0)
    for piece, index in ((first, mine), (second, mine ^ 2), (third, mine ^ 1), (fourth, mine ^ 3)):
        full = lax.dynamic_update_slice_in_dim(full, piece, there + index * quarter, 0)
    return full


def norm_grad(grad, gain, scaled, inverse):
    weighted = grad * gain
    return inverse * (weighted - scaled * jnp.mean(weighted * scaled, axis=-1, keepdims=True))


def paired_local(
    group_size,
    inputs,
    segments,
    out_grad,
    attention_gain,
    query_weight,
    key_weight,
    value_weight,
    output_weight,
    feedforward_gain,
    gate_weight,
    up_weight,
    down_weight,
):
    places = Places(group_size)
    y = places.y
    span, length, width = inputs.shape[1], segments.shape[1], inputs.shape[2]
    q_width = query_weight.shape[1]

    def whole_sequence(blocks):
        own = lax.dynamic_index_in_dim(blocks, y, 0, False)
        other = places.swap(lax.dynamic_index_in_dim(blocks, 1 - y, 0, False), "y")
        return in_order(y, own, other, 0)

    def own_blocks(rows):
        own = part_of(rows, 0, y)
        other = places.swap(part_of(rows, 0, 1 - y), "y")
        return in_order(y, own[None], other[None], 0)

    gains = jnp.stack([attention_gain, feedforward_gain])
    gains = in_order(y, gains, places.swap(gains, "y"), 1).astype(jnp.float32)
    gain_a, gain_f = gains[0:1], gains[1:2]
    tokens = whole_sequence(inputs)
    qkv_weight = gather_rows(places, jnp.concatenate([query_weight, key_weight, value_weight], axis=1))
    mix_weight = gather_rows(places, output_weight)
    full_gate = gather_rows(places, gate_weight)
    full_up = gather_rows(places, up_weight)
    full_down = gather_rows(places, down_weight)
    c = whole_sequence(out_grad)

    segment = lax.dynamic_index_in_dim(segments, y, 0, False)
    seg_col, seg_row = segment[:, None], segment[None, :]
    cosines, sines = rope_tables(length)
    normed_a, qkv = project(tokens, gain_a, qkv_weight, cosines, sines)
    mixed, lse = attend(qkv, seg_col, seg_row)

    values = tokens.astype(jnp.float32)
    residual = values + mm(mixed, mix_weight)
    inverse_f = lax.rsqrt(jnp.mean(residual * residual, axis=-1, keepdims=True) + epsilon)
    normed_f = low(residual * inverse_f * gain_f)
    turned_f = normed_f.T

    core = places.bit("core")
    theirs = feed((1 - core).reshape(1), normed_f, turned_f, c, full_gate, full_up, full_down)
    mine = feed(core.reshape(1), normed_f, turned_f, c, full_gate, full_up, full_down)
    result = low(residual + theirs[0] + mine[0])
    outputs = own_blocks(result)

    normed_f_grad = theirs[1] + mine[1]
    scaled_f = residual * inverse_f
    feed_gain_term = jnp.sum(normed_f_grad * scaled_f, axis=0)
    residual_grad = c.astype(jnp.float32) + norm_grad(normed_f_grad, gain_f, scaled_f, inverse_f)
    residual_low = low(residual_grad)
    mix_term = low(mm_tn(mixed, residual_low))
    mixed_grad = low(mm_nt(residual_low, mix_weight))

    orders = (("y", "x", "zlo", "zhi"), ("x", "zlo", "y", "zhi"), ("zlo", "y", "x", "zhi"))
    backs = (("zhi", "zlo", "x"), ("zhi", "x", "zlo"), ("zhi", "zlo", "x"))
    dims = {"y": 0, "x": 1, "zlo": 2, "zhi": 3}
    pieces = []
    for index in range(3):
        shape = mine[2 + index].shape
        split = (2, 2, 2, shape[0] // 8, shape[1])
        terms = [mine[2 + index].reshape(split), places.swap(theirs[2 + index], "core").reshape(split)]
        piece = reduce_down(places, terms, [(name, dims[name]) for name in orders[index]])
        pieces.append(gather_up(places, piece, [(name, dims[name]) for name in backs[index]]))

    def hidden_columns(piece):
        wide = piece.shape[-1] // 2
        piece = piece.reshape(width // 2, 2, wide)
        other = places.swap(piece, "core")
        return in_order(core, piece[:, :, None], other[:, :, None], 2).reshape(width // 2, 4 * wide)

    gate_sum_grad = hidden_columns(pieces[0]).astype(jnp.float32)
    up_sum_grad = hidden_columns(pieces[1]).astype(jnp.float32)
    down_piece = pieces[2].reshape(-1, width)
    down_sum_grad = in_order(core, down_piece, places.swap(down_piece, "core"), 0).astype(jnp.float32)

    dq, dk, dv = attend_back(qkv, mixed_grad, mixed, lse, seg_col, seg_row, cosines, sines)
    lows = jnp.concatenate([dq, dk, dv], axis=1)
    qkv_term = low(mm_tn(normed_a, lows))
    normed_a_grad = mm_nt(lows, qkv_weight)
    inverse_a = lax.rsqrt(jnp.mean(values * values, axis=-1, keepdims=True) + epsilon)
    scaled_a = values * inverse_a
    attention_gain_term = jnp.sum(normed_a_grad * scaled_a, axis=0)
    token_grad = low(residual_grad + norm_grad(normed_a_grad, gain_a, scaled_a, inverse_a))
    input_grads = own_blocks(token_grad)

    dims = {"y": 0, "core": 1, "x": 2, "zlo": 3, "zhi": 4}

    def whole_sum(term, order, back):
        term = term.reshape(2, 2, 2, 2, term.shape[0] // 16, term.shape[1])
        piece = reduce_down(places, [term], [(name, dims[name]) for name in order])
        piece = gather_up(places, piece, [(name, dims[name]) for name in back])
        return piece.reshape(-1, piece.shape[-1])

    mix_sum_grad = whole_sum(
        mix_term, ("core", "x", "y", "zlo", "zhi"), ("zhi", "zlo", "x", "core")
    ).astype(jnp.float32)
    third = qkv_term.shape[1] // 3
    qkv_sum = jnp.concatenate(
        [
            whole_sum(
                qkv_term[:, i * third : (i + 1) * third],
                ("core",) + orders[i],
                backs[i] + ("core",),
            )
            for i in range(3)
        ],
        axis=1,
    ).astype(jnp.float32)

    gain_terms = jnp.stack([attention_gain_term, feed_gain_term])
    for name in ("core", "y", "x", "zlo", "zhi"):
        gain_terms = gain_terms + places.swap(gain_terms, name)
    gain_grads = part_of(gain_terms, 1, y)
    k_width = key_weight.shape[1]
    return (
        outputs,
        input_grads,
        gain_grads[0],
        qkv_sum[:, :q_width],
        qkv_sum[:, q_width : q_width + k_width],
        qkv_sum[:, q_width + k_width :],
        mix_sum_grad,
        gain_grads[1],
        gate_sum_grad,
        up_sum_grad,
        down_sum_grad,
    )


def solution(mesh):
    placed = (
        P("group", "fsdp", None),
        P("group", None),
        P("group", "fsdp", None),
        P("fsdp"),
        P("fsdp", None),
        P("fsdp", None),
        P("fsdp", None),
        P("fsdp", None),
        P("fsdp"),
        P("fsdp", None),
        P("fsdp", None),
        P("fsdp", None),
    )
    group_size, fsdp_size = mesh.shape["group"], mesh.shape["fsdp"]

    def local(*arrays):
        if group_size == 16 and fsdp_size == 2 and arrays[0].shape[0] == 2:
            return paired_local(group_size, *arrays)
        return plain_local(*arrays)

    return jax.shard_map(
        local,
        mesh=mesh,
        in_specs=placed,
        out_specs=(
            P("group", "fsdp", None),
            P("group", "fsdp", None),
            P("fsdp"),
            P("fsdp", None),
            P("fsdp", None),
            P("fsdp", None),
            P("fsdp", None),
            P("fsdp"),
            P("fsdp", None),
            P("fsdp", None),
            P("fsdp", None),
        ),
        check_vma=False,
    )
```

```python
import functools
import math

import jax
import jax.numpy as jnp
from jax import lax
from jax.experimental import pallas as pl
from jax.experimental.pallas import tpu as pltpu
from jax.sharding import PartitionSpec as P

HEADS = 18
KV_HEADS = 6
HEAD = 64
epsilon = 1e-05
rope_base = 10000.0
BLOCK = 256
WIDE = 128
VMEM_MOST = 66 * 1024 * 1024 - 3 * 1024 * 1024


def mm(left, right):
    return jnp.dot(left, right, preferred_element_type=jnp.float32)


def mm_nt(left, right):
    return lax.dot_general(
        left, right, (((1,), (1,)), ((), ())), preferred_element_type=jnp.float32
    )


def mm_tn(left, right):
    return lax.dot_general(
        left, right, (((0,), (0,)), ((), ())), preferred_element_type=jnp.float32
    )


def low(values):
    return values.astype(jnp.bfloat16)


def lanes_below(rows, period, limit):
    lane = lax.broadcasted_iota(jnp.int32, (rows, WIDE), 1)
    return lane % period < limit


def swap_halves(tile):
    ahead = pltpu.roll(tile, WIDE - HEAD // 2, 1)
    behind = pltpu.roll(tile, HEAD // 2, 1)
    return jnp.where(lanes_below(tile.shape[0], HEAD, HEAD // 2), ahead, behind)


def rope_tables(length):
    half_width = HEAD // 2
    freqs = jnp.exp(
        jnp.arange(half_width, dtype=jnp.float32) * (-2.0 * math.log(rope_base) / HEAD)
    )
    angles = jnp.arange(length, dtype=jnp.float32)[:, None] * freqs[None, :]
    cosines, sines = jnp.cos(angles), jnp.sin(angles)
    return (
        jnp.concatenate([cosines] * 4, axis=1),
        jnp.concatenate([-sines, sines] * 2, axis=1),
    )


def project_body(x_ref, gain_ref, w_ref, cos_ref, sin_ref, normed_ref, qkv_ref):
    values = x_ref[...].astype(jnp.float32)
    inverse = lax.rsqrt(jnp.mean(values * values, axis=-1, keepdims=True) + epsilon)
    normed = low(values * inverse * gain_ref[...])
    normed_ref[...] = normed
    cosines, sines = cos_ref[...], sin_ref[...]
    width = qkv_ref.shape[1]
    q_width, k_width = HEADS * HEAD, KV_HEADS * HEAD
    step = 384
    for at in range(0, width, step):
        wide = mm(normed, w_ref[:, at : at + step])
        for part in range(0, step, WIDE):
            tile = wide[:, part : part + WIDE]
            if at + part < q_width + k_width:
                tile = tile * cosines + swap_halves(tile) * sines
            if at + part < q_width:
                tile = tile * HEAD ** (-0.5)
            qkv_ref[:, at + part : at + part + WIDE] = low(tile)


def project(x, gain, w, cosines, sines):
    length, width = x.shape
    out = w.shape[1]
    rows = pl.BlockSpec((BLOCK, width), lambda i: (i, 0))
    table = pl.BlockSpec((BLOCK, WIDE), lambda i: (i, 0))
    return pl.pallas_call(
        project_body,
        grid=(length // BLOCK,),
        in_specs=[
            rows,
            pl.BlockSpec((1, width), lambda i: (0, 0)),
            pl.BlockSpec((width, out), lambda i: (0, 0), pipeline_mode=pl.Buffered(1)),
            table,
            table,
        ],
        out_specs=[rows, pl.BlockSpec((BLOCK, out), lambda i: (i, 0))],
        out_shape=[
            jax.ShapeDtypeStruct((length, width), jnp.bfloat16),
            jax.ShapeDtypeStruct((length, out), jnp.bfloat16),
        ],
        cost_estimate=pl.CostEstimate(
            flops=2 * length * width * out,
            bytes_accessed=2 * (2 * length * width + length * out + width * out),
            transcendentals=0,
        ),
        name="project",
    )(x, gain, w, cosines, sines)


MESH = pl.DeviceIdType.MESH
MASKS = {"core": 1, "x": 2, "zlo": 4, "zhi": 8}


def bit_of(name):
    if name == "y":
        return lax.axis_index("fsdp")
    return (lax.axis_index("group") // MASKS[name]) % 2


def peer_of(name):
    if name == "y":
        return {"fsdp": 1 - lax.axis_index("fsdp")}
    return {"group": lax.axis_index("group") + MASKS[name] * (1 - 2 * bit_of(name))}


def greet(names):
    barrier = pltpu.get_barrier_semaphore()
    for name in names:
        pl.semaphore_signal(barrier, inc=1, device_id=peer_of(name), device_id_type=MESH)
    pl.semaphore_wait(barrier, len(names))


def across(source, target, sems, slot, name):
    return pltpu.make_async_remote_copy(
        src_ref=source,
        dst_ref=target,
        send_sem=sems.at[0, slot],
        recv_sem=sems.at[1, slot],
        device_id=peer_of(name),
        device_id_type=MESH,
    )


class Spread:
    def __init__(self, shard, full, order, sems, slot, columns=None):
        self.shard, self.full, self.order, self.sems, self.slot = shard, full, order, sems, slot
        self.columns = columns

    def copy(self, stage):
        y = lax.axis_index("fsdp")
        index = 0
        for at, name in enumerate(self.order):
            index = index + bit_of(name) * 2**at
        slot = self.slot + stage
        where = (slice(None), slice(None)) if self.columns is None else (slice(None), self.columns)
        if stage == 0:
            return across(
                self.shard.at[index], self.full.at[(y * 8 + index,) + where], self.sems, slot, "y"
            )
        count = 2 ** (stage - 1)
        block = self.full.at[(pl.ds((1 - y) * 8 + index // count * count, count),) + where]
        return across(block, block, self.sems, slot, self.order[stage - 1])

    def advance(self, stage):
        if stage >= 0:
            self.copy(stage).wait_recv()
        if stage < len(self.order):
            self.copy(stage + 1).start()

    def finish(self):
        for stage in range(len(self.order) + 1):
            self.copy(stage).wait_send()


def fetch_body(inputs, query, key, value, gains, tokens, weight, both_gains,
               held, held_weight, sems, near):
    y = lax.axis_index("fsdp")
    q_width, k_width = query.shape[2], key.shape[2]
    places = (
        slice(0, q_width),
        slice(q_width, q_width + k_width),
        slice(q_width + k_width, q_width + 2 * k_width),
    )
    shards = (query, key, value)
    loads = [pltpu.make_async_copy(inputs.at[y], held, near.at[0])] + [
        pltpu.make_async_copy(shard, held_weight.at[:, :, place], near.at[1 + at])
        for at, (shard, place) in enumerate(zip(shards, places))
    ]
    for load in loads:
        load.start()
    greet(("y", "x", "zlo", "core"))
    index = bit_of("x") + 2 * bit_of("zlo") + 4 * bit_of("core")
    first = [
        across(shard.at[index], weight.at[y * 8 + index, :, place], sems, at, "y")
        for at, (shard, place) in enumerate(zip(shards, places))
    ]
    span = held.shape[0]
    swap = across(
        inputs.at[1 - y], tokens.at[pl.ds(pl.multiple_of(y * span, span), span)], sems, 3, "y"
    )
    gain_swap = across(gains, both_gains.at[y], sems, 4, "y")
    for copy in first + [gain_swap, swap]:
        copy.start()
    for load in loads:
        load.wait()
    stores = [
        pltpu.make_async_copy(
            held, tokens.at[pl.ds(pl.multiple_of(y * span, span), span)], near.at[4]
        ),
        pltpu.make_async_copy(held_weight, weight.at[pl.ds(y * 8, 8)], near.at[5]),
        pltpu.make_async_copy(gains, both_gains.at[y], near.at[6]),
    ]
    for store in stores:
        store.start()
    for copy in first:
        copy.wait_recv()
    later = []
    for at, name in enumerate(("x", "zlo", "core")):
        count = 2**at
        block = weight.at[pl.ds((1 - y) * 8 + index // count * count, count)]
        copy = across(block, block, sems, 5 + at, name)
        copy.start()
        copy.wait_recv()
        later.append(copy)
    swap.wait_recv()
    gain_swap.wait_recv()
    for copy in first + [gain_swap, swap] + later:
        copy.wait_send()
    for store in stores:
        store.wait()


def fetch(inputs, query, key, value, gains):
    span, width = inputs.shape[1:]
    total = query.shape[1] + 2 * key.shape[1]
    eight = lambda shard: shard.reshape(8, shard.shape[0] // 8, shard.shape[1])
    rows = query.shape[0] // 8
    anywhere = pl.BlockSpec(memory_space=pl.ANY)
    tokens, weight, both_gains = pl.pallas_call(
        fetch_body,
        in_specs=[anywhere] * 5,
        out_specs=[anywhere] * 3,
        out_shape=[
            jax.ShapeDtypeStruct((2 * span, width), inputs.dtype),
            jax.ShapeDtypeStruct((16, rows, total), query.dtype),
            jax.ShapeDtypeStruct((2,) + gains.shape, gains.dtype),
        ],
        scratch_shapes=[
            pltpu.VMEM((span, width), inputs.dtype),
            pltpu.VMEM((8, rows, total), query.dtype),
            pltpu.SemaphoreType.DMA((2, 8)),
            pltpu.SemaphoreType.DMA((7,)),
        ],
        compiler_params=pltpu.CompilerParams(collective_id=1, has_side_effects=True),
        name="fetch",
    )(inputs, eight(query), eight(key), eight(value), gains)
    return tokens, weight.reshape(16 * rows, total), both_gains


def place_heads(tile, variants_ref):
    wide = tile.astype(jnp.float32)
    turned = pltpu.roll(wide, HEAD, 1)
    low_lanes = lanes_below(tile.shape[0], WIDE, HEAD)
    variants_ref[0] = low(jnp.where(low_lanes, wide, 0.0))
    variants_ref[1] = low(jnp.where(low_lanes, 0.0, turned))
    variants_ref[2] = low(jnp.where(low_lanes, turned, 0.0))
    variants_ref[3] = low(jnp.where(low_lanes, 0.0, wide))


def allowed_block(seg_k, seg_q, diagonal):
    same = seg_k == seg_q
    if diagonal:
        rows = lax.broadcasted_iota(jnp.int32, same.shape, 0)
        lanes = lax.broadcasted_iota(jnp.int32, same.shape, 1)
        same = same & (rows <= lanes)
    return same


def attend_body(
    q_ref, k_ref, v_ref, seg_col_ref, seg_row_ref, out_grad, mix_w, gate_w, up_w, down_w,
    mixed_ref, lse_ref, whole_grad, mix_full, gate_full, up_full, down_full,
    ks, vt, acc, stats, sems, near, held_mix, held_gate, held_up, held_down, held_grad
):
    block = pl.program_id(1)
    now = pl.program_id(0) * pl.num_programs(1) + block
    most = pl.num_programs(0) * pl.num_programs(1) - 1
    y = lax.axis_index("fsdp")
    spreads = {
        "mix": Spread(mix_w, mix_full, ("x", "zlo", "core"), sems, 0),
        "gate": Spread(gate_w, gate_full, ("zlo", "x", "core"), sems, 4),
        "up": Spread(up_w, up_full, ("x", "zlo", "core"), sems, 8),
        "down": Spread(down_w, down_full, ("zlo", "x", "core"), sems, 12),
    }
    span = out_grad.shape[1]
    mine = whole_grad.at[pl.ds(pl.multiple_of(y * span, span), span)]
    grad_swap = across(out_grad.at[1 - y], mine, sems, 16, "y")
    half = pl.ds(y * 8, 8)
    own = (
        (mix_w, held_mix, mix_full.at[half]),
        (gate_w, held_gate, gate_full.at[half]),
        (up_w, held_up, up_full.at[half]),
        (down_w, held_down, down_full.at[half]),
        (out_grad.at[y], held_grad, mine),
    )
    loads = [pltpu.make_async_copy(a, b, near.at[0, at]) for at, (a, b, _) in enumerate(own)]
    stores = [pltpu.make_async_copy(b, c, near.at[1, at]) for at, (_, b, c) in enumerate(own)]
    plan = {
        1: (("mix", 0),),
        2: (("mix", 1),),
        3: (("gate", 0), ("mix", 2)),
        5: (("up", 0), ("gate", 1)),
        7: (("down", 0), ("up", 1)),
        9: (("gate", 2), ("down", 1)),
        10: (("up", 2),),
    }

    @pl.when(now == 0)
    def _():
        for load in loads:
            load.start()
        greet(("y", "x", "zlo", "core"))
        for name in ("mix", "gate", "up", "down"):
            spreads[name].advance(-1)
        grad_swap.start()

    @pl.when(now == 1)
    def _():
        for load, store in zip(loads, stores):
            load.wait()
            store.start()

    for at, steps in plan.items():

        @pl.when(now == at)
        def _(steps=steps):
            for name, stage in steps:
                spreads[name].advance(stage)

    @pl.when(block == 0)
    def _():
        place_heads(k_ref[...], ks)
        vt[...] = low(v_ref[...].astype(jnp.float32).T)

    acc[...] = jnp.zeros_like(acc)
    stats[0] = jnp.full((8, BLOCK), -1e30, jnp.float32)
    stats[1] = jnp.zeros((8, BLOCK), jnp.float32)
    seg_q = seg_row_ref[...]

    def step(j, diagonal):
        rows = pl.ds(pl.multiple_of(j * BLOCK, BLOCK), BLOCK)
        seg_k = seg_col_ref[rows, :]
        allowed = allowed_block(seg_k, seg_q, diagonal)
        for head in range(6):
            part, side, kv = head // 2, head % 2, head // 3
            q_tile = q_ref[:, part * WIDE : (part + 1) * WIDE]
            scores = mm_nt(ks[kv * 2 + side, rows, :], q_tile)
            scores = jnp.where(allowed, scores, -1e30)
            before = stats[0, head : head + 1, :]
            highest = jnp.maximum(before, jnp.max(scores, axis=0, keepdims=True))
            shrink = jnp.exp(before - highest)
            chances = jnp.exp(scores - highest)
            stats[0, head : head + 1, :] = highest
            stats[1, head : head + 1, :] = stats[1, head : head + 1, :] * shrink + jnp.sum(
                chances, axis=0, keepdims=True
            )
            values = vt[kv * HEAD : (kv + 1) * HEAD, rows]
            at = head * HEAD
            acc[at : at + HEAD, :] = acc[at : at + HEAD, :] * shrink + mm(values, low(chances))

    @pl.loop(0, block)
    def _(j):
        step(j, False)

    step(block, True)
    total = stats[1]
    for part in range(3):
        at = part * WIDE
        both = jnp.concatenate(
            [
                acc[at : at + HEAD, :] / total[2 * part : 2 * part + 1, :],
                acc[at + HEAD : at + WIDE, :] / total[2 * part + 1 : 2 * part + 2, :],
            ],
            axis=0,
        )
        mixed_ref[:, at : at + WIDE] = low(both.T)
    lse_ref[0] = stats[0] + jnp.log(jnp.maximum(total, 1e-30))

    @pl.when(now == most)
    def _():
        spreads["down"].advance(2)
        for spread in spreads.values():
            spread.advance(3)
            spread.finish()
        grad_swap.wait()
        for store in stores:
            store.wait()


def attend(qkv, seg_col, seg_row, out_grad, mix_w, gate_w, up_w, down_w):
    length = qkv.shape[0]
    pairs = KV_HEADS // 2
    q_tiles = HEADS * HEAD // WIDE
    anywhere = pl.BlockSpec(memory_space=pl.ANY)
    shards = [w.reshape(8, w.shape[0] // 8, w.shape[1]) for w in (mix_w, gate_w, up_w, down_w)]
    fulls = [jax.ShapeDtypeStruct((16,) + w.shape[1:], w.dtype) for w in shards]
    found = pl.pallas_call(
        attend_body,
        grid=(pairs, length // BLOCK),
        in_specs=[
            pl.BlockSpec((BLOCK, 3 * WIDE), lambda b, i: (i, b)),
            pl.BlockSpec((length, WIDE), lambda b, i: (0, q_tiles + b)),
            pl.BlockSpec((length, WIDE), lambda b, i: (0, q_tiles + pairs + b)),
            pl.BlockSpec((length, 1), lambda b, i: (0, 0)),
            pl.BlockSpec((1, BLOCK), lambda b, i: (0, i)),
        ]
        + [anywhere] * 5,
        out_specs=[
            pl.BlockSpec((BLOCK, 3 * WIDE), lambda b, i: (i, b)),
            pl.BlockSpec((1, 8, BLOCK), lambda b, i: (b, 0, i)),
        ]
        + [anywhere] * 5,
        out_shape=[
            jax.ShapeDtypeStruct((length, HEADS * HEAD), jnp.bfloat16),
            jax.ShapeDtypeStruct((pairs, 8, length), jnp.float32),
            jax.ShapeDtypeStruct((length, out_grad.shape[2]), out_grad.dtype),
        ]
        + fulls,
        scratch_shapes=[
            pltpu.VMEM((4, length, WIDE), jnp.bfloat16),
            pltpu.VMEM((WIDE, length), jnp.bfloat16),
            pltpu.VMEM((6 * HEAD, BLOCK), jnp.float32),
            pltpu.VMEM((2, 8, BLOCK), jnp.float32),
            pltpu.SemaphoreType.DMA((2, 17)),
            pltpu.SemaphoreType.DMA((2, 5)),
        ]
        + [pltpu.VMEM(w.shape, w.dtype) for w in shards]
        + [pltpu.VMEM(out_grad.shape[1:], out_grad.dtype)],
        compiler_params=pltpu.CompilerParams(
            collective_id=2, has_side_effects=True, vmem_limit_bytes=VMEM_MOST
        ),
        cost_estimate=pl.CostEstimate(
            flops=16 * length * length * HEADS * HEAD // 2,
            bytes_accessed=6 * length * HEADS * HEAD,
            transcendentals=HEADS * length * length // 2,
        ),
        name="attend",
    )(qkv, qkv, qkv, seg_col, seg_row, out_grad, *shards)
    return tuple(found[:3]) + tuple(w.reshape(-1, w.shape[2]) for w in found[3:])


def attend_back_body(
    q_ref, k_ref, v_ref, grad_ref, mixed_ref, lse_ref, seg_col_ref, seg_row_ref, cos_ref, sin_ref,
    dq_ref, dk_ref, dv_ref, ks, vs, kt, k_acc, v_acc, q_acc, sides, delta
):
    block = pl.program_id(1)
    length = k_ref.shape[0]

    @pl.when(block == 0)
    def _():
        place_heads(k_ref[...], ks)
        place_heads(v_ref[...], vs)
        kt[...] = low(k_ref[...].astype(jnp.float32).T)
        k_acc[...] = jnp.zeros_like(k_acc)
        v_acc[...] = jnp.zeros_like(v_acc)

    q_acc[...] = jnp.zeros_like(q_acc)
    seg_q = seg_row_ref[...]
    low_lanes = lanes_below(BLOCK, WIDE, HEAD)
    zero = jnp.zeros((BLOCK, WIDE), jnp.bfloat16)
    for part in range(3):
        at = part * WIDE
        tile, grad = q_ref[:, at : at + WIDE], grad_ref[:, at : at + WIDE]
        sides[0, part, 0:BLOCK, :] = jnp.where(low_lanes, tile, zero)
        sides[0, part, BLOCK : 2 * BLOCK, :] = jnp.where(low_lanes, zero, tile)
        sides[1, part, 0:BLOCK, :] = jnp.where(low_lanes, grad, zero)
        sides[1, part, BLOCK : 2 * BLOCK, :] = jnp.where(low_lanes, zero, grad)
        product = (grad.astype(jnp.float32) * mixed_ref[:, at : at + WIDE].astype(jnp.float32)).T
        delta[2 * part : 2 * part + 1, :] = jnp.sum(product[:HEAD], axis=0, keepdims=True)
        delta[2 * part + 1 : 2 * part + 2, :] = jnp.sum(product[HEAD:], axis=0, keepdims=True)

    def step(j, diagonal):
        rows = pl.ds(pl.multiple_of(j * BLOCK, BLOCK), BLOCK)
        allowed = allowed_block(seg_col_ref[rows, :], seg_q, diagonal)
        for part in range(3):
            at = part * WIDE
            q_tile, grad_tile = q_ref[:, at : at + WIDE], grad_ref[:, at : at + WIDE]
            chances_pair, score_pair = [], []
            for side in range(2):
                head = 2 * part + side
                kv = head // 3
                scores = mm_nt(ks[kv * 2 + side, rows, :], q_tile)
                scores = jnp.where(allowed, scores, -1e30)
                chances = jnp.exp(scores - lse_ref[0, head : head + 1, :])
                onto = mm_nt(vs[kv * 2 + side, rows, :], grad_tile)
                score_grad = low(chances * (onto - delta[head : head + 1, :]))
                chances_pair.append(low(chances))
                score_pair.append(score_grad)
                to = head * HEAD
                q_acc[to : to + HEAD, :] += mm(kt[kv * HEAD : (kv + 1) * HEAD, rows], score_grad)
            v_acc[part, rows, :] += mm(jnp.concatenate(chances_pair, axis=1), sides[1, part])
            k_acc[part, rows, :] += mm(jnp.concatenate(score_pair, axis=1), sides[0, part])

    @pl.loop(0, block)
    def _(j):
        step(j, False)

    step(block, True)
    here = pl.ds(pl.multiple_of(block * BLOCK, BLOCK), BLOCK)
    for part in range(3):
        at = part * WIDE
        tile = q_acc[at : at + WIDE, :].T * HEAD ** (-0.5)
        tile = tile * cos_ref[here, :] - swap_halves(tile) * sin_ref[here, :]
        dq_ref[:, at : at + WIDE] = low(tile)

    @pl.when(block == length // BLOCK - 1)
    def _():
        for j in range(0, length, BLOCK):
            rows = slice(j, j + BLOCK)

            def gather(acc):
                first, middle, last = acc[0, rows, :], acc[1, rows, :], acc[2, rows, :]
                return middle + jnp.where(
                    low_lanes, first + pltpu.roll(first, HEAD, 1), last + pltpu.roll(last, HEAD, 1)
                )

            tile = gather(k_acc)
            tile = tile * cos_ref[rows, :] - swap_halves(tile) * sin_ref[rows, :]
            dk_ref[rows, :] = low(tile)
            dv_ref[rows, :] = low(gather(v_acc))


def attend_back(qkv, mixed_grad, mixed, lse, seg_col, seg_row, cosines, sines):
    length = qkv.shape[0]
    pairs = KV_HEADS // 2
    q_tiles = HEADS * HEAD // WIDE
    q_block = pl.BlockSpec((BLOCK, 3 * WIDE), lambda b, i: (i, b))
    kv_block = pl.BlockSpec((length, WIDE), lambda b, i: (0, b))
    table = pl.BlockSpec((length, WIDE), lambda b, i: (0, 0), pipeline_mode=pl.Buffered(1))
    return pl.pallas_call(
        attend_back_body,
        grid=(pairs, length // BLOCK),
        in_specs=[
            q_block,
            pl.BlockSpec((length, WIDE), lambda b, i: (0, q_tiles + b)),
            pl.BlockSpec((length, WIDE), lambda b, i: (0, q_tiles + pairs + b)),
            q_block,
            q_block,
            pl.BlockSpec((1, 8, BLOCK), lambda b, i: (b, 0, i)),
            pl.BlockSpec((length, 1), lambda b, i: (0, 0)),
            pl.BlockSpec((1, BLOCK), lambda b, i: (0, i)),
            table,
            table,
        ],
        out_specs=[q_block, kv_block, kv_block],
        out_shape=[
            jax.ShapeDtypeStruct((length, HEADS * HEAD), jnp.bfloat16),
            jax.ShapeDtypeStruct((length, KV_HEADS * HEAD), jnp.bfloat16),
            jax.ShapeDtypeStruct((length, KV_HEADS * HEAD), jnp.bfloat16),
        ],
        scratch_shapes=[
            pltpu.VMEM((4, length, WIDE), jnp.bfloat16),
            pltpu.VMEM((4, length, WIDE), jnp.bfloat16),
            pltpu.VMEM((WIDE, length), jnp.bfloat16),
            pltpu.VMEM((3, length, WIDE), jnp.float32),
            pltpu.VMEM((3, length, WIDE), jnp.float32),
            pltpu.VMEM((6 * HEAD, BLOCK), jnp.float32),
            pltpu.VMEM((2, 3, 2 * BLOCK, WIDE), jnp.bfloat16),
            pltpu.VMEM((8, BLOCK), jnp.float32),
        ],
        cost_estimate=pl.CostEstimate(
            flops=40 * length * length * HEADS * HEAD // 2,
            bytes_accessed=12 * length * HEADS * HEAD,
            transcendentals=HEADS * length * length // 2,
        ),
        name="attend_back",
    )(qkv, qkv, qkv, mixed_grad, mixed, lse, seg_col, seg_row, cosines, sines)


def feed_body(which_ref, normed_ref, turned_ref, c_ref, gate_ref, up_ref, down_ref,
              out_ref, back_ref, gate_grad_ref, up_grad_ref, down_grad_ref,
              hidden_t, gate_low, up_low):
    first = pl.program_id(0) == 0
    length, width = normed_ref.shape

    @pl.when(first)
    def _():
        out_ref[...] = jnp.zeros_like(out_ref)
        back_ref[...] = jnp.zeros_like(back_ref)

    for at in range(0, length, BLOCK):
        rows = slice(at, at + BLOCK)
        normed = normed_ref[rows, :]
        gate_sum = mm(normed, gate_ref[...])
        up_sum = mm(normed, up_ref[...])
        hidden_grad = mm_nt(c_ref[rows, :], down_ref[...])
        sigmoid = jax.nn.sigmoid(gate_sum)
        activated = gate_sum * sigmoid
        hidden = low(activated * up_sum)
        gate_grad = low(hidden_grad * up_sum * (sigmoid + activated * (1.0 - sigmoid)))
        up_grad = low(hidden_grad * activated)
        hidden_t[:, rows] = hidden.T
        gate_low[rows, :] = gate_grad
        up_low[rows, :] = up_grad
        out_ref[rows, :] += mm(hidden, down_ref[...])
        back_ref[rows, :] += mm_nt(gate_grad, gate_ref[...]) + mm_nt(up_grad, up_ref[...])
    step = 384
    for at in range(0, width, step):
        rows = slice(at, at + step)
        gate_grad_ref[rows, :] = low(mm(turned_ref[rows, :], gate_low[...]))
        up_grad_ref[rows, :] = low(mm(turned_ref[rows, :], up_low[...]))
        down_grad_ref[:, rows] = low(mm(hidden_t[...], c_ref[:, rows]))


def feed(which, normed, turned, c, gate, up, down):
    length, width = normed.shape
    wide = gate.shape[1] // 4
    whole = pl.BlockSpec((length, width), lambda t, w: (0, 0), pipeline_mode=pl.Buffered(1))
    columns = pl.BlockSpec((width, wide), lambda t, w: (0, w[0] + 2 * t))
    rows = pl.BlockSpec((wide, width), lambda t, w: (w[0] + 2 * t, 0))
    total = pl.BlockSpec((length, width), lambda t, w: (0, 0), pipeline_mode=pl.Buffered(1))
    columns_out = pl.BlockSpec((width, wide), lambda t, w: (0, t))
    return pl.pallas_call(
        feed_body,
        grid_spec=pltpu.PrefetchScalarGridSpec(
            num_scalar_prefetch=1,
            grid=(2,),
            in_specs=[
                whole,
                pl.BlockSpec((width, length), lambda t, w: (0, 0), pipeline_mode=pl.Buffered(1)),
                whole,
                columns,
                columns,
                rows,
            ],
            out_specs=[
                total,
                total,
                columns_out,
                columns_out,
                pl.BlockSpec((wide, width), lambda t, w: (t, 0)),
            ],
            scratch_shapes=[
                pltpu.VMEM((wide, length), jnp.bfloat16),
                pltpu.VMEM((length, wide), jnp.bfloat16),
                pltpu.VMEM((length, wide), jnp.bfloat16),
            ],
        ),
        out_shape=[
            jax.ShapeDtypeStruct((length, width), jnp.float32),
            jax.ShapeDtypeStruct((length, width), jnp.float32),
            jax.ShapeDtypeStruct((width, 2 * wide), jnp.bfloat16),
            jax.ShapeDtypeStruct((width, 2 * wide), jnp.bfloat16),
            jax.ShapeDtypeStruct((2 * wide, width), jnp.bfloat16),
        ],
        compiler_params=pltpu.CompilerParams(vmem_limit_bytes=VMEM_MOST),
        cost_estimate=pl.CostEstimate(
            flops=18 * length * width * wide * 2,
            bytes_accessed=12 * width * wide * 2 + 16 * length * width,
            transcendentals=length * wide * 2,
        ),
        name="feed",
    )(which, normed, turned, c, gate, up, down)


def shortened(array):
    return jax.tree.map(lambda a: a.astype(jnp.bfloat16) if a.dtype == jnp.float32 else a, array)


def product(left, right):
    return jnp.dot(left, right, preferred_element_type=jnp.float32)


def product_tn(left, right):
    return lax.dot_general(
        left, right, (((0,), (0,)), ((), ())), preferred_element_type=jnp.float32
    )


def product_nt(left, right):
    return lax.dot_general(
        left, right, (((1,), (1,)), ((), ())), preferred_element_type=jnp.float32
    )


def rotary_tables(positions, width):
    half_width = width // 2
    freqs = jnp.exp(
        jnp.arange(half_width, dtype=jnp.float32) * (-2.0 * math.log(rope_base) / width)
    )
    angles = positions[:, None] * freqs[None, :]
    return (jnp.cos(angles), jnp.sin(angles))


def rotate(values, cosines, sines):
    half_width = values.shape[-1] // 2
    first = values[..., :half_width]
    second = values[..., half_width:]
    return jnp.concatenate(
        [first * cosines - second * sines, second * cosines + first * sines], axis=-1
    )


def unrotate(values, cosines, sines):
    half_width = values.shape[-1] // 2
    first = values[..., :half_width]
    second = values[..., half_width:]
    return jnp.concatenate(
        [first * cosines + second * sines, second * cosines - first * sines], axis=-1
    )


def norm_back(grad_rows, gain, scaled, inverse):
    weighted = grad_rows * gain
    return inverse * (weighted - scaled * jnp.mean(weighted * scaled, axis=-1, keepdims=True))


def plain_local(
    inputs,
    segments,
    out_grad,
    attention_gain,
    query_weight,
    key_weight,
    value_weight,
    output_weight,
    feedforward_gain,
    gate_weight,
    up_weight,
    down_weight,
):
    gathered = (
        lax.all_gather(attention_gain, "fsdp", axis=0, tiled=True),
        lax.all_gather(query_weight, "fsdp", axis=0, tiled=True),
        lax.all_gather(key_weight, "fsdp", axis=0, tiled=True),
        lax.all_gather(value_weight, "fsdp", axis=0, tiled=True),
        lax.all_gather(output_weight, "fsdp", axis=0, tiled=True),
        lax.all_gather(feedforward_gain, "fsdp", axis=0, tiled=True),
        lax.all_gather(gate_weight, "fsdp", axis=0, tiled=True),
        lax.all_gather(up_weight, "fsdp", axis=0, tiled=True),
        lax.all_gather(down_weight, "fsdp", axis=0, tiled=True),
    )
    full_query, full_key, full_value, full_output = (
        gathered[1],
        gathered[2],
        gathered[3],
        gathered[4],
    )
    full_gate, full_up, full_down = (gathered[6], gathered[7], gathered[8])
    gain_attention = gathered[0].astype(jnp.float32)
    gain_feed = gathered[5].astype(jnp.float32)
    span = inputs.shape[1]
    length = segments.shape[1]
    groups_q = HEADS // KV_HEADS
    key_width = KV_HEADS * HEAD
    start = lax.axis_index("fsdp") * span
    query_pos = start + jnp.arange(span, dtype=jnp.int32)
    key_pos = jnp.arange(length, dtype=jnp.int32)
    cosines, sines = rotary_tables(query_pos.astype(jnp.float32), HEAD)
    cos_four, sin_four = (cosines[:, None, None, :], sines[:, None, None, :])
    cos_three, sin_three = (cosines[:, None, :], sines[:, None, :])
    causal = query_pos[:, None] >= key_pos[None, :]
    scale = HEAD ** (-0.5)

    def micro_step(totals, sequence):
        tokens, segment_row, cotangent = sequence
        own_segment = lax.dynamic_slice_in_dim(segment_row, start, span)
        allowed = causal & (own_segment[:, None] == segment_row[None, :])
        values = tokens.astype(jnp.float32)
        inverse_a = lax.rsqrt(jnp.mean(values * values, axis=-1, keepdims=True) + epsilon)
        scaled_a = values * inverse_a
        normed_a = (scaled_a * gain_attention).astype(jnp.bfloat16)
        query_lin = product(normed_a, full_query).reshape(span, KV_HEADS, groups_q, HEAD)
        queries = rotate(query_lin, cos_four, sin_four).astype(jnp.bfloat16)
        key_lin = product(normed_a, full_key).reshape(span, KV_HEADS, HEAD)
        key_rows = (
            rotate(key_lin, cos_three, sin_three).astype(jnp.bfloat16).reshape(span, key_width)
        )
        value_rows = product(normed_a, full_value).astype(jnp.bfloat16)
        all_keys, all_values = (
            lax.all_gather(key_rows, "fsdp", axis=0, tiled=True),
            lax.all_gather(value_rows, "fsdp", axis=0, tiled=True),
        )
        all_keys = all_keys.reshape(length, KV_HEADS, HEAD)
        all_values = all_values.reshape(length, KV_HEADS, HEAD)
        scores = (
            jnp.einsum("qhgd,khd->hgqk", queries, all_keys, preferred_element_type=jnp.float32)
            * scale
        )
        scores = jnp.where(allowed, scores, -1e30)
        highest = jnp.max(scores, axis=-1, keepdims=True)
        expo_scores = jnp.exp(scores - highest)
        attention = expo_scores / jnp.sum(expo_scores, axis=-1, keepdims=True)
        attention_low = attention.astype(jnp.bfloat16)
        mixed = jnp.einsum(
            "hgqk,khd->qhgd", attention_low, all_values, preferred_element_type=jnp.float32
        )
        mixed = mixed.reshape(span, HEADS * HEAD).astype(jnp.bfloat16)
        residual = values + product(mixed, full_output)
        inverse_f = lax.rsqrt(jnp.mean(residual * residual, axis=-1, keepdims=True) + epsilon)
        scaled_f = residual * inverse_f
        normed_f = (scaled_f * gain_feed).astype(jnp.bfloat16)
        gate_sum = product(normed_f, full_gate)
        up_sum = product(normed_f, full_up)
        sigmoid_gate = jax.nn.sigmoid(gate_sum)
        activated = gate_sum * sigmoid_gate
        hidden = (activated * up_sum).astype(jnp.bfloat16)
        result = (residual + product(hidden, full_down)).astype(jnp.bfloat16)
        down_wgrad = product_tn(hidden, cotangent)
        hidden_grad = product_nt(cotangent, full_down)
        gate_grad = (
            hidden_grad * up_sum * sigmoid_gate * (1.0 + gate_sum * (1.0 - sigmoid_gate))
        ).astype(jnp.bfloat16)
        up_grad = (hidden_grad * activated).astype(jnp.bfloat16)
        gate_wgrad = product_tn(normed_f, gate_grad)
        up_wgrad = product_tn(normed_f, up_grad)
        normed_f_grad = product_nt(gate_grad, full_gate) + product_nt(up_grad, full_up)
        feed_gain_grad = jnp.sum(normed_f_grad * scaled_f, axis=0)
        residual_grad = cotangent.astype(jnp.float32) + norm_back(
            normed_f_grad, gain_feed, scaled_f, inverse_f
        )
        residual_low = residual_grad.astype(jnp.bfloat16)
        output_wgrad = product_tn(mixed, residual_low)
        mixed_grad = (
            product_nt(residual_low, full_output)
            .astype(jnp.bfloat16)
            .reshape(span, KV_HEADS, groups_q, HEAD)
        )
        attention_grad = jnp.einsum(
            "qhgd,khd->hgqk", mixed_grad, all_values, preferred_element_type=jnp.float32
        )
        row_totals = jnp.sum(attention * attention_grad, axis=-1, keepdims=True)
        score_grad = (attention * (attention_grad - row_totals) * scale).astype(jnp.bfloat16)
        value_grads = jnp.einsum(
            "hgqk,qhgd->khd", attention_low, mixed_grad, preferred_element_type=jnp.float32
        ).reshape(length, key_width)
        key_grads = jnp.einsum(
            "hgqk,qhgd->khd", score_grad, queries, preferred_element_type=jnp.float32
        ).reshape(length, key_width)
        query_grad = jnp.einsum(
            "hgqk,khd->qhgd", score_grad, all_keys, preferred_element_type=jnp.float32
        )
        key_back, value_back = (
            lax.psum_scatter(key_grads, "fsdp", scatter_dimension=0, tiled=True),
            lax.psum_scatter(value_grads, "fsdp", scatter_dimension=0, tiled=True),
        )
        query_low = (
            unrotate(query_grad, cos_four, sin_four)
            .reshape(span, HEADS * HEAD)
            .astype(jnp.bfloat16)
        )
        key_low = (
            unrotate(key_back.reshape(span, KV_HEADS, HEAD), cos_three, sin_three)
            .reshape(span, key_width)
            .astype(jnp.bfloat16)
        )
        value_low = value_back.astype(jnp.bfloat16)
        query_wgrad = product_tn(normed_a, query_low)
        key_wgrad = product_tn(normed_a, key_low)
        value_wgrad = product_tn(normed_a, value_low)
        normed_a_grad = (
            product_nt(query_low, full_query)
            + product_nt(key_low, full_key)
            + product_nt(value_low, full_value)
        )
        attention_gain_term = jnp.sum(normed_a_grad * scaled_a, axis=0)
        token_grad = (
            residual_grad + norm_back(normed_a_grad, gain_attention, scaled_a, inverse_a)
        ).astype(jnp.bfloat16)
        terms = (
            attention_gain_term,
            query_wgrad,
            key_wgrad,
            value_wgrad,
            output_wgrad,
            feed_gain_grad,
            gate_wgrad,
            up_wgrad,
            down_wgrad,
        )
        totals = tuple((left + right for left, right in zip(totals, terms)))
        return (totals, (result, token_grad))

    initial = tuple((jnp.zeros(weight.shape, jnp.float32) for weight in gathered))
    totals, (outputs, input_grads) = lax.scan(micro_step, initial, (inputs, segments, out_grad))
    shards = jax.tree.map(
        lambda part: part.astype(jnp.float32),
        lax.psum_scatter(shortened(totals), "fsdp", scatter_dimension=0, tiled=True),
    )
    summed = lax.psum(shards, "group")
    return (
        outputs,
        input_grads,
        summed[0],
        summed[1],
        summed[2],
        summed[3],
        summed[4],
        summed[5],
        summed[6],
        summed[7],
        summed[8],
    )


class Places:
    def __init__(self, group_size):
        self.group = lax.axis_index("group")
        self.y = lax.axis_index("fsdp")
        self.size = group_size
        self.masks = {"core": 1, "x": 2, "zlo": 4, "zhi": 8}

    def bit(self, name):
        if name == "y":
            return self.y
        return (self.group // self.masks[name]) % 2

    def swap(self, array, name):
        if name == "y":
            return lax.ppermute(array, "fsdp", [(0, 1), (1, 0)])
        mask = self.masks[name]
        return lax.ppermute(array, "group", [(i, i ^ mask) for i in range(self.size)])


def part_of(array, axis, bit):
    size = array.shape[axis] // 2
    return lax.dynamic_slice_in_dim(array, bit * size, size, axis)


def add_up(terms):
    total = terms[0].astype(jnp.float32)
    for term in terms[1:]:
        total = total + term.astype(jnp.float32)
    return low(total)


def in_order(bit, own, other, axis):
    return jnp.where(
        bit == 0,
        jnp.concatenate([own, other], axis=axis),
        jnp.concatenate([other, own], axis=axis),
    )


def reduce_down(places, terms, stages):
    for name, axis in stages:
        bit = places.bit(name)
        sent = add_up([part_of(term, axis, 1 - bit) for term in terms])
        terms = [part_of(term, axis, bit) for term in terms] + [places.swap(sent, name)]
    return add_up(terms)


def gather_up(places, piece, stages):
    for name, axis in stages:
        piece = in_order(places.bit(name), piece, places.swap(piece, name), axis)
    return piece


def norm_grad(grad, gain, scaled, inverse):
    weighted = grad * gain
    return inverse * (weighted - scaled * jnp.mean(weighted * scaled, axis=-1, keepdims=True))


def paired_local(
    group_size,
    inputs,
    segments,
    out_grad,
    attention_gain,
    query_weight,
    key_weight,
    value_weight,
    output_weight,
    feedforward_gain,
    gate_weight,
    up_weight,
    down_weight,
):
    places = Places(group_size)
    y = places.y
    span, length, width = inputs.shape[1], segments.shape[1], inputs.shape[2]
    q_width = query_weight.shape[1]

    def own_blocks(rows):
        own = part_of(rows, 0, y)
        other = places.swap(part_of(rows, 0, 1 - y), "y")
        return in_order(y, own[None], other[None], 0)

    gains = jnp.pad(
        jnp.stack([attention_gain, feedforward_gain]).astype(jnp.float32), ((0, 6), (0, 0))
    )
    tokens, qkv_weight, gains = fetch(inputs, query_weight, key_weight, value_weight, gains)
    gains = gains.transpose(1, 0, 2).reshape(8, width)
    gain_a, gain_f = gains[0:1], gains[1:2]

    segment = lax.dynamic_index_in_dim(segments, y, 0, False)
    seg_col, seg_row = segment[:, None], segment[None, :]
    cosines, sines = rope_tables(length)
    normed_a, qkv = project(tokens, gain_a, qkv_weight, cosines, sines)
    mixed, lse, c, mix_weight, full_gate, full_up, full_down = attend(
        qkv, seg_col, seg_row, out_grad, output_weight, gate_weight, up_weight, down_weight
    )

    values = tokens.astype(jnp.float32)
    residual = values + mm(mixed, mix_weight)
    inverse_f = lax.rsqrt(jnp.mean(residual * residual, axis=-1, keepdims=True) + epsilon)
    normed_f = low(residual * inverse_f * gain_f)
    turned_f = normed_f.T

    core = places.bit("core")
    theirs = feed((1 - core).reshape(1), normed_f, turned_f, c, full_gate, full_up, full_down)
    mine = feed(core.reshape(1), normed_f, turned_f, c, full_gate, full_up, full_down)
    result = low(residual + theirs[0] + mine[0])
    outputs = own_blocks(result)

    normed_f_grad = theirs[1] + mine[1]
    scaled_f = residual * inverse_f
    feed_gain_term = jnp.sum(normed_f_grad * scaled_f, axis=0)
    residual_grad = c.astype(jnp.float32) + norm_grad(normed_f_grad, gain_f, scaled_f, inverse_f)
    residual_low = low(residual_grad)
    mix_term = low(mm_tn(mixed, residual_low))
    mixed_grad = low(mm_nt(residual_low, mix_weight))

    orders = (("y", "x", "zlo", "zhi"), ("x", "zlo", "y", "zhi"), ("zlo", "y", "x", "zhi"))
    backs = (("zhi", "zlo", "x"), ("zhi", "x", "zlo"), ("zhi", "zlo", "x"))
    dims = {"y": 0, "x": 1, "zlo": 2, "zhi": 3}
    pieces = []
    for index in range(3):
        shape = mine[2 + index].shape
        split = (2, 2, 2, shape[0] // 8, shape[1])
        terms = [mine[2 + index].reshape(split), places.swap(theirs[2 + index], "core").reshape(split)]
        piece = reduce_down(places, terms, [(name, dims[name]) for name in orders[index]])
        pieces.append(gather_up(places, piece, [(name, dims[name]) for name in backs[index]]))

    def hidden_columns(piece):
        wide = piece.shape[-1] // 2
        piece = piece.reshape(width // 2, 2, wide)
        other = places.swap(piece, "core")
        return in_order(core, piece[:, :, None], other[:, :, None], 2).reshape(width // 2, 4 * wide)

    gate_sum_grad = hidden_columns(pieces[0]).astype(jnp.float32)
    up_sum_grad = hidden_columns(pieces[1]).astype(jnp.float32)
    down_piece = pieces[2].reshape(-1, width)
    down_sum_grad = in_order(core, down_piece, places.swap(down_piece, "core"), 0).astype(jnp.float32)

    dq, dk, dv = attend_back(qkv, mixed_grad, mixed, lse, seg_col, seg_row, cosines, sines)
    lows = jnp.concatenate([dq, dk, dv], axis=1)
    qkv_term = low(mm_tn(normed_a, lows))
    normed_a_grad = mm_nt(lows, qkv_weight)
    inverse_a = lax.rsqrt(jnp.mean(values * values, axis=-1, keepdims=True) + epsilon)
    scaled_a = values * inverse_a
    attention_gain_term = jnp.sum(normed_a_grad * scaled_a, axis=0)
    token_grad = low(residual_grad + norm_grad(normed_a_grad, gain_a, scaled_a, inverse_a))
    input_grads = own_blocks(token_grad)

    dims = {"y": 0, "core": 1, "x": 2, "zlo": 3, "zhi": 4}

    def whole_sum(term, order, back):
        term = term.reshape(2, 2, 2, 2, term.shape[0] // 16, term.shape[1])
        piece = reduce_down(places, [term], [(name, dims[name]) for name in order])
        piece = gather_up(places, piece, [(name, dims[name]) for name in back])
        return piece.reshape(-1, piece.shape[-1])

    mix_sum_grad = whole_sum(
        mix_term, ("core", "x", "y", "zlo", "zhi"), ("zhi", "zlo", "x", "core")
    ).astype(jnp.float32)
    third = qkv_term.shape[1] // 3
    qkv_sum = jnp.concatenate(
        [
            whole_sum(
                qkv_term[:, i * third : (i + 1) * third],
                ("core",) + orders[i],
                backs[i] + ("core",),
            )
            for i in range(3)
        ],
        axis=1,
    ).astype(jnp.float32)

    gain_terms = jnp.stack([attention_gain_term, feed_gain_term])
    for name in ("core", "y", "x", "zlo", "zhi"):
        gain_terms = gain_terms + places.swap(gain_terms, name)
    gain_grads = part_of(gain_terms, 1, y)
    k_width = key_weight.shape[1]
    return (
        outputs,
        input_grads,
        gain_grads[0],
        qkv_sum[:, :q_width],
        qkv_sum[:, q_width : q_width + k_width],
        qkv_sum[:, q_width + k_width :],
        mix_sum_grad,
        gain_grads[1],
        gate_sum_grad,
        up_sum_grad,
        down_sum_grad,
    )


def solution(mesh):
    placed = (
        P("group", "fsdp", None),
        P("group", None),
        P("group", "fsdp", None),
        P("fsdp"),
        P("fsdp", None),
        P("fsdp", None),
        P("fsdp", None),
        P("fsdp", None),
        P("fsdp"),
        P("fsdp", None),
        P("fsdp", None),
        P("fsdp", None),
    )
    group_size, fsdp_size = mesh.shape["group"], mesh.shape["fsdp"]

    def local(*arrays):
        if group_size == 16 and fsdp_size == 2 and arrays[0].shape[0] == 2:
            return paired_local(group_size, *arrays)
        return plain_local(*arrays)

    return jax.shard_map(
        local,
        mesh=mesh,
        in_specs=placed,
        out_specs=(
            P("group", "fsdp", None),
            P("group", "fsdp", None),
            P("fsdp"),
            P("fsdp", None),
            P("fsdp", None),
            P("fsdp", None),
            P("fsdp", None),
            P("fsdp"),
            P("fsdp", None),
            P("fsdp", None),
            P("fsdp", None),
        ),
        check_vma=False,
    )
```

```python
import functools
import math

import jax
import jax.numpy as jnp
from jax import lax
from jax.experimental import pallas as pl
from jax.experimental.pallas import tpu as pltpu
from jax.sharding import PartitionSpec as P

HEADS = 18
KV_HEADS = 6
HEAD = 64
epsilon = 1e-05
rope_base = 10000.0
BLOCK = 256
WIDE = 128
VMEM_MOST = 66 * 1024 * 1024 - 3 * 1024 * 1024


def mm(left, right):
    return jnp.dot(left, right, preferred_element_type=jnp.float32)


def mm_nt(left, right):
    return lax.dot_general(
        left, right, (((1,), (1,)), ((), ())), preferred_element_type=jnp.float32
    )


def mm_tn(left, right):
    return lax.dot_general(
        left, right, (((0,), (0,)), ((), ())), preferred_element_type=jnp.float32
    )


def low(values):
    return values.astype(jnp.bfloat16)


def lanes_below(rows, period, limit):
    lane = lax.broadcasted_iota(jnp.int32, (rows, WIDE), 1)
    return lane % period < limit


def swap_halves(tile):
    ahead = pltpu.roll(tile, WIDE - HEAD // 2, 1)
    behind = pltpu.roll(tile, HEAD // 2, 1)
    return jnp.where(lanes_below(tile.shape[0], HEAD, HEAD // 2), ahead, behind)


def rope_tables(length):
    half_width = HEAD // 2
    freqs = jnp.exp(
        jnp.arange(half_width, dtype=jnp.float32) * (-2.0 * math.log(rope_base) / HEAD)
    )
    angles = jnp.arange(length, dtype=jnp.float32)[:, None] * freqs[None, :]
    cosines, sines = jnp.cos(angles), jnp.sin(angles)
    return (
        jnp.concatenate([cosines] * 4, axis=1),
        jnp.concatenate([-sines, sines] * 2, axis=1),
    )


def project_body(x_ref, gain_ref, w_ref, cos_ref, sin_ref, normed_ref, qkv_ref):
    values = x_ref[...].astype(jnp.float32)
    inverse = lax.rsqrt(jnp.mean(values * values, axis=-1, keepdims=True) + epsilon)
    normed = low(values * inverse * gain_ref[...])
    normed_ref[...] = normed
    cosines, sines = cos_ref[...], sin_ref[...]
    width = qkv_ref.shape[1]
    q_width, k_width = HEADS * HEAD, KV_HEADS * HEAD
    step = 384
    for at in range(0, width, step):
        wide = mm(normed, w_ref[:, at : at + step])
        for part in range(0, step, WIDE):
            tile = wide[:, part : part + WIDE]
            if at + part < q_width + k_width:
                tile = tile * cosines + swap_halves(tile) * sines
            if at + part < q_width:
                tile = tile * HEAD ** (-0.5)
            qkv_ref[:, at + part : at + part + WIDE] = low(tile)


def project(x, gain, w, cosines, sines):
    length, width = x.shape
    out = w.shape[1]
    rows = pl.BlockSpec((BLOCK, width), lambda i: (i, 0))
    table = pl.BlockSpec((BLOCK, WIDE), lambda i: (i, 0))
    return pl.pallas_call(
        project_body,
        grid=(length // BLOCK,),
        in_specs=[
            rows,
            pl.BlockSpec((1, width), lambda i: (0, 0)),
            pl.BlockSpec((width, out), lambda i: (0, 0), pipeline_mode=pl.Buffered(1)),
            table,
            table,
        ],
        out_specs=[rows, pl.BlockSpec((BLOCK, out), lambda i: (i, 0))],
        out_shape=[
            jax.ShapeDtypeStruct((length, width), jnp.bfloat16),
            jax.ShapeDtypeStruct((length, out), jnp.bfloat16),
        ],
        cost_estimate=pl.CostEstimate(
            flops=2 * length * width * out,
            bytes_accessed=2 * (2 * length * width + length * out + width * out),
            transcendentals=0,
        ),
        name="project",
    )(x, gain, w, cosines, sines)


MESH = pl.DeviceIdType.MESH
MASKS = {"core": 1, "x": 2, "zlo": 4, "zhi": 8}


def bit_of(name):
    if name == "y":
        return lax.axis_index("fsdp")
    return (lax.axis_index("group") // MASKS[name]) % 2


def peer_of(name):
    if name == "y":
        return {"fsdp": 1 - lax.axis_index("fsdp")}
    return {"group": lax.axis_index("group") + MASKS[name] * (1 - 2 * bit_of(name))}


def greet(names):
    barrier = pltpu.get_barrier_semaphore()
    for name in names:
        pl.semaphore_signal(barrier, inc=1, device_id=peer_of(name), device_id_type=MESH)
    pl.semaphore_wait(barrier, len(names))


def across(source, target, sems, slot, name):
    return pltpu.make_async_remote_copy(
        src_ref=source,
        dst_ref=target,
        send_sem=sems.at[0, slot],
        recv_sem=sems.at[1, slot],
        device_id=peer_of(name),
        device_id_type=MESH,
    )


class Spread:
    def __init__(self, shard, full, order, sems, slot, columns=None):
        self.shard, self.full, self.order, self.sems, self.slot = shard, full, order, sems, slot
        self.columns = columns

    def copy(self, stage):
        y = lax.axis_index("fsdp")
        index = 0
        for at, name in enumerate(self.order):
            index = index + bit_of(name) * 2**at
        slot = self.slot + stage
        where = (slice(None), slice(None)) if self.columns is None else (slice(None), self.columns)
        if stage == 0:
            return across(
                self.shard.at[index], self.full.at[(y * 8 + index,) + where], self.sems, slot, "y"
            )
        count = 2 ** (stage - 1)
        block = self.full.at[(pl.ds((1 - y) * 8 + index // count * count, count),) + where]
        return across(block, block, self.sems, slot, self.order[stage - 1])

    def advance(self, stage):
        if stage >= 0:
            self.copy(stage).wait_recv()
        if stage < len(self.order):
            self.copy(stage + 1).start()

    def finish(self):
        for stage in range(len(self.order) + 1):
            self.copy(stage).wait_send()


def fetch_body(inputs, query, key, value, gains, tokens, weight, both_gains,
               held, held_weight, sems, near):
    y = lax.axis_index("fsdp")
    q_width, k_width = query.shape[2], key.shape[2]
    places = (
        slice(0, q_width),
        slice(q_width, q_width + k_width),
        slice(q_width + k_width, q_width + 2 * k_width),
    )
    shards = (query, key, value)
    loads = [pltpu.make_async_copy(inputs.at[y], held, near.at[0])] + [
        pltpu.make_async_copy(shard, held_weight.at[:, :, place], near.at[1 + at])
        for at, (shard, place) in enumerate(zip(shards, places))
    ]
    for load in loads:
        load.start()
    greet(("y", "x", "zlo", "core"))
    index = bit_of("x") + 2 * bit_of("zlo") + 4 * bit_of("core")
    first = [
        across(shard.at[index], weight.at[y * 8 + index, :, place], sems, at, "y")
        for at, (shard, place) in enumerate(zip(shards, places))
    ]
    span = held.shape[0]
    swap = across(
        inputs.at[1 - y], tokens.at[pl.ds(pl.multiple_of(y * span, span), span)], sems, 3, "y"
    )
    gain_swap = across(gains, both_gains.at[y], sems, 4, "y")
    for copy in first + [gain_swap, swap]:
        copy.start()
    for load in loads:
        load.wait()
    stores = [
        pltpu.make_async_copy(
            held, tokens.at[pl.ds(pl.multiple_of(y * span, span), span)], near.at[4]
        ),
        pltpu.make_async_copy(held_weight, weight.at[pl.ds(y * 8, 8)], near.at[5]),
        pltpu.make_async_copy(gains, both_gains.at[y], near.at[6]),
    ]
    for store in stores:
        store.start()
    for copy in first:
        copy.wait_recv()
    later = []
    for at, name in enumerate(("x", "zlo", "core")):
        count = 2**at
        block = weight.at[pl.ds((1 - y) * 8 + index // count * count, count)]
        copy = across(block, block, sems, 5 + at, name)
        copy.start()
        copy.wait_recv()
        later.append(copy)
    swap.wait_recv()
    gain_swap.wait_recv()
    for copy in first + [gain_swap, swap] + later:
        copy.wait_send()
    for store in stores:
        store.wait()


def fetch(inputs, query, key, value, gains):
    span, width = inputs.shape[1:]
    total = query.shape[1] + 2 * key.shape[1]
    eight = lambda shard: shard.reshape(8, shard.shape[0] // 8, shard.shape[1])
    rows = query.shape[0] // 8
    anywhere = pl.BlockSpec(memory_space=pl.ANY)
    tokens, weight, both_gains = pl.pallas_call(
        fetch_body,
        in_specs=[anywhere] * 5,
        out_specs=[anywhere] * 3,
        out_shape=[
            jax.ShapeDtypeStruct((2 * span, width), inputs.dtype),
            jax.ShapeDtypeStruct((16, rows, total), query.dtype),
            jax.ShapeDtypeStruct((2,) + gains.shape, gains.dtype),
        ],
        scratch_shapes=[
            pltpu.VMEM((span, width), inputs.dtype),
            pltpu.VMEM((8, rows, total), query.dtype),
            pltpu.SemaphoreType.DMA((2, 8)),
            pltpu.SemaphoreType.DMA((7,)),
        ],
        compiler_params=pltpu.CompilerParams(collective_id=1, has_side_effects=True),
        name="fetch",
    )(inputs, eight(query), eight(key), eight(value), gains)
    return tokens, weight.reshape(16 * rows, total), both_gains


AXES = ("y", "x", "zlo", "zhi")


class Fold:
    def __init__(self, source, kept, received, order, sems, slot, near, near_slot):
        self.source, self.kept, self.received = source, kept, received
        self.order, self.sems, self.slot = order, sems, slot
        self.near, self.near_slot = near, near_slot

    def pick(self, stage, bit):
        left = [name for name in AXES if name not in self.order[:stage]]
        return (slice(None),) * left.index(self.order[stage]) + (bit,)

    def held(self, stage):
        return self.source if stage == 0 else self.received[stage - 1]

    def copy(self, stage):
        name = self.order[stage]
        source = self.held(stage).at[self.pick(stage, 1 - bit_of(name))]
        return across(source, self.received[stage], self.sems, self.slot + stage, name)

    def load(self):
        source = self.source.at[self.pick(0, bit_of(self.order[0]))]
        return pltpu.make_async_copy(source, self.kept, self.near.at[self.near_slot])

    def begin(self):
        self.copy(0).start()
        if self.kept is not None:
            self.load().start()

    def advance(self, stage):
        self.copy(stage).wait_recv()
        target = self.received[stage]
        lead = target.ndim - 2
        if stage == 0 and self.kept is not None:
            self.load().wait()
            mine, at, bit = self.kept, 0, None
        else:
            bit = bit_of(self.order[stage])
            mine, at = self.held(stage), len(self.pick(stage, 0)) - 1

        @pl.loop(0, 2**lead)
        def _(n):
            index = tuple(n // 2 ** (lead - 1 - k) % 2 for k in range(lead))
            from_ = index if bit is None else index[:at] + (bit,) + index[at:]
            total = target[index].astype(jnp.float32) + mine[from_].astype(jnp.float32)
            target[index] = low(total)

        if stage + 1 < len(self.order):
            self.copy(stage + 1).start()

    def finish(self):
        for stage in range(len(self.order)):
            self.copy(stage).wait_send()


class Rise:
    def __init__(self, whole, order, columns, sems, slot):
        self.whole, self.order, self.columns, self.sems, self.slot = whole, order, columns, sems, slot

    def block(self, stage):
        index = tuple(
            slice(None) if name in self.order[:stage] else bit_of(name) for name in AXES[1:]
        )
        if self.whole.ndim == 6:
            return [self.whole.at[(bit_of("core"),) + index]]
        return [self.whole.at[index + (slice(None), columns)] for columns in self.columns]

    def copies(self, stage, first=None):
        blocks = self.block(stage)
        count = len(blocks)
        return [
            across(
                block if first is None else first,
                block,
                self.sems,
                self.slot + stage * count + at,
                self.order[stage],
            )
            for at, block in enumerate(blocks)
        ]

    def begin(self, first=None):
        for copy in self.copies(0, first):
            copy.start()

    def advance(self, stage):
        for copy in self.copies(stage):
            copy.wait_recv()
        if stage + 1 < len(self.order):
            for copy in self.copies(stage + 1):
                copy.start()

    def finish(self):
        for stage in range(len(self.order)):
            for copy in self.copies(stage):
                copy.wait_send()


ORDERS = (("y", "x", "zlo", "zhi"), ("x", "zlo", "y", "zhi"), ("zlo", "y", "x", "zhi"))
BACKS = (
    ("zhi", "zlo", "x", "core"),
    ("zhi", "x", "zlo", "core"),
    ("zhi", "zlo", "x", "core"),
)


def hidden_columns(wide):
    core = bit_of("core")
    return [
        pl.ds(pl.multiple_of(core * wide, WIDE), wide),
        pl.ds(pl.multiple_of((2 + core) * wide, WIDE), wide),
    ]


def finish_body(term, gains, result, token_grad, gate_in, up_in, down_in,
                gate, up, down, sums, outputs, input_grads, gain_sums,
                r0, r1, r2, r3, r4, k0, gain_held, gain_came, rows_held, sems, near):
    core, y = bit_of("core"), lax.axis_index("fsdp")
    third = term.shape[-1] // 3
    wide = third // 2
    hidden = gate.shape[-1] // 4
    columns = [
        [pl.ds(pl.multiple_of(t * third + side * wide, WIDE), wide) for side in (core, 1 - core)]
        for t in range(3)
    ]
    everything = (slice(None),) * 5
    span = outputs.shape[1]
    rows = [pl.ds(pl.multiple_of(at * span, span), span) for at in (y, 1 - y)]
    loads = [
        pltpu.make_async_copy(term.at[everything + (columns[t][0],)], k0.at[t], near.at[t])
        for t in range(3)
    ] + [
        pltpu.make_async_copy(result.at[rows[0]], rows_held.at[0], near.at[3]),
        pltpu.make_async_copy(token_grad.at[rows[0]], rows_held.at[1], near.at[4]),
    ]
    for load in loads:
        load.start()
    greet(("core", "y", "x", "zlo", "zhi"))
    cores = [
        across(term.at[everything + (columns[t][1],)], r0.at[t], sems, t, "core") for t in range(3)
    ]
    for copy in cores:
        copy.start()
    rises = [
        Rise(gate, BACKS[0], hidden_columns(hidden), sems, 3),
        Rise(up, BACKS[1], hidden_columns(hidden), sems, 11),
        Rise(down, BACKS[2], None, sems, 19),
    ]
    folds = [
        Fold(
            r0.at[t], None, [r1.at[t], r2.at[t], r3.at[t], r4.at[t]], ORDERS[t], sems, 23 + 4 * t,
            None, None,
        )
        for t in range(3)
    ]
    tops = [Rise(sums, BACKS[t], [columns[t][0]], sems, 35 + 4 * t) for t in range(3)]
    swaps = [
        across(result.at[rows[1]], outputs.at[y], sems, 52, "y"),
        across(token_grad.at[rows[1]], input_grads.at[y], sems, 53, "y"),
    ]
    names = ("core",) + AXES
    gain_copies = [
        across(gain_held.at[at], gain_came.at[at], sems, 47 + at, name)
        for at, name in enumerate(names)
    ]
    gain_held[0] = gains[...]
    for rise in rises:
        rise.begin()

    def gain_step(at):
        gain_copies[at].wait_recv()
        gain_held[at + 1] = gain_held[at] + gain_came[at]
        if at + 1 < len(names):
            gain_copies[at + 1].start()

    gain_copies[0].start()
    for t in range(3):
        cores[t].wait_recv()
        loads[t].wait()

        @pl.loop(0, 16)
        def _(n, t=t):
            index = (t, n // 8, n // 4 % 2, n // 2 % 2, n % 2)
            r0[index] = low(r0[index].astype(jnp.float32) + k0[index].astype(jnp.float32))

        folds[t].begin()
    stores = [
        pltpu.make_async_copy(rows_held.at[0], outputs.at[y], near.at[5]),
        pltpu.make_async_copy(rows_held.at[1], input_grads.at[y], near.at[6]),
    ]
    for at in range(2):
        swaps[at].start()
        loads[3 + at].wait()
        stores[at].start()
    gain_step(0)
    for t in range(3):
        folds[t].advance(0)
    gain_step(1)
    for rise in rises:
        rise.advance(0)
    for t in range(3):
        folds[t].advance(1)
    gain_step(2)
    for t in range(3):
        folds[t].advance(2)
    gain_step(3)
    tops_here = []
    for t in range(3):
        folds[t].advance(3)
        tops[t].begin(r4.at[t])
        store = pltpu.make_async_copy(r4.at[t], tops[t].block(0)[0], near.at[7 + t])
        store.start()
        tops_here.append(store)
    for rise in rises:
        rise.advance(1)
    for t in range(3):
        tops_here[t].wait()
        tops[t].advance(0)
    gain_step(4)
    for t in range(3):
        tops[t].advance(1)
    for rise in rises:
        rise.advance(2)
    for t in range(3):
        tops[t].advance(2)
    for rise in rises + tops:
        rise.advance(3)
    for copy in cores + swaps + gain_copies:
        copy.wait_send()
    for part in rises + tops + folds:
        part.finish()
    for copy in swaps:
        copy.wait_recv()
    for store in stores:
        store.wait()
    gain_sums[...] = gain_held[len(names)]


def finish(term, gains, result, token_grad, gate, up, down):
    length, width = result.shape
    term = term.reshape(2, 2, 2, 2, term.shape[0] // 16, term.shape[1])
    rows, total = term.shape[4:]
    wide = total // 6
    anywhere = pl.BlockSpec(memory_space=pl.ANY)
    vmem = pl.BlockSpec(memory_space=pltpu.VMEM)
    halves = jax.ShapeDtypeStruct((2, length // 2, width), result.dtype)
    return pl.pallas_call(
        finish_body,
        in_specs=[anywhere, vmem] + [anywhere] * 5,
        out_specs=[anywhere] * 6 + [vmem],
        out_shape=[
            jax.ShapeDtypeStruct(gate.shape, gate.dtype),
            jax.ShapeDtypeStruct(up.shape, up.dtype),
            jax.ShapeDtypeStruct(down.shape, down.dtype),
            jax.ShapeDtypeStruct((2, 2, 2, rows, total), term.dtype),
            halves,
            halves,
            jax.ShapeDtypeStruct(gains.shape, gains.dtype),
        ],
        input_output_aliases={4: 0, 5: 1, 6: 2},
        scratch_shapes=[
            pltpu.VMEM((3,) + (2,) * left + (rows, wide), jnp.bfloat16) for left in (4, 3, 2, 1, 0)
        ]
        + [
            pltpu.VMEM((3, 2, 2, 2, 2, rows, wide), jnp.bfloat16),
            pltpu.VMEM((6,) + gains.shape, jnp.float32),
            pltpu.VMEM((5,) + gains.shape, jnp.float32),
            pltpu.VMEM((2, length // 2, width), result.dtype),
            pltpu.SemaphoreType.DMA((2, 54)),
            pltpu.SemaphoreType.DMA((10,)),
        ],
        compiler_params=pltpu.CompilerParams(
            collective_id=4, has_side_effects=True, vmem_limit_bytes=VMEM_MOST
        ),
        name="finish",
    )(term, gains, result, token_grad, gate, up, down)


def place_heads(tile, variants_ref):
    wide = tile.astype(jnp.float32)
    turned = pltpu.roll(wide, HEAD, 1)
    low_lanes = lanes_below(tile.shape[0], WIDE, HEAD)
    variants_ref[0] = low(jnp.where(low_lanes, wide, 0.0))
    variants_ref[1] = low(jnp.where(low_lanes, 0.0, turned))
    variants_ref[2] = low(jnp.where(low_lanes, turned, 0.0))
    variants_ref[3] = low(jnp.where(low_lanes, 0.0, wide))


def allowed_block(seg_k, seg_q, diagonal):
    same = seg_k == seg_q
    if diagonal:
        rows = lax.broadcasted_iota(jnp.int32, same.shape, 0)
        lanes = lax.broadcasted_iota(jnp.int32, same.shape, 1)
        same = same & (rows <= lanes)
    return same


def attend_body(
    q_ref, k_ref, v_ref, seg_col_ref, seg_row_ref, out_grad, mix_w, gate_w, up_w, down_w,
    mixed_ref, lse_ref, whole_grad, mix_full, gate_full, up_full, down_full,
    ks, vt, acc, stats, sems, near, held_mix, held_gate, held_up, held_down, held_grad
):
    block = pl.program_id(1)
    now = pl.program_id(0) * pl.num_programs(1) + block
    most = pl.num_programs(0) * pl.num_programs(1) - 1
    y = lax.axis_index("fsdp")
    spreads = {
        "mix": Spread(mix_w, mix_full, ("x", "zlo", "core"), sems, 0),
        "gate": Spread(gate_w, gate_full, ("zlo", "x", "core"), sems, 4),
        "up": Spread(up_w, up_full, ("x", "zlo", "core"), sems, 8),
        "down": Spread(down_w, down_full, ("zlo", "x", "core"), sems, 12),
    }
    span = out_grad.shape[1]
    mine = whole_grad.at[pl.ds(pl.multiple_of(y * span, span), span)]
    grad_swap = across(out_grad.at[1 - y], mine, sems, 16, "y")
    half = pl.ds(y * 8, 8)
    own = (
        (mix_w, held_mix, mix_full.at[half]),
        (gate_w, held_gate, gate_full.at[half]),
        (up_w, held_up, up_full.at[half]),
        (down_w, held_down, down_full.at[half]),
        (out_grad.at[y], held_grad, mine),
    )
    loads = [pltpu.make_async_copy(a, b, near.at[0, at]) for at, (a, b, _) in enumerate(own)]
    stores = [pltpu.make_async_copy(b, c, near.at[1, at]) for at, (_, b, c) in enumerate(own)]
    plan = {
        1: (("mix", 0),),
        2: (("mix", 1),),
        3: (("gate", 0), ("mix", 2)),
        5: (("up", 0), ("gate", 1)),
        7: (("down", 0), ("up", 1)),
        9: (("gate", 2), ("down", 1)),
        10: (("up", 2),),
    }

    @pl.when(now == 0)
    def _():
        for load in loads:
            load.start()
        greet(("y", "x", "zlo", "core"))
        for name in ("mix", "gate", "up", "down"):
            spreads[name].advance(-1)
        grad_swap.start()

    @pl.when(now == 1)
    def _():
        for load, store in zip(loads, stores):
            load.wait()
            store.start()

    for at, steps in plan.items():

        @pl.when(now == at)
        def _(steps=steps):
            for name, stage in steps:
                spreads[name].advance(stage)

    @pl.when(block == 0)
    def _():
        place_heads(k_ref[...], ks)
        vt[...] = low(v_ref[...].astype(jnp.float32).T)

    acc[...] = jnp.zeros_like(acc)
    stats[0] = jnp.full((8, BLOCK), -1e30, jnp.float32)
    stats[1] = jnp.zeros((8, BLOCK), jnp.float32)
    seg_q = seg_row_ref[...]

    def step(j, diagonal):
        rows = pl.ds(pl.multiple_of(j * BLOCK, BLOCK), BLOCK)
        seg_k = seg_col_ref[rows, :]
        allowed = allowed_block(seg_k, seg_q, diagonal)
        for head in range(6):
            part, side, kv = head // 2, head % 2, head // 3
            q_tile = q_ref[:, part * WIDE : (part + 1) * WIDE]
            scores = mm_nt(ks[kv * 2 + side, rows, :], q_tile)
            scores = jnp.where(allowed, scores, -1e30)
            before = stats[0, head : head + 1, :]
            highest = jnp.maximum(before, jnp.max(scores, axis=0, keepdims=True))
            shrink = jnp.exp(before - highest)
            chances = jnp.exp(scores - highest)
            stats[0, head : head + 1, :] = highest
            stats[1, head : head + 1, :] = stats[1, head : head + 1, :] * shrink + jnp.sum(
                chances, axis=0, keepdims=True
            )
            values = vt[kv * HEAD : (kv + 1) * HEAD, rows]
            at = head * HEAD
            acc[at : at + HEAD, :] = acc[at : at + HEAD, :] * shrink + mm(values, low(chances))

    @pl.loop(0, block)
    def _(j):
        step(j, False)

    step(block, True)
    total = stats[1]
    for part in range(3):
        at = part * WIDE
        both = jnp.concatenate(
            [
                acc[at : at + HEAD, :] / total[2 * part : 2 * part + 1, :],
                acc[at + HEAD : at + WIDE, :] / total[2 * part + 1 : 2 * part + 2, :],
            ],
            axis=0,
        )
        mixed_ref[:, at : at + WIDE] = low(both.T)
    lse_ref[0] = stats[0] + jnp.log(jnp.maximum(total, 1e-30))

    @pl.when(now == most)
    def _():
        spreads["down"].advance(2)
        for spread in spreads.values():
            spread.advance(3)
            spread.finish()
        grad_swap.wait()
        for store in stores:
            store.wait()


def attend(qkv, seg_col, seg_row, out_grad, mix_w, gate_w, up_w, down_w):
    length = qkv.shape[0]
    pairs = KV_HEADS // 2
    q_tiles = HEADS * HEAD // WIDE
    anywhere = pl.BlockSpec(memory_space=pl.ANY)
    shards = [w.reshape(8, w.shape[0] // 8, w.shape[1]) for w in (mix_w, gate_w, up_w, down_w)]
    fulls = [jax.ShapeDtypeStruct((16,) + w.shape[1:], w.dtype) for w in shards]
    found = pl.pallas_call(
        attend_body,
        grid=(pairs, length // BLOCK),
        in_specs=[
            pl.BlockSpec((BLOCK, 3 * WIDE), lambda b, i: (i, b)),
            pl.BlockSpec((length, WIDE), lambda b, i: (0, q_tiles + b)),
            pl.BlockSpec((length, WIDE), lambda b, i: (0, q_tiles + pairs + b)),
            pl.BlockSpec((length, 1), lambda b, i: (0, 0)),
            pl.BlockSpec((1, BLOCK), lambda b, i: (0, i)),
        ]
        + [anywhere] * 5,
        out_specs=[
            pl.BlockSpec((BLOCK, 3 * WIDE), lambda b, i: (i, b)),
            pl.BlockSpec((1, 8, BLOCK), lambda b, i: (b, 0, i)),
        ]
        + [anywhere] * 5,
        out_shape=[
            jax.ShapeDtypeStruct((length, HEADS * HEAD), jnp.bfloat16),
            jax.ShapeDtypeStruct((pairs, 8, length), jnp.float32),
            jax.ShapeDtypeStruct((length, out_grad.shape[2]), out_grad.dtype),
        ]
        + fulls,
        scratch_shapes=[
            pltpu.VMEM((4, length, WIDE), jnp.bfloat16),
            pltpu.VMEM((WIDE, length), jnp.bfloat16),
            pltpu.VMEM((6 * HEAD, BLOCK), jnp.float32),
            pltpu.VMEM((2, 8, BLOCK), jnp.float32),
            pltpu.SemaphoreType.DMA((2, 17)),
            pltpu.SemaphoreType.DMA((2, 5)),
        ]
        + [pltpu.VMEM(w.shape, w.dtype) for w in shards]
        + [pltpu.VMEM(out_grad.shape[1:], out_grad.dtype)],
        compiler_params=pltpu.CompilerParams(
            collective_id=2, has_side_effects=True, vmem_limit_bytes=VMEM_MOST
        ),
        cost_estimate=pl.CostEstimate(
            flops=16 * length * length * HEADS * HEAD // 2,
            bytes_accessed=6 * length * HEADS * HEAD,
            transcendentals=HEADS * length * length // 2,
        ),
        name="attend",
    )(qkv, qkv, qkv, seg_col, seg_row, out_grad, *shards)
    return tuple(found[:3]) + tuple(w.reshape(-1, w.shape[2]) for w in found[3:])


def attend_back_body(
    q_ref, k_ref, v_ref, grad_ref, mixed_ref, lse_ref, seg_col_ref, seg_row_ref, cos_ref, sin_ref,
    gate_term, up_term, down_term,
    dq_ref, dk_ref, dv_ref, gate_sum, up_sum, down_sum,
    ks, vs, kt, k_acc, v_acc, q_acc, sides, delta, sems, near, kept, *received
):
    block = pl.program_id(1)
    length = k_ref.shape[0]
    now = pl.program_id(0) * pl.num_programs(1) + block
    most = pl.num_programs(0) * pl.num_programs(1) - 1
    down_kept, down_received = received[4], received[5:]
    folds = [
        Fold(
            term,
            kept.at[at] if at < 2 else down_kept,
            [r.at[at] for r in received[:4]] if at < 2 else list(down_received),
            ORDERS[at],
            sems,
            4 * at,
            near,
            at,
        )
        for at, term in enumerate((gate_term, up_term, down_term))
    ]

    @pl.when(now == 0)
    def _():
        greet(AXES)
        for fold in folds:
            fold.begin()

    for stage, at in ((0, 7), (1, 11)):

        @pl.when(now == at)
        def _(stage=stage):
            for fold in folds:
                fold.advance(stage)

    @pl.when(block == 0)
    def _():
        place_heads(k_ref[...], ks)
        place_heads(v_ref[...], vs)
        kt[...] = low(k_ref[...].astype(jnp.float32).T)
        k_acc[...] = jnp.zeros_like(k_acc)
        v_acc[...] = jnp.zeros_like(v_acc)

    q_acc[...] = jnp.zeros_like(q_acc)
    seg_q = seg_row_ref[...]
    low_lanes = lanes_below(BLOCK, WIDE, HEAD)
    zero = jnp.zeros((BLOCK, WIDE), jnp.bfloat16)
    for part in range(3):
        at = part * WIDE
        tile, grad = q_ref[:, at : at + WIDE], grad_ref[:, at : at + WIDE]
        sides[0, part, 0:BLOCK, :] = jnp.where(low_lanes, tile, zero)
        sides[0, part, BLOCK : 2 * BLOCK, :] = jnp.where(low_lanes, zero, tile)
        sides[1, part, 0:BLOCK, :] = jnp.where(low_lanes, grad, zero)
        sides[1, part, BLOCK : 2 * BLOCK, :] = jnp.where(low_lanes, zero, grad)
        product = (grad.astype(jnp.float32) * mixed_ref[:, at : at + WIDE].astype(jnp.float32)).T
        delta[2 * part : 2 * part + 1, :] = jnp.sum(product[:HEAD], axis=0, keepdims=True)
        delta[2 * part + 1 : 2 * part + 2, :] = jnp.sum(product[HEAD:], axis=0, keepdims=True)

    def step(j, diagonal):
        rows = pl.ds(pl.multiple_of(j * BLOCK, BLOCK), BLOCK)
        allowed = allowed_block(seg_col_ref[rows, :], seg_q, diagonal)
        for part in range(3):
            at = part * WIDE
            q_tile, grad_tile = q_ref[:, at : at + WIDE], grad_ref[:, at : at + WIDE]
            chances_pair, score_pair = [], []
            for side in range(2):
                head = 2 * part + side
                kv = head // 3
                scores = mm_nt(ks[kv * 2 + side, rows, :], q_tile)
                scores = jnp.where(allowed, scores, -1e30)
                chances = jnp.exp(scores - lse_ref[0, head : head + 1, :])
                onto = mm_nt(vs[kv * 2 + side, rows, :], grad_tile)
                score_grad = low(chances * (onto - delta[head : head + 1, :]))
                chances_pair.append(low(chances))
                score_pair.append(score_grad)
                to = head * HEAD
                q_acc[to : to + HEAD, :] += mm(kt[kv * HEAD : (kv + 1) * HEAD, rows], score_grad)
            v_acc[part, rows, :] += mm(jnp.concatenate(chances_pair, axis=1), sides[1, part])
            k_acc[part, rows, :] += mm(jnp.concatenate(score_pair, axis=1), sides[0, part])

    @pl.loop(0, block)
    def _(j):
        step(j, False)

    step(block, True)
    here = pl.ds(pl.multiple_of(block * BLOCK, BLOCK), BLOCK)
    for part in range(3):
        at = part * WIDE
        tile = q_acc[at : at + WIDE, :].T * HEAD ** (-0.5)
        tile = tile * cos_ref[here, :] - swap_halves(tile) * sin_ref[here, :]
        dq_ref[:, at : at + WIDE] = low(tile)

    @pl.when(block == length // BLOCK - 1)
    def _():
        for j in range(0, length, BLOCK):
            rows = slice(j, j + BLOCK)

            def gather(acc):
                first, middle, last = acc[0, rows, :], acc[1, rows, :], acc[2, rows, :]
                return middle + jnp.where(
                    low_lanes, first + pltpu.roll(first, HEAD, 1), last + pltpu.roll(last, HEAD, 1)
                )

            tile = gather(k_acc)
            tile = tile * cos_ref[rows, :] - swap_halves(tile) * sin_ref[rows, :]
            dk_ref[rows, :] = low(tile)
            dv_ref[rows, :] = low(gather(v_acc))

    @pl.when(now == most)
    def _():
        for stage in (2, 3):
            for fold in folds:
                fold.advance(stage)
        place = tuple(bit_of(name) for name in AXES[1:])
        wide = gate_sum.shape[-1] // 4
        stores = [
            pltpu.make_async_copy(
                folds[at].received[3].at[:, half * wide : (half + 1) * wide],
                whole.at[place + (slice(None), columns)],
                near.at[3 + 2 * at + half],
            )
            for at, whole in enumerate((gate_sum, up_sum))
            for half, columns in enumerate(hidden_columns(wide))
        ]
        stores.append(
            pltpu.make_async_copy(
                folds[2].received[3], down_sum.at[(bit_of("core"),) + place], near.at[7]
            )
        )
        for store in stores:
            store.start()
        for fold in folds:
            fold.finish()
        for store in stores:
            store.wait()


def attend_back(qkv, mixed_grad, mixed, lse, seg_col, seg_row, cosines, sines, gate_term, up_term, down_term):
    length = qkv.shape[0]
    terms = [t.reshape(2, 2, 2, 2, t.shape[0] // 16, t.shape[1]) for t in (gate_term, up_term, down_term)]
    rows, wide = terms[0].shape[4:]
    down_rows, width = terms[2].shape[4:]
    anywhere = pl.BlockSpec(memory_space=pl.ANY)
    pairs = KV_HEADS // 2
    q_tiles = HEADS * HEAD // WIDE
    q_block = pl.BlockSpec((BLOCK, 3 * WIDE), lambda b, i: (i, b))
    kv_block = pl.BlockSpec((length, WIDE), lambda b, i: (0, b))
    table = pl.BlockSpec((length, WIDE), lambda b, i: (0, 0), pipeline_mode=pl.Buffered(1))
    return pl.pallas_call(
        attend_back_body,
        grid=(pairs, length // BLOCK),
        in_specs=[
            q_block,
            pl.BlockSpec((length, WIDE), lambda b, i: (0, q_tiles + b)),
            pl.BlockSpec((length, WIDE), lambda b, i: (0, q_tiles + pairs + b)),
            q_block,
            q_block,
            pl.BlockSpec((1, 8, BLOCK), lambda b, i: (b, 0, i)),
            pl.BlockSpec((length, 1), lambda b, i: (0, 0)),
            pl.BlockSpec((1, BLOCK), lambda b, i: (0, i)),
            table,
            table,
        ]
        + [anywhere] * 3,
        out_specs=[q_block, kv_block, kv_block] + [anywhere] * 3,
        out_shape=[
            jax.ShapeDtypeStruct((length, HEADS * HEAD), jnp.bfloat16),
            jax.ShapeDtypeStruct((length, KV_HEADS * HEAD), jnp.bfloat16),
            jax.ShapeDtypeStruct((length, KV_HEADS * HEAD), jnp.bfloat16),
            jax.ShapeDtypeStruct((2, 2, 2, rows, 2 * wide), jnp.bfloat16),
            jax.ShapeDtypeStruct((2, 2, 2, rows, 2 * wide), jnp.bfloat16),
            jax.ShapeDtypeStruct((2, 2, 2, 2, down_rows, width), jnp.bfloat16),
        ],
        scratch_shapes=[
            pltpu.VMEM((4, length, WIDE), jnp.bfloat16),
            pltpu.VMEM((4, length, WIDE), jnp.bfloat16),
            pltpu.VMEM((WIDE, length), jnp.bfloat16),
            pltpu.VMEM((3, length, WIDE), jnp.float32),
            pltpu.VMEM((3, length, WIDE), jnp.float32),
            pltpu.VMEM((6 * HEAD, BLOCK), jnp.float32),
            pltpu.VMEM((2, 3, 2 * BLOCK, WIDE), jnp.bfloat16),
            pltpu.VMEM((8, BLOCK), jnp.float32),
            pltpu.SemaphoreType.DMA((2, 12)),
            pltpu.SemaphoreType.DMA((8,)),
        ]
        + [pltpu.VMEM((2,) + (2,) * left + (rows, wide), jnp.bfloat16) for left in (3, 3, 2, 1, 0)]
        + [pltpu.VMEM((2,) * left + (down_rows, width), jnp.bfloat16) for left in (3, 3, 2, 1, 0)],
        compiler_params=pltpu.CompilerParams(
            collective_id=3, has_side_effects=True, vmem_limit_bytes=VMEM_MOST
        ),
        cost_estimate=pl.CostEstimate(
            flops=40 * length * length * HEADS * HEAD // 2,
            bytes_accessed=12 * length * HEADS * HEAD,
            transcendentals=HEADS * length * length // 2,
        ),
        name="attend_back",
    )(qkv, qkv, qkv, mixed_grad, mixed, lse, seg_col, seg_row, cosines, sines, *terms)


def mix_body(x_ref, mixed_ref, w_ref, gain_ref, residual_ref, normed_ref, turned_ref):
    residual = x_ref[...].astype(jnp.float32) + mm(mixed_ref[...], w_ref[...])
    residual_ref[...] = residual
    inverse = lax.rsqrt(jnp.mean(residual * residual, axis=-1, keepdims=True) + epsilon)
    normed = residual * inverse * gain_ref[...]
    normed_ref[...] = low(normed)
    turned_ref[...] = low(normed.T)


def mix(x, mixed, w, gain):
    length, width = x.shape
    rows = pl.BlockSpec((BLOCK, width), lambda i: (i, 0))
    return pl.pallas_call(
        mix_body,
        grid=(length // BLOCK,),
        in_specs=[
            rows,
            rows,
            pl.BlockSpec(w.shape, lambda i: (0, 0), pipeline_mode=pl.Buffered(1)),
            pl.BlockSpec((1, width), lambda i: (0, 0)),
        ],
        out_specs=[rows, rows, pl.BlockSpec((width, BLOCK), lambda i: (0, i))],
        out_shape=[
            jax.ShapeDtypeStruct((length, width), jnp.float32),
            jax.ShapeDtypeStruct((length, width), jnp.bfloat16),
            jax.ShapeDtypeStruct((width, length), jnp.bfloat16),
        ],
        cost_estimate=pl.CostEstimate(
            flops=2 * length * width * width, bytes_accessed=12 * length * width, transcendentals=0
        ),
        name="mix",
    )(x, mixed, w, gain)


def norm_grad(grad, gain, scaled, inverse):
    weighted = grad * gain
    return inverse * (weighted - scaled * jnp.mean(weighted * scaled, axis=-1, keepdims=True))


def turn_body(residual_ref, out_a, out_b, back_a, back_b, c_ref, mixed_ref, w_ref, gain_ref,
              result_ref, grad_ref, mixed_grad_ref, term_ref, gain_term_ref, total):
    step = pl.program_id(0)
    residual = residual_ref[...]
    result_ref[...] = low(residual + out_a[...] + out_b[...])
    inverse = lax.rsqrt(jnp.mean(residual * residual, axis=-1, keepdims=True) + epsilon)
    scaled = residual * inverse
    normed_grad = back_a[...] + back_b[...]
    gain_term = jnp.sum(normed_grad * scaled, axis=0, keepdims=True)
    grad = c_ref[...].astype(jnp.float32) + norm_grad(normed_grad, gain_ref[...], scaled, inverse)
    grad_ref[...] = grad
    grad_low = low(grad)
    mixed_grad_ref[...] = low(mm_nt(grad_low, w_ref[...]))
    term = mm_tn(mixed_ref[...], grad_low)

    @pl.when(step == 0)
    def _():
        total[...] = term
        gain_term_ref[...] = jnp.broadcast_to(gain_term, gain_term_ref.shape)

    @pl.when(step > 0)
    def _():
        total[...] += term
        gain_term_ref[...] += jnp.broadcast_to(gain_term, gain_term_ref.shape)

    @pl.when(step == pl.num_programs(0) - 1)
    def _():
        term_ref[...] = low(total[...])


def turn(residual, out_a, out_b, back_a, back_b, c, mixed, w, gain):
    length, width = residual.shape
    rows = pl.BlockSpec((BLOCK, width), lambda i: (i, 0))
    whole = lambda shape: pl.BlockSpec(shape, lambda i: (0, 0), pipeline_mode=pl.Buffered(1))
    return pl.pallas_call(
        turn_body,
        grid=(length // BLOCK,),
        in_specs=[rows] * 7 + [whole(w.shape), pl.BlockSpec((1, width), lambda i: (0, 0))],
        out_specs=[
            rows, rows, rows, whole((width, width)), pl.BlockSpec((8, width), lambda i: (0, 0)),
        ],
        out_shape=[
            jax.ShapeDtypeStruct((length, width), jnp.bfloat16),
            jax.ShapeDtypeStruct((length, width), jnp.float32),
            jax.ShapeDtypeStruct((length, width), jnp.bfloat16),
            jax.ShapeDtypeStruct((width, width), jnp.bfloat16),
            jax.ShapeDtypeStruct((8, width), jnp.float32),
        ],
        scratch_shapes=[pltpu.VMEM((width, width), jnp.float32)],
        compiler_params=pltpu.CompilerParams(vmem_limit_bytes=VMEM_MOST),
        cost_estimate=pl.CostEstimate(
            flops=4 * length * width * width, bytes_accessed=32 * length * width, transcendentals=0
        ),
        name="turn",
    )(residual, out_a, out_b, back_a, back_b, c, mixed, w, gain)


def close_body(dq_ref, dk_ref, dv_ref, normed_ref, x_ref, grad_ref, w_ref, gain_ref, mix_term_ref,
               term_ref, token_grad_ref, gain_term_ref, turned):
    step = pl.program_id(0)
    rows_each = x_ref.shape[0]
    length = normed_ref.shape[0]
    q_width, k_width = dq_ref.shape[1], dk_ref.shape[1]

    @pl.when(step == 0)
    def _():
        for at in range(0, length, BLOCK):
            turned[:, at : at + BLOCK] = normed_ref[at : at + BLOCK, :].T

    for chunk in range(3):

        @pl.when(step == chunk)
        def _(chunk=chunk):
            at = chunk * k_width
            term_ref[...] = low(mm(turned[...], dq_ref[:, at : at + k_width]))

    @pl.when(step == 3)
    def _():
        term_ref[...] = low(mm(turned[...], dk_ref[...]))

    @pl.when(step == 4)
    def _():
        term_ref[...] = low(mm(turned[...], dv_ref[...]))

    @pl.when(step > 4)
    def _():
        term_ref[...] = mix_term_ref[...]

    rows = pl.ds(pl.multiple_of(step * rows_each, rows_each), rows_each)
    normed_grad = (
        mm_nt(dq_ref[rows, :], w_ref[:, :q_width])
        + mm_nt(dk_ref[rows, :], w_ref[:, q_width : q_width + k_width])
        + mm_nt(dv_ref[rows, :], w_ref[:, q_width + k_width :])
    )
    values = x_ref[...].astype(jnp.float32)
    inverse = lax.rsqrt(jnp.mean(values * values, axis=-1, keepdims=True) + epsilon)
    scaled = values * inverse
    gain_term = jnp.sum(normed_grad * scaled, axis=0, keepdims=True)
    token_grad_ref[...] = low(
        grad_ref[...] + norm_grad(normed_grad, gain_ref[...], scaled, inverse)
    )

    @pl.when(step == 0)
    def _():
        gain_term_ref[...] = jnp.broadcast_to(gain_term, gain_term_ref.shape)

    @pl.when(step > 0)
    def _():
        gain_term_ref[...] += jnp.broadcast_to(gain_term, gain_term_ref.shape)


def close(dq, dk, dv, normed, x, grad, w, gain, mix_term):
    length, width = x.shape
    k_width = dk.shape[1]
    steps = (w.shape[1] + mix_term.shape[1]) // k_width
    rows = pl.BlockSpec((length // steps, width), lambda i: (i, 0))
    whole = lambda a: pl.BlockSpec(a.shape, lambda i: (0, 0), pipeline_mode=pl.Buffered(1))
    return pl.pallas_call(
        close_body,
        grid=(steps,),
        in_specs=[whole(dq), whole(dk), whole(dv), whole(normed), rows, rows, whole(w),
                  pl.BlockSpec((1, width), lambda i: (0, 0)),
                  pl.BlockSpec((width, k_width), lambda i: (0, jnp.maximum(i - 5, 0)))],
        out_specs=[
            pl.BlockSpec((width, k_width), lambda i: (0, i)),
            rows,
            pl.BlockSpec((8, width), lambda i: (0, 0)),
        ],
        out_shape=[
            jax.ShapeDtypeStruct((width, steps * k_width), jnp.bfloat16),
            jax.ShapeDtypeStruct((length, width), jnp.bfloat16),
            jax.ShapeDtypeStruct((8, width), jnp.float32),
        ],
        scratch_shapes=[pltpu.VMEM((width, length), jnp.bfloat16)],
        compiler_params=pltpu.CompilerParams(vmem_limit_bytes=VMEM_MOST),
        cost_estimate=pl.CostEstimate(
            flops=4 * length * width * w.shape[1], bytes_accessed=24 * length * width, transcendentals=0
        ),
        name="close",
    )(dq, dk, dv, normed, x, grad, w, gain, mix_term)


def feed_body(which_ref, normed_ref, turned_ref, c_ref, gate_ref, up_ref, down_ref,
              out_ref, back_ref, gate_grad_ref, up_grad_ref, down_grad_ref,
              hidden_t, gate_low, up_low):
    first = pl.program_id(0) == 0
    length, width = normed_ref.shape

    @pl.when(first)
    def _():
        out_ref[...] = jnp.zeros_like(out_ref)
        back_ref[...] = jnp.zeros_like(back_ref)

    for at in range(0, length, BLOCK):
        rows = slice(at, at + BLOCK)
        normed = normed_ref[rows, :]
        gate_sum = mm(normed, gate_ref[...])
        up_sum = mm(normed, up_ref[...])
        hidden_grad = mm_nt(c_ref[rows, :], down_ref[...])
        sigmoid = jax.nn.sigmoid(gate_sum)
        activated = gate_sum * sigmoid
        hidden = low(activated * up_sum)
        gate_grad = low(hidden_grad * up_sum * (sigmoid + activated * (1.0 - sigmoid)))
        up_grad = low(hidden_grad * activated)
        hidden_t[:, rows] = hidden.T
        gate_low[rows, :] = gate_grad
        up_low[rows, :] = up_grad
        out_ref[rows, :] += mm(hidden, down_ref[...])
        back_ref[rows, :] += mm_nt(gate_grad, gate_ref[...]) + mm_nt(up_grad, up_ref[...])
    step = 384
    for at in range(0, width, step):
        rows = slice(at, at + step)
        gate_grad_ref[rows, :] = low(mm(turned_ref[rows, :], gate_low[...]))
        up_grad_ref[rows, :] = low(mm(turned_ref[rows, :], up_low[...]))
        down_grad_ref[:, rows] = low(mm(hidden_t[...], c_ref[:, rows]))


def feed(which, normed, turned, c, gate, up, down):
    length, width = normed.shape
    wide = gate.shape[1] // 4
    whole = pl.BlockSpec((length, width), lambda t, w: (0, 0), pipeline_mode=pl.Buffered(1))
    columns = pl.BlockSpec((width, wide), lambda t, w: (0, w[0] + 2 * t))
    rows = pl.BlockSpec((wide, width), lambda t, w: (w[0] + 2 * t, 0))
    total = pl.BlockSpec((length, width), lambda t, w: (0, 0), pipeline_mode=pl.Buffered(1))
    columns_out = pl.BlockSpec((width, wide), lambda t, w: (0, t))
    return pl.pallas_call(
        feed_body,
        grid_spec=pltpu.PrefetchScalarGridSpec(
            num_scalar_prefetch=1,
            grid=(2,),
            in_specs=[
                whole,
                pl.BlockSpec((width, length), lambda t, w: (0, 0), pipeline_mode=pl.Buffered(1)),
                whole,
                columns,
                columns,
                rows,
            ],
            out_specs=[
                total,
                total,
                columns_out,
                columns_out,
                pl.BlockSpec((wide, width), lambda t, w: (t, 0)),
            ],
            scratch_shapes=[
                pltpu.VMEM((wide, length), jnp.bfloat16),
                pltpu.VMEM((length, wide), jnp.bfloat16),
                pltpu.VMEM((length, wide), jnp.bfloat16),
            ],
        ),
        out_shape=[
            jax.ShapeDtypeStruct((length, width), jnp.float32),
            jax.ShapeDtypeStruct((length, width), jnp.float32),
            jax.ShapeDtypeStruct((width, 2 * wide), jnp.bfloat16),
            jax.ShapeDtypeStruct((width, 2 * wide), jnp.bfloat16),
            jax.ShapeDtypeStruct((2 * wide, width), jnp.bfloat16),
        ],
        compiler_params=pltpu.CompilerParams(vmem_limit_bytes=VMEM_MOST),
        cost_estimate=pl.CostEstimate(
            flops=18 * length * width * wide * 2,
            bytes_accessed=12 * width * wide * 2 + 16 * length * width,
            transcendentals=length * wide * 2,
        ),
        name="feed",
    )(which, normed, turned, c, gate, up, down)


def shortened(array):
    return jax.tree.map(lambda a: a.astype(jnp.bfloat16) if a.dtype == jnp.float32 else a, array)


def product(left, right):
    return jnp.dot(left, right, preferred_element_type=jnp.float32)


def product_tn(left, right):
    return lax.dot_general(
        left, right, (((0,), (0,)), ((), ())), preferred_element_type=jnp.float32
    )


def product_nt(left, right):
    return lax.dot_general(
        left, right, (((1,), (1,)), ((), ())), preferred_element_type=jnp.float32
    )


def rotary_tables(positions, width):
    half_width = width // 2
    freqs = jnp.exp(
        jnp.arange(half_width, dtype=jnp.float32) * (-2.0 * math.log(rope_base) / width)
    )
    angles = positions[:, None] * freqs[None, :]
    return (jnp.cos(angles), jnp.sin(angles))


def rotate(values, cosines, sines):
    half_width = values.shape[-1] // 2
    first = values[..., :half_width]
    second = values[..., half_width:]
    return jnp.concatenate(
        [first * cosines - second * sines, second * cosines + first * sines], axis=-1
    )


def unrotate(values, cosines, sines):
    half_width = values.shape[-1] // 2
    first = values[..., :half_width]
    second = values[..., half_width:]
    return jnp.concatenate(
        [first * cosines + second * sines, second * cosines - first * sines], axis=-1
    )


def norm_back(grad_rows, gain, scaled, inverse):
    weighted = grad_rows * gain
    return inverse * (weighted - scaled * jnp.mean(weighted * scaled, axis=-1, keepdims=True))


def plain_local(
    inputs,
    segments,
    out_grad,
    attention_gain,
    query_weight,
    key_weight,
    value_weight,
    output_weight,
    feedforward_gain,
    gate_weight,
    up_weight,
    down_weight,
):
    gathered = (
        lax.all_gather(attention_gain, "fsdp", axis=0, tiled=True),
        lax.all_gather(query_weight, "fsdp", axis=0, tiled=True),
        lax.all_gather(key_weight, "fsdp", axis=0, tiled=True),
        lax.all_gather(value_weight, "fsdp", axis=0, tiled=True),
        lax.all_gather(output_weight, "fsdp", axis=0, tiled=True),
        lax.all_gather(feedforward_gain, "fsdp", axis=0, tiled=True),
        lax.all_gather(gate_weight, "fsdp", axis=0, tiled=True),
        lax.all_gather(up_weight, "fsdp", axis=0, tiled=True),
        lax.all_gather(down_weight, "fsdp", axis=0, tiled=True),
    )
    full_query, full_key, full_value, full_output = (
        gathered[1],
        gathered[2],
        gathered[3],
        gathered[4],
    )
    full_gate, full_up, full_down = (gathered[6], gathered[7], gathered[8])
    gain_attention = gathered[0].astype(jnp.float32)
    gain_feed = gathered[5].astype(jnp.float32)
    span = inputs.shape[1]
    length = segments.shape[1]
    groups_q = HEADS // KV_HEADS
    key_width = KV_HEADS * HEAD
    start = lax.axis_index("fsdp") * span
    query_pos = start + jnp.arange(span, dtype=jnp.int32)
    key_pos = jnp.arange(length, dtype=jnp.int32)
    cosines, sines = rotary_tables(query_pos.astype(jnp.float32), HEAD)
    cos_four, sin_four = (cosines[:, None, None, :], sines[:, None, None, :])
    cos_three, sin_three = (cosines[:, None, :], sines[:, None, :])
    causal = query_pos[:, None] >= key_pos[None, :]
    scale = HEAD ** (-0.5)

    def micro_step(totals, sequence):
        tokens, segment_row, cotangent = sequence
        own_segment = lax.dynamic_slice_in_dim(segment_row, start, span)
        allowed = causal & (own_segment[:, None] == segment_row[None, :])
        values = tokens.astype(jnp.float32)
        inverse_a = lax.rsqrt(jnp.mean(values * values, axis=-1, keepdims=True) + epsilon)
        scaled_a = values * inverse_a
        normed_a = (scaled_a * gain_attention).astype(jnp.bfloat16)
        query_lin = product(normed_a, full_query).reshape(span, KV_HEADS, groups_q, HEAD)
        queries = rotate(query_lin, cos_four, sin_four).astype(jnp.bfloat16)
        key_lin = product(normed_a, full_key).reshape(span, KV_HEADS, HEAD)
        key_rows = (
            rotate(key_lin, cos_three, sin_three).astype(jnp.bfloat16).reshape(span, key_width)
        )
        value_rows = product(normed_a, full_value).astype(jnp.bfloat16)
        all_keys, all_values = (
            lax.all_gather(key_rows, "fsdp", axis=0, tiled=True),
            lax.all_gather(value_rows, "fsdp", axis=0, tiled=True),
        )
        all_keys = all_keys.reshape(length, KV_HEADS, HEAD)
        all_values = all_values.reshape(length, KV_HEADS, HEAD)
        scores = (
            jnp.einsum("qhgd,khd->hgqk", queries, all_keys, preferred_element_type=jnp.float32)
            * scale
        )
        scores = jnp.where(allowed, scores, -1e30)
        highest = jnp.max(scores, axis=-1, keepdims=True)
        expo_scores = jnp.exp(scores - highest)
        attention = expo_scores / jnp.sum(expo_scores, axis=-1, keepdims=True)
        attention_low = attention.astype(jnp.bfloat16)
        mixed = jnp.einsum(
            "hgqk,khd->qhgd", attention_low, all_values, preferred_element_type=jnp.float32
        )
        mixed = mixed.reshape(span, HEADS * HEAD).astype(jnp.bfloat16)
        residual = values + product(mixed, full_output)
        inverse_f = lax.rsqrt(jnp.mean(residual * residual, axis=-1, keepdims=True) + epsilon)
        scaled_f = residual * inverse_f
        normed_f = (scaled_f * gain_feed).astype(jnp.bfloat16)
        gate_sum = product(normed_f, full_gate)
        up_sum = product(normed_f, full_up)
        sigmoid_gate = jax.nn.sigmoid(gate_sum)
        activated = gate_sum * sigmoid_gate
        hidden = (activated * up_sum).astype(jnp.bfloat16)
        result = (residual + product(hidden, full_down)).astype(jnp.bfloat16)
        down_wgrad = product_tn(hidden, cotangent)
        hidden_grad = product_nt(cotangent, full_down)
        gate_grad = (
            hidden_grad * up_sum * sigmoid_gate * (1.0 + gate_sum * (1.0 - sigmoid_gate))
        ).astype(jnp.bfloat16)
        up_grad = (hidden_grad * activated).astype(jnp.bfloat16)
        gate_wgrad = product_tn(normed_f, gate_grad)
        up_wgrad = product_tn(normed_f, up_grad)
        normed_f_grad = product_nt(gate_grad, full_gate) + product_nt(up_grad, full_up)
        feed_gain_grad = jnp.sum(normed_f_grad * scaled_f, axis=0)
        residual_grad = cotangent.astype(jnp.float32) + norm_back(
            normed_f_grad, gain_feed, scaled_f, inverse_f
        )
        residual_low = residual_grad.astype(jnp.bfloat16)
        output_wgrad = product_tn(mixed, residual_low)
        mixed_grad = (
            product_nt(residual_low, full_output)
            .astype(jnp.bfloat16)
            .reshape(span, KV_HEADS, groups_q, HEAD)
        )
        attention_grad = jnp.einsum(
            "qhgd,khd->hgqk", mixed_grad, all_values, preferred_element_type=jnp.float32
        )
        row_totals = jnp.sum(attention * attention_grad, axis=-1, keepdims=True)
        score_grad = (attention * (attention_grad - row_totals) * scale).astype(jnp.bfloat16)
        value_grads = jnp.einsum(
            "hgqk,qhgd->khd", attention_low, mixed_grad, preferred_element_type=jnp.float32
        ).reshape(length, key_width)
        key_grads = jnp.einsum(
            "hgqk,qhgd->khd", score_grad, queries, preferred_element_type=jnp.float32
        ).reshape(length, key_width)
        query_grad = jnp.einsum(
            "hgqk,khd->qhgd", score_grad, all_keys, preferred_element_type=jnp.float32
        )
        key_back, value_back = (
            lax.psum_scatter(key_grads, "fsdp", scatter_dimension=0, tiled=True),
            lax.psum_scatter(value_grads, "fsdp", scatter_dimension=0, tiled=True),
        )
        query_low = (
            unrotate(query_grad, cos_four, sin_four)
            .reshape(span, HEADS * HEAD)
            .astype(jnp.bfloat16)
        )
        key_low = (
            unrotate(key_back.reshape(span, KV_HEADS, HEAD), cos_three, sin_three)
            .reshape(span, key_width)
            .astype(jnp.bfloat16)
        )
        value_low = value_back.astype(jnp.bfloat16)
        query_wgrad = product_tn(normed_a, query_low)
        key_wgrad = product_tn(normed_a, key_low)
        value_wgrad = product_tn(normed_a, value_low)
        normed_a_grad = (
            product_nt(query_low, full_query)
            + product_nt(key_low, full_key)
            + product_nt(value_low, full_value)
        )
        attention_gain_term = jnp.sum(normed_a_grad * scaled_a, axis=0)
        token_grad = (
            residual_grad + norm_back(normed_a_grad, gain_attention, scaled_a, inverse_a)
        ).astype(jnp.bfloat16)
        terms = (
            attention_gain_term,
            query_wgrad,
            key_wgrad,
            value_wgrad,
            output_wgrad,
            feed_gain_grad,
            gate_wgrad,
            up_wgrad,
            down_wgrad,
        )
        totals = tuple((left + right for left, right in zip(totals, terms)))
        return (totals, (result, token_grad))

    initial = tuple((jnp.zeros(weight.shape, jnp.float32) for weight in gathered))
    totals, (outputs, input_grads) = lax.scan(micro_step, initial, (inputs, segments, out_grad))
    shards = jax.tree.map(
        lambda part: part.astype(jnp.float32),
        lax.psum_scatter(shortened(totals), "fsdp", scatter_dimension=0, tiled=True),
    )
    summed = lax.psum(shards, "group")
    return (
        outputs,
        input_grads,
        summed[0],
        summed[1],
        summed[2],
        summed[3],
        summed[4],
        summed[5],
        summed[6],
        summed[7],
        summed[8],
    )


class Places:
    def __init__(self, group_size):
        self.group = lax.axis_index("group")
        self.y = lax.axis_index("fsdp")
        self.size = group_size
        self.masks = {"core": 1, "x": 2, "zlo": 4, "zhi": 8}

    def bit(self, name):
        if name == "y":
            return self.y
        return (self.group // self.masks[name]) % 2

    def swap(self, array, name):
        if name == "y":
            return lax.ppermute(array, "fsdp", [(0, 1), (1, 0)])
        mask = self.masks[name]
        return lax.ppermute(array, "group", [(i, i ^ mask) for i in range(self.size)])


def part_of(array, axis, bit):
    size = array.shape[axis] // 2
    return lax.dynamic_slice_in_dim(array, bit * size, size, axis)


def add_up(terms):
    total = terms[0].astype(jnp.float32)
    for term in terms[1:]:
        total = total + term.astype(jnp.float32)
    return low(total)


def in_order(bit, own, other, axis):
    return jnp.where(
        bit == 0,
        jnp.concatenate([own, other], axis=axis),
        jnp.concatenate([other, own], axis=axis),
    )


def paired_local(
    group_size,
    inputs,
    segments,
    out_grad,
    attention_gain,
    query_weight,
    key_weight,
    value_weight,
    output_weight,
    feedforward_gain,
    gate_weight,
    up_weight,
    down_weight,
):
    places = Places(group_size)
    y = places.y
    span, length, width = inputs.shape[1], segments.shape[1], inputs.shape[2]
    q_width = query_weight.shape[1]

    gains = jnp.pad(
        jnp.stack([attention_gain, feedforward_gain]).astype(jnp.float32), ((0, 6), (0, 0))
    )
    tokens, qkv_weight, gains = fetch(inputs, query_weight, key_weight, value_weight, gains)
    gains = gains.transpose(1, 0, 2).reshape(8, width)
    gain_a, gain_f = gains[0:1], gains[1:2]

    segment = lax.dynamic_index_in_dim(segments, y, 0, False)
    seg_col, seg_row = segment[:, None], segment[None, :]
    cosines, sines = rope_tables(length)
    normed_a, qkv = project(tokens, gain_a, qkv_weight, cosines, sines)
    mixed, lse, c, mix_weight, full_gate, full_up, full_down = attend(
        qkv, seg_col, seg_row, out_grad, output_weight, gate_weight, up_weight, down_weight
    )

    residual, normed_f, turned_f = mix(tokens, mixed, mix_weight, gain_f)

    core = places.bit("core")
    theirs = feed((1 - core).reshape(1), normed_f, turned_f, c, full_gate, full_up, full_down)
    came = [places.swap(term, "core") for term in theirs[2:]]
    mine = feed(core.reshape(1), normed_f, turned_f, c, full_gate, full_up, full_down)
    hidden_terms = [add_up([own, other]) for own, other in zip(mine[2:], came)]
    result, residual_grad, mixed_grad, mix_term, feed_gain_term = turn(
        residual, theirs[0], mine[0], theirs[1], mine[1], c, mixed, mix_weight, gain_f
    )
    dq, dk, dv, gate_sum, up_sum, down_sum = attend_back(
        qkv, mixed_grad, mixed, lse, seg_col, seg_row, cosines, sines, *hidden_terms
    )
    term, token_grad, attention_gain_term = close(
        dq, dk, dv, normed_a, tokens, residual_grad, qkv_weight, gain_a, mix_term
    )
    gain_terms = jnp.concatenate(
        [attention_gain_term[0:1], feed_gain_term[0:1], jnp.zeros_like(gains[2:])], axis=0
    )
    gate_sum, up_sum, down_sum, sums, outputs, input_grads, gain_sums = finish(
        term, gain_terms, result, token_grad, gate_sum, up_sum, down_sum
    )
    gain_grads = lax.dynamic_slice_in_dim(gain_sums, y * (width // 2), width // 2, 1)
    k_width = key_weight.shape[1]
    sums = sums.reshape(width // 2, -1).astype(jnp.float32)
    ends = (0, q_width, q_width + k_width, q_width + 2 * k_width, sums.shape[1])
    parts = [sums[:, a:b] for a, b in zip(ends[:-1], ends[1:])]
    return (
        outputs,
        input_grads,
        gain_grads[0],
        *parts,
        gain_grads[1],
        gate_sum.reshape(width // 2, -1).astype(jnp.float32),
        up_sum.reshape(width // 2, -1).astype(jnp.float32),
        down_sum.reshape(-1, width).astype(jnp.float32),
    )


def solution(mesh):
    placed = (
        P("group", "fsdp", None),
        P("group", None),
        P("group", "fsdp", None),
        P("fsdp"),
        P("fsdp", None),
        P("fsdp", None),
        P("fsdp", None),
        P("fsdp", None),
        P("fsdp"),
        P("fsdp", None),
        P("fsdp", None),
        P("fsdp", None),
    )
    group_size, fsdp_size = mesh.shape["group"], mesh.shape["fsdp"]

    def local(*arrays):
        if group_size == 16 and fsdp_size == 2 and arrays[0].shape[0] == 2:
            return paired_local(group_size, *arrays)
        return plain_local(*arrays)

    return jax.shard_map(
        local,
        mesh=mesh,
        in_specs=placed,
        out_specs=(
            P("group", "fsdp", None),
            P("group", "fsdp", None),
            P("fsdp"),
            P("fsdp", None),
            P("fsdp", None),
            P("fsdp", None),
            P("fsdp", None),
            P("fsdp"),
            P("fsdp", None),
            P("fsdp", None),
            P("fsdp", None),
        ),
        check_vma=False,
    )
```

```python
import functools
import math

import jax
import jax.numpy as jnp
from jax import lax
from jax.experimental import pallas as pl
from jax.experimental.pallas import tpu as pltpu
from jax.sharding import PartitionSpec as P

HEADS = 18
KV_HEADS = 6
HEAD = 64
epsilon = 1e-05
rope_base = 10000.0
BLOCK = 256
WIDE = 128
VMEM_MOST = 66 * 1024 * 1024 - 3 * 1024 * 1024


def mm(left, right):
    return jnp.dot(left, right, preferred_element_type=jnp.float32)


def mm_nt(left, right):
    return lax.dot_general(
        left, right, (((1,), (1,)), ((), ())), preferred_element_type=jnp.float32
    )


def mm_tn(left, right):
    return lax.dot_general(
        left, right, (((0,), (0,)), ((), ())), preferred_element_type=jnp.float32
    )


def low(values):
    return values.astype(jnp.bfloat16)


def lanes_below(rows, period, limit):
    lane = lax.broadcasted_iota(jnp.int32, (rows, WIDE), 1)
    return lane % period < limit


def swap_halves(tile):
    ahead = pltpu.roll(tile, WIDE - HEAD // 2, 1)
    behind = pltpu.roll(tile, HEAD // 2, 1)
    return jnp.where(lanes_below(tile.shape[0], HEAD, HEAD // 2), ahead, behind)


def rope_tables(length):
    half_width = HEAD // 2
    freqs = jnp.exp(
        jnp.arange(half_width, dtype=jnp.float32) * (-2.0 * math.log(rope_base) / HEAD)
    )
    angles = jnp.arange(length, dtype=jnp.float32)[:, None] * freqs[None, :]
    cosines, sines = jnp.cos(angles), jnp.sin(angles)
    return (
        jnp.concatenate([cosines] * 4, axis=1),
        jnp.concatenate([-sines, sines] * 2, axis=1),
    )


def project_body(x_ref, gain_ref, w_ref, cos_ref, sin_ref, normed_ref, qkv_ref):
    values = x_ref[...].astype(jnp.float32)
    inverse = lax.rsqrt(jnp.mean(values * values, axis=-1, keepdims=True) + epsilon)
    normed = low(values * inverse * gain_ref[...])
    normed_ref[...] = normed
    cosines, sines = cos_ref[...], sin_ref[...]
    width = qkv_ref.shape[1]
    q_width, k_width = HEADS * HEAD, KV_HEADS * HEAD
    step = 384
    for at in range(0, width, step):
        wide = mm(normed, w_ref[:, at : at + step])
        for part in range(0, step, WIDE):
            tile = wide[:, part : part + WIDE]
            if at + part < q_width + k_width:
                tile = tile * cosines + swap_halves(tile) * sines
            if at + part < q_width:
                tile = tile * HEAD ** (-0.5)
            qkv_ref[:, at + part : at + part + WIDE] = low(tile)


def project(x, gain, w, cosines, sines):
    length, width = x.shape
    out = w.shape[1]
    rows = pl.BlockSpec((BLOCK, width), lambda i: (i, 0))
    table = pl.BlockSpec((BLOCK, WIDE), lambda i: (i, 0))
    return pl.pallas_call(
        project_body,
        grid=(length // BLOCK,),
        in_specs=[
            rows,
            pl.BlockSpec((1, width), lambda i: (0, 0)),
            pl.BlockSpec((width, out), lambda i: (0, 0), pipeline_mode=pl.Buffered(1)),
            table,
            table,
        ],
        out_specs=[rows, pl.BlockSpec((BLOCK, out), lambda i: (i, 0))],
        out_shape=[
            jax.ShapeDtypeStruct((length, width), jnp.bfloat16),
            jax.ShapeDtypeStruct((length, out), jnp.bfloat16),
        ],
        cost_estimate=pl.CostEstimate(
            flops=2 * length * width * out,
            bytes_accessed=2 * (2 * length * width + length * out + width * out),
            transcendentals=0,
        ),
        name="project",
    )(x, gain, w, cosines, sines)


MESH = pl.DeviceIdType.MESH
MASKS = {"core": 1, "x": 2, "zlo": 4, "zhi": 8}


def bit_of(name):
    if name == "y":
        return lax.axis_index("fsdp")
    return (lax.axis_index("group") // MASKS[name]) % 2


def peer_of(name):
    if name == "y":
        return {"fsdp": 1 - lax.axis_index("fsdp")}
    return {"group": lax.axis_index("group") + MASKS[name] * (1 - 2 * bit_of(name))}


def greet(names):
    barrier = pltpu.get_barrier_semaphore()
    for name in names:
        pl.semaphore_signal(barrier, inc=1, device_id=peer_of(name), device_id_type=MESH)
    pl.semaphore_wait(barrier, len(names))


def across(source, target, sems, slot, name):
    return pltpu.make_async_remote_copy(
        src_ref=source,
        dst_ref=target,
        send_sem=sems.at[0, slot],
        recv_sem=sems.at[1, slot],
        device_id=peer_of(name),
        device_id_type=MESH,
    )


class Spread:
    def __init__(self, shard, full, order, sems, slot, columns=None):
        self.shard, self.full, self.order, self.sems, self.slot = shard, full, order, sems, slot
        self.columns = columns

    def copy(self, stage):
        y = lax.axis_index("fsdp")
        index = 0
        for at, name in enumerate(self.order):
            index = index + bit_of(name) * 2**at
        slot = self.slot + stage
        where = (slice(None), slice(None)) if self.columns is None else (slice(None), self.columns)
        if stage == 0:
            return across(
                self.shard.at[index], self.full.at[(y * 8 + index,) + where], self.sems, slot, "y"
            )
        count = 2 ** (stage - 1)
        block = self.full.at[(pl.ds((1 - y) * 8 + index // count * count, count),) + where]
        return across(block, block, self.sems, slot, self.order[stage - 1])

    def advance(self, stage):
        if stage >= 0:
            self.copy(stage).wait_recv()
        if stage < len(self.order):
            self.copy(stage + 1).start()

    def finish(self):
        for stage in range(len(self.order) + 1):
            self.copy(stage).wait_send()


def fetch_body(inputs, query, key, value, gains, tokens, weight, both_gains,
               held, held_weight, sems, near):
    y = lax.axis_index("fsdp")
    q_width, k_width = query.shape[2], key.shape[2]
    places = (
        slice(0, q_width),
        slice(q_width, q_width + k_width),
        slice(q_width + k_width, q_width + 2 * k_width),
    )
    shards = (query, key, value)
    loads = [pltpu.make_async_copy(inputs.at[y], held, near.at[0])] + [
        pltpu.make_async_copy(shard, held_weight.at[:, :, place], near.at[1 + at])
        for at, (shard, place) in enumerate(zip(shards, places))
    ]
    for load in loads:
        load.start()
    greet(("y", "x", "zlo", "core"))
    index = bit_of("x") + 2 * bit_of("zlo") + 4 * bit_of("core")
    first = [
        across(shard.at[index], weight.at[y * 8 + index, :, place], sems, at, "y")
        for at, (shard, place) in enumerate(zip(shards, places))
    ]
    span = held.shape[0]
    swap = across(
        inputs.at[1 - y], tokens.at[pl.ds(pl.multiple_of(y * span, span), span)], sems, 3, "y"
    )
    gain_swap = across(gains, both_gains.at[y], sems, 4, "y")
    for copy in first + [gain_swap, swap]:
        copy.start()
    for load in loads:
        load.wait()
    stores = [
        pltpu.make_async_copy(
            held, tokens.at[pl.ds(pl.multiple_of(y * span, span), span)], near.at[4]
        ),
        pltpu.make_async_copy(held_weight, weight.at[pl.ds(y * 8, 8)], near.at[5]),
        pltpu.make_async_copy(gains, both_gains.at[y], near.at[6]),
    ]
    for store in stores:
        store.start()
    for copy in first:
        copy.wait_recv()
    later = []
    for at, name in enumerate(("x", "zlo", "core")):
        count = 2**at
        block = weight.at[pl.ds((1 - y) * 8 + index // count * count, count)]
        copy = across(block, block, sems, 5 + at, name)
        copy.start()
        copy.wait_recv()
        later.append(copy)
    swap.wait_recv()
    gain_swap.wait_recv()
    for copy in first + [gain_swap, swap] + later:
        copy.wait_send()
    for store in stores:
        store.wait()


def fetch(inputs, query, key, value, gains):
    span, width = inputs.shape[1:]
    total = query.shape[1] + 2 * key.shape[1]
    eight = lambda shard: shard.reshape(8, shard.shape[0] // 8, shard.shape[1])
    rows = query.shape[0] // 8
    anywhere = pl.BlockSpec(memory_space=pl.ANY)
    tokens, weight, both_gains = pl.pallas_call(
        fetch_body,
        in_specs=[anywhere] * 5,
        out_specs=[anywhere] * 3,
        out_shape=[
            jax.ShapeDtypeStruct((2 * span, width), inputs.dtype),
            jax.ShapeDtypeStruct((16, rows, total), query.dtype),
            jax.ShapeDtypeStruct((2,) + gains.shape, gains.dtype),
        ],
        scratch_shapes=[
            pltpu.VMEM((span, width), inputs.dtype),
            pltpu.VMEM((8, rows, total), query.dtype),
            pltpu.SemaphoreType.DMA((2, 8)),
            pltpu.SemaphoreType.DMA((7,)),
        ],
        compiler_params=pltpu.CompilerParams(collective_id=1, has_side_effects=True),
        name="fetch",
    )(inputs, eight(query), eight(key), eight(value), gains)
    return tokens, weight.reshape(16 * rows, total), both_gains


AXES = ("y", "x", "zlo", "zhi")


class Fold:
    def __init__(self, source, kept, received, order, sems, slot, near, near_slot):
        self.source, self.kept, self.received = source, kept, received
        self.order, self.sems, self.slot = order, sems, slot
        self.near, self.near_slot = near, near_slot

    def pick(self, stage, bit):
        left = [name for name in AXES if name not in self.order[:stage]]
        return (slice(None),) * left.index(self.order[stage]) + (bit,)

    def held(self, stage):
        return self.source if stage == 0 else self.received[stage - 1]

    def copy(self, stage):
        name = self.order[stage]
        source = self.held(stage).at[self.pick(stage, 1 - bit_of(name))]
        return across(source, self.received[stage], self.sems, self.slot + stage, name)

    def load(self):
        source = self.source.at[self.pick(0, bit_of(self.order[0]))]
        return pltpu.make_async_copy(source, self.kept, self.near.at[self.near_slot])

    def begin(self):
        self.copy(0).start()
        if self.kept is not None:
            self.load().start()

    def advance(self, stage):
        self.copy(stage).wait_recv()
        target = self.received[stage]
        lead = target.ndim - 2
        if stage == 0 and self.kept is not None:
            self.load().wait()
            mine, at, bit = self.kept, 0, None
        else:
            bit = bit_of(self.order[stage])
            mine, at = self.held(stage), len(self.pick(stage, 0)) - 1

        @pl.loop(0, 2**lead)
        def _(n):
            index = tuple(n // 2 ** (lead - 1 - k) % 2 for k in range(lead))
            from_ = index if bit is None else index[:at] + (bit,) + index[at:]
            total = target[index].astype(jnp.float32) + mine[from_].astype(jnp.float32)
            target[index] = low(total)

        if stage + 1 < len(self.order):
            self.copy(stage + 1).start()

    def finish(self):
        for stage in range(len(self.order)):
            self.copy(stage).wait_send()


class Rise:
    def __init__(self, whole, order, columns, sems, slot):
        self.whole, self.order, self.columns, self.sems, self.slot = whole, order, columns, sems, slot

    def block(self, stage):
        index = tuple(
            slice(None) if name in self.order[:stage] + ("zhi",) else bit_of(name)
            for name in AXES[1:]
        )
        if self.whole.ndim == 6:
            return [self.whole.at[(bit_of("core"),) + index]]
        return [self.whole.at[index + (slice(None), columns)] for columns in self.columns]

    def copies(self, stage, first=None):
        blocks = self.block(stage)
        count = len(blocks)
        return [
            across(
                block if first is None else first[at],
                block,
                self.sems,
                self.slot + stage * count + at,
                self.order[stage],
            )
            for at, block in enumerate(blocks)
        ]

    def begin(self, first):
        for copy in self.copies(0, first):
            copy.start()

    def advance(self, stage):
        for copy in self.copies(stage):
            copy.wait_recv()
        if stage + 1 < len(self.order):
            for copy in self.copies(stage + 1):
                copy.start()

    def finish(self):
        for stage in range(len(self.order)):
            for copy in self.copies(stage):
                copy.wait_send()


ORDERS = (("y", "x", "zlo"), ("x", "zlo", "y"), ("zlo", "y", "x"))
BACKS = (("zlo", "x", "core"), ("x", "zlo", "core"), ("zlo", "x", "core"))
PART_ORDERS = (("x", "y", "zlo"), ("x", "y", "zlo"), ("y", "x", "zlo"))
PART_BACKS = (("zlo", "x", "core"), ("x", "zlo", "core"), ("zlo", "x", "core"))


def hidden_columns(wide):
    core = bit_of("core")
    return [
        pl.ds(pl.multiple_of(core * wide, WIDE), wide),
        pl.ds(pl.multiple_of((2 + core) * wide, WIDE), wide),
    ]


def place_heads(tile, variants_ref):
    wide = tile.astype(jnp.float32)
    turned = pltpu.roll(wide, HEAD, 1)
    low_lanes = lanes_below(tile.shape[0], WIDE, HEAD)
    variants_ref[0] = low(jnp.where(low_lanes, wide, 0.0))
    variants_ref[1] = low(jnp.where(low_lanes, 0.0, turned))
    variants_ref[2] = low(jnp.where(low_lanes, turned, 0.0))
    variants_ref[3] = low(jnp.where(low_lanes, 0.0, wide))


def allowed_block(seg_k, seg_q, diagonal):
    same = seg_k == seg_q
    if diagonal:
        rows = lax.broadcasted_iota(jnp.int32, same.shape, 0)
        lanes = lax.broadcasted_iota(jnp.int32, same.shape, 1)
        same = same & (rows <= lanes)
    return same


def attend_body(
    q_ref, k_ref, v_ref, seg_col_ref, seg_row_ref, out_grad, mix_w, gate_w, up_w, down_w,
    mixed_ref, lse_ref, whole_grad, mix_full, gate_full, up_full, down_full,
    ks, vt, acc, stats, sems, near, held_mix, held_gate, held_up, held_down, held_grad
):
    block = pl.program_id(1)
    now = pl.program_id(0) * pl.num_programs(1) + block
    most = pl.num_programs(0) * pl.num_programs(1) - 1
    y = lax.axis_index("fsdp")
    spreads = {
        "mix": Spread(mix_w, mix_full, ("x", "zlo", "core"), sems, 0),
        "gate": Spread(gate_w, gate_full, ("zlo", "x", "core"), sems, 4),
        "up": Spread(up_w, up_full, ("x", "zlo", "core"), sems, 8),
        "down": Spread(down_w, down_full, ("zlo", "x", "core"), sems, 12),
    }
    span = out_grad.shape[1]
    mine = whole_grad.at[pl.ds(pl.multiple_of(y * span, span), span)]
    grad_swap = across(out_grad.at[1 - y], mine, sems, 16, "y")
    half = pl.ds(y * 8, 8)
    own = (
        (mix_w, held_mix, mix_full.at[half]),
        (gate_w, held_gate, gate_full.at[half]),
        (up_w, held_up, up_full.at[half]),
        (down_w, held_down, down_full.at[half]),
        (out_grad.at[y], held_grad, mine),
    )
    loads = [pltpu.make_async_copy(a, b, near.at[0, at]) for at, (a, b, _) in enumerate(own)]
    stores = [pltpu.make_async_copy(b, c, near.at[1, at]) for at, (_, b, c) in enumerate(own)]
    plan = {
        1: (("mix", 0),),
        2: (("mix", 1),),
        3: (("gate", 0), ("mix", 2)),
        5: (("up", 0), ("gate", 1)),
        7: (("down", 0), ("up", 1)),
        9: (("gate", 2), ("down", 1)),
        10: (("up", 2),),
    }

    @pl.when(now == 0)
    def _():
        for load in loads:
            load.start()
        greet(("y", "x", "zlo", "core"))
        for name in ("mix", "gate", "up", "down"):
            spreads[name].advance(-1)
        grad_swap.start()

    @pl.when(now == 1)
    def _():
        for load, store in zip(loads, stores):
            load.wait()
            store.start()

    for at, steps in plan.items():

        @pl.when(now == at)
        def _(steps=steps):
            for name, stage in steps:
                spreads[name].advance(stage)

    @pl.when(block == 0)
    def _():
        place_heads(k_ref[...], ks)
        vt[...] = low(v_ref[...].astype(jnp.float32).T)

    acc[...] = jnp.zeros_like(acc)
    stats[0] = jnp.full((8, BLOCK), -1e30, jnp.float32)
    stats[1] = jnp.zeros((8, BLOCK), jnp.float32)
    seg_q = seg_row_ref[...]

    def step(j, diagonal):
        rows = pl.ds(pl.multiple_of(j * BLOCK, BLOCK), BLOCK)
        seg_k = seg_col_ref[rows, :]
        allowed = allowed_block(seg_k, seg_q, diagonal)
        for head in range(6):
            part, side, kv = head // 2, head % 2, head // 3
            q_tile = q_ref[:, part * WIDE : (part + 1) * WIDE]
            scores = mm_nt(ks[kv * 2 + side, rows, :], q_tile)
            scores = jnp.where(allowed, scores, -1e30)
            before = stats[0, head : head + 1, :]
            highest = jnp.maximum(before, jnp.max(scores, axis=0, keepdims=True))
            shrink = jnp.exp(before - highest)
            chances = jnp.exp(scores - highest)
            stats[0, head : head + 1, :] = highest
            stats[1, head : head + 1, :] = stats[1, head : head + 1, :] * shrink + jnp.sum(
                chances, axis=0, keepdims=True
            )
            values = vt[kv * HEAD : (kv + 1) * HEAD, rows]
            at = head * HEAD
            acc[at : at + HEAD, :] = acc[at : at + HEAD, :] * shrink + mm(values, low(chances))

    @pl.loop(0, block)
    def _(j):
        step(j, False)

    step(block, True)
    total = stats[1]
    for part in range(3):
        at = part * WIDE
        both = jnp.concatenate(
            [
                acc[at : at + HEAD, :] / total[2 * part : 2 * part + 1, :],
                acc[at + HEAD : at + WIDE, :] / total[2 * part + 1 : 2 * part + 2, :],
            ],
            axis=0,
        )
        mixed_ref[:, at : at + WIDE] = low(both.T)
    lse_ref[0] = stats[0] + jnp.log(jnp.maximum(total, 1e-30))

    @pl.when(now == most)
    def _():
        spreads["down"].advance(2)
        for spread in spreads.values():
            spread.advance(3)
            spread.finish()
        grad_swap.wait()
        for store in stores:
            store.wait()


def attend(qkv, seg_col, seg_row, out_grad, mix_w, gate_w, up_w, down_w):
    length = qkv.shape[0]
    pairs = KV_HEADS // 2
    q_tiles = HEADS * HEAD // WIDE
    anywhere = pl.BlockSpec(memory_space=pl.ANY)
    shards = [w.reshape(8, w.shape[0] // 8, w.shape[1]) for w in (mix_w, gate_w, up_w, down_w)]
    fulls = [jax.ShapeDtypeStruct((16,) + w.shape[1:], w.dtype) for w in shards]
    found = pl.pallas_call(
        attend_body,
        grid=(pairs, length // BLOCK),
        in_specs=[
            pl.BlockSpec((BLOCK, 3 * WIDE), lambda b, i: (i, b)),
            pl.BlockSpec((length, WIDE), lambda b, i: (0, q_tiles + b)),
            pl.BlockSpec((length, WIDE), lambda b, i: (0, q_tiles + pairs + b)),
            pl.BlockSpec((length, 1), lambda b, i: (0, 0)),
            pl.BlockSpec((1, BLOCK), lambda b, i: (0, i)),
        ]
        + [anywhere] * 5,
        out_specs=[
            pl.BlockSpec((BLOCK, 3 * WIDE), lambda b, i: (i, b)),
            pl.BlockSpec((1, 8, BLOCK), lambda b, i: (b, 0, i)),
        ]
        + [anywhere] * 5,
        out_shape=[
            jax.ShapeDtypeStruct((length, HEADS * HEAD), jnp.bfloat16),
            jax.ShapeDtypeStruct((pairs, 8, length), jnp.float32),
            jax.ShapeDtypeStruct((length, out_grad.shape[2]), out_grad.dtype),
        ]
        + fulls,
        scratch_shapes=[
            pltpu.VMEM((4, length, WIDE), jnp.bfloat16),
            pltpu.VMEM((WIDE, length), jnp.bfloat16),
            pltpu.VMEM((6 * HEAD, BLOCK), jnp.float32),
            pltpu.VMEM((2, 8, BLOCK), jnp.float32),
            pltpu.SemaphoreType.DMA((2, 17)),
            pltpu.SemaphoreType.DMA((2, 5)),
        ]
        + [pltpu.VMEM(w.shape, w.dtype) for w in shards]
        + [pltpu.VMEM(out_grad.shape[1:], out_grad.dtype)],
        compiler_params=pltpu.CompilerParams(
            collective_id=2, has_side_effects=True, vmem_limit_bytes=VMEM_MOST
        ),
        cost_estimate=pl.CostEstimate(
            flops=16 * length * length * HEADS * HEAD // 2,
            bytes_accessed=6 * length * HEADS * HEAD,
            transcendentals=HEADS * length * length // 2,
        ),
        name="attend",
    )(qkv, qkv, qkv, seg_col, seg_row, out_grad, *shards)
    return tuple(found[:3]) + tuple(w.reshape(-1, w.shape[2]) for w in found[3:])


def attend_back_body(
    q_ref, k_ref, v_ref, grad_ref, mixed_ref, lse_ref, seg_col_ref, seg_row_ref, cos_ref, sin_ref,
    gate_term, up_term, down_term,
    dq_ref, dk_ref, dv_ref, gate_half, up_half, down_half,
    ks, vs, kt, k_acc, v_acc, q_acc, sides, delta, sems, near, kept, *received
):
    block = pl.program_id(1)
    length = k_ref.shape[0]
    now = pl.program_id(0) * pl.num_programs(1) + block
    most = pl.num_programs(0) * pl.num_programs(1) - 1
    down_kept, down_received = received[2], received[3:]
    folds = [
        Fold(
            term,
            kept.at[at] if at < 2 else down_kept,
            [r.at[at] for r in received[:2]] if at < 2 else list(down_received),
            ORDERS[at][:2],
            sems,
            2 * at,
            near,
            at,
        )
        for at, term in enumerate((gate_term, up_term, down_term))
    ]

    @pl.when(now == 0)
    def _():
        greet(AXES)
        for fold in folds:
            fold.begin()

    @pl.when(now == 7)
    def _():
        for fold in folds:
            fold.advance(0)

    @pl.when(block == 0)
    def _():
        place_heads(k_ref[...], ks)
        place_heads(v_ref[...], vs)
        kt[...] = low(k_ref[...].astype(jnp.float32).T)
        k_acc[...] = jnp.zeros_like(k_acc)
        v_acc[...] = jnp.zeros_like(v_acc)

    q_acc[...] = jnp.zeros_like(q_acc)
    seg_q = seg_row_ref[...]
    low_lanes = lanes_below(BLOCK, WIDE, HEAD)
    zero = jnp.zeros((BLOCK, WIDE), jnp.bfloat16)
    for part in range(3):
        at = part * WIDE
        tile, grad = q_ref[:, at : at + WIDE], grad_ref[:, at : at + WIDE]
        sides[0, part, 0:BLOCK, :] = jnp.where(low_lanes, tile, zero)
        sides[0, part, BLOCK : 2 * BLOCK, :] = jnp.where(low_lanes, zero, tile)
        sides[1, part, 0:BLOCK, :] = jnp.where(low_lanes, grad, zero)
        sides[1, part, BLOCK : 2 * BLOCK, :] = jnp.where(low_lanes, zero, grad)
        product = (grad.astype(jnp.float32) * mixed_ref[:, at : at + WIDE].astype(jnp.float32)).T
        delta[2 * part : 2 * part + 1, :] = jnp.sum(product[:HEAD], axis=0, keepdims=True)
        delta[2 * part + 1 : 2 * part + 2, :] = jnp.sum(product[HEAD:], axis=0, keepdims=True)

    def step(j, diagonal):
        rows = pl.ds(pl.multiple_of(j * BLOCK, BLOCK), BLOCK)
        allowed = allowed_block(seg_col_ref[rows, :], seg_q, diagonal)
        for part in range(3):
            at = part * WIDE
            q_tile, grad_tile = q_ref[:, at : at + WIDE], grad_ref[:, at : at + WIDE]
            chances_pair, score_pair = [], []
            for side in range(2):
                head = 2 * part + side
                kv = head // 3
                scores = mm_nt(ks[kv * 2 + side, rows, :], q_tile)
                scores = jnp.where(allowed, scores, -1e30)
                chances = jnp.exp(scores - lse_ref[0, head : head + 1, :])
                onto = mm_nt(vs[kv * 2 + side, rows, :], grad_tile)
                score_grad = low(chances * (onto - delta[head : head + 1, :]))
                chances_pair.append(low(chances))
                score_pair.append(score_grad)
                to = head * HEAD
                q_acc[to : to + HEAD, :] += mm(kt[kv * HEAD : (kv + 1) * HEAD, rows], score_grad)
            v_acc[part, rows, :] += mm(jnp.concatenate(chances_pair, axis=1), sides[1, part])
            k_acc[part, rows, :] += mm(jnp.concatenate(score_pair, axis=1), sides[0, part])

    @pl.loop(0, block)
    def _(j):
        step(j, False)

    step(block, True)
    here = pl.ds(pl.multiple_of(block * BLOCK, BLOCK), BLOCK)
    for part in range(3):
        at = part * WIDE
        tile = q_acc[at : at + WIDE, :].T * HEAD ** (-0.5)
        tile = tile * cos_ref[here, :] - swap_halves(tile) * sin_ref[here, :]
        dq_ref[:, at : at + WIDE] = low(tile)

    @pl.when(block == length // BLOCK - 1)
    def _():
        for j in range(0, length, BLOCK):
            rows = slice(j, j + BLOCK)

            def gather(acc):
                first, middle, last = acc[0, rows, :], acc[1, rows, :], acc[2, rows, :]
                return middle + jnp.where(
                    low_lanes, first + pltpu.roll(first, HEAD, 1), last + pltpu.roll(last, HEAD, 1)
                )

            tile = gather(k_acc)
            tile = tile * cos_ref[rows, :] - swap_halves(tile) * sin_ref[rows, :]
            dk_ref[rows, :] = low(tile)
            dv_ref[rows, :] = low(gather(v_acc))

    @pl.when(now == most)
    def _():
        for fold in folds:
            fold.advance(1)
        stores = [
            pltpu.make_async_copy(folds[at].received[1], half, near.at[3 + at])
            for at, half in enumerate((gate_half, up_half, down_half))
        ]
        for store in stores:
            store.start()
        for fold in folds:
            fold.finish()
        for store in stores:
            store.wait()


def attend_back(qkv, mixed_grad, mixed, lse, seg_col, seg_row, cosines, sines, gate_term, up_term, down_term):
    length = qkv.shape[0]
    terms = [t.reshape(2, 2, 2, 2, t.shape[0] // 16, t.shape[1]) for t in (gate_term, up_term, down_term)]
    rows, wide = terms[0].shape[4:]
    down_rows, width = terms[2].shape[4:]
    anywhere = pl.BlockSpec(memory_space=pl.ANY)
    pairs = KV_HEADS // 2
    q_tiles = HEADS * HEAD // WIDE
    q_block = pl.BlockSpec((BLOCK, 3 * WIDE), lambda b, i: (i, b))
    kv_block = pl.BlockSpec((length, WIDE), lambda b, i: (0, b))
    table = pl.BlockSpec((length, WIDE), lambda b, i: (0, 0), pipeline_mode=pl.Buffered(1))
    return pl.pallas_call(
        attend_back_body,
        grid=(pairs, length // BLOCK),
        in_specs=[
            q_block,
            pl.BlockSpec((length, WIDE), lambda b, i: (0, q_tiles + b)),
            pl.BlockSpec((length, WIDE), lambda b, i: (0, q_tiles + pairs + b)),
            q_block,
            q_block,
            pl.BlockSpec((1, 8, BLOCK), lambda b, i: (b, 0, i)),
            pl.BlockSpec((length, 1), lambda b, i: (0, 0)),
            pl.BlockSpec((1, BLOCK), lambda b, i: (0, i)),
            table,
            table,
        ]
        + [anywhere] * 3,
        out_specs=[q_block, kv_block, kv_block] + [anywhere] * 3,
        out_shape=[
            jax.ShapeDtypeStruct((length, HEADS * HEAD), jnp.bfloat16),
            jax.ShapeDtypeStruct((length, KV_HEADS * HEAD), jnp.bfloat16),
            jax.ShapeDtypeStruct((length, KV_HEADS * HEAD), jnp.bfloat16),
            jax.ShapeDtypeStruct((2, 2, rows, wide), jnp.bfloat16),
            jax.ShapeDtypeStruct((2, 2, rows, wide), jnp.bfloat16),
            jax.ShapeDtypeStruct((2, 2, down_rows, width), jnp.bfloat16),
        ],
        scratch_shapes=[
            pltpu.VMEM((4, length, WIDE), jnp.bfloat16),
            pltpu.VMEM((4, length, WIDE), jnp.bfloat16),
            pltpu.VMEM((WIDE, length), jnp.bfloat16),
            pltpu.VMEM((3, length, WIDE), jnp.float32),
            pltpu.VMEM((3, length, WIDE), jnp.float32),
            pltpu.VMEM((6 * HEAD, BLOCK), jnp.float32),
            pltpu.VMEM((2, 3, 2 * BLOCK, WIDE), jnp.bfloat16),
            pltpu.VMEM((8, BLOCK), jnp.float32),
            pltpu.SemaphoreType.DMA((2, 6)),
            pltpu.SemaphoreType.DMA((6,)),
        ]
        + [pltpu.VMEM((2,) + (2,) * left + (rows, wide), jnp.bfloat16) for left in (3, 3, 2)]
        + [pltpu.VMEM((2,) * left + (down_rows, width), jnp.bfloat16) for left in (3, 3, 2)],
        compiler_params=pltpu.CompilerParams(
            collective_id=3, has_side_effects=True, vmem_limit_bytes=VMEM_MOST
        ),
        cost_estimate=pl.CostEstimate(
            flops=40 * length * length * HEADS * HEAD // 2,
            bytes_accessed=12 * length * HEADS * HEAD,
            transcendentals=HEADS * length * length // 2,
        ),
        name="attend_back",
    )(qkv, qkv, qkv, mixed_grad, mixed, lse, seg_col, seg_row, cosines, sines, *terms)


def mix_body(x_ref, mixed_ref, w_ref, gain_ref, residual_ref, normed_ref, turned_ref):
    residual = x_ref[...].astype(jnp.float32) + mm(mixed_ref[...], w_ref[...])
    residual_ref[...] = residual
    inverse = lax.rsqrt(jnp.mean(residual * residual, axis=-1, keepdims=True) + epsilon)
    normed = residual * inverse * gain_ref[...]
    normed_ref[...] = low(normed)
    turned_ref[...] = low(normed.T)


def mix(x, mixed, w, gain):
    length, width = x.shape
    rows = pl.BlockSpec((BLOCK, width), lambda i: (i, 0))
    return pl.pallas_call(
        mix_body,
        grid=(length // BLOCK,),
        in_specs=[
            rows,
            rows,
            pl.BlockSpec(w.shape, lambda i: (0, 0), pipeline_mode=pl.Buffered(1)),
            pl.BlockSpec((1, width), lambda i: (0, 0)),
        ],
        out_specs=[rows, rows, pl.BlockSpec((width, BLOCK), lambda i: (0, i))],
        out_shape=[
            jax.ShapeDtypeStruct((length, width), jnp.float32),
            jax.ShapeDtypeStruct((length, width), jnp.bfloat16),
            jax.ShapeDtypeStruct((width, length), jnp.bfloat16),
        ],
        cost_estimate=pl.CostEstimate(
            flops=2 * length * width * width, bytes_accessed=12 * length * width, transcendentals=0
        ),
        name="mix",
    )(x, mixed, w, gain)


def norm_grad(grad, gain, scaled, inverse):
    weighted = grad * gain
    return inverse * (weighted - scaled * jnp.mean(weighted * scaled, axis=-1, keepdims=True))


def turn_body(residual_ref, out_a, out_b, back_a, back_b, c_ref, mixed_ref, w_ref, gain_ref,
              result_ref, grad_ref, mixed_grad_ref, term_ref, gain_term_ref, total):
    step = pl.program_id(0)
    residual = residual_ref[...]
    result_ref[...] = low(residual + out_a[...] + out_b[...])
    inverse = lax.rsqrt(jnp.mean(residual * residual, axis=-1, keepdims=True) + epsilon)
    scaled = residual * inverse
    normed_grad = back_a[...] + back_b[...]
    gain_term = jnp.sum(normed_grad * scaled, axis=0, keepdims=True)
    grad = c_ref[...].astype(jnp.float32) + norm_grad(normed_grad, gain_ref[...], scaled, inverse)
    grad_ref[...] = grad
    grad_low = low(grad)
    mixed_grad_ref[...] = low(mm_nt(grad_low, w_ref[...]))
    term = mm_tn(mixed_ref[...], grad_low)

    @pl.when(step == 0)
    def _():
        total[...] = term
        gain_term_ref[...] = jnp.broadcast_to(gain_term, gain_term_ref.shape)

    @pl.when(step > 0)
    def _():
        total[...] += term
        gain_term_ref[...] += jnp.broadcast_to(gain_term, gain_term_ref.shape)

    @pl.when(step == pl.num_programs(0) - 1)
    def _():
        term_ref[...] = low(total[...])


def turn(residual, out_a, out_b, back_a, back_b, c, mixed, w, gain):
    length, width = residual.shape
    rows = pl.BlockSpec((BLOCK, width), lambda i: (i, 0))
    whole = lambda shape: pl.BlockSpec(shape, lambda i: (0, 0), pipeline_mode=pl.Buffered(1))
    return pl.pallas_call(
        turn_body,
        grid=(length // BLOCK,),
        in_specs=[rows] * 7 + [whole(w.shape), pl.BlockSpec((1, width), lambda i: (0, 0))],
        out_specs=[
            rows, rows, rows, whole((width, width)), pl.BlockSpec((8, width), lambda i: (0, 0)),
        ],
        out_shape=[
            jax.ShapeDtypeStruct((length, width), jnp.bfloat16),
            jax.ShapeDtypeStruct((length, width), jnp.float32),
            jax.ShapeDtypeStruct((length, width), jnp.bfloat16),
            jax.ShapeDtypeStruct((width, width), jnp.bfloat16),
            jax.ShapeDtypeStruct((8, width), jnp.float32),
        ],
        scratch_shapes=[pltpu.VMEM((width, width), jnp.float32)],
        compiler_params=pltpu.CompilerParams(vmem_limit_bytes=VMEM_MOST),
        cost_estimate=pl.CostEstimate(
            flops=4 * length * width * width, bytes_accessed=32 * length * width, transcendentals=0
        ),
        name="turn",
    )(residual, out_a, out_b, back_a, back_b, c, mixed, w, gain)


def end_body(dq_ref, dk_ref, dv_ref, normed_ref, x_ref, grad_ref, w_ref, gain_ref, feed_gain_ref,
             mix_term, result, gate_half, up_half, down_half,
             gate, up, down, sums, outputs, input_grads, gain_sums,
             turned, term, tokens, r0, r1, r2, r3, exchanged, hidden_r2, hidden_r3, hidden_came,
             down_r2, down_r3, down_came, gain_held, gain_came, rows_held, sems, near):
    step = pl.program_id(0)
    last = pl.num_programs(0) - 1
    rows_each = x_ref.shape[0]
    length = normed_ref.shape[0]
    q_width, k_width = dq_ref.shape[1], dk_ref.shape[1]
    core, y = bit_of("core"), lax.axis_index("fsdp")
    third = term.shape[-1] // 3
    wide = third // 2
    everything = (slice(None),) * 4 + (slice(None),)
    columns = [
        [pl.ds(pl.multiple_of(t * third + side * wide, WIDE), wide) for side in (core, 1 - core)]
        for t in range(3)
    ]
    span = outputs.shape[1]
    rows = [pl.ds(pl.multiple_of(at * span, span), span) for at in (y, 1 - y)]
    hidden = gate.shape[-1] // 4
    halves = (gate_half, up_half, down_half)
    seconds = [hidden_r2.at[0], hidden_r2.at[1], down_r2]
    thirds = [hidden_r3.at[0], hidden_r3.at[1], down_r3]
    came = [hidden_came.at[0], hidden_came.at[1], down_came]
    loads = [pltpu.make_async_copy(halves[f], seconds[f], near.at[f]) for f in range(3)]
    mix_load = pltpu.make_async_copy(
        mix_term, term.at[everything + (slice(q_width + 2 * k_width, term.shape[-1]),)], near.at[3]
    )
    result_load = pltpu.make_async_copy(result.at[rows[0]], rows_held, near.at[4])
    result_store = pltpu.make_async_copy(rows_held, outputs.at[y], near.at[5])
    token_store = pltpu.make_async_copy(tokens.at[rows[0]], input_grads.at[y], near.at[6])
    folds = [
        Fold(halves[f], None, [None, seconds[f], thirds[f]], ORDERS[f], sems, 3 * f, None, None)
        for f in range(3)
    ]
    zs = [across(thirds[f], came[f], sems, 9 + f, "zhi") for f in range(3)]
    rises = [
        Rise(gate, BACKS[0], hidden_columns(hidden), sems, 12),
        Rise(up, BACKS[1], hidden_columns(hidden), sems, 18),
        Rise(down, BACKS[2], None, sems, 24),
    ]
    cores = [
        across(term.at[everything + (columns[t][1],)], r0.at[t], sems, 27 + t, "core")
        for t in range(3)
    ]
    parts = [
        Fold(r0.at[t], None, [r1.at[t], r2.at[t], r3.at[t]], PART_ORDERS[t], sems, 30 + 3 * t, None, None)
        for t in range(3)
    ]
    part_zs = [across(r3.at[t], exchanged.at[t], sems, 39 + t, "zhi") for t in range(3)]
    tops = [Rise(sums, PART_BACKS[t], [columns[t][0]], sems, 42 + 3 * t) for t in range(3)]
    swaps = [
        across(result.at[rows[1]], outputs.at[y], sems, 51, "y"),
        across(tokens.at[rows[1]], input_grads.at[y], sems, 52, "y"),
    ]
    names = ("core",) + AXES
    gain_copies = [
        across(gain_held.at[at], gain_came.at[at], sems, 53 + at, name)
        for at, name in enumerate(names)
    ]

    def own_stores(f):
        if f == 2:
            return [pltpu.make_async_copy(down_came, rises[2].block(0)[0], near.at[11])]
        return [
            pltpu.make_async_copy(
                came[f].at[:, :, half * hidden : (half + 1) * hidden], block, near.at[7 + 2 * f + half]
            )
            for half, block in enumerate(rises[f].block(0))
        ]

    def part_store(t):
        return pltpu.make_async_copy(exchanged.at[t], tops[t].block(0)[0], near.at[12 + t])

    def settle(copy, mine, theirs):
        copy.wait_recv()
        for n in range(2):
            theirs[n] = low(mine[n].astype(jnp.float32) + theirs[n].astype(jnp.float32))

    def hidden_settle(f):
        settle(zs[f], thirds[f], came[f])
        stores = own_stores(f)
        for store in stores:
            store.start()
        if f == 2:
            rises[f].begin([down_came])
        else:
            rises[f].begin([came[f].at[:, :, h * hidden : (h + 1) * hidden] for h in range(2)])

    def part_settle(t):
        settle(part_zs[t], r3.at[t], exchanged.at[t])
        part_store(t).start()
        tops[t].begin([exchanged.at[t]])

    def core_sum(t):
        cores[t].wait_recv()

        @pl.loop(0, 16)
        def _(n):
            index = (n // 8, n // 4 % 2, n // 2 % 2, n % 2)
            mine = term[index + (slice(None), columns[t][0])]
            r0[(t,) + index] = low(r0[(t,) + index].astype(jnp.float32) + mine.astype(jnp.float32))

        parts[t].begin()

    def gain_step(at):
        gain_copies[at].wait_recv()
        gain_held[at + 1] = gain_held[at] + gain_came[at]
        if at + 1 < len(names):
            gain_copies[at + 1].start()

    @pl.when(step == 0)
    def _():
        for load in loads + [mix_load, result_load]:
            load.start()
        greet(names)
        for f in range(3):
            loads[f].wait()
            folds[f].copy(2).start()
        mix_load.wait()
        cores[2].start()
        for at in range(0, length, BLOCK):
            turned[:, at : at + BLOCK] = normed_ref[at : at + BLOCK, :].T

    @pl.when(step == 1)
    def _():
        core_sum(2)
        swaps[0].start()
        result_load.wait()
        result_store.start()

    @pl.when(step == 2)
    def _():
        for f in range(3):
            folds[f].advance(2)
        zs[0].start()

    @pl.when(step == 3)
    def _():
        cores[0].start()
        zs[1].start()

    @pl.when(step == 4)
    def _():
        core_sum(0)
        zs[2].start()

    def chunk(low_rows, at):
        wide_term = mm(turned[...], low_rows).reshape(16, turned.shape[0] // 16, k_width)
        for n in range(16):
            index = (n // 8, n // 4 % 2, n // 2 % 2, n % 2, slice(None), slice(at, at + k_width))
            term[index] = low(wide_term[n])

    for at in range(3):

        @pl.when(step == at)
        def _(at=at):
            chunk(dq_ref[:, at * k_width : (at + 1) * k_width], at * k_width)

    @pl.when(step == 3)
    def _():
        chunk(dk_ref[...], q_width)

    @pl.when(step == 4)
    def _():
        chunk(dv_ref[...], q_width + k_width)

    @pl.when(step < last)
    def _():
        here = pl.ds(pl.multiple_of(step * rows_each, rows_each), rows_each)
        normed_grad = (
            mm_nt(dq_ref[here, :], w_ref[:, :q_width])
            + mm_nt(dk_ref[here, :], w_ref[:, q_width : q_width + k_width])
            + mm_nt(dv_ref[here, :], w_ref[:, q_width + k_width :])
        )
        values = x_ref[...].astype(jnp.float32)
        inverse = lax.rsqrt(jnp.mean(values * values, axis=-1, keepdims=True) + epsilon)
        scaled = values * inverse
        gain_term = jnp.sum(normed_grad * scaled, axis=0, keepdims=True)
        tokens[here, :] = low(
            grad_ref[...] + norm_grad(normed_grad, gain_ref[...], scaled, inverse)
        )

        @pl.when(step == 0)
        def _():
            gain_held[0, 0:1, :] = gain_term
            gain_held[0, 1:2, :] = feed_gain_ref[0:1, :]
            gain_held[0, 2:8, :] = jnp.zeros_like(gain_held[0, 2:8, :])

        @pl.when(step > 0)
        def _():
            gain_held[0, 0:1, :] += gain_term

    @pl.when(step == last)
    def _():
        cores[1].start()
        gain_copies[0].start()
        token_store.start()
        parts[2].advance(0)
        core_sum(1)
        gain_step(0)
        hidden_settle(0)
        parts[0].advance(0)
        parts[2].advance(1)
        parts[1].advance(0)
        gain_step(1)
        hidden_settle(1)
        parts[0].advance(1)
        parts[1].advance(1)
        swaps[1].start()
        gain_step(2)
        for store in own_stores(0):
            store.wait()
        rises[0].advance(0)
        for t in (2, 0, 1):
            parts[t].advance(2)
            part_zs[t].start()
        hidden_settle(2)
        gain_step(3)
        for store in own_stores(1):
            store.wait()
        rises[1].advance(0)
        for t in (2, 0, 1):
            part_settle(t)
        gain_step(4)
        for store in own_stores(2):
            store.wait()
        rises[2].advance(0)
        for t in (2, 0, 1):
            part_store(t).wait()
            tops[t].advance(0)
        rises[0].advance(1)
        rises[1].advance(1)
        for t in (2, 0, 1):
            tops[t].advance(1)
        rises[2].advance(1)
        for part in rises + tops:
            part.advance(2)
        for copy in cores + swaps + gain_copies + zs + part_zs:
            copy.wait_send()
        for fold in folds:
            fold.copy(2).wait_send()
        for part in rises + tops + parts:
            part.finish()
        for copy in swaps:
            copy.wait_recv()
        result_store.wait()
        token_store.wait()
        gain_sums[...] = gain_held[len(names)]


def end(dq, dk, dv, normed, x, grad, w, gain, feed_gain_term, mix_term, result, gate_half, up_half, down_half):
    length, width = x.shape
    k_width = dk.shape[1]
    total = w.shape[1] + mix_term.shape[1]
    wide = total // 6
    mix_term = mix_term.reshape(2, 2, 2, 2, mix_term.shape[0] // 16, mix_term.shape[1])
    rows = mix_term.shape[4]
    hidden_rows, hidden = gate_half.shape[2:]
    down_rows = down_half.shape[2]
    block = pl.BlockSpec((BLOCK, width), lambda i: (jnp.minimum(i, length // BLOCK - 1), 0))
    whole = lambda a: pl.BlockSpec(a.shape, lambda i: (0,) * a.ndim, pipeline_mode=pl.Buffered(1))
    anywhere = pl.BlockSpec(memory_space=pl.ANY)
    both = jax.ShapeDtypeStruct((2, length // 2, width), result.dtype)
    low_type = jnp.bfloat16
    return pl.pallas_call(
        end_body,
        grid=(w.shape[1] // k_width,),
        in_specs=[whole(dq), whole(dk), whole(dv), whole(normed), block, block, whole(w), whole(gain),
                  whole(feed_gain_term)] + [anywhere] * 5,
        out_specs=[anywhere] * 6 + [pl.BlockSpec((8, width), lambda i: (0, 0))],
        out_shape=[
            jax.ShapeDtypeStruct((2, 2, 2, hidden_rows, 2 * hidden), low_type),
            jax.ShapeDtypeStruct((2, 2, 2, hidden_rows, 2 * hidden), low_type),
            jax.ShapeDtypeStruct((2, 2, 2, 2, down_rows, width), low_type),
            jax.ShapeDtypeStruct((2, 2, 2, rows, total), low_type),
            both,
            both,
            jax.ShapeDtypeStruct((8, width), jnp.float32),
        ],
        scratch_shapes=[
            pltpu.VMEM((width, length), low_type),
            pltpu.VMEM((2, 2, 2, 2, rows, total), low_type),
            pltpu.VMEM((length, width), low_type),
        ]
        + [pltpu.VMEM((3,) + (2,) * left + (rows, wide), low_type) for left in (4, 3, 2, 1, 1)]
        + [pltpu.VMEM((2,) + (2,) * left + (hidden_rows, hidden), low_type) for left in (2, 1, 1)]
        + [pltpu.VMEM((2,) * left + (down_rows, width), low_type) for left in (2, 1, 1)]
        + [
            pltpu.VMEM((6, 8, width), jnp.float32),
            pltpu.VMEM((5, 8, width), jnp.float32),
            pltpu.VMEM((length // 2, width), low_type),
            pltpu.SemaphoreType.DMA((2, 58)),
            pltpu.SemaphoreType.DMA((15,)),
        ],
        compiler_params=pltpu.CompilerParams(
            collective_id=4, has_side_effects=True, vmem_limit_bytes=VMEM_MOST
        ),
        name="end",
    )(dq, dk, dv, normed, x, grad, w, gain, feed_gain_term, mix_term, result, gate_half, up_half, down_half)


def feed_body(which_ref, normed_ref, turned_ref, c_ref, gate_ref, up_ref, down_ref,
              out_ref, back_ref, gate_grad_ref, up_grad_ref, down_grad_ref,
              hidden_t, gate_low, up_low):
    first = pl.program_id(0) == 0
    length, width = normed_ref.shape

    @pl.when(first)
    def _():
        out_ref[...] = jnp.zeros_like(out_ref)
        back_ref[...] = jnp.zeros_like(back_ref)

    for at in range(0, length, BLOCK):
        rows = slice(at, at + BLOCK)
        normed = normed_ref[rows, :]
        gate_sum = mm(normed, gate_ref[...])
        up_sum = mm(normed, up_ref[...])
        hidden_grad = mm_nt(c_ref[rows, :], down_ref[...])
        sigmoid = jax.nn.sigmoid(gate_sum)
        activated = gate_sum * sigmoid
        hidden = low(activated * up_sum)
        gate_grad = low(hidden_grad * up_sum * (sigmoid + activated * (1.0 - sigmoid)))
        up_grad = low(hidden_grad * activated)
        hidden_t[:, rows] = hidden.T
        gate_low[rows, :] = gate_grad
        up_low[rows, :] = up_grad
        out_ref[rows, :] += mm(hidden, down_ref[...])
        back_ref[rows, :] += mm_nt(gate_grad, gate_ref[...]) + mm_nt(up_grad, up_ref[...])
    step = 384
    for at in range(0, width, step):
        rows = slice(at, at + step)
        gate_grad_ref[rows, :] = low(mm(turned_ref[rows, :], gate_low[...]))
        up_grad_ref[rows, :] = low(mm(turned_ref[rows, :], up_low[...]))
        down_grad_ref[:, rows] = low(mm(hidden_t[...], c_ref[:, rows]))


def feed(which, normed, turned, c, gate, up, down):
    length, width = normed.shape
    wide = gate.shape[1] // 4
    whole = pl.BlockSpec((length, width), lambda t, w: (0, 0), pipeline_mode=pl.Buffered(1))
    columns = pl.BlockSpec((width, wide), lambda t, w: (0, w[0] + 2 * t))
    rows = pl.BlockSpec((wide, width), lambda t, w: (w[0] + 2 * t, 0))
    total = pl.BlockSpec((length, width), lambda t, w: (0, 0), pipeline_mode=pl.Buffered(1))
    columns_out = pl.BlockSpec((width, wide), lambda t, w: (0, t))
    return pl.pallas_call(
        feed_body,
        grid_spec=pltpu.PrefetchScalarGridSpec(
            num_scalar_prefetch=1,
            grid=(2,),
            in_specs=[
                whole,
                pl.BlockSpec((width, length), lambda t, w: (0, 0), pipeline_mode=pl.Buffered(1)),
                whole,
                columns,
                columns,
                rows,
            ],
            out_specs=[
                total,
                total,
                columns_out,
                columns_out,
                pl.BlockSpec((wide, width), lambda t, w: (t, 0)),
            ],
            scratch_shapes=[
                pltpu.VMEM((wide, length), jnp.bfloat16),
                pltpu.VMEM((length, wide), jnp.bfloat16),
                pltpu.VMEM((length, wide), jnp.bfloat16),
            ],
        ),
        out_shape=[
            jax.ShapeDtypeStruct((length, width), jnp.float32),
            jax.ShapeDtypeStruct((length, width), jnp.float32),
            jax.ShapeDtypeStruct((width, 2 * wide), jnp.bfloat16),
            jax.ShapeDtypeStruct((width, 2 * wide), jnp.bfloat16),
            jax.ShapeDtypeStruct((2 * wide, width), jnp.bfloat16),
        ],
        compiler_params=pltpu.CompilerParams(vmem_limit_bytes=VMEM_MOST),
        cost_estimate=pl.CostEstimate(
            flops=18 * length * width * wide * 2,
            bytes_accessed=12 * width * wide * 2 + 16 * length * width,
            transcendentals=length * wide * 2,
        ),
        name="feed",
    )(which, normed, turned, c, gate, up, down)


def shortened(array):
    return jax.tree.map(lambda a: a.astype(jnp.bfloat16) if a.dtype == jnp.float32 else a, array)


def product(left, right):
    return jnp.dot(left, right, preferred_element_type=jnp.float32)


def product_tn(left, right):
    return lax.dot_general(
        left, right, (((0,), (0,)), ((), ())), preferred_element_type=jnp.float32
    )


def product_nt(left, right):
    return lax.dot_general(
        left, right, (((1,), (1,)), ((), ())), preferred_element_type=jnp.float32
    )


def rotary_tables(positions, width):
    half_width = width // 2
    freqs = jnp.exp(
        jnp.arange(half_width, dtype=jnp.float32) * (-2.0 * math.log(rope_base) / width)
    )
    angles = positions[:, None] * freqs[None, :]
    return (jnp.cos(angles), jnp.sin(angles))


def rotate(values, cosines, sines):
    half_width = values.shape[-1] // 2
    first = values[..., :half_width]
    second = values[..., half_width:]
    return jnp.concatenate(
        [first * cosines - second * sines, second * cosines + first * sines], axis=-1
    )


def unrotate(values, cosines, sines):
    half_width = values.shape[-1] // 2
    first = values[..., :half_width]
    second = values[..., half_width:]
    return jnp.concatenate(
        [first * cosines + second * sines, second * cosines - first * sines], axis=-1
    )


def norm_back(grad_rows, gain, scaled, inverse):
    weighted = grad_rows * gain
    return inverse * (weighted - scaled * jnp.mean(weighted * scaled, axis=-1, keepdims=True))


def plain_local(
    inputs,
    segments,
    out_grad,
    attention_gain,
    query_weight,
    key_weight,
    value_weight,
    output_weight,
    feedforward_gain,
    gate_weight,
    up_weight,
    down_weight,
):
    gathered = (
        lax.all_gather(attention_gain, "fsdp", axis=0, tiled=True),
        lax.all_gather(query_weight, "fsdp", axis=0, tiled=True),
        lax.all_gather(key_weight, "fsdp", axis=0, tiled=True),
        lax.all_gather(value_weight, "fsdp", axis=0, tiled=True),
        lax.all_gather(output_weight, "fsdp", axis=0, tiled=True),
        lax.all_gather(feedforward_gain, "fsdp", axis=0, tiled=True),
        lax.all_gather(gate_weight, "fsdp", axis=0, tiled=True),
        lax.all_gather(up_weight, "fsdp", axis=0, tiled=True),
        lax.all_gather(down_weight, "fsdp", axis=0, tiled=True),
    )
    full_query, full_key, full_value, full_output = (
        gathered[1],
        gathered[2],
        gathered[3],
        gathered[4],
    )
    full_gate, full_up, full_down = (gathered[6], gathered[7], gathered[8])
    gain_attention = gathered[0].astype(jnp.float32)
    gain_feed = gathered[5].astype(jnp.float32)
    span = inputs.shape[1]
    length = segments.shape[1]
    groups_q = HEADS // KV_HEADS
    key_width = KV_HEADS * HEAD
    start = lax.axis_index("fsdp") * span
    query_pos = start + jnp.arange(span, dtype=jnp.int32)
    key_pos = jnp.arange(length, dtype=jnp.int32)
    cosines, sines = rotary_tables(query_pos.astype(jnp.float32), HEAD)
    cos_four, sin_four = (cosines[:, None, None, :], sines[:, None, None, :])
    cos_three, sin_three = (cosines[:, None, :], sines[:, None, :])
    causal = query_pos[:, None] >= key_pos[None, :]
    scale = HEAD ** (-0.5)

    def micro_step(totals, sequence):
        tokens, segment_row, cotangent = sequence
        own_segment = lax.dynamic_slice_in_dim(segment_row, start, span)
        allowed = causal & (own_segment[:, None] == segment_row[None, :])
        values = tokens.astype(jnp.float32)
        inverse_a = lax.rsqrt(jnp.mean(values * values, axis=-1, keepdims=True) + epsilon)
        scaled_a = values * inverse_a
        normed_a = (scaled_a * gain_attention).astype(jnp.bfloat16)
        query_lin = product(normed_a, full_query).reshape(span, KV_HEADS, groups_q, HEAD)
        queries = rotate(query_lin, cos_four, sin_four).astype(jnp.bfloat16)
        key_lin = product(normed_a, full_key).reshape(span, KV_HEADS, HEAD)
        key_rows = (
            rotate(key_lin, cos_three, sin_three).astype(jnp.bfloat16).reshape(span, key_width)
        )
        value_rows = product(normed_a, full_value).astype(jnp.bfloat16)
        all_keys, all_values = (
            lax.all_gather(key_rows, "fsdp", axis=0, tiled=True),
            lax.all_gather(value_rows, "fsdp", axis=0, tiled=True),
        )
        all_keys = all_keys.reshape(length, KV_HEADS, HEAD)
        all_values = all_values.reshape(length, KV_HEADS, HEAD)
        scores = (
            jnp.einsum("qhgd,khd->hgqk", queries, all_keys, preferred_element_type=jnp.float32)
            * scale
        )
        scores = jnp.where(allowed, scores, -1e30)
        highest = jnp.max(scores, axis=-1, keepdims=True)
        expo_scores = jnp.exp(scores - highest)
        attention = expo_scores / jnp.sum(expo_scores, axis=-1, keepdims=True)
        attention_low = attention.astype(jnp.bfloat16)
        mixed = jnp.einsum(
            "hgqk,khd->qhgd", attention_low, all_values, preferred_element_type=jnp.float32
        )
        mixed = mixed.reshape(span, HEADS * HEAD).astype(jnp.bfloat16)
        residual = values + product(mixed, full_output)
        inverse_f = lax.rsqrt(jnp.mean(residual * residual, axis=-1, keepdims=True) + epsilon)
        scaled_f = residual * inverse_f
        normed_f = (scaled_f * gain_feed).astype(jnp.bfloat16)
        gate_sum = product(normed_f, full_gate)
        up_sum = product(normed_f, full_up)
        sigmoid_gate = jax.nn.sigmoid(gate_sum)
        activated = gate_sum * sigmoid_gate
        hidden = (activated * up_sum).astype(jnp.bfloat16)
        result = (residual + product(hidden, full_down)).astype(jnp.bfloat16)
        down_wgrad = product_tn(hidden, cotangent)
        hidden_grad = product_nt(cotangent, full_down)
        gate_grad = (
            hidden_grad * up_sum * sigmoid_gate * (1.0 + gate_sum * (1.0 - sigmoid_gate))
        ).astype(jnp.bfloat16)
        up_grad = (hidden_grad * activated).astype(jnp.bfloat16)
        gate_wgrad = product_tn(normed_f, gate_grad)
        up_wgrad = product_tn(normed_f, up_grad)
        normed_f_grad = product_nt(gate_grad, full_gate) + product_nt(up_grad, full_up)
        feed_gain_grad = jnp.sum(normed_f_grad * scaled_f, axis=0)
        residual_grad = cotangent.astype(jnp.float32) + norm_back(
            normed_f_grad, gain_feed, scaled_f, inverse_f
        )
        residual_low = residual_grad.astype(jnp.bfloat16)
        output_wgrad = product_tn(mixed, residual_low)
        mixed_grad = (
            product_nt(residual_low, full_output)
            .astype(jnp.bfloat16)
            .reshape(span, KV_HEADS, groups_q, HEAD)
        )
        attention_grad = jnp.einsum(
            "qhgd,khd->hgqk", mixed_grad, all_values, preferred_element_type=jnp.float32
        )
        row_totals = jnp.sum(attention * attention_grad, axis=-1, keepdims=True)
        score_grad = (attention * (attention_grad - row_totals) * scale).astype(jnp.bfloat16)
        value_grads = jnp.einsum(
            "hgqk,qhgd->khd", attention_low, mixed_grad, preferred_element_type=jnp.float32
        ).reshape(length, key_width)
        key_grads = jnp.einsum(
            "hgqk,qhgd->khd", score_grad, queries, preferred_element_type=jnp.float32
        ).reshape(length, key_width)
        query_grad = jnp.einsum(
            "hgqk,khd->qhgd", score_grad, all_keys, preferred_element_type=jnp.float32
        )
        key_back, value_back = (
            lax.psum_scatter(key_grads, "fsdp", scatter_dimension=0, tiled=True),
            lax.psum_scatter(value_grads, "fsdp", scatter_dimension=0, tiled=True),
        )
        query_low = (
            unrotate(query_grad, cos_four, sin_four)
            .reshape(span, HEADS * HEAD)
            .astype(jnp.bfloat16)
        )
        key_low = (
            unrotate(key_back.reshape(span, KV_HEADS, HEAD), cos_three, sin_three)
            .reshape(span, key_width)
            .astype(jnp.bfloat16)
        )
        value_low = value_back.astype(jnp.bfloat16)
        query_wgrad = product_tn(normed_a, query_low)
        key_wgrad = product_tn(normed_a, key_low)
        value_wgrad = product_tn(normed_a, value_low)
        normed_a_grad = (
            product_nt(query_low, full_query)
            + product_nt(key_low, full_key)
            + product_nt(value_low, full_value)
        )
        attention_gain_term = jnp.sum(normed_a_grad * scaled_a, axis=0)
        token_grad = (
            residual_grad + norm_back(normed_a_grad, gain_attention, scaled_a, inverse_a)
        ).astype(jnp.bfloat16)
        terms = (
            attention_gain_term,
            query_wgrad,
            key_wgrad,
            value_wgrad,
            output_wgrad,
            feed_gain_grad,
            gate_wgrad,
            up_wgrad,
            down_wgrad,
        )
        totals = tuple((left + right for left, right in zip(totals, terms)))
        return (totals, (result, token_grad))

    initial = tuple((jnp.zeros(weight.shape, jnp.float32) for weight in gathered))
    totals, (outputs, input_grads) = lax.scan(micro_step, initial, (inputs, segments, out_grad))
    shards = jax.tree.map(
        lambda part: part.astype(jnp.float32),
        lax.psum_scatter(shortened(totals), "fsdp", scatter_dimension=0, tiled=True),
    )
    summed = lax.psum(shards, "group")
    return (
        outputs,
        input_grads,
        summed[0],
        summed[1],
        summed[2],
        summed[3],
        summed[4],
        summed[5],
        summed[6],
        summed[7],
        summed[8],
    )


class Places:
    def __init__(self, group_size):
        self.group = lax.axis_index("group")
        self.y = lax.axis_index("fsdp")
        self.size = group_size
        self.masks = {"core": 1, "x": 2, "zlo": 4, "zhi": 8}

    def bit(self, name):
        if name == "y":
            return self.y
        return (self.group // self.masks[name]) % 2

    def swap(self, array, name):
        if name == "y":
            return lax.ppermute(array, "fsdp", [(0, 1), (1, 0)])
        mask = self.masks[name]
        return lax.ppermute(array, "group", [(i, i ^ mask) for i in range(self.size)])


def part_of(array, axis, bit):
    size = array.shape[axis] // 2
    return lax.dynamic_slice_in_dim(array, bit * size, size, axis)


def add_up(terms):
    total = terms[0].astype(jnp.float32)
    for term in terms[1:]:
        total = total + term.astype(jnp.float32)
    return low(total)


def in_order(bit, own, other, axis):
    return jnp.where(
        bit == 0,
        jnp.concatenate([own, other], axis=axis),
        jnp.concatenate([other, own], axis=axis),
    )


def paired_local(
    group_size,
    inputs,
    segments,
    out_grad,
    attention_gain,
    query_weight,
    key_weight,
    value_weight,
    output_weight,
    feedforward_gain,
    gate_weight,
    up_weight,
    down_weight,
):
    places = Places(group_size)
    y = places.y
    span, length, width = inputs.shape[1], segments.shape[1], inputs.shape[2]
    q_width = query_weight.shape[1]

    gains = jnp.pad(
        jnp.stack([attention_gain, feedforward_gain]).astype(jnp.float32), ((0, 6), (0, 0))
    )
    tokens, qkv_weight, gains = fetch(inputs, query_weight, key_weight, value_weight, gains)
    gains = gains.transpose(1, 0, 2).reshape(8, width)
    gain_a, gain_f = gains[0:1], gains[1:2]

    segment = lax.dynamic_index_in_dim(segments, y, 0, False)
    seg_col, seg_row = segment[:, None], segment[None, :]
    cosines, sines = rope_tables(length)
    normed_a, qkv = project(tokens, gain_a, qkv_weight, cosines, sines)
    mixed, lse, c, mix_weight, full_gate, full_up, full_down = attend(
        qkv, seg_col, seg_row, out_grad, output_weight, gate_weight, up_weight, down_weight
    )

    residual, normed_f, turned_f = mix(tokens, mixed, mix_weight, gain_f)

    core = places.bit("core")
    theirs = feed((1 - core).reshape(1), normed_f, turned_f, c, full_gate, full_up, full_down)
    came = [places.swap(term, "core") for term in theirs[2:]]
    mine = feed(core.reshape(1), normed_f, turned_f, c, full_gate, full_up, full_down)
    hidden_terms = [add_up([own, other]) for own, other in zip(mine[2:], came)]
    result, residual_grad, mixed_grad, mix_term, feed_gain_term = turn(
        residual, theirs[0], mine[0], theirs[1], mine[1], c, mixed, mix_weight, gain_f
    )
    dq, dk, dv, gate_half, up_half, down_half = attend_back(
        qkv, mixed_grad, mixed, lse, seg_col, seg_row, cosines, sines, *hidden_terms
    )
    gate_sum, up_sum, down_sum, sums, outputs, input_grads, gain_sums = end(
        dq, dk, dv, normed_a, tokens, residual_grad, qkv_weight, gain_a, feed_gain_term,
        mix_term, result, gate_half, up_half, down_half,
    )
    gain_grads = lax.dynamic_slice_in_dim(gain_sums, y * (width // 2), width // 2, 1)
    k_width = key_weight.shape[1]
    sums = sums.reshape(width // 2, -1).astype(jnp.float32)
    ends = (0, q_width, q_width + k_width, q_width + 2 * k_width, sums.shape[1])
    parts = [sums[:, a:b] for a, b in zip(ends[:-1], ends[1:])]
    return (
        outputs,
        input_grads,
        gain_grads[0],
        *parts,
        gain_grads[1],
        gate_sum.reshape(width // 2, -1).astype(jnp.float32),
        up_sum.reshape(width // 2, -1).astype(jnp.float32),
        down_sum.reshape(-1, width).astype(jnp.float32),
    )


def solution(mesh):
    placed = (
        P("group", "fsdp", None),
        P("group", None),
        P("group", "fsdp", None),
        P("fsdp"),
        P("fsdp", None),
        P("fsdp", None),
        P("fsdp", None),
        P("fsdp", None),
        P("fsdp"),
        P("fsdp", None),
        P("fsdp", None),
        P("fsdp", None),
    )
    group_size, fsdp_size = mesh.shape["group"], mesh.shape["fsdp"]

    def local(*arrays):
        if group_size == 16 and fsdp_size == 2 and arrays[0].shape[0] == 2:
            return paired_local(group_size, *arrays)
        return plain_local(*arrays)

    return jax.shard_map(
        local,
        mesh=mesh,
        in_specs=placed,
        out_specs=(
            P("group", "fsdp", None),
            P("group", "fsdp", None),
            P("fsdp"),
            P("fsdp", None),
            P("fsdp", None),
            P("fsdp", None),
            P("fsdp", None),
            P("fsdp"),
            P("fsdp", None),
            P("fsdp", None),
            P("fsdp", None),
        ),
        check_vma=False,
    )
```

```python
import functools
import math

import jax
import jax.numpy as jnp
from jax import lax
from jax.experimental import pallas as pl
from jax.experimental.pallas import tpu as pltpu
from jax.sharding import PartitionSpec as P

HEADS = 18
KV_HEADS = 6
HEAD = 64
epsilon = 1e-05
rope_base = 10000.0
BLOCK = 256
WIDE = 128
VMEM_MOST = 66 * 1024 * 1024 - 3 * 1024 * 1024


def mm(left, right):
    return jnp.dot(left, right, preferred_element_type=jnp.float32)


def mm_nt(left, right):
    return lax.dot_general(
        left, right, (((1,), (1,)), ((), ())), preferred_element_type=jnp.float32
    )


def mm_tn(left, right):
    return lax.dot_general(
        left, right, (((0,), (0,)), ((), ())), preferred_element_type=jnp.float32
    )


def low(values):
    return values.astype(jnp.bfloat16)


def lanes_below(rows, period, limit):
    lane = lax.broadcasted_iota(jnp.int32, (rows, WIDE), 1)
    return lane % period < limit


def swap_halves(tile):
    ahead = pltpu.roll(tile, WIDE - HEAD // 2, 1)
    behind = pltpu.roll(tile, HEAD // 2, 1)
    return jnp.where(lanes_below(tile.shape[0], HEAD, HEAD // 2), ahead, behind)


def rope_tables(length):
    half_width = HEAD // 2
    freqs = jnp.exp(
        jnp.arange(half_width, dtype=jnp.float32) * (-2.0 * math.log(rope_base) / HEAD)
    )
    angles = jnp.arange(length, dtype=jnp.float32)[:, None] * freqs[None, :]
    cosines, sines = jnp.cos(angles), jnp.sin(angles)
    return (
        jnp.concatenate([cosines] * 4, axis=1),
        jnp.concatenate([-sines, sines] * 2, axis=1),
    )


def project_body(x_ref, gain_ref, w_ref, cos_ref, sin_ref, normed_ref, qkv_ref):
    values = x_ref[...].astype(jnp.float32)
    inverse = lax.rsqrt(jnp.mean(values * values, axis=-1, keepdims=True) + epsilon)
    normed = low(values * inverse * gain_ref[...])
    normed_ref[...] = normed
    cosines, sines = cos_ref[...], sin_ref[...]
    width = qkv_ref.shape[1]
    q_width, k_width = HEADS * HEAD, KV_HEADS * HEAD
    step = 384
    for at in range(0, width, step):
        wide = mm(normed, w_ref[:, at : at + step])
        for part in range(0, step, WIDE):
            tile = wide[:, part : part + WIDE]
            if at + part < q_width + k_width:
                tile = tile * cosines + swap_halves(tile) * sines
            if at + part < q_width:
                tile = tile * HEAD ** (-0.5)
            qkv_ref[:, at + part : at + part + WIDE] = low(tile)


def project(x, gain, w, cosines, sines):
    length, width = x.shape
    out = w.shape[1]
    rows = pl.BlockSpec((BLOCK, width), lambda i: (i, 0))
    table = pl.BlockSpec((BLOCK, WIDE), lambda i: (i, 0))
    return pl.pallas_call(
        project_body,
        grid=(length // BLOCK,),
        in_specs=[
            rows,
            pl.BlockSpec((1, width), lambda i: (0, 0)),
            pl.BlockSpec((width, out), lambda i: (0, 0), pipeline_mode=pl.Buffered(1)),
            table,
            table,
        ],
        out_specs=[rows, pl.BlockSpec((BLOCK, out), lambda i: (i, 0))],
        out_shape=[
            jax.ShapeDtypeStruct((length, width), jnp.bfloat16),
            jax.ShapeDtypeStruct((length, out), jnp.bfloat16),
        ],
        cost_estimate=pl.CostEstimate(
            flops=2 * length * width * out,
            bytes_accessed=2 * (2 * length * width + length * out + width * out),
            transcendentals=0,
        ),
        name="project",
    )(x, gain, w, cosines, sines)


MESH = pl.DeviceIdType.MESH
MASKS = {"core": 1, "x": 2, "zlo": 4, "zhi": 8}


def bit_of(name):
    if name == "y":
        return lax.axis_index("fsdp")
    return (lax.axis_index("group") // MASKS[name]) % 2


def peer_of(name):
    if name == "y":
        return {"fsdp": 1 - lax.axis_index("fsdp")}
    return {"group": lax.axis_index("group") + MASKS[name] * (1 - 2 * bit_of(name))}


def greet(names):
    barrier = pltpu.get_barrier_semaphore()
    for name in names:
        pl.semaphore_signal(barrier, inc=1, device_id=peer_of(name), device_id_type=MESH)
    pl.semaphore_wait(barrier, len(names))


def across(source, target, sems, slot, name):
    return pltpu.make_async_remote_copy(
        src_ref=source,
        dst_ref=target,
        send_sem=sems.at[0, slot],
        recv_sem=sems.at[1, slot],
        device_id=peer_of(name),
        device_id_type=MESH,
    )


class Spread:
    def __init__(self, shard, full, order, sems, slot, columns=None):
        self.shard, self.full, self.order, self.sems, self.slot = shard, full, order, sems, slot
        self.columns = columns

    def copy(self, stage):
        y = lax.axis_index("fsdp")
        index = 0
        for at, name in enumerate(self.order):
            index = index + bit_of(name) * 2**at
        slot = self.slot + stage
        where = (slice(None), slice(None)) if self.columns is None else (slice(None), self.columns)
        if stage == 0:
            return across(
                self.shard.at[index], self.full.at[(y * 8 + index,) + where], self.sems, slot, "y"
            )
        count = 2 ** (stage - 1)
        block = self.full.at[(pl.ds((1 - y) * 8 + index // count * count, count),) + where]
        return across(block, block, self.sems, slot, self.order[stage - 1])

    def advance(self, stage):
        if stage >= 0:
            self.copy(stage).wait_recv()
        if stage < len(self.order):
            self.copy(stage + 1).start()

    def finish(self):
        for stage in range(len(self.order) + 1):
            self.copy(stage).wait_send()


def fetch_body(inputs, query, key, value, gains, tokens, weight, both_gains,
               held, held_weight, sems, near):
    y = lax.axis_index("fsdp")
    q_width, k_width = query.shape[2], key.shape[2]
    places = (
        slice(0, q_width),
        slice(q_width, q_width + k_width),
        slice(q_width + k_width, q_width + 2 * k_width),
    )
    shards = (query, key, value)
    loads = [pltpu.make_async_copy(inputs.at[y], held, near.at[0])] + [
        pltpu.make_async_copy(shard, held_weight.at[:, :, place], near.at[1 + at])
        for at, (shard, place) in enumerate(zip(shards, places))
    ]
    for load in loads:
        load.start()
    greet(("y", "x", "zlo", "core"))
    index = bit_of("x") + 2 * bit_of("zlo") + 4 * bit_of("core")
    first = [
        across(shard.at[index], weight.at[y * 8 + index, :, place], sems, at, "y")
        for at, (shard, place) in enumerate(zip(shards, places))
    ]
    span = held.shape[0]
    swap = across(
        inputs.at[1 - y], tokens.at[pl.ds(pl.multiple_of(y * span, span), span)], sems, 3, "y"
    )
    gain_swap = across(gains, both_gains.at[y], sems, 4, "y")
    for copy in first + [gain_swap, swap]:
        copy.start()
    for load in loads:
        load.wait()
    stores = [
        pltpu.make_async_copy(
            held, tokens.at[pl.ds(pl.multiple_of(y * span, span), span)], near.at[4]
        ),
        pltpu.make_async_copy(held_weight, weight.at[pl.ds(y * 8, 8)], near.at[5]),
        pltpu.make_async_copy(gains, both_gains.at[y], near.at[6]),
    ]
    for store in stores:
        store.start()
    for copy in first:
        copy.wait_recv()
    later = []
    for at, name in enumerate(("x", "zlo", "core")):
        count = 2**at
        block = weight.at[pl.ds((1 - y) * 8 + index // count * count, count)]
        copy = across(block, block, sems, 5 + at, name)
        copy.start()
        copy.wait_recv()
        later.append(copy)
    swap.wait_recv()
    gain_swap.wait_recv()
    for copy in first + [gain_swap, swap] + later:
        copy.wait_send()
    for store in stores:
        store.wait()


def fetch(inputs, query, key, value, gains):
    span, width = inputs.shape[1:]
    total = query.shape[1] + 2 * key.shape[1]
    eight = lambda shard: shard.reshape(8, shard.shape[0] // 8, shard.shape[1])
    rows = query.shape[0] // 8
    anywhere = pl.BlockSpec(memory_space=pl.ANY)
    tokens, weight, both_gains = pl.pallas_call(
        fetch_body,
        in_specs=[anywhere] * 5,
        out_specs=[anywhere] * 3,
        out_shape=[
            jax.ShapeDtypeStruct((2 * span, width), inputs.dtype),
            jax.ShapeDtypeStruct((16, rows, total), query.dtype),
            jax.ShapeDtypeStruct((2,) + gains.shape, gains.dtype),
        ],
        scratch_shapes=[
            pltpu.VMEM((span, width), inputs.dtype),
            pltpu.VMEM((8, rows, total), query.dtype),
            pltpu.SemaphoreType.DMA((2, 8)),
            pltpu.SemaphoreType.DMA((7,)),
        ],
        compiler_params=pltpu.CompilerParams(collective_id=1, has_side_effects=True),
        name="fetch",
    )(inputs, eight(query), eight(key), eight(value), gains)
    return tokens, weight.reshape(16 * rows, total), both_gains


AXES = ("y", "x", "zlo", "zhi")


class Fold:
    def __init__(self, source, kept, received, order, sems, slot, near, near_slot):
        self.source, self.kept, self.received = source, kept, received
        self.order, self.sems, self.slot = order, sems, slot
        self.near, self.near_slot = near, near_slot

    def pick(self, stage, bit):
        left = [name for name in AXES if name not in self.order[:stage]]
        return (slice(None),) * left.index(self.order[stage]) + (bit,)

    def held(self, stage):
        return self.source if stage == 0 else self.received[stage - 1]

    def copy(self, stage):
        name = self.order[stage]
        source = self.held(stage).at[self.pick(stage, 1 - bit_of(name))]
        return across(source, self.received[stage], self.sems, self.slot + stage, name)

    def load(self):
        source = self.source.at[self.pick(0, bit_of(self.order[0]))]
        return pltpu.make_async_copy(source, self.kept, self.near.at[self.near_slot])

    def begin(self):
        self.copy(0).start()
        if self.kept is not None:
            self.load().start()

    def advance(self, stage):
        self.copy(stage).wait_recv()
        target = self.received[stage]
        lead = target.ndim - 2
        if stage == 0 and self.kept is not None:
            self.load().wait()
            mine, at, bit = self.kept, 0, None
        else:
            bit = bit_of(self.order[stage])
            mine, at = self.held(stage), len(self.pick(stage, 0)) - 1

        @pl.loop(0, 2**lead)
        def _(n):
            index = tuple(n // 2 ** (lead - 1 - k) % 2 for k in range(lead))
            from_ = index if bit is None else index[:at] + (bit,) + index[at:]
            total = target[index].astype(jnp.float32) + mine[from_].astype(jnp.float32)
            target[index] = low(total)

        if stage + 1 < len(self.order):
            self.copy(stage + 1).start()

    def finish(self):
        for stage in range(len(self.order)):
            self.copy(stage).wait_send()


class Rise:
    def __init__(self, whole, order, columns, sems, slot):
        self.whole, self.order, self.columns, self.sems, self.slot = whole, order, columns, sems, slot

    def block(self, stage):
        index = tuple(
            slice(None) if name in self.order[:stage] + ("zhi",) else bit_of(name)
            for name in AXES[1:]
        )
        if self.whole.ndim == 7:
            return [self.whole.at[(bit_of("core"), self.columns) + index]]
        return [self.whole.at[index + (slice(None), columns)] for columns in self.columns]

    def copies(self, stage, first=None):
        blocks = self.block(stage)
        count = len(blocks)
        return [
            across(
                block if first is None else first[at],
                block,
                self.sems,
                self.slot + stage * count + at,
                self.order[stage],
            )
            for at, block in enumerate(blocks)
        ]

    def begin(self, first):
        for copy in self.copies(0, first):
            copy.start()

    def advance(self, stage):
        for copy in self.copies(stage):
            copy.wait_recv()
        if stage + 1 < len(self.order):
            for copy in self.copies(stage + 1):
                copy.start()

    def finish(self):
        for stage in range(len(self.order)):
            for copy in self.copies(stage):
                copy.wait_send()


ORDERS = (("y", "x", "zlo"), ("x", "zlo", "y"), ("zlo", "y", "x"))
BACKS = (("zlo", "x", "core"), ("x", "zlo", "core"), ("zlo", "x", "core"))
PART_ORDERS = (("x", "y", "zlo"), ("x", "y", "zlo"), ("y", "x", "zlo"))
PART_BACKS = (("zlo", "x", "core"), ("x", "zlo", "core"), ("zlo", "x", "core"))


def hidden_columns(part, chunk):
    at = (2 * bit_of("core") + chunk) * part
    return [pl.ds(pl.multiple_of(side * 4 * part + at, WIDE), part) for side in range(2)]


def place_heads(tile, variants_ref):
    wide = tile.astype(jnp.float32)
    turned = pltpu.roll(wide, HEAD, 1)
    low_lanes = lanes_below(tile.shape[0], WIDE, HEAD)
    variants_ref[0] = low(jnp.where(low_lanes, wide, 0.0))
    variants_ref[1] = low(jnp.where(low_lanes, 0.0, turned))
    variants_ref[2] = low(jnp.where(low_lanes, turned, 0.0))
    variants_ref[3] = low(jnp.where(low_lanes, 0.0, wide))


def allowed_block(seg_k, seg_q, diagonal):
    same = seg_k == seg_q
    if diagonal:
        rows = lax.broadcasted_iota(jnp.int32, same.shape, 0)
        lanes = lax.broadcasted_iota(jnp.int32, same.shape, 1)
        same = same & (rows <= lanes)
    return same


def attend_body(
    q_ref, k_ref, v_ref, seg_col_ref, seg_row_ref, out_grad, mix_w, gate_w, up_w, down_w,
    mixed_ref, lse_ref, whole_grad, mix_full, gate_full, up_full, down_full,
    ks, vt, acc, stats, sems, near, held_mix, held_gate, held_up, held_down, held_grad
):
    block = pl.program_id(1)
    now = pl.program_id(0) * pl.num_programs(1) + block
    most = pl.num_programs(0) * pl.num_programs(1) - 1
    y = lax.axis_index("fsdp")
    spreads = {
        "mix": Spread(mix_w, mix_full, ("x", "zlo", "core"), sems, 0),
        "gate": Spread(gate_w, gate_full, ("zlo", "x", "core"), sems, 4),
        "up": Spread(up_w, up_full, ("x", "zlo", "core"), sems, 8),
        "down": Spread(down_w, down_full, ("zlo", "x", "core"), sems, 12),
    }
    span = out_grad.shape[1]
    mine = whole_grad.at[pl.ds(pl.multiple_of(y * span, span), span)]
    grad_swap = across(out_grad.at[1 - y], mine, sems, 16, "y")
    half = pl.ds(y * 8, 8)
    own = (
        (mix_w, held_mix, mix_full.at[half]),
        (gate_w, held_gate, gate_full.at[half]),
        (up_w, held_up, up_full.at[half]),
        (down_w, held_down, down_full.at[half]),
        (out_grad.at[y], held_grad, mine),
    )
    loads = [pltpu.make_async_copy(a, b, near.at[0, at]) for at, (a, b, _) in enumerate(own)]
    stores = [pltpu.make_async_copy(b, c, near.at[1, at]) for at, (_, b, c) in enumerate(own)]
    plan = {
        1: (("mix", 0),),
        2: (("mix", 1),),
        3: (("gate", 0), ("mix", 2)),
        5: (("up", 0), ("gate", 1)),
        7: (("down", 0), ("up", 1)),
        9: (("gate", 2), ("down", 1)),
        10: (("up", 2),),
    }

    @pl.when(now == 0)
    def _():
        for load in loads:
            load.start()
        greet(("y", "x", "zlo", "core"))
        for name in ("mix", "gate", "up", "down"):
            spreads[name].advance(-1)
        grad_swap.start()

    @pl.when(now == 1)
    def _():
        for load, store in zip(loads, stores):
            load.wait()
            store.start()

    for at, steps in plan.items():

        @pl.when(now == at)
        def _(steps=steps):
            for name, stage in steps:
                spreads[name].advance(stage)

    @pl.when(block == 0)
    def _():
        place_heads(k_ref[...], ks)
        vt[...] = low(v_ref[...].astype(jnp.float32).T)

    acc[...] = jnp.zeros_like(acc)
    stats[0] = jnp.full((8, BLOCK), -1e30, jnp.float32)
    stats[1] = jnp.zeros((8, BLOCK), jnp.float32)
    seg_q = seg_row_ref[...]

    def step(j, diagonal):
        rows = pl.ds(pl.multiple_of(j * BLOCK, BLOCK), BLOCK)
        seg_k = seg_col_ref[rows, :]
        allowed = allowed_block(seg_k, seg_q, diagonal)
        for head in range(6):
            part, side, kv = head // 2, head % 2, head // 3
            q_tile = q_ref[:, part * WIDE : (part + 1) * WIDE]
            scores = mm_nt(ks[kv * 2 + side, rows, :], q_tile)
            scores = jnp.where(allowed, scores, -1e30)
            before = stats[0, head : head + 1, :]
            highest = jnp.maximum(before, jnp.max(scores, axis=0, keepdims=True))
            shrink = jnp.exp(before - highest)
            chances = jnp.exp(scores - highest)
            stats[0, head : head + 1, :] = highest
            stats[1, head : head + 1, :] = stats[1, head : head + 1, :] * shrink + jnp.sum(
                chances, axis=0, keepdims=True
            )
            values = vt[kv * HEAD : (kv + 1) * HEAD, rows]
            at = head * HEAD
            acc[at : at + HEAD, :] = acc[at : at + HEAD, :] * shrink + mm(values, low(chances))

    @pl.loop(0, block)
    def _(j):
        step(j, False)

    step(block, True)
    total = stats[1]
    for part in range(3):
        at = part * WIDE
        both = jnp.concatenate(
            [
                acc[at : at + HEAD, :] / total[2 * part : 2 * part + 1, :],
                acc[at + HEAD : at + WIDE, :] / total[2 * part + 1 : 2 * part + 2, :],
            ],
            axis=0,
        )
        mixed_ref[:, at : at + WIDE] = low(both.T)
    lse_ref[0] = stats[0] + jnp.log(jnp.maximum(total, 1e-30))

    @pl.when(now == most)
    def _():
        spreads["down"].advance(2)
        for spread in spreads.values():
            spread.advance(3)
            spread.finish()
        grad_swap.wait()
        for store in stores:
            store.wait()


def attend(qkv, seg_col, seg_row, out_grad, mix_w, gate_w, up_w, down_w):
    length = qkv.shape[0]
    pairs = KV_HEADS // 2
    q_tiles = HEADS * HEAD // WIDE
    anywhere = pl.BlockSpec(memory_space=pl.ANY)
    shards = [w.reshape(8, w.shape[0] // 8, w.shape[1]) for w in (mix_w, gate_w, up_w, down_w)]
    fulls = [jax.ShapeDtypeStruct((16,) + w.shape[1:], w.dtype) for w in shards]
    found = pl.pallas_call(
        attend_body,
        grid=(pairs, length // BLOCK),
        in_specs=[
            pl.BlockSpec((BLOCK, 3 * WIDE), lambda b, i: (i, b)),
            pl.BlockSpec((length, WIDE), lambda b, i: (0, q_tiles + b)),
            pl.BlockSpec((length, WIDE), lambda b, i: (0, q_tiles + pairs + b)),
            pl.BlockSpec((length, 1), lambda b, i: (0, 0)),
            pl.BlockSpec((1, BLOCK), lambda b, i: (0, i)),
        ]
        + [anywhere] * 5,
        out_specs=[
            pl.BlockSpec((BLOCK, 3 * WIDE), lambda b, i: (i, b)),
            pl.BlockSpec((1, 8, BLOCK), lambda b, i: (b, 0, i)),
        ]
        + [anywhere] * 5,
        out_shape=[
            jax.ShapeDtypeStruct((length, HEADS * HEAD), jnp.bfloat16),
            jax.ShapeDtypeStruct((pairs, 8, length), jnp.float32),
            jax.ShapeDtypeStruct((length, out_grad.shape[2]), out_grad.dtype),
        ]
        + fulls,
        scratch_shapes=[
            pltpu.VMEM((4, length, WIDE), jnp.bfloat16),
            pltpu.VMEM((WIDE, length), jnp.bfloat16),
            pltpu.VMEM((6 * HEAD, BLOCK), jnp.float32),
            pltpu.VMEM((2, 8, BLOCK), jnp.float32),
            pltpu.SemaphoreType.DMA((2, 17)),
            pltpu.SemaphoreType.DMA((2, 5)),
        ]
        + [pltpu.VMEM(w.shape, w.dtype) for w in shards]
        + [pltpu.VMEM(out_grad.shape[1:], out_grad.dtype)],
        compiler_params=pltpu.CompilerParams(
            collective_id=2, has_side_effects=True, vmem_limit_bytes=VMEM_MOST
        ),
        cost_estimate=pl.CostEstimate(
            flops=16 * length * length * HEADS * HEAD // 2,
            bytes_accessed=6 * length * HEADS * HEAD,
            transcendentals=HEADS * length * length // 2,
        ),
        name="attend",
    )(qkv, qkv, qkv, seg_col, seg_row, out_grad, *shards)
    return tuple(found[:3]) + tuple(w.reshape(-1, w.shape[2]) for w in found[3:])


def attend_back_body(
    q_ref, k_ref, v_ref, grad_ref, mixed_ref, lse_ref, seg_col_ref, seg_row_ref, cos_ref, sin_ref,
    gate_term, up_term, down_term, gate_third, up_third, down_third,
    dq_ref, dk_ref, dv_ref, gate_left, up_left, down_left, gate_both, up_both, down_both,
    ks, vs, kt, k_acc, v_acc, q_acc, sides, delta, sems, near,
    kept_h, r1_h, r2_h, r3_h, own_h, came_h, kept_d, r1_d, r2_d, r3_d, own_d, came_d
):
    block = pl.program_id(1)
    length = k_ref.shape[0]
    now = pl.program_id(0) * pl.num_programs(1) + block
    most = pl.num_programs(0) * pl.num_programs(1) - 1
    pick = lambda pair, single: [pair.at[0], pair.at[1], single]
    kept, owns, came = pick(kept_h, kept_d), pick(own_h, own_d), pick(came_h, came_d)
    ones, twos, threes = pick(r1_h, r1_d), pick(r2_h, r2_d), pick(r3_h, r3_d)
    folds = [
        Fold(term, kept[f], [ones[f], twos[f], threes[f]], ORDERS[f], sems, 3 * f, near, f)
        for f, term in enumerate((gate_term, up_term, down_term))
    ]
    loads = [
        pltpu.make_async_copy(third, owns[f], near.at[3 + f])
        for f, third in enumerate((gate_third, up_third, down_third))
    ]
    zs = [across(owns[f], came[f], sems, 9 + f, "zhi") for f in range(3)]
    stores = [
        pltpu.make_async_copy(threes[f], left, near.at[6 + f])
        for f, left in enumerate((gate_left, up_left, down_left))
    ] + [
        pltpu.make_async_copy(came[f], both, near.at[9 + f])
        for f, both in enumerate((gate_both, up_both, down_both))
    ]

    @pl.when(now == 0)
    def _():
        for load in loads:
            load.start()
        greet(AXES)
        for fold in folds:
            fold.begin()
        for load in loads:
            load.wait()
        zs[0].start()

    for at, stage in ((4, 0), (7, 1)):

        @pl.when(now == at)
        def _(stage=stage):
            for fold in folds:
                fold.advance(stage)
            zs[stage + 1].start()

    @pl.when(block == 0)
    def _():
        place_heads(k_ref[...], ks)
        place_heads(v_ref[...], vs)
        kt[...] = low(k_ref[...].astype(jnp.float32).T)
        k_acc[...] = jnp.zeros_like(k_acc)
        v_acc[...] = jnp.zeros_like(v_acc)

    q_acc[...] = jnp.zeros_like(q_acc)
    seg_q = seg_row_ref[...]
    low_lanes = lanes_below(BLOCK, WIDE, HEAD)
    zero = jnp.zeros((BLOCK, WIDE), jnp.bfloat16)
    for part in range(3):
        at = part * WIDE
        tile, grad = q_ref[:, at : at + WIDE], grad_ref[:, at : at + WIDE]
        sides[0, part, 0:BLOCK, :] = jnp.where(low_lanes, tile, zero)
        sides[0, part, BLOCK : 2 * BLOCK, :] = jnp.where(low_lanes, zero, tile)
        sides[1, part, 0:BLOCK, :] = jnp.where(low_lanes, grad, zero)
        sides[1, part, BLOCK : 2 * BLOCK, :] = jnp.where(low_lanes, zero, grad)
        product = (grad.astype(jnp.float32) * mixed_ref[:, at : at + WIDE].astype(jnp.float32)).T
        delta[2 * part : 2 * part + 1, :] = jnp.sum(product[:HEAD], axis=0, keepdims=True)
        delta[2 * part + 1 : 2 * part + 2, :] = jnp.sum(product[HEAD:], axis=0, keepdims=True)

    def step(j, diagonal):
        rows = pl.ds(pl.multiple_of(j * BLOCK, BLOCK), BLOCK)
        allowed = allowed_block(seg_col_ref[rows, :], seg_q, diagonal)
        for part in range(3):
            at = part * WIDE
            q_tile, grad_tile = q_ref[:, at : at + WIDE], grad_ref[:, at : at + WIDE]
            chances_pair, score_pair = [], []
            for side in range(2):
                head = 2 * part + side
                kv = head // 3
                scores = mm_nt(ks[kv * 2 + side, rows, :], q_tile)
                scores = jnp.where(allowed, scores, -1e30)
                chances = jnp.exp(scores - lse_ref[0, head : head + 1, :])
                onto = mm_nt(vs[kv * 2 + side, rows, :], grad_tile)
                score_grad = low(chances * (onto - delta[head : head + 1, :]))
                chances_pair.append(low(chances))
                score_pair.append(score_grad)
                to = head * HEAD
                q_acc[to : to + HEAD, :] += mm(kt[kv * HEAD : (kv + 1) * HEAD, rows], score_grad)
            v_acc[part, rows, :] += mm(jnp.concatenate(chances_pair, axis=1), sides[1, part])
            k_acc[part, rows, :] += mm(jnp.concatenate(score_pair, axis=1), sides[0, part])

    @pl.loop(0, block)
    def _(j):
        step(j, False)

    step(block, True)
    here = pl.ds(pl.multiple_of(block * BLOCK, BLOCK), BLOCK)
    for part in range(3):
        at = part * WIDE
        tile = q_acc[at : at + WIDE, :].T * HEAD ** (-0.5)
        tile = tile * cos_ref[here, :] - swap_halves(tile) * sin_ref[here, :]
        dq_ref[:, at : at + WIDE] = low(tile)

    @pl.when(block == length // BLOCK - 1)
    def _():
        for j in range(0, length, BLOCK):
            rows = slice(j, j + BLOCK)

            def gather(acc):
                first, middle, last = acc[0, rows, :], acc[1, rows, :], acc[2, rows, :]
                return middle + jnp.where(
                    low_lanes, first + pltpu.roll(first, HEAD, 1), last + pltpu.roll(last, HEAD, 1)
                )

            tile = gather(k_acc)
            tile = tile * cos_ref[rows, :] - swap_halves(tile) * sin_ref[rows, :]
            dk_ref[rows, :] = low(tile)
            dv_ref[rows, :] = low(gather(v_acc))

    @pl.when(now == most)
    def _():
        for f in range(3):
            zs[f].wait_recv()
            for n in range(2):
                came[f][n] = low(owns[f][n].astype(jnp.float32) + came[f][n].astype(jnp.float32))
            stores[3 + f].start()
        for fold in folds:
            fold.advance(2)
        for store in stores[:3]:
            store.start()
        for fold in folds:
            fold.finish()
        for copy in zs:
            copy.wait_send()
        for store in stores:
            store.wait()


def attend_back(qkv, mixed_grad, mixed, lse, seg_col, seg_row, cosines, sines, *terms):
    length = qkv.shape[0]
    rows, wide = terms[0].shape[4:]
    down_rows, width = terms[2].shape[4:]
    anywhere = pl.BlockSpec(memory_space=pl.ANY)
    pairs = KV_HEADS // 2
    q_tiles = HEADS * HEAD // WIDE
    q_block = pl.BlockSpec((BLOCK, 3 * WIDE), lambda b, i: (i, b))
    kv_block = pl.BlockSpec((length, WIDE), lambda b, i: (0, b))
    table = pl.BlockSpec((length, WIDE), lambda b, i: (0, 0), pipeline_mode=pl.Buffered(1))
    return pl.pallas_call(
        attend_back_body,
        grid=(pairs, length // BLOCK),
        in_specs=[
            q_block,
            pl.BlockSpec((length, WIDE), lambda b, i: (0, q_tiles + b)),
            pl.BlockSpec((length, WIDE), lambda b, i: (0, q_tiles + pairs + b)),
            q_block,
            q_block,
            pl.BlockSpec((1, 8, BLOCK), lambda b, i: (b, 0, i)),
            pl.BlockSpec((length, 1), lambda b, i: (0, 0)),
            pl.BlockSpec((1, BLOCK), lambda b, i: (0, i)),
            table,
            table,
        ]
        + [anywhere] * 6,
        out_specs=[q_block, kv_block, kv_block] + [anywhere] * 6,
        out_shape=[
            jax.ShapeDtypeStruct((length, HEADS * HEAD), jnp.bfloat16),
            jax.ShapeDtypeStruct((length, KV_HEADS * HEAD), jnp.bfloat16),
            jax.ShapeDtypeStruct((length, KV_HEADS * HEAD), jnp.bfloat16),
        ]
        + [
            jax.ShapeDtypeStruct((2,) + shape, jnp.bfloat16)
            for shape in ((rows, wide), (rows, wide), (down_rows, width)) * 2
        ],
        scratch_shapes=[
            pltpu.VMEM((4, length, WIDE), jnp.bfloat16),
            pltpu.VMEM((4, length, WIDE), jnp.bfloat16),
            pltpu.VMEM((WIDE, length), jnp.bfloat16),
            pltpu.VMEM((3, length, WIDE), jnp.float32),
            pltpu.VMEM((3, length, WIDE), jnp.float32),
            pltpu.VMEM((6 * HEAD, BLOCK), jnp.float32),
            pltpu.VMEM((2, 3, 2 * BLOCK, WIDE), jnp.bfloat16),
            pltpu.VMEM((8, BLOCK), jnp.float32),
            pltpu.SemaphoreType.DMA((2, 12)),
            pltpu.SemaphoreType.DMA((12,)),
        ]
        + [pltpu.VMEM((2,) + (2,) * left + (rows, wide), jnp.bfloat16) for left in (3, 3, 2, 1, 1, 1)]
        + [pltpu.VMEM((2,) * left + (down_rows, width), jnp.bfloat16) for left in (3, 3, 2, 1, 1, 1)],
        compiler_params=pltpu.CompilerParams(
            collective_id=3, has_side_effects=True, vmem_limit_bytes=VMEM_MOST
        ),
        cost_estimate=pl.CostEstimate(
            flops=40 * length * length * HEADS * HEAD // 2,
            bytes_accessed=12 * length * HEADS * HEAD,
            transcendentals=HEADS * length * length // 2,
        ),
        name="attend_back",
    )(qkv, qkv, qkv, mixed_grad, mixed, lse, seg_col, seg_row, cosines, sines, *terms)


def mix_body(x_ref, mixed_ref, w_ref, gain_ref, residual_ref, normed_ref, turned_ref):
    residual = x_ref[...].astype(jnp.float32) + mm(mixed_ref[...], w_ref[...])
    residual_ref[...] = residual
    inverse = lax.rsqrt(jnp.mean(residual * residual, axis=-1, keepdims=True) + epsilon)
    normed = residual * inverse * gain_ref[...]
    normed_ref[...] = low(normed)
    turned_ref[...] = low(normed.T)


def mix(x, mixed, w, gain):
    length, width = x.shape
    rows = pl.BlockSpec((BLOCK, width), lambda i: (i, 0))
    return pl.pallas_call(
        mix_body,
        grid=(length // BLOCK,),
        in_specs=[
            rows,
            rows,
            pl.BlockSpec(w.shape, lambda i: (0, 0), pipeline_mode=pl.Buffered(1)),
            pl.BlockSpec((1, width), lambda i: (0, 0)),
        ],
        out_specs=[rows, rows, pl.BlockSpec((width, BLOCK), lambda i: (0, i))],
        out_shape=[
            jax.ShapeDtypeStruct((length, width), jnp.float32),
            jax.ShapeDtypeStruct((length, width), jnp.bfloat16),
            jax.ShapeDtypeStruct((width, length), jnp.bfloat16),
        ],
        cost_estimate=pl.CostEstimate(
            flops=2 * length * width * width, bytes_accessed=12 * length * width, transcendentals=0
        ),
        name="mix",
    )(x, mixed, w, gain)


def norm_grad(grad, gain, scaled, inverse):
    weighted = grad * gain
    return inverse * (weighted - scaled * jnp.mean(weighted * scaled, axis=-1, keepdims=True))


def turn_body(residual_ref, out_ref, back_ref, c_ref, mixed_ref, w_ref, gain_ref,
              result_ref, grad_ref, mixed_grad_ref, term_ref, gain_term_ref, total):
    step = pl.program_id(0)
    residual = residual_ref[...]
    result_ref[...] = low(residual + out_ref[...])
    inverse = lax.rsqrt(jnp.mean(residual * residual, axis=-1, keepdims=True) + epsilon)
    scaled = residual * inverse
    normed_grad = back_ref[...]
    gain_term = jnp.sum(normed_grad * scaled, axis=0, keepdims=True)
    grad = c_ref[...].astype(jnp.float32) + norm_grad(normed_grad, gain_ref[...], scaled, inverse)
    grad_ref[...] = grad
    grad_low = low(grad)
    mixed_grad_ref[...] = low(mm_nt(grad_low, w_ref[...]))
    term = mm_tn(mixed_ref[...], grad_low)

    @pl.when(step == 0)
    def _():
        total[...] = term
        gain_term_ref[...] = jnp.broadcast_to(gain_term, gain_term_ref.shape)

    @pl.when(step > 0)
    def _():
        total[...] += term
        gain_term_ref[...] += jnp.broadcast_to(gain_term, gain_term_ref.shape)

    @pl.when(step == pl.num_programs(0) - 1)
    def _():
        term_ref[...] = low(total[...])


def turn(residual, out, back, c, mixed, w, gain):
    length, width = residual.shape
    rows = pl.BlockSpec((BLOCK, width), lambda i: (i, 0))
    whole = lambda shape: pl.BlockSpec(shape, lambda i: (0, 0), pipeline_mode=pl.Buffered(1))
    return pl.pallas_call(
        turn_body,
        grid=(length // BLOCK,),
        in_specs=[rows] * 5 + [whole(w.shape), pl.BlockSpec((1, width), lambda i: (0, 0))],
        out_specs=[
            rows, rows, rows, whole((width, width)), pl.BlockSpec((8, width), lambda i: (0, 0)),
        ],
        out_shape=[
            jax.ShapeDtypeStruct((length, width), jnp.bfloat16),
            jax.ShapeDtypeStruct((length, width), jnp.float32),
            jax.ShapeDtypeStruct((length, width), jnp.bfloat16),
            jax.ShapeDtypeStruct((width, width), jnp.bfloat16),
            jax.ShapeDtypeStruct((8, width), jnp.float32),
        ],
        scratch_shapes=[pltpu.VMEM((width, width), jnp.float32)],
        compiler_params=pltpu.CompilerParams(vmem_limit_bytes=VMEM_MOST),
        cost_estimate=pl.CostEstimate(
            flops=4 * length * width * width, bytes_accessed=32 * length * width, transcendentals=0
        ),
        name="turn",
    )(residual, out, back, c, mixed, w, gain)


def end_body(dq_ref, dk_ref, dv_ref, normed_ref, x_ref, grad_ref, w_ref, gain_ref, feed_gain_ref,
             mix_term, result, gate_left, up_left, down_left, gate_both, up_both, down_both,
             gate, up, down, sums, outputs, input_grads, gain_sums,
             turned, term, tokens, r0, r1, r2, r3, exchanged, hidden_a, hidden_b, hidden_came,
             down_a, down_b, down_came, gain_held, gain_came, rows_held, sems, near):
    step = pl.program_id(0)
    last = pl.num_programs(0) - 1
    rows_each = x_ref.shape[0]
    length = normed_ref.shape[0]
    q_width, k_width = dq_ref.shape[1], dk_ref.shape[1]
    core, y = bit_of("core"), lax.axis_index("fsdp")
    third = term.shape[-1] // 3
    wide = third // 2
    everything = (slice(None),) * 4 + (slice(None),)
    columns = [
        [pl.ds(pl.multiple_of(t * third + side * wide, WIDE), wide) for side in (core, 1 - core)]
        for t in range(3)
    ]
    span = outputs.shape[1]
    rows = [pl.ds(pl.multiple_of(at * span, span), span) for at in (y, 1 - y)]
    part = gate.shape[-1] // 8
    pick = lambda pair, single: [pair.at[0], pair.at[1], single]
    a_sums, b_left, came = pick(hidden_a, down_a), pick(hidden_b, down_b), pick(hidden_came, down_came)
    loads = [
        pltpu.make_async_copy(whole, held, near.at[n])
        for n, (whole, held) in enumerate(
            zip((gate_both, up_both, down_both, gate_left, up_left, down_left), a_sums + b_left)
        )
    ]
    mix_load = pltpu.make_async_copy(
        mix_term, term.at[everything + (slice(q_width + 2 * k_width, term.shape[-1]),)], near.at[6]
    )
    result_load = pltpu.make_async_copy(result.at[rows[0]], rows_held, near.at[7])
    result_store = pltpu.make_async_copy(rows_held, outputs.at[y], near.at[8])
    token_store = pltpu.make_async_copy(tokens.at[rows[0]], input_grads.at[y], near.at[9])
    zs = [across(b_left[f], came[f], sems, f, "zhi") for f in range(3)]
    rises = [
        [
            Rise(gate, BACKS[0], hidden_columns(part, h), sems, 60 + 15 * h),
            Rise(up, BACKS[1], hidden_columns(part, h), sems, 66 + 15 * h),
            Rise(down, BACKS[2], h, sems, 72 + 15 * h),
        ]
        for h in range(2)
    ]
    cores = [
        across(term.at[everything + (columns[t][1],)], r0.at[t], sems, 27 + t, "core")
        for t in range(3)
    ]
    parts = [
        Fold(r0.at[t], None, [r1.at[t], r2.at[t], r3.at[t]], PART_ORDERS[t], sems, 30 + 3 * t, None, None)
        for t in range(3)
    ]
    part_zs = [across(r3.at[t], exchanged.at[t], sems, 39 + t, "zhi") for t in range(3)]
    tops = [Rise(sums, PART_BACKS[t], [columns[t][0]], sems, 42 + 3 * t) for t in range(3)]
    swaps = [
        across(result.at[rows[1]], outputs.at[y], sems, 51, "y"),
        across(tokens.at[rows[1]], input_grads.at[y], sems, 52, "y"),
    ]
    names = ("core",) + AXES
    gain_copies = [
        across(gain_held.at[at], gain_came.at[at], sems, 53 + at, name)
        for at, name in enumerate(names)
    ]

    def pieces(h, f):
        held = (a_sums, came)[h][f]
        if f == 2:
            return [held]
        return [held.at[:, :, side * part : (side + 1) * part] for side in range(2)]

    def own_stores(h, f):
        return [
            pltpu.make_async_copy(piece, block, near.at[10 + 5 * h + 2 * f + n])
            for n, (piece, block) in enumerate(zip(pieces(h, f), rises[h][f].block(0)))
        ]

    def rise_begin(h, f):
        for store in own_stores(h, f):
            store.start()
        rises[h][f].begin(pieces(h, f))

    def rise_next(h, f):
        for store in own_stores(h, f):
            store.wait()
        rises[h][f].advance(0)

    def part_store(t):
        return pltpu.make_async_copy(exchanged.at[t], tops[t].block(0)[0], near.at[20 + t])

    def settle(copy, mine, theirs):
        copy.wait_recv()
        for n in range(2):
            theirs[n] = low(mine[n].astype(jnp.float32) + theirs[n].astype(jnp.float32))

    def hidden_settle(f):
        settle(zs[f], b_left[f], came[f])
        rise_begin(1, f)

    def part_settle(t):
        settle(part_zs[t], r3.at[t], exchanged.at[t])
        part_store(t).start()
        tops[t].begin([exchanged.at[t]])

    def core_sum(t):
        cores[t].wait_recv()

        @pl.loop(0, 16)
        def _(n):
            index = (n // 8, n // 4 % 2, n // 2 % 2, n % 2)
            mine = term[index + (slice(None), columns[t][0])]
            r0[(t,) + index] = low(r0[(t,) + index].astype(jnp.float32) + mine.astype(jnp.float32))

        parts[t].begin()

    def gain_step(at):
        gain_copies[at].wait_recv()
        gain_held[at + 1] = gain_held[at] + gain_came[at]
        if at + 1 < len(names):
            gain_copies[at + 1].start()

    @pl.when(step == 0)
    def _():
        for load in loads + [mix_load, result_load]:
            load.start()
        greet(names)
        for f in range(3):
            loads[f].wait()
            rise_begin(0, f)
        for load in loads[3:]:
            load.wait()
        zs[0].start()
        mix_load.wait()
        cores[2].start()
        for at in range(0, length, BLOCK):
            turned[:, at : at + BLOCK] = normed_ref[at : at + BLOCK, :].T

    @pl.when(step == 1)
    def _():
        core_sum(2)
        zs[1].start()
        swaps[0].start()
        result_load.wait()
        result_store.start()

    @pl.when(step == 2)
    def _():
        for f in range(3):
            rise_next(0, f)
        zs[2].start()

    @pl.when(step == 3)
    def _():
        cores[0].start()

    @pl.when(step == 4)
    def _():
        core_sum(0)
        hidden_settle(0)

    def chunk(low_rows, at):
        wide_term = mm(turned[...], low_rows).reshape(16, turned.shape[0] // 16, k_width)
        for n in range(16):
            index = (n // 8, n // 4 % 2, n // 2 % 2, n % 2, slice(None), slice(at, at + k_width))
            term[index] = low(wide_term[n])

    for at in range(3):

        @pl.when(step == at)
        def _(at=at):
            chunk(dq_ref[:, at * k_width : (at + 1) * k_width], at * k_width)

    @pl.when(step == 3)
    def _():
        chunk(dk_ref[...], q_width)

    @pl.when(step == 4)
    def _():
        chunk(dv_ref[...], q_width + k_width)

    @pl.when(step < last)
    def _():
        here = pl.ds(pl.multiple_of(step * rows_each, rows_each), rows_each)
        normed_grad = (
            mm_nt(dq_ref[here, :], w_ref[:, :q_width])
            + mm_nt(dk_ref[here, :], w_ref[:, q_width : q_width + k_width])
            + mm_nt(dv_ref[here, :], w_ref[:, q_width + k_width :])
        )
        values = x_ref[...].astype(jnp.float32)
        inverse = lax.rsqrt(jnp.mean(values * values, axis=-1, keepdims=True) + epsilon)
        scaled = values * inverse
        gain_term = jnp.sum(normed_grad * scaled, axis=0, keepdims=True)
        tokens[here, :] = low(
            grad_ref[...] + norm_grad(normed_grad, gain_ref[...], scaled, inverse)
        )

        @pl.when(step == 0)
        def _():
            gain_held[0, 0:1, :] = gain_term
            gain_held[0, 1:2, :] = feed_gain_ref[0:1, :]
            gain_held[0, 2:8, :] = jnp.zeros_like(gain_held[0, 2:8, :])

        @pl.when(step > 0)
        def _():
            gain_held[0, 0:1, :] += gain_term

    @pl.when(step == last)
    def _():
        cores[1].start()
        gain_copies[0].start()
        token_store.start()
        parts[2].advance(0)
        core_sum(1)
        gain_step(0)
        hidden_settle(1)
        parts[0].advance(0)
        parts[2].advance(1)
        parts[1].advance(0)
        gain_step(1)
        for f in range(3):
            rises[0][f].advance(1)
        rise_next(1, 0)
        hidden_settle(2)
        parts[0].advance(1)
        parts[1].advance(1)
        swaps[1].start()
        gain_step(2)
        for t in (2, 0, 1):
            parts[t].advance(2)
            part_zs[t].start()
        rise_next(1, 1)
        gain_step(3)
        for t in (2, 0, 1):
            part_settle(t)
        rise_next(1, 2)
        gain_step(4)
        for t in (2, 0, 1):
            part_store(t).wait()
            tops[t].advance(0)
        for f in range(3):
            rises[1][f].advance(1)
        for t in (2, 0, 1):
            tops[t].advance(1)
        every = rises[0] + rises[1] + tops
        for one in every:
            one.advance(2)
        for copy in cores + swaps + gain_copies + zs + part_zs:
            copy.wait_send()
        for one in every + parts:
            one.finish()
        for copy in swaps:
            copy.wait_recv()
        result_store.wait()
        token_store.wait()
        gain_sums[...] = gain_held[len(names)]


def end(dq, dk, dv, normed, x, grad, w, gain, feed_gain_term, mix_term, result, *sums):
    length, width = x.shape
    k_width = dk.shape[1]
    total = w.shape[1] + mix_term.shape[1]
    wide = total // 6
    mix_term = mix_term.reshape(2, 2, 2, 2, mix_term.shape[0] // 16, mix_term.shape[1])
    rows = mix_term.shape[4]
    hidden_rows, hidden = sums[0].shape[1:]
    down_rows = sums[2].shape[1]
    block = pl.BlockSpec((BLOCK, width), lambda i: (jnp.minimum(i, length // BLOCK - 1), 0))
    whole = lambda a: pl.BlockSpec(a.shape, lambda i: (0,) * a.ndim, pipeline_mode=pl.Buffered(1))
    anywhere = pl.BlockSpec(memory_space=pl.ANY)
    both = jax.ShapeDtypeStruct((2, length // 2, width), result.dtype)
    low_type = jnp.bfloat16
    return pl.pallas_call(
        end_body,
        grid=(w.shape[1] // k_width,),
        in_specs=[whole(dq), whole(dk), whole(dv), whole(normed), block, block, whole(w), whole(gain),
                  whole(feed_gain_term)] + [anywhere] * 8,
        out_specs=[anywhere] * 6 + [pl.BlockSpec((8, width), lambda i: (0, 0))],
        out_shape=[
            jax.ShapeDtypeStruct((2, 2, 2, hidden_rows, 4 * hidden), low_type),
            jax.ShapeDtypeStruct((2, 2, 2, hidden_rows, 4 * hidden), low_type),
            jax.ShapeDtypeStruct((2, 2, 2, 2, 2, down_rows, width), low_type),
            jax.ShapeDtypeStruct((2, 2, 2, rows, total), low_type),
            both,
            both,
            jax.ShapeDtypeStruct((8, width), jnp.float32),
        ],
        scratch_shapes=[
            pltpu.VMEM((width, length), low_type),
            pltpu.VMEM((2, 2, 2, 2, rows, total), low_type),
            pltpu.VMEM((length, width), low_type),
        ]
        + [pltpu.VMEM((3,) + (2,) * left + (rows, wide), low_type) for left in (4, 3, 2, 1, 1)]
        + [pltpu.VMEM((2, 2, hidden_rows, hidden), low_type)] * 3
        + [pltpu.VMEM((2, down_rows, width), low_type)] * 3
        + [
            pltpu.VMEM((6, 8, width), jnp.float32),
            pltpu.VMEM((5, 8, width), jnp.float32),
            pltpu.VMEM((length // 2, width), low_type),
            pltpu.SemaphoreType.DMA((2, 90)),
            pltpu.SemaphoreType.DMA((23,)),
        ],
        compiler_params=pltpu.CompilerParams(
            collective_id=4, has_side_effects=True, vmem_limit_bytes=VMEM_MOST
        ),
        name="end",
    )(dq, dk, dv, normed, x, grad, w, gain, feed_gain_term, mix_term, result, *sums)


def sixteenth(n):
    return (n // 8, n // 4 % 2, n // 2 % 2, n % 2)


def feed_body(normed_ref, turned_ref, c_ref, gate_w, up_w, down_w,
              out_ref, back_ref, gate_a, up_a, down_a, gate_b, up_b, down_b,
              gate_v, up_v, down_v, hidden_t, gate_low, up_low,
              hold_h, hold_d, came_h, came_d, own_h, own_d,
              r1_h, r2_h, r3_h, r1_d, r2_d, r3_d, sems, near, weight_sems, free):
    step = pl.program_id(0)
    length, width = normed_ref.shape
    core = bit_of("core")
    slot = step % 2
    part = gate_v.shape[2] // 2
    side_width = gate_w.shape[1] // 2

    def weights(of, into):
        owner = (core + 1 + of) % 2
        at = (2 * owner + of // 2) * part
        found = []
        for side in range(2):
            here = pl.ds(pl.multiple_of(side * side_width + at, WIDE), part)
            there = slice(side * part, (side + 1) * part)
            found += [
                (gate_w.at[:, here], gate_v.at[into, :, there]),
                (up_w.at[:, here], up_v.at[into, :, there]),
                (down_w.at[here], down_v.at[into, there]),
            ]
        return [
            pltpu.make_async_copy(a, b, weight_sems.at[into, n]) for n, (a, b) in enumerate(found)
        ]

    holds = (hold_h.at[0], hold_h.at[1], hold_d)
    arrived = (came_h.at[0], came_h.at[1], came_d)
    owns = (own_h.at[0], own_h.at[1], own_d)
    cores = [across(holds[f], arrived[f], sems, f, "core") for f in range(3)]
    received = (
        [r1_h.at[0], r2_h.at[0], r3_h.at[0]],
        [r1_h.at[1], r2_h.at[1], r3_h.at[1]],
        [r1_d, r2_d, r3_d],
    )
    folds = [
        Fold(owns[f], None, received[f], ORDERS[f], sems, 3 + 3 * f, None, None) for f in range(3)
    ]
    stores_a = [
        pltpu.make_async_copy(received[f][2], half, near.at[f])
        for f, half in enumerate((gate_a, up_a, down_a))
    ]
    stores_b = [
        pltpu.make_async_copy(owns[f], whole, near.at[3 + f])
        for f, whole in enumerate((gate_b, up_b, down_b))
    ]

    @pl.when(step == 0)
    def _():
        for load in weights(step, slot):
            load.start()
        out_ref[...] = jnp.zeros_like(out_ref)
        back_ref[...] = jnp.zeros_like(back_ref)
        greet(("core",) + AXES[:3])

    for load in weights(step, slot):
        load.wait()

    @pl.when(step < 3)
    def _():
        for load in weights(step + 1, 1 - slot):
            load.start()

    gate, up, down = gate_v.at[slot], up_v.at[slot], down_v.at[slot]
    for at in range(0, length, BLOCK):
        rows = slice(at, at + BLOCK)
        normed = normed_ref[rows, :]
        gate_sum = mm(normed, gate[...])
        up_sum = mm(normed, up[...])
        hidden_grad = mm_nt(c_ref[rows, :], down[...])
        sigmoid = jax.nn.sigmoid(gate_sum)
        activated = gate_sum * sigmoid
        hidden = low(activated * up_sum)
        gate_grad = low(hidden_grad * up_sum * (sigmoid + activated * (1.0 - sigmoid)))
        up_grad = low(hidden_grad * activated)
        hidden_t[:, rows] = hidden.T
        gate_low[rows, :] = gate_grad
        up_low[rows, :] = up_grad
        out_ref[rows, :] += mm(hidden, down[...])
        back_ref[rows, :] += mm_nt(gate_grad, gate[...]) + mm_nt(up_grad, up[...])

    theirs = slot == 0

    @pl.when(step == 3)
    def _():
        for fold in folds:
            fold.copy(0).wait_send()
            fold.advance(1)

    @pl.when(jnp.logical_not(theirs))
    def _():
        for copy in cores:
            copy.wait_recv()

    def put(blocks, hold, came, own):
        @pl.when(theirs)
        def _():
            for index, block in blocks:
                hold[index] = low(block)

        @pl.when(jnp.logical_not(theirs))
        def _():
            for index, block in blocks:
                own[index] = low(block + came[index].astype(jnp.float32))

    quarter = width // 4
    for n in range(4):
        rows = slice(n * quarter, (n + 1) * quarter)
        for f, grads in enumerate((gate_low, up_low)):
            value = mm(turned_ref[rows, :], grads[...]).reshape(4, quarter // 4, 2 * part)
            put(
                [((f,) + sixteenth(4 * n + k), value[k]) for k in range(4)], hold_h, came_h, own_h
            )
    third = width // 3
    for n in range(3):
        columns = slice(n * third, (n + 1) * third)
        value = mm(hidden_t[...], c_ref[:, columns]).reshape(16, part // 8, third)
        put(
            [(sixteenth(k) + (slice(None), columns), value[k]) for k in range(16)],
            hold_d, came_d, own_d,
        )

    @pl.when(step == 2)
    def _():
        pl.semaphore_wait(free, 1)

    @pl.when(theirs)
    def _():
        for copy in cores:
            copy.start()

    @pl.when(step == 2)
    def _():
        for fold in folds:
            fold.advance(0)

    @pl.when(jnp.logical_not(theirs))
    def _():
        for copy in cores:
            copy.wait_send()

    @pl.when(step == 1)
    def _():
        pl.semaphore_signal(free, inc=1, device_id=peer_of("core"), device_id_type=MESH)
        for fold in folds:
            fold.begin()

    @pl.when(step == 3)
    def _():
        for store in stores_b:
            store.start()
        for fold in folds:
            fold.advance(2)
        for store in stores_a:
            store.start()
        for fold in folds:
            for stage in (1, 2):
                fold.copy(stage).wait_send()
        for store in stores_a + stores_b:
            store.wait()


def feed(normed, turned, c, gate, up, down):
    length, width = normed.shape
    part = gate.shape[1] // 8
    rows, down_rows = width // 16, part // 8
    whole = lambda a: pl.BlockSpec(a.shape, lambda t: (0, 0), pipeline_mode=pl.Buffered(1))
    total = pl.BlockSpec((length, width), lambda t: (0, 0), pipeline_mode=pl.Buffered(1))
    anywhere = pl.BlockSpec(memory_space=pl.ANY)
    low_type = jnp.bfloat16
    hidden = lambda left: (2,) * left + (rows, 2 * part)
    down_shape = lambda left: (2,) * left + (down_rows, width)
    return pl.pallas_call(
        feed_body,
        grid=(4,),
        in_specs=[whole(normed), whole(turned), whole(c)] + [anywhere] * 3,
        out_specs=[total, total] + [anywhere] * 6,
        out_shape=[
            jax.ShapeDtypeStruct((length, width), jnp.float32),
            jax.ShapeDtypeStruct((length, width), jnp.float32),
        ]
        + [
            jax.ShapeDtypeStruct(shape, low_type)
            for left in (1, 4)
            for shape in (hidden(left), hidden(left), down_shape(left))
        ],
        scratch_shapes=[
            pltpu.VMEM((2, width, 2 * part), low_type),
            pltpu.VMEM((2, width, 2 * part), low_type),
            pltpu.VMEM((2, 2 * part, width), low_type),
            pltpu.VMEM((2 * part, length), low_type),
            pltpu.VMEM((length, 2 * part), low_type),
            pltpu.VMEM((length, 2 * part), low_type),
        ]
        + [pltpu.VMEM(shape, low_type) for _ in range(3) for shape in ((2,) + hidden(4), down_shape(4))]
        + [pltpu.VMEM((2,) + hidden(left), low_type) for left in (3, 2, 1)]
        + [pltpu.VMEM(down_shape(left), low_type) for left in (3, 2, 1)]
        + [
            pltpu.SemaphoreType.DMA((2, 12)),
            pltpu.SemaphoreType.DMA((6,)),
            pltpu.SemaphoreType.DMA((2, 6)),
            pltpu.SemaphoreType.REGULAR,
        ],
        compiler_params=pltpu.CompilerParams(
            collective_id=5, has_side_effects=True, vmem_limit_bytes=VMEM_MOST
        ),
        cost_estimate=pl.CostEstimate(
            flops=18 * length * width * gate.shape[1],
            bytes_accessed=12 * width * gate.shape[1] + 16 * length * width,
            transcendentals=length * gate.shape[1],
        ),
        name="feed",
    )(normed, turned, c, gate, up, down)


def shortened(array):
    return jax.tree.map(lambda a: a.astype(jnp.bfloat16) if a.dtype == jnp.float32 else a, array)


def product(left, right):
    return jnp.dot(left, right, preferred_element_type=jnp.float32)


def product_tn(left, right):
    return lax.dot_general(
        left, right, (((0,), (0,)), ((), ())), preferred_element_type=jnp.float32
    )


def product_nt(left, right):
    return lax.dot_general(
        left, right, (((1,), (1,)), ((), ())), preferred_element_type=jnp.float32
    )


def rotary_tables(positions, width):
    half_width = width // 2
    freqs = jnp.exp(
        jnp.arange(half_width, dtype=jnp.float32) * (-2.0 * math.log(rope_base) / width)
    )
    angles = positions[:, None] * freqs[None, :]
    return (jnp.cos(angles), jnp.sin(angles))


def rotate(values, cosines, sines):
    half_width = values.shape[-1] // 2
    first = values[..., :half_width]
    second = values[..., half_width:]
    return jnp.concatenate(
        [first * cosines - second * sines, second * cosines + first * sines], axis=-1
    )


def unrotate(values, cosines, sines):
    half_width = values.shape[-1] // 2
    first = values[..., :half_width]
    second = values[..., half_width:]
    return jnp.concatenate(
        [first * cosines + second * sines, second * cosines - first * sines], axis=-1
    )


def norm_back(grad_rows, gain, scaled, inverse):
    weighted = grad_rows * gain
    return inverse * (weighted - scaled * jnp.mean(weighted * scaled, axis=-1, keepdims=True))


def plain_local(
    inputs,
    segments,
    out_grad,
    attention_gain,
    query_weight,
    key_weight,
    value_weight,
    output_weight,
    feedforward_gain,
    gate_weight,
    up_weight,
    down_weight,
):
    gathered = (
        lax.all_gather(attention_gain, "fsdp", axis=0, tiled=True),
        lax.all_gather(query_weight, "fsdp", axis=0, tiled=True),
        lax.all_gather(key_weight, "fsdp", axis=0, tiled=True),
        lax.all_gather(value_weight, "fsdp", axis=0, tiled=True),
        lax.all_gather(output_weight, "fsdp", axis=0, tiled=True),
        lax.all_gather(feedforward_gain, "fsdp", axis=0, tiled=True),
        lax.all_gather(gate_weight, "fsdp", axis=0, tiled=True),
        lax.all_gather(up_weight, "fsdp", axis=0, tiled=True),
        lax.all_gather(down_weight, "fsdp", axis=0, tiled=True),
    )
    full_query, full_key, full_value, full_output = (
        gathered[1],
        gathered[2],
        gathered[3],
        gathered[4],
    )
    full_gate, full_up, full_down = (gathered[6], gathered[7], gathered[8])
    gain_attention = gathered[0].astype(jnp.float32)
    gain_feed = gathered[5].astype(jnp.float32)
    span = inputs.shape[1]
    length = segments.shape[1]
    groups_q = HEADS // KV_HEADS
    key_width = KV_HEADS * HEAD
    start = lax.axis_index("fsdp") * span
    query_pos = start + jnp.arange(span, dtype=jnp.int32)
    key_pos = jnp.arange(length, dtype=jnp.int32)
    cosines, sines = rotary_tables(query_pos.astype(jnp.float32), HEAD)
    cos_four, sin_four = (cosines[:, None, None, :], sines[:, None, None, :])
    cos_three, sin_three = (cosines[:, None, :], sines[:, None, :])
    causal = query_pos[:, None] >= key_pos[None, :]
    scale = HEAD ** (-0.5)

    def micro_step(totals, sequence):
        tokens, segment_row, cotangent = sequence
        own_segment = lax.dynamic_slice_in_dim(segment_row, start, span)
        allowed = causal & (own_segment[:, None] == segment_row[None, :])
        values = tokens.astype(jnp.float32)
        inverse_a = lax.rsqrt(jnp.mean(values * values, axis=-1, keepdims=True) + epsilon)
        scaled_a = values * inverse_a
        normed_a = (scaled_a * gain_attention).astype(jnp.bfloat16)
        query_lin = product(normed_a, full_query).reshape(span, KV_HEADS, groups_q, HEAD)
        queries = rotate(query_lin, cos_four, sin_four).astype(jnp.bfloat16)
        key_lin = product(normed_a, full_key).reshape(span, KV_HEADS, HEAD)
        key_rows = (
            rotate(key_lin, cos_three, sin_three).astype(jnp.bfloat16).reshape(span, key_width)
        )
        value_rows = product(normed_a, full_value).astype(jnp.bfloat16)
        all_keys, all_values = (
            lax.all_gather(key_rows, "fsdp", axis=0, tiled=True),
            lax.all_gather(value_rows, "fsdp", axis=0, tiled=True),
        )
        all_keys = all_keys.reshape(length, KV_HEADS, HEAD)
        all_values = all_values.reshape(length, KV_HEADS, HEAD)
        scores = (
            jnp.einsum("qhgd,khd->hgqk", queries, all_keys, preferred_element_type=jnp.float32)
            * scale
        )
        scores = jnp.where(allowed, scores, -1e30)
        highest = jnp.max(scores, axis=-1, keepdims=True)
        expo_scores = jnp.exp(scores - highest)
        attention = expo_scores / jnp.sum(expo_scores, axis=-1, keepdims=True)
        attention_low = attention.astype(jnp.bfloat16)
        mixed = jnp.einsum(
            "hgqk,khd->qhgd", attention_low, all_values, preferred_element_type=jnp.float32
        )
        mixed = mixed.reshape(span, HEADS * HEAD).astype(jnp.bfloat16)
        residual = values + product(mixed, full_output)
        inverse_f = lax.rsqrt(jnp.mean(residual * residual, axis=-1, keepdims=True) + epsilon)
        scaled_f = residual * inverse_f
        normed_f = (scaled_f * gain_feed).astype(jnp.bfloat16)
        gate_sum = product(normed_f, full_gate)
        up_sum = product(normed_f, full_up)
        sigmoid_gate = jax.nn.sigmoid(gate_sum)
        activated = gate_sum * sigmoid_gate
        hidden = (activated * up_sum).astype(jnp.bfloat16)
        result = (residual + product(hidden, full_down)).astype(jnp.bfloat16)
        down_wgrad = product_tn(hidden, cotangent)
        hidden_grad = product_nt(cotangent, full_down)
        gate_grad = (
            hidden_grad * up_sum * sigmoid_gate * (1.0 + gate_sum * (1.0 - sigmoid_gate))
        ).astype(jnp.bfloat16)
        up_grad = (hidden_grad * activated).astype(jnp.bfloat16)
        gate_wgrad = product_tn(normed_f, gate_grad)
        up_wgrad = product_tn(normed_f, up_grad)
        normed_f_grad = product_nt(gate_grad, full_gate) + product_nt(up_grad, full_up)
        feed_gain_grad = jnp.sum(normed_f_grad * scaled_f, axis=0)
        residual_grad = cotangent.astype(jnp.float32) + norm_back(
            normed_f_grad, gain_feed, scaled_f, inverse_f
        )
        residual_low = residual_grad.astype(jnp.bfloat16)
        output_wgrad = product_tn(mixed, residual_low)
        mixed_grad = (
            product_nt(residual_low, full_output)
            .astype(jnp.bfloat16)
            .reshape(span, KV_HEADS, groups_q, HEAD)
        )
        attention_grad = jnp.einsum(
            "qhgd,khd->hgqk", mixed_grad, all_values, preferred_element_type=jnp.float32
        )
        row_totals = jnp.sum(attention * attention_grad, axis=-1, keepdims=True)
        score_grad = (attention * (attention_grad - row_totals) * scale).astype(jnp.bfloat16)
        value_grads = jnp.einsum(
            "hgqk,qhgd->khd", attention_low, mixed_grad, preferred_element_type=jnp.float32
        ).reshape(length, key_width)
        key_grads = jnp.einsum(
            "hgqk,qhgd->khd", score_grad, queries, preferred_element_type=jnp.float32
        ).reshape(length, key_width)
        query_grad = jnp.einsum(
            "hgqk,khd->qhgd", score_grad, all_keys, preferred_element_type=jnp.float32
        )
        key_back, value_back = (
            lax.psum_scatter(key_grads, "fsdp", scatter_dimension=0, tiled=True),
            lax.psum_scatter(value_grads, "fsdp", scatter_dimension=0, tiled=True),
        )
        query_low = (
            unrotate(query_grad, cos_four, sin_four)
            .reshape(span, HEADS * HEAD)
            .astype(jnp.bfloat16)
        )
        key_low = (
            unrotate(key_back.reshape(span, KV_HEADS, HEAD), cos_three, sin_three)
            .reshape(span, key_width)
            .astype(jnp.bfloat16)
        )
        value_low = value_back.astype(jnp.bfloat16)
        query_wgrad = product_tn(normed_a, query_low)
        key_wgrad = product_tn(normed_a, key_low)
        value_wgrad = product_tn(normed_a, value_low)
        normed_a_grad = (
            product_nt(query_low, full_query)
            + product_nt(key_low, full_key)
            + product_nt(value_low, full_value)
        )
        attention_gain_term = jnp.sum(normed_a_grad * scaled_a, axis=0)
        token_grad = (
            residual_grad + norm_back(normed_a_grad, gain_attention, scaled_a, inverse_a)
        ).astype(jnp.bfloat16)
        terms = (
            attention_gain_term,
            query_wgrad,
            key_wgrad,
            value_wgrad,
            output_wgrad,
            feed_gain_grad,
            gate_wgrad,
            up_wgrad,
            down_wgrad,
        )
        totals = tuple((left + right for left, right in zip(totals, terms)))
        return (totals, (result, token_grad))

    initial = tuple((jnp.zeros(weight.shape, jnp.float32) for weight in gathered))
    totals, (outputs, input_grads) = lax.scan(micro_step, initial, (inputs, segments, out_grad))
    shards = jax.tree.map(
        lambda part: part.astype(jnp.float32),
        lax.psum_scatter(shortened(totals), "fsdp", scatter_dimension=0, tiled=True),
    )
    summed = lax.psum(shards, "group")
    return (
        outputs,
        input_grads,
        summed[0],
        summed[1],
        summed[2],
        summed[3],
        summed[4],
        summed[5],
        summed[6],
        summed[7],
        summed[8],
    )


def paired_local(
    inputs,
    segments,
    out_grad,
    attention_gain,
    query_weight,
    key_weight,
    value_weight,
    output_weight,
    feedforward_gain,
    gate_weight,
    up_weight,
    down_weight,
):
    y = lax.axis_index("fsdp")
    span, length, width = inputs.shape[1], segments.shape[1], inputs.shape[2]
    q_width = query_weight.shape[1]

    gains = jnp.pad(
        jnp.stack([attention_gain, feedforward_gain]).astype(jnp.float32), ((0, 6), (0, 0))
    )
    tokens, qkv_weight, gains = fetch(inputs, query_weight, key_weight, value_weight, gains)
    gains = gains.transpose(1, 0, 2).reshape(8, width)
    gain_a, gain_f = gains[0:1], gains[1:2]

    segment = lax.dynamic_index_in_dim(segments, y, 0, False)
    seg_col, seg_row = segment[:, None], segment[None, :]
    cosines, sines = rope_tables(length)
    normed_a, qkv = project(tokens, gain_a, qkv_weight, cosines, sines)
    mixed, lse, c, mix_weight, full_gate, full_up, full_down = attend(
        qkv, seg_col, seg_row, out_grad, output_weight, gate_weight, up_weight, down_weight
    )

    residual, normed_f, turned_f = mix(tokens, mixed, mix_weight, gain_f)

    out, back, *chunks = feed(normed_f, turned_f, c, full_gate, full_up, full_down)
    result, residual_grad, mixed_grad, mix_term, feed_gain_term = turn(
        residual, out, back, c, mixed, mix_weight, gain_f
    )
    dq, dk, dv, *halves = attend_back(
        qkv, mixed_grad, mixed, lse, seg_col, seg_row, cosines, sines, *chunks[3:], *chunks[:3]
    )
    gate_sum, up_sum, down_sum, sums, outputs, input_grads, gain_sums = end(
        dq, dk, dv, normed_a, tokens, residual_grad, qkv_weight, gain_a, feed_gain_term,
        mix_term, result, *halves,
    )
    gain_grads = lax.dynamic_slice_in_dim(gain_sums, y * (width // 2), width // 2, 1)
    k_width = key_weight.shape[1]
    sums = sums.reshape(width // 2, -1).astype(jnp.float32)
    ends = (0, q_width, q_width + k_width, q_width + 2 * k_width, sums.shape[1])
    parts = [sums[:, a:b] for a, b in zip(ends[:-1], ends[1:])]
    return (
        outputs,
        input_grads,
        gain_grads[0],
        *parts,
        gain_grads[1],
        gate_sum.reshape(width // 2, -1).astype(jnp.float32),
        up_sum.reshape(width // 2, -1).astype(jnp.float32),
        down_sum.reshape(-1, width).astype(jnp.float32),
    )


def solution(mesh):
    placed = (
        P("group", "fsdp", None),
        P("group", None),
        P("group", "fsdp", None),
        P("fsdp"),
        P("fsdp", None),
        P("fsdp", None),
        P("fsdp", None),
        P("fsdp", None),
        P("fsdp"),
        P("fsdp", None),
        P("fsdp", None),
        P("fsdp", None),
    )
    group_size, fsdp_size = mesh.shape["group"], mesh.shape["fsdp"]

    def local(*arrays):
        if group_size == 16 and fsdp_size == 2 and arrays[0].shape[0] == 2:
            return paired_local(*arrays)
        return plain_local(*arrays)

    return jax.shard_map(
        local,
        mesh=mesh,
        in_specs=placed,
        out_specs=(
            P("group", "fsdp", None),
            P("group", "fsdp", None),
            P("fsdp"),
            P("fsdp", None),
            P("fsdp", None),
            P("fsdp", None),
            P("fsdp", None),
            P("fsdp"),
            P("fsdp", None),
            P("fsdp", None),
            P("fsdp", None),
        ),
        check_vma=False,
    )
```

```python
import functools
import math

import jax
import jax.numpy as jnp
from jax import lax
from jax.experimental import pallas as pl
from jax.experimental.pallas import tpu as pltpu
from jax.sharding import PartitionSpec as P

HEADS = 18
KV_HEADS = 6
HEAD = 64
epsilon = 1e-05
rope_base = 10000.0
BLOCK = 256
WIDE = 128
VMEM_MOST = 66 * 1024 * 1024 - 3 * 1024 * 1024


def mm(left, right):
    return jnp.dot(left, right, preferred_element_type=jnp.float32)


def mm_nt(left, right):
    return lax.dot_general(
        left, right, (((1,), (1,)), ((), ())), preferred_element_type=jnp.float32
    )


def mm_tn(left, right):
    return lax.dot_general(
        left, right, (((0,), (0,)), ((), ())), preferred_element_type=jnp.float32
    )


def low(values):
    return values.astype(jnp.bfloat16)


def lanes_below(rows, period, limit):
    lane = lax.broadcasted_iota(jnp.int32, (rows, WIDE), 1)
    return lane % period < limit


def swap_halves(tile):
    ahead = pltpu.roll(tile, WIDE - HEAD // 2, 1)
    behind = pltpu.roll(tile, HEAD // 2, 1)
    return jnp.where(lanes_below(tile.shape[0], HEAD, HEAD // 2), ahead, behind)


def rope_tables(length):
    half_width = HEAD // 2
    freqs = jnp.exp(
        jnp.arange(half_width, dtype=jnp.float32) * (-2.0 * math.log(rope_base) / HEAD)
    )
    angles = jnp.arange(length, dtype=jnp.float32)[:, None] * freqs[None, :]
    cosines, sines = jnp.cos(angles), jnp.sin(angles)
    return (
        jnp.concatenate([cosines] * 4, axis=1),
        jnp.concatenate([-sines, sines] * 2, axis=1),
    )


def project_body(x_ref, gain_ref, w_ref, cos_ref, sin_ref, mix_w, gate_w,
                 normed_ref, qkv_ref, mix_full, gate_full, sems):
    step = pl.program_id(0)
    spreads = (
        Spread(mix_w, mix_full, SPREADS["mix"], sems, 0),
        Spread(gate_w, gate_full, SPREADS["gate"], sems, 1),
    )

    @pl.when(step == 0)
    def _():
        greet(("y",))
        for spread in spreads:
            spread.copy(0).start()

    values = x_ref[...].astype(jnp.float32)
    inverse = lax.rsqrt(jnp.mean(values * values, axis=-1, keepdims=True) + epsilon)
    normed = low(values * inverse * gain_ref[...])
    normed_ref[...] = normed
    cosines, sines = cos_ref[...], sin_ref[...]
    width = qkv_ref.shape[1]
    q_width, k_width = HEADS * HEAD, KV_HEADS * HEAD
    chunk = 384
    for at in range(0, width, chunk):
        wide = mm(normed, w_ref[:, at : at + chunk])
        for part in range(0, chunk, WIDE):
            tile = wide[:, part : part + WIDE]
            if at + part < q_width + k_width:
                tile = tile * cosines + swap_halves(tile) * sines
            if at + part < q_width:
                tile = tile * HEAD ** (-0.5)
            qkv_ref[:, at + part : at + part + WIDE] = low(tile)

    @pl.when(step == pl.num_programs(0) - 1)
    def _():
        for spread in spreads:
            spread.copy(0).wait()


def eighths(w):
    return w.reshape(8, w.shape[0] // 8, w.shape[1])


def project(x, gain, w, cosines, sines, mix_w, gate_w):
    length, width = x.shape
    out = w.shape[1]
    rows = pl.BlockSpec((BLOCK, width), lambda i: (i, 0))
    table = pl.BlockSpec((BLOCK, WIDE), lambda i: (i, 0))
    anywhere = pl.BlockSpec(memory_space=pl.ANY)
    return pl.pallas_call(
        project_body,
        grid=(length // BLOCK,),
        in_specs=[
            rows,
            pl.BlockSpec((1, width), lambda i: (0, 0)),
            pl.BlockSpec((width, out), lambda i: (0, 0), pipeline_mode=pl.Buffered(1)),
            table,
            table,
            anywhere,
            anywhere,
        ],
        out_specs=[rows, pl.BlockSpec((BLOCK, out), lambda i: (i, 0)), anywhere, anywhere],
        out_shape=[
            jax.ShapeDtypeStruct((length, width), jnp.bfloat16),
            jax.ShapeDtypeStruct((length, out), jnp.bfloat16),
        ]
        + [jax.ShapeDtypeStruct((16,) + eighths(w).shape[1:], w.dtype) for w in (mix_w, gate_w)],
        scratch_shapes=[pltpu.SemaphoreType.DMA((2, 2))],
        compiler_params=pltpu.CompilerParams(collective_id=6, has_side_effects=True),
        cost_estimate=pl.CostEstimate(
            flops=2 * length * width * out,
            bytes_accessed=2 * (2 * length * width + length * out + width * out),
            transcendentals=0,
        ),
        name="project",
    )(x, gain, w, cosines, sines, eighths(mix_w), eighths(gate_w))


MESH = pl.DeviceIdType.MESH
MASKS = {"core": 1, "x": 2, "zlo": 4, "zhi": 8}


def bit_of(name):
    if name == "y":
        return lax.axis_index("fsdp")
    return (lax.axis_index("group") // MASKS[name]) % 2


def peer_of(name):
    if name == "y":
        return {"fsdp": 1 - lax.axis_index("fsdp")}
    return {"group": lax.axis_index("group") + MASKS[name] * (1 - 2 * bit_of(name))}


def greet(names):
    barrier = pltpu.get_barrier_semaphore()
    for name in names:
        pl.semaphore_signal(barrier, inc=1, device_id=peer_of(name), device_id_type=MESH)
    pl.semaphore_wait(barrier, len(names))


def across(source, target, sems, slot, name):
    return pltpu.make_async_remote_copy(
        src_ref=source,
        dst_ref=target,
        send_sem=sems.at[0, slot],
        recv_sem=sems.at[1, slot],
        device_id=peer_of(name),
        device_id_type=MESH,
    )


class Spread:
    def __init__(self, shard, full, order, sems, slot, columns=None):
        self.shard, self.full, self.order, self.sems, self.slot = shard, full, order, sems, slot
        self.columns = columns

    def copy(self, stage):
        y = lax.axis_index("fsdp")
        index = 0
        for at, name in enumerate(self.order):
            index = index + bit_of(name) * 2**at
        slot = self.slot + stage
        where = (slice(None), slice(None)) if self.columns is None else (slice(None), self.columns)
        if stage == 0:
            return across(
                self.shard.at[index], self.full.at[(y * 8 + index,) + where], self.sems, slot, "y"
            )
        count = 2 ** (stage - 1)
        block = self.full.at[(pl.ds((1 - y) * 8 + index // count * count, count),) + where]
        return across(block, block, self.sems, slot, self.order[stage - 1])

    def advance(self, stage):
        if stage >= 0:
            self.copy(stage).wait_recv()
        if stage < len(self.order):
            self.copy(stage + 1).start()

    def finish(self, first=0):
        for stage in range(first, len(self.order) + 1):
            self.copy(stage).wait_send()


SPREADS = {
    "mix": ("x", "zlo", "core"),
    "gate": ("zlo", "x", "core"),
    "up": ("x", "zlo", "core"),
    "down": ("zlo", "x", "core"),
}


def fetch_body(inputs, query, key, value, gains, tokens, weight, both_gains,
               held, held_weight, sems, near):
    y = lax.axis_index("fsdp")
    q_width, k_width = query.shape[2], key.shape[2]
    places = (
        slice(0, q_width),
        slice(q_width, q_width + k_width),
        slice(q_width + k_width, q_width + 2 * k_width),
    )
    shards = (query, key, value)
    loads = [pltpu.make_async_copy(inputs.at[y], held, near.at[0])] + [
        pltpu.make_async_copy(shard, held_weight.at[:, :, place], near.at[1 + at])
        for at, (shard, place) in enumerate(zip(shards, places))
    ]
    for load in loads:
        load.start()
    greet(("y", "x", "zlo", "core"))
    index = bit_of("x") + 2 * bit_of("zlo") + 4 * bit_of("core")
    first = [
        across(shard.at[index], weight.at[y * 8 + index, :, place], sems, at, "y")
        for at, (shard, place) in enumerate(zip(shards, places))
    ]
    span = held.shape[0]
    swap = across(
        inputs.at[1 - y], tokens.at[pl.ds(pl.multiple_of(y * span, span), span)], sems, 3, "y"
    )
    gain_swap = across(gains, both_gains.at[y], sems, 4, "y")
    for copy in first + [gain_swap, swap]:
        copy.start()
    for load in loads:
        load.wait()
    stores = [
        pltpu.make_async_copy(
            held, tokens.at[pl.ds(pl.multiple_of(y * span, span), span)], near.at[4]
        ),
        pltpu.make_async_copy(held_weight, weight.at[pl.ds(y * 8, 8)], near.at[5]),
        pltpu.make_async_copy(gains, both_gains.at[y], near.at[6]),
    ]
    for store in stores:
        store.start()
    for copy in first:
        copy.wait_recv()
    later = []
    for at, name in enumerate(("x", "zlo", "core")):
        count = 2**at
        block = weight.at[pl.ds((1 - y) * 8 + index // count * count, count)]
        copy = across(block, block, sems, 5 + at, name)
        copy.start()
        copy.wait_recv()
        later.append(copy)
    swap.wait_recv()
    gain_swap.wait_recv()
    for copy in first + [gain_swap, swap] + later:
        copy.wait_send()
    for store in stores:
        store.wait()


def fetch(inputs, query, key, value, gains):
    span, width = inputs.shape[1:]
    total = query.shape[1] + 2 * key.shape[1]
    eight = lambda shard: shard.reshape(8, shard.shape[0] // 8, shard.shape[1])
    rows = query.shape[0] // 8
    anywhere = pl.BlockSpec(memory_space=pl.ANY)
    tokens, weight, both_gains = pl.pallas_call(
        fetch_body,
        in_specs=[anywhere] * 5,
        out_specs=[anywhere] * 3,
        out_shape=[
            jax.ShapeDtypeStruct((2 * span, width), inputs.dtype),
            jax.ShapeDtypeStruct((16, rows, total), query.dtype),
            jax.ShapeDtypeStruct((2,) + gains.shape, gains.dtype),
        ],
        scratch_shapes=[
            pltpu.VMEM((span, width), inputs.dtype),
            pltpu.VMEM((8, rows, total), query.dtype),
            pltpu.SemaphoreType.DMA((2, 8)),
            pltpu.SemaphoreType.DMA((7,)),
        ],
        compiler_params=pltpu.CompilerParams(collective_id=1, has_side_effects=True),
        name="fetch",
    )(inputs, eight(query), eight(key), eight(value), gains)
    return tokens, weight.reshape(16 * rows, total), both_gains


AXES = ("y", "x", "zlo", "zhi")


class Fold:
    def __init__(self, source, kept, received, order, sems, slot, near, near_slot):
        self.source, self.kept, self.received = source, kept, received
        self.order, self.sems, self.slot = order, sems, slot
        self.near, self.near_slot = near, near_slot

    def pick(self, stage, bit):
        left = [name for name in AXES if name not in self.order[:stage]]
        return (slice(None),) * left.index(self.order[stage]) + (bit,)

    def held(self, stage):
        return self.source if stage == 0 else self.received[stage - 1]

    def copy(self, stage):
        name = self.order[stage]
        source = self.held(stage).at[self.pick(stage, 1 - bit_of(name))]
        return across(source, self.received[stage], self.sems, self.slot + stage, name)

    def load(self):
        source = self.source.at[self.pick(0, bit_of(self.order[0]))]
        return pltpu.make_async_copy(source, self.kept, self.near.at[self.near_slot])

    def begin(self):
        self.copy(0).start()
        if self.kept is not None:
            self.load().start()

    def advance(self, stage):
        self.copy(stage).wait_recv()
        target = self.received[stage]
        lead = target.ndim - 2
        if stage == 0 and self.kept is not None:
            self.load().wait()
            mine, at, bit = self.kept, 0, None
        else:
            bit = bit_of(self.order[stage])
            mine, at = self.held(stage), len(self.pick(stage, 0)) - 1

        @pl.loop(0, 2**lead)
        def _(n):
            index = tuple(n // 2 ** (lead - 1 - k) % 2 for k in range(lead))
            from_ = index if bit is None else index[:at] + (bit,) + index[at:]
            total = target[index].astype(jnp.float32) + mine[from_].astype(jnp.float32)
            target[index] = low(total)

        if stage + 1 < len(self.order):
            self.copy(stage + 1).start()

    def finish(self):
        for stage in range(len(self.order)):
            self.copy(stage).wait_send()


class Rise:
    def __init__(self, whole, order, columns, sems, slot):
        self.whole, self.order, self.columns, self.sems, self.slot = whole, order, columns, sems, slot

    def block(self, stage):
        index = tuple(
            slice(None) if name in self.order[:stage] + ("zhi",) else bit_of(name)
            for name in AXES[1:]
        )
        if self.whole.ndim == 7:
            return [self.whole.at[(bit_of("core"), self.columns) + index]]
        return [self.whole.at[index + (slice(None), columns)] for columns in self.columns]

    def copies(self, stage, first=None):
        blocks = self.block(stage)
        count = len(blocks)
        return [
            across(
                block if first is None else first[at],
                block,
                self.sems,
                self.slot + stage * count + at,
                self.order[stage],
            )
            for at, block in enumerate(blocks)
        ]

    def begin(self, first):
        for copy in self.copies(0, first):
            copy.start()

    def advance(self, stage):
        for copy in self.copies(stage):
            copy.wait_recv()
        if stage + 1 < len(self.order):
            for copy in self.copies(stage + 1):
                copy.start()

    def finish(self):
        for stage in range(len(self.order)):
            for copy in self.copies(stage):
                copy.wait_send()


ORDERS = (("y", "x", "zlo"), ("x", "zlo", "y"), ("zlo", "y", "x"))
BACKS = (("zlo", "x", "core"), ("x", "zlo", "core"), ("zlo", "x", "core"))
LATE_ORDERS = (("y", "x", "zlo"), ("x", "y", "zlo"), ("y", "x", "zlo"))
PART_ORDERS = (("x", "y", "zlo"), ("y", "x", "zlo"), ("x", "y", "zlo"))
PART_BACKS = (("zlo", "x", "core"), ("x", "zlo", "core"), ("zlo", "x", "core"))


class Sums:
    def __init__(self, wholes, held, chunk, sems, slot, near, near_slot):
        gate, up, down = wholes
        self.held, self.near, self.near_slot = held, near, near_slot
        self.part = gate.shape[-1] // 8
        columns = hidden_columns(self.part, chunk)
        self.rises = [
            Rise(gate, BACKS[0], columns, sems, slot),
            Rise(up, BACKS[1], columns, sems, slot + 6),
            Rise(down, BACKS[2], chunk, sems, slot + 12),
        ]

    def pieces(self, f):
        if f == 2:
            return [self.held[f]]
        part = self.part
        return [self.held[f].at[:, :, side * part : (side + 1) * part] for side in range(2)]

    def stores(self, f):
        return [
            pltpu.make_async_copy(piece, block, self.near.at[self.near_slot + 2 * f + n])
            for n, (piece, block) in enumerate(zip(self.pieces(f), self.rises[f].block(0)))
        ]

    def begin(self, f):
        for store in self.stores(f):
            store.start()
        self.rises[f].begin(self.pieces(f))

    def follow(self, f):
        for store in self.stores(f):
            store.wait()
        self.rises[f].advance(0)


def hidden_columns(part, chunk):
    at = (2 * bit_of("core") + chunk) * part
    return [pl.ds(pl.multiple_of(side * 4 * part + at, WIDE), part) for side in range(2)]


def place_heads(tile, variants_ref):
    wide = tile.astype(jnp.float32)
    turned = pltpu.roll(wide, HEAD, 1)
    low_lanes = lanes_below(tile.shape[0], WIDE, HEAD)
    variants_ref[0] = low(jnp.where(low_lanes, wide, 0.0))
    variants_ref[1] = low(jnp.where(low_lanes, 0.0, turned))
    variants_ref[2] = low(jnp.where(low_lanes, turned, 0.0))
    variants_ref[3] = low(jnp.where(low_lanes, 0.0, wide))


def allowed_block(seg_k, seg_q, diagonal):
    same = seg_k == seg_q
    if diagonal:
        rows = lax.broadcasted_iota(jnp.int32, same.shape, 0)
        lanes = lax.broadcasted_iota(jnp.int32, same.shape, 1)
        same = same & (rows <= lanes)
    return same


def attend_body(
    q_ref, k_ref, v_ref, seg_col_ref, seg_row_ref, out_grad, mix_w, gate_w, up_w, down_w,
    mix_begun, gate_begun, mixed_ref, lse_ref, whole_grad, mix_full, gate_full, up_full, down_full,
    ks, vt, acc, stats, sems, near, held_mix, held_gate, held_up, held_down, held_grad
):
    block = pl.program_id(1)
    now = pl.program_id(0) * pl.num_programs(1) + block
    most = pl.num_programs(0) * pl.num_programs(1) - 1
    y = lax.axis_index("fsdp")
    spreads = {
        "mix": Spread(mix_w, mix_full, SPREADS["mix"], sems, 0),
        "gate": Spread(gate_w, gate_full, SPREADS["gate"], sems, 4),
        "up": Spread(up_w, up_full, SPREADS["up"], sems, 8),
        "down": Spread(down_w, down_full, SPREADS["down"], sems, 12),
    }
    span = out_grad.shape[1]
    mine = whole_grad.at[pl.ds(pl.multiple_of(y * span, span), span)]
    grad_swap = across(out_grad.at[1 - y], mine, sems, 16, "y")
    half = pl.ds(y * 8, 8)
    own = (
        (mix_w, held_mix, mix_full.at[half]),
        (gate_w, held_gate, gate_full.at[half]),
        (up_w, held_up, up_full.at[half]),
        (down_w, held_down, down_full.at[half]),
        (out_grad.at[y], held_grad, mine),
    )
    loads = [pltpu.make_async_copy(a, b, near.at[0, at]) for at, (a, b, _) in enumerate(own)]
    stores = [pltpu.make_async_copy(b, c, near.at[1, at]) for at, (_, b, c) in enumerate(own)]
    plan = {
        3: (("mix", 1),),
        4: (("up", 0), ("gate", 1)),
        7: (("down", 0), ("up", 1), ("mix", 2)),
        11: (("down", 1),),
    }

    @pl.when(now == 0)
    def _():
        for load in loads:
            load.start()
        greet(("y", "x", "zlo", "core"))
        spreads["up"].advance(-1)
        spreads["down"].advance(-1)
        grad_swap.start()
        spreads["gate"].copy(1).start()
        spreads["mix"].copy(1).start()

    @pl.when(now == 1)
    def _():
        for load, store in zip(loads, stores):
            load.wait()
            store.start()

    for at, steps in plan.items():

        @pl.when(now == at)
        def _(steps=steps):
            for name, stage in steps:
                spreads[name].advance(stage)

    @pl.when(block == 0)
    def _():
        place_heads(k_ref[...], ks)
        vt[...] = low(v_ref[...].astype(jnp.float32).T)

    acc[...] = jnp.zeros_like(acc)
    stats[0] = jnp.full((8, BLOCK), -1e30, jnp.float32)
    stats[1] = jnp.zeros((8, BLOCK), jnp.float32)
    seg_q = seg_row_ref[...]

    def step(j, diagonal):
        rows = pl.ds(pl.multiple_of(j * BLOCK, BLOCK), BLOCK)
        seg_k = seg_col_ref[rows, :]
        allowed = allowed_block(seg_k, seg_q, diagonal)
        scores = []
        for head in range(6):
            part, side, kv = head // 2, head % 2, head // 3
            q_tile = q_ref[:, part * WIDE : (part + 1) * WIDE]
            scores.append(jnp.where(allowed, mm_nt(ks[kv * 2 + side, rows, :], q_tile), -1e30))
        before = stats[0]
        highest = [
            jnp.maximum(before[head : head + 1], jnp.max(scores[head], axis=0, keepdims=True))
            for head in range(6)
        ]
        chances = [jnp.exp(scores[head] - highest[head]) for head in range(6)]
        shrink = [jnp.exp(before[head : head + 1] - highest[head]) for head in range(6)]
        for head in range(6):
            kv = head // 3
            stats[0, head : head + 1, :] = highest[head]
            stats[1, head : head + 1, :] = stats[1, head : head + 1, :] * shrink[head] + jnp.sum(
                chances[head], axis=0, keepdims=True
            )
            values = vt[kv * HEAD : (kv + 1) * HEAD, rows]
            at = head * HEAD
            acc[at : at + HEAD, :] = acc[at : at + HEAD, :] * shrink[head] + mm(
                values, low(chances[head])
            )

    @pl.loop(0, block)
    def _(j):
        step(j, False)

    step(block, True)
    total = stats[1]
    for part in range(3):
        at = part * WIDE
        both = jnp.concatenate(
            [
                acc[at : at + HEAD, :] / total[2 * part : 2 * part + 1, :],
                acc[at + HEAD : at + WIDE, :] / total[2 * part + 1 : 2 * part + 2, :],
            ],
            axis=0,
        )
        mixed_ref[:, at : at + WIDE] = low(both.T)
    lse_ref[0] = stats[0] + jnp.log(jnp.maximum(total, 1e-30))

    @pl.when(now == most)
    def _():
        spreads["gate"].advance(2)
        spreads["up"].advance(2)
        spreads["down"].advance(2)
        for name, spread in spreads.items():
            spread.advance(3)
            spread.finish(1 if name in ("mix", "gate") else 0)
        grad_swap.wait()
        for store in stores:
            store.wait()


def attend(qkv, seg_col, seg_row, out_grad, mix_w, gate_w, up_w, down_w, mix_begun, gate_begun):
    length = qkv.shape[0]
    pairs = KV_HEADS // 2
    q_tiles = HEADS * HEAD // WIDE
    anywhere = pl.BlockSpec(memory_space=pl.ANY)
    shards = [eighths(w) for w in (mix_w, gate_w, up_w, down_w)]
    fulls = [jax.ShapeDtypeStruct((16,) + w.shape[1:], w.dtype) for w in shards]
    found = pl.pallas_call(
        attend_body,
        grid=(pairs, length // BLOCK),
        in_specs=[
            pl.BlockSpec((BLOCK, 3 * WIDE), lambda b, i: (i, b)),
            pl.BlockSpec((length, WIDE), lambda b, i: (0, q_tiles + b)),
            pl.BlockSpec((length, WIDE), lambda b, i: (0, q_tiles + pairs + b)),
            pl.BlockSpec((length, 1), lambda b, i: (0, 0)),
            pl.BlockSpec((1, BLOCK), lambda b, i: (0, i)),
        ]
        + [anywhere] * 7,
        out_specs=[
            pl.BlockSpec((BLOCK, 3 * WIDE), lambda b, i: (i, b)),
            pl.BlockSpec((1, 8, BLOCK), lambda b, i: (b, 0, i)),
        ]
        + [anywhere] * 5,
        out_shape=[
            jax.ShapeDtypeStruct((length, HEADS * HEAD), jnp.bfloat16),
            jax.ShapeDtypeStruct((pairs, 8, length), jnp.float32),
            jax.ShapeDtypeStruct((length, out_grad.shape[2]), out_grad.dtype),
        ]
        + fulls,
        input_output_aliases={10: 3, 11: 4},
        scratch_shapes=[
            pltpu.VMEM((4, length, WIDE), jnp.bfloat16),
            pltpu.VMEM((WIDE, length), jnp.bfloat16),
            pltpu.VMEM((6 * HEAD, BLOCK), jnp.float32),
            pltpu.VMEM((2, 8, BLOCK), jnp.float32),
            pltpu.SemaphoreType.DMA((2, 17)),
            pltpu.SemaphoreType.DMA((2, 5)),
        ]
        + [pltpu.VMEM(w.shape, w.dtype) for w in shards]
        + [pltpu.VMEM(out_grad.shape[1:], out_grad.dtype)],
        compiler_params=pltpu.CompilerParams(
            collective_id=2, has_side_effects=True, vmem_limit_bytes=VMEM_MOST
        ),
        cost_estimate=pl.CostEstimate(
            flops=16 * length * length * HEADS * HEAD // 2,
            bytes_accessed=6 * length * HEADS * HEAD,
            transcendentals=HEADS * length * length // 2,
        ),
        name="attend",
    )(qkv, qkv, qkv, seg_col, seg_row, out_grad, *shards, mix_begun, gate_begun)
    return tuple(found[:3]) + tuple(w.reshape(-1, w.shape[2]) for w in found[3:])


def attend_back_body(
    q_ref, k_ref, v_ref, grad_ref, mixed_ref, lse_ref, seg_col_ref, seg_row_ref, cos_ref, sin_ref,
    gate_term, up_term, down_term, gate_third, up_third, down_third,
    dq_ref, dk_ref, dv_ref, gate_left, up_left, down_left, gate_sum, up_sum, down_sum,
    ks, vs, kt, k_acc, v_acc, q_acc, sides, delta, sems, near,
    kept_h, r1_h, r2_h, r3_h, own_h, came_h, kept_d, r1_d, r2_d, r3_d, own_d, came_d
):
    block = pl.program_id(1)
    length = k_ref.shape[0]
    now = pl.program_id(0) * pl.num_programs(1) + block
    most = pl.num_programs(0) * pl.num_programs(1) - 1
    pick = lambda pair, single: [pair.at[0], pair.at[1], single]
    kept, owns, came = pick(kept_h, kept_d), pick(own_h, own_d), pick(came_h, came_d)
    ones, twos, threes = pick(r1_h, r1_d), pick(r2_h, r2_d), pick(r3_h, r3_d)
    folds = [
        Fold(term, kept[f], [ones[f], twos[f], threes[f]], LATE_ORDERS[f], sems, 3 * f, near, f)
        for f, term in enumerate((gate_term, up_term, down_term))
    ]
    loads = [
        pltpu.make_async_copy(third, owns[f], near.at[3 + f])
        for f, third in enumerate((gate_third, up_third, down_third))
    ]
    zs = [across(owns[f], came[f], sems, 9 + f, "zhi") for f in range(3)]
    stores = [
        pltpu.make_async_copy(threes[f], left, near.at[6 + f])
        for f, left in enumerate((gate_left, up_left, down_left))
    ]
    sums = Sums((gate_sum, up_sum, down_sum), came, 0, sems, 12, near, 9)

    def settle(f):
        zs[f].wait_recv()
        for n in range(2):
            came[f][n] = low(owns[f][n].astype(jnp.float32) + came[f][n].astype(jnp.float32))
        sums.begin(f)

    @pl.when(now == 0)
    def _():
        for load in loads:
            load.start()
        greet(("core",) + AXES)
        for fold in folds:
            fold.begin()
        for load, copy in zip(loads, zs):
            load.wait()
            copy.start()

    @pl.when(now == 5)
    def _():
        folds[0].advance(0)
        folds[1].advance(0)

    @pl.when(now == 7)
    def _():
        settle(0)
        settle(1)

    @pl.when(now == 8)
    def _():
        settle(2)
        folds[0].advance(1)

    @pl.when(now == 10)
    def _():
        folds[2].advance(0)
        sums.follow(0)
        sums.follow(1)

    @pl.when(now == 11)
    def _():
        sums.follow(2)

    @pl.when(block == 0)
    def _():
        place_heads(k_ref[...], ks)
        place_heads(v_ref[...], vs)
        kt[...] = low(k_ref[...].astype(jnp.float32).T)
        k_acc[...] = jnp.zeros_like(k_acc)
        v_acc[...] = jnp.zeros_like(v_acc)

    q_acc[...] = jnp.zeros_like(q_acc)
    seg_q = seg_row_ref[...]
    low_lanes = lanes_below(BLOCK, WIDE, HEAD)
    zero = jnp.zeros((BLOCK, WIDE), jnp.bfloat16)
    for part in range(3):
        at = part * WIDE
        tile, grad = q_ref[:, at : at + WIDE], grad_ref[:, at : at + WIDE]
        sides[0, part, 0:BLOCK, :] = jnp.where(low_lanes, tile, zero)
        sides[0, part, BLOCK : 2 * BLOCK, :] = jnp.where(low_lanes, zero, tile)
        sides[1, part, 0:BLOCK, :] = jnp.where(low_lanes, grad, zero)
        sides[1, part, BLOCK : 2 * BLOCK, :] = jnp.where(low_lanes, zero, grad)
        product = (grad.astype(jnp.float32) * mixed_ref[:, at : at + WIDE].astype(jnp.float32)).T
        delta[2 * part : 2 * part + 1, :] = jnp.sum(product[:HEAD], axis=0, keepdims=True)
        delta[2 * part + 1 : 2 * part + 2, :] = jnp.sum(product[HEAD:], axis=0, keepdims=True)

    def step(j, diagonal):
        rows = pl.ds(pl.multiple_of(j * BLOCK, BLOCK), BLOCK)
        allowed = allowed_block(seg_col_ref[rows, :], seg_q, diagonal)
        heads = range(6)
        tiles = [q_ref[:, p * WIDE : (p + 1) * WIDE] for p in range(3)]
        grads = [grad_ref[:, p * WIDE : (p + 1) * WIDE] for p in range(3)]
        scores = [mm_nt(ks[h // 3 * 2 + h % 2, rows, :], tiles[h // 2]) for h in heads]
        onto = [mm_nt(vs[h // 3 * 2 + h % 2, rows, :], grads[h // 2]) for h in heads]
        chances = [
            jnp.exp(jnp.where(allowed, scores[h], -1e30) - lse_ref[0, h : h + 1, :]) for h in heads
        ]
        score_grads = [low(chances[h] * (onto[h] - delta[h : h + 1, :])) for h in heads]
        chances = [low(chances[h]) for h in heads]
        for h in heads:
            to = h * HEAD
            q_acc[to : to + HEAD, :] += mm(kt[h // 3 * HEAD : (h // 3 + 1) * HEAD, rows], score_grads[h])
        for p in range(3):
            v_acc[p, rows, :] += mm(jnp.concatenate(chances[2 * p : 2 * p + 2], axis=1), sides[1, p])
            k_acc[p, rows, :] += mm(jnp.concatenate(score_grads[2 * p : 2 * p + 2], axis=1), sides[0, p])

    @pl.loop(0, block)
    def _(j):
        step(j, False)

    step(block, True)
    here = pl.ds(pl.multiple_of(block * BLOCK, BLOCK), BLOCK)
    for part in range(3):
        at = part * WIDE
        tile = q_acc[at : at + WIDE, :].T * HEAD ** (-0.5)
        tile = tile * cos_ref[here, :] - swap_halves(tile) * sin_ref[here, :]
        dq_ref[:, at : at + WIDE] = low(tile)

    @pl.when(block == length // BLOCK - 1)
    def _():
        for j in range(0, length, BLOCK):
            rows = slice(j, j + BLOCK)

            def gather(acc):
                first, middle, last = acc[0, rows, :], acc[1, rows, :], acc[2, rows, :]
                return middle + jnp.where(
                    low_lanes, first + pltpu.roll(first, HEAD, 1), last + pltpu.roll(last, HEAD, 1)
                )

            tile = gather(k_acc)
            tile = tile * cos_ref[rows, :] - swap_halves(tile) * sin_ref[rows, :]
            dk_ref[rows, :] = low(tile)
            dv_ref[rows, :] = low(gather(v_acc))

    @pl.when(now == most)
    def _():
        folds[1].advance(1)
        folds[2].advance(1)
        folds[0].advance(2)
        for f in range(3):
            sums.rises[f].advance(1)
        folds[1].advance(2)
        folds[2].advance(2)
        for store in stores:
            store.start()
        for f in range(3):
            sums.rises[f].advance(2)
        for fold in folds + sums.rises:
            fold.finish()
        for copy in zs:
            copy.wait_send()
        for store in stores:
            store.wait()


def attend_back(qkv, mixed_grad, mixed, lse, seg_col, seg_row, cosines, sines, *terms):
    length = qkv.shape[0]
    rows, wide = terms[0].shape[4:]
    down_rows, width = terms[2].shape[4:]
    anywhere = pl.BlockSpec(memory_space=pl.ANY)
    pairs = KV_HEADS // 2
    q_tiles = HEADS * HEAD // WIDE
    q_block = pl.BlockSpec((BLOCK, 3 * WIDE), lambda b, i: (i, b))
    kv_block = pl.BlockSpec((length, WIDE), lambda b, i: (0, b))
    table = pl.BlockSpec((length, WIDE), lambda b, i: (0, 0), pipeline_mode=pl.Buffered(1))
    return pl.pallas_call(
        attend_back_body,
        grid=(pairs, length // BLOCK),
        in_specs=[
            q_block,
            pl.BlockSpec((length, WIDE), lambda b, i: (0, q_tiles + b)),
            pl.BlockSpec((length, WIDE), lambda b, i: (0, q_tiles + pairs + b)),
            q_block,
            q_block,
            pl.BlockSpec((1, 8, BLOCK), lambda b, i: (b, 0, i)),
            pl.BlockSpec((length, 1), lambda b, i: (0, 0)),
            pl.BlockSpec((1, BLOCK), lambda b, i: (0, i)),
            table,
            table,
        ]
        + [anywhere] * 6,
        out_specs=[q_block, kv_block, kv_block] + [anywhere] * 6,
        out_shape=[
            jax.ShapeDtypeStruct((length, HEADS * HEAD), jnp.bfloat16),
            jax.ShapeDtypeStruct((length, KV_HEADS * HEAD), jnp.bfloat16),
            jax.ShapeDtypeStruct((length, KV_HEADS * HEAD), jnp.bfloat16),
        ]
        + [
            jax.ShapeDtypeStruct((2,) + shape, jnp.bfloat16)
            for shape in ((rows, wide), (rows, wide), (down_rows, width))
        ]
        + [
            jax.ShapeDtypeStruct((2, 2, 2, rows, 4 * wide), jnp.bfloat16),
            jax.ShapeDtypeStruct((2, 2, 2, rows, 4 * wide), jnp.bfloat16),
            jax.ShapeDtypeStruct((2, 2, 2, 2, 2, down_rows, width), jnp.bfloat16),
        ],
        scratch_shapes=[
            pltpu.VMEM((4, length, WIDE), jnp.bfloat16),
            pltpu.VMEM((4, length, WIDE), jnp.bfloat16),
            pltpu.VMEM((WIDE, length), jnp.bfloat16),
            pltpu.VMEM((3, length, WIDE), jnp.float32),
            pltpu.VMEM((3, length, WIDE), jnp.float32),
            pltpu.VMEM((6 * HEAD, BLOCK), jnp.float32),
            pltpu.VMEM((2, 3, 2 * BLOCK, WIDE), jnp.bfloat16),
            pltpu.VMEM((8, BLOCK), jnp.float32),
            pltpu.SemaphoreType.DMA((2, 27)),
            pltpu.SemaphoreType.DMA((14,)),
        ]
        + [pltpu.VMEM((2,) + (2,) * left + (rows, wide), jnp.bfloat16) for left in (3, 3, 2, 1, 1, 1)]
        + [pltpu.VMEM((2,) * left + (down_rows, width), jnp.bfloat16) for left in (3, 3, 2, 1, 1, 1)],
        compiler_params=pltpu.CompilerParams(
            collective_id=3, has_side_effects=True, vmem_limit_bytes=VMEM_MOST
        ),
        cost_estimate=pl.CostEstimate(
            flops=40 * length * length * HEADS * HEAD // 2,
            bytes_accessed=12 * length * HEADS * HEAD,
            transcendentals=HEADS * length * length // 2,
        ),
        name="attend_back",
    )(qkv, qkv, qkv, mixed_grad, mixed, lse, seg_col, seg_row, cosines, sines, *terms)


def mix_body(x_ref, mixed_ref, w_ref, gain_ref, residual_ref, normed_ref, turned_ref):
    residual = x_ref[...].astype(jnp.float32) + mm(mixed_ref[...], w_ref[...])
    residual_ref[...] = residual
    inverse = lax.rsqrt(jnp.mean(residual * residual, axis=-1, keepdims=True) + epsilon)
    normed = residual * inverse * gain_ref[...]
    normed_ref[...] = low(normed)
    turned_ref[...] = low(normed.T)


def mix(x, mixed, w, gain):
    length, width = x.shape
    rows = pl.BlockSpec((BLOCK, width), lambda i: (i, 0))
    return pl.pallas_call(
        mix_body,
        grid=(length // BLOCK,),
        in_specs=[
            rows,
            rows,
            pl.BlockSpec(w.shape, lambda i: (0, 0), pipeline_mode=pl.Buffered(1)),
            pl.BlockSpec((1, width), lambda i: (0, 0)),
        ],
        out_specs=[rows, rows, pl.BlockSpec((width, BLOCK), lambda i: (0, i))],
        out_shape=[
            jax.ShapeDtypeStruct((length, width), jnp.float32),
            jax.ShapeDtypeStruct((length, width), jnp.bfloat16),
            jax.ShapeDtypeStruct((width, length), jnp.bfloat16),
        ],
        cost_estimate=pl.CostEstimate(
            flops=2 * length * width * width, bytes_accessed=12 * length * width, transcendentals=0
        ),
        name="mix",
    )(x, mixed, w, gain)


def norm_grad(grad, gain, scaled, inverse):
    weighted = grad * gain
    return inverse * (weighted - scaled * jnp.mean(weighted * scaled, axis=-1, keepdims=True))


def turn_body(residual_ref, out_ref, back_ref, c_ref, mixed_ref, w_ref, gain_ref,
              result_ref, grad_ref, mixed_grad_ref, term_ref, gain_term_ref, total):
    step = pl.program_id(0)
    residual = residual_ref[...]
    result_ref[...] = low(residual + out_ref[...])
    inverse = lax.rsqrt(jnp.mean(residual * residual, axis=-1, keepdims=True) + epsilon)
    scaled = residual * inverse
    normed_grad = back_ref[...]
    gain_term = jnp.sum(normed_grad * scaled, axis=0, keepdims=True)
    grad = c_ref[...].astype(jnp.float32) + norm_grad(normed_grad, gain_ref[...], scaled, inverse)
    grad_ref[...] = grad
    grad_low = low(grad)
    mixed_grad_ref[...] = low(mm_nt(grad_low, w_ref[...]))
    term = mm_tn(mixed_ref[...], grad_low)

    @pl.when(step == 0)
    def _():
        total[...] = term
        gain_term_ref[...] = jnp.broadcast_to(gain_term, gain_term_ref.shape)

    @pl.when(step > 0)
    def _():
        total[...] += term
        gain_term_ref[...] += jnp.broadcast_to(gain_term, gain_term_ref.shape)

    @pl.when(step == pl.num_programs(0) - 1)
    def _():
        term_ref[...] = low(total[...])


def turn(residual, out, back, c, mixed, w, gain):
    length, width = residual.shape
    rows = pl.BlockSpec((BLOCK, width), lambda i: (i, 0))
    whole = lambda shape: pl.BlockSpec(shape, lambda i: (0, 0), pipeline_mode=pl.Buffered(1))
    return pl.pallas_call(
        turn_body,
        grid=(length // BLOCK,),
        in_specs=[rows] * 5 + [whole(w.shape), pl.BlockSpec((1, width), lambda i: (0, 0))],
        out_specs=[
            rows, rows, rows, whole((width, width)), pl.BlockSpec((8, width), lambda i: (0, 0)),
        ],
        out_shape=[
            jax.ShapeDtypeStruct((length, width), jnp.bfloat16),
            jax.ShapeDtypeStruct((length, width), jnp.float32),
            jax.ShapeDtypeStruct((length, width), jnp.bfloat16),
            jax.ShapeDtypeStruct((width, width), jnp.bfloat16),
            jax.ShapeDtypeStruct((8, width), jnp.float32),
        ],
        scratch_shapes=[pltpu.VMEM((width, width), jnp.float32)],
        compiler_params=pltpu.CompilerParams(vmem_limit_bytes=VMEM_MOST),
        cost_estimate=pl.CostEstimate(
            flops=4 * length * width * width, bytes_accessed=32 * length * width, transcendentals=0
        ),
        name="turn",
    )(residual, out, back, c, mixed, w, gain)


def end_body(dq_ref, dk_ref, dv_ref, normed_ref, x_ref, grad_ref, w_ref, gain_ref, feed_gain_ref,
             mix_term, result, gate_left, up_left, down_left, gate_begun, up_begun, down_begun,
             gate, up, down, sums, outputs, input_grads, gain_sums,
             turned, term, tokens, r0, r1, r2, r3, exchanged, hidden_b, hidden_came,
             down_b, down_came, gain_held, gain_came, rows_held, sems, near):
    step = pl.program_id(0)
    last = pl.num_programs(0) - 1
    rows_each = x_ref.shape[0]
    length = normed_ref.shape[0]
    q_width, k_width = dq_ref.shape[1], dk_ref.shape[1]
    core, y = bit_of("core"), lax.axis_index("fsdp")
    third = term.shape[-1] // 3
    wide = third // 2
    everything = (slice(None),) * 4 + (slice(None),)
    columns = [
        [pl.ds(pl.multiple_of(t * third + side * wide, WIDE), wide) for side in (core, 1 - core)]
        for t in range(3)
    ]
    span = outputs.shape[1]
    rows = [pl.ds(pl.multiple_of(at * span, span), span) for at in (y, 1 - y)]
    pick = lambda pair, single: [pair.at[0], pair.at[1], single]
    b_left, came = pick(hidden_b, down_b), pick(hidden_came, down_came)
    loads = [
        pltpu.make_async_copy(whole, held, near.at[f])
        for f, (whole, held) in enumerate(zip((gate_left, up_left, down_left), b_left))
    ]
    mix_load = pltpu.make_async_copy(
        mix_term, term.at[everything + (slice(q_width + 2 * k_width, term.shape[-1]),)], near.at[6]
    )
    result_load = pltpu.make_async_copy(result.at[rows[0]], rows_held, near.at[7])
    result_store = pltpu.make_async_copy(rows_held, outputs.at[y], near.at[8])
    token_store = pltpu.make_async_copy(tokens.at[rows[0]], input_grads.at[y], near.at[9])
    zs = [across(b_left[f], came[f], sems, f, "zhi") for f in range(3)]
    hidden = Sums((gate, up, down), came, 1, sems, 60, near, 10)
    cores = [
        across(term.at[everything + (columns[t][1],)], r0.at[t], sems, 27 + t, "core")
        for t in range(3)
    ]
    parts = [
        Fold(r0.at[t], None, [r1.at[t], r2.at[t], r3.at[t]], PART_ORDERS[t], sems, 30 + 3 * t, None, None)
        for t in range(3)
    ]
    part_zs = [across(r3.at[t], exchanged.at[t], sems, 39 + t, "zhi") for t in range(3)]
    tops = [Rise(sums, PART_BACKS[t], [columns[t][0]], sems, 42 + 3 * t) for t in range(3)]
    swaps = [
        across(result.at[rows[1]], outputs.at[y], sems, 51, "y"),
        across(tokens.at[rows[1]], input_grads.at[y], sems, 52, "y"),
    ]
    names = ("core",) + AXES
    gain_copies = [
        across(gain_held.at[at], gain_came.at[at], sems, 53 + at, name)
        for at, name in enumerate(names)
    ]

    def part_store(t):
        return pltpu.make_async_copy(exchanged.at[t], tops[t].block(0)[0], near.at[20 + t])

    def settle(copy, mine, theirs):
        copy.wait_recv()
        for n in range(2):
            theirs[n] = low(mine[n].astype(jnp.float32) + theirs[n].astype(jnp.float32))

    def hidden_settle(f):
        settle(zs[f], b_left[f], came[f])
        hidden.begin(f)

    def part_settle(t):
        settle(part_zs[t], r3.at[t], exchanged.at[t])
        part_store(t).start()
        tops[t].begin([exchanged.at[t]])

    def core_sum(t):
        cores[t].wait_recv()

        @pl.loop(0, 16)
        def _(n):
            index = (n // 8, n // 4 % 2, n // 2 % 2, n % 2)
            mine = term[index + (slice(None), columns[t][0])]
            r0[(t,) + index] = low(r0[(t,) + index].astype(jnp.float32) + mine.astype(jnp.float32))

        parts[t].begin()

    def gain_step(at):
        gain_copies[at].wait_recv()
        gain_held[at + 1] = gain_held[at] + gain_came[at]
        if at + 1 < len(names):
            gain_copies[at + 1].start()

    @pl.when(step == 0)
    def _():
        for load in loads + [mix_load, result_load]:
            load.start()
        greet(names)
        swaps[0].start()
        for f in range(3):
            loads[f].wait()
            zs[f].start()
        mix_load.wait()
        cores[2].start()
        for at in range(0, length, BLOCK):
            turned[:, at : at + BLOCK] = normed_ref[at : at + BLOCK, :].T

    @pl.when(step == 1)
    def _():
        core_sum(2)
        result_load.wait()
        result_store.start()

    @pl.when(step == 3)
    def _():
        cores[0].start()

    @pl.when(step == 4)
    def _():
        core_sum(0)

    @pl.when(step == 5)
    def _():
        cores[1].start()
        hidden_settle(0)

    @pl.when(step == 6)
    def _():
        core_sum(1)
        parts[2].advance(0)

    @pl.when(step == 7)
    def _():
        hidden_settle(1)

    @pl.when(step == 8)
    def _():
        hidden.follow(0)
        parts[0].advance(0)

    def chunk(low_rows, at):
        wide_term = mm(turned[...], low_rows).reshape(16, turned.shape[0] // 16, k_width)
        for n in range(16):
            index = (n // 8, n // 4 % 2, n // 2 % 2, n % 2, slice(None), slice(at, at + k_width))
            term[index] = low(wide_term[n])

    for at in range(3):

        @pl.when(step == at)
        def _(at=at):
            chunk(dq_ref[:, at * k_width : (at + 1) * k_width], at * k_width)

    @pl.when(step == 3)
    def _():
        chunk(dk_ref[...], q_width)

    @pl.when(step == 4)
    def _():
        chunk(dv_ref[...], q_width + k_width)

    first = last + 1 - length // rows_each

    @pl.when(step >= first)
    def _():
        here = pl.ds(pl.multiple_of((step - first) * rows_each, rows_each), rows_each)
        normed_grad = (
            mm_nt(dq_ref[here, :], w_ref[:, :q_width])
            + mm_nt(dk_ref[here, :], w_ref[:, q_width : q_width + k_width])
            + mm_nt(dv_ref[here, :], w_ref[:, q_width + k_width :])
        )
        values = x_ref[...].astype(jnp.float32)
        inverse = lax.rsqrt(jnp.mean(values * values, axis=-1, keepdims=True) + epsilon)
        scaled = values * inverse
        gain_term = jnp.sum(normed_grad * scaled, axis=0, keepdims=True)
        tokens[here, :] = low(
            grad_ref[...] + norm_grad(normed_grad, gain_ref[...], scaled, inverse)
        )

        @pl.when(step == first)
        def _():
            gain_held[0, 0:1, :] = gain_term
            gain_held[0, 1:2, :] = feed_gain_ref[0:1, :]
            gain_held[0, 2:8, :] = jnp.zeros_like(gain_held[0, 2:8, :])

        @pl.when(step > first)
        def _():
            gain_held[0, 0:1, :] += gain_term

    @pl.when(step == last)
    def _():
        gain_copies[0].start()
        token_store.start()
        swaps[1].start()
        hidden_settle(2)
        hidden.follow(1)
        gain_step(0)
        parts[1].advance(0)
        hidden.follow(2)
        gain_step(1)
        parts[2].advance(1)
        parts[1].advance(1)
        gain_step(2)
        parts[0].advance(1)
        hidden.rises[0].advance(1)
        for t in (2, 1, 0):
            parts[t].advance(2)
            part_zs[t].start()
        gain_step(3)
        hidden.rises[1].advance(1)
        hidden.rises[2].advance(1)
        for t in (2, 1, 0):
            part_settle(t)
        gain_step(4)
        for t in (2, 1, 0):
            part_store(t).wait()
            tops[t].advance(0)
        for t in (2, 1, 0):
            tops[t].advance(1)
        every = hidden.rises + tops
        for one in every:
            one.advance(2)
        for copy in cores + swaps + gain_copies + zs + part_zs:
            copy.wait_send()
        for one in every + parts:
            one.finish()
        for copy in swaps:
            copy.wait_recv()
        result_store.wait()
        token_store.wait()
        gain_sums[...] = gain_held[len(names)]


def end(dq, dk, dv, normed, x, grad, w, gain, feed_gain_term, mix_term, result, *sums):
    length, width = x.shape
    k_width = dk.shape[1]
    total = w.shape[1] + mix_term.shape[1]
    wide = total // 6
    mix_term = mix_term.reshape(2, 2, 2, 2, mix_term.shape[0] // 16, mix_term.shape[1])
    rows = mix_term.shape[4]
    hidden_rows, hidden = sums[0].shape[1:]
    down_rows = sums[2].shape[1]
    chunks, blocks = w.shape[1] // k_width, length // BLOCK
    block = pl.BlockSpec((BLOCK, width), lambda i: (jnp.maximum(i - chunks, 0), 0))
    whole = lambda a: pl.BlockSpec(a.shape, lambda i: (0,) * a.ndim, pipeline_mode=pl.Buffered(1))
    anywhere = pl.BlockSpec(memory_space=pl.ANY)
    both = jax.ShapeDtypeStruct((2, length // 2, width), result.dtype)
    low_type = jnp.bfloat16
    return pl.pallas_call(
        end_body,
        grid=(chunks + blocks,),
        in_specs=[whole(dq), whole(dk), whole(dv), whole(normed), block, block, whole(w), whole(gain),
                  whole(feed_gain_term)] + [anywhere] * 8,
        out_specs=[anywhere] * 6 + [pl.BlockSpec((8, width), lambda i: (0, 0))],
        out_shape=[
            jax.ShapeDtypeStruct((2, 2, 2, hidden_rows, 4 * hidden), low_type),
            jax.ShapeDtypeStruct((2, 2, 2, hidden_rows, 4 * hidden), low_type),
            jax.ShapeDtypeStruct((2, 2, 2, 2, 2, down_rows, width), low_type),
            jax.ShapeDtypeStruct((2, 2, 2, rows, total), low_type),
            both,
            both,
            jax.ShapeDtypeStruct((8, width), jnp.float32),
        ],
        input_output_aliases={14: 0, 15: 1, 16: 2},
        scratch_shapes=[
            pltpu.VMEM((width, length), low_type),
            pltpu.VMEM((2, 2, 2, 2, rows, total), low_type),
            pltpu.VMEM((length, width), low_type),
        ]
        + [pltpu.VMEM((3,) + (2,) * left + (rows, wide), low_type) for left in (4, 3, 2, 1, 1)]
        + [pltpu.VMEM((2, 2, hidden_rows, hidden), low_type)] * 2
        + [pltpu.VMEM((2, down_rows, width), low_type)] * 2
        + [
            pltpu.VMEM((6, 8, width), jnp.float32),
            pltpu.VMEM((5, 8, width), jnp.float32),
            pltpu.VMEM((length // 2, width), low_type),
            pltpu.SemaphoreType.DMA((2, 75)),
            pltpu.SemaphoreType.DMA((23,)),
        ],
        compiler_params=pltpu.CompilerParams(
            collective_id=4, has_side_effects=True, vmem_limit_bytes=VMEM_MOST
        ),
        name="end",
    )(dq, dk, dv, normed, x, grad, w, gain, feed_gain_term, mix_term, result, *sums)


def sixteenth(n):
    return (n // 8, n // 4 % 2, n // 2 % 2, n % 2)


def feed_body(normed_ref, turned_ref, c_ref, gate_w, up_w, down_w,
              out_ref, back_ref, gate_a, up_a, down_a, gate_b, up_b, down_b,
              gate_v, up_v, down_v, hidden_t, gate_low, up_low,
              hold_h, hold_d, came_h, came_d, own_h, own_d,
              r1_h, r2_h, r3_h, r1_d, r2_d, r3_d, sems, near, weight_sems, free):
    step = pl.program_id(0)
    length, width = normed_ref.shape
    core = bit_of("core")
    slot = step % 2
    part = gate_v.shape[2] // 2
    side_width = gate_w.shape[1] // 2

    def weights(of, into):
        owner = (core + 1 + of) % 2
        at = (2 * owner + of // 2) * part
        found = []
        for side in range(2):
            here = pl.ds(pl.multiple_of(side * side_width + at, WIDE), part)
            there = slice(side * part, (side + 1) * part)
            found += [
                (gate_w.at[:, here], gate_v.at[into, :, there]),
                (up_w.at[:, here], up_v.at[into, :, there]),
                (down_w.at[here], down_v.at[into, there]),
            ]
        return [
            pltpu.make_async_copy(a, b, weight_sems.at[into, n]) for n, (a, b) in enumerate(found)
        ]

    holds = (hold_h.at[0], hold_h.at[1], hold_d)
    arrived = (came_h.at[0], came_h.at[1], came_d)
    owns = (own_h.at[0], own_h.at[1], own_d)
    cores = [across(holds[f], arrived[f], sems, f, "core") for f in range(3)]
    received = (
        [r1_h.at[0], r2_h.at[0], r3_h.at[0]],
        [r1_h.at[1], r2_h.at[1], r3_h.at[1]],
        [r1_d, r2_d, r3_d],
    )
    folds = [
        Fold(owns[f], None, received[f], ORDERS[f], sems, 3 + 3 * f, None, None) for f in range(3)
    ]
    stores_a = [
        pltpu.make_async_copy(received[f][2], half, near.at[f])
        for f, half in enumerate((gate_a, up_a, down_a))
    ]
    stores_b = [
        pltpu.make_async_copy(owns[f], whole, near.at[3 + f])
        for f, whole in enumerate((gate_b, up_b, down_b))
    ]

    @pl.when(step == 0)
    def _():
        for load in weights(step, slot):
            load.start()
        out_ref[...] = jnp.zeros_like(out_ref)
        back_ref[...] = jnp.zeros_like(back_ref)
        greet(("core",) + AXES[:3])

    for load in weights(step, slot):
        load.wait()

    @pl.when(step < 3)
    def _():
        for load in weights(step + 1, 1 - slot):
            load.start()

    gate, up, down = gate_v.at[slot], up_v.at[slot], down_v.at[slot]
    for at in range(0, length, BLOCK):
        rows = slice(at, at + BLOCK)
        normed = normed_ref[rows, :]
        gate_sum = mm(normed, gate[...])
        up_sum = mm(normed, up[...])
        hidden_grad = mm_nt(c_ref[rows, :], down[...])
        sigmoid = jax.nn.sigmoid(gate_sum)
        activated = gate_sum * sigmoid
        hidden = low(activated * up_sum)
        gate_grad = low(hidden_grad * up_sum * (sigmoid + activated * (1.0 - sigmoid)))
        up_grad = low(hidden_grad * activated)
        hidden_t[:, rows] = hidden.T
        gate_low[rows, :] = gate_grad
        up_low[rows, :] = up_grad
        out_ref[rows, :] += mm(hidden, down[...])
        back_ref[rows, :] += mm_nt(gate_grad, gate[...]) + mm_nt(up_grad, up[...])

    theirs = slot == 0

    @pl.when(step == 3)
    def _():
        for fold in folds:
            fold.copy(0).wait_send()
            fold.advance(1)

    @pl.when(jnp.logical_not(theirs))
    def _():
        for copy in cores:
            copy.wait_recv()

    def put(blocks, hold, came, own):
        @pl.when(theirs)
        def _():
            for index, block in blocks:
                hold[index] = low(block)

        @pl.when(jnp.logical_not(theirs))
        def _():
            for index, block in blocks:
                own[index] = low(block + came[index].astype(jnp.float32))

    quarter = width // 4
    for n in range(4):
        rows = slice(n * quarter, (n + 1) * quarter)
        for f, grads in enumerate((gate_low, up_low)):
            value = mm(turned_ref[rows, :], grads[...]).reshape(4, quarter // 4, 2 * part)
            put(
                [((f,) + sixteenth(4 * n + k), value[k]) for k in range(4)], hold_h, came_h, own_h
            )
    third = width // 3
    for n in range(3):
        columns = slice(n * third, (n + 1) * third)
        value = mm(hidden_t[...], c_ref[:, columns]).reshape(16, part // 8, third)
        put(
            [(sixteenth(k) + (slice(None), columns), value[k]) for k in range(16)],
            hold_d, came_d, own_d,
        )

    @pl.when(step == 2)
    def _():
        pl.semaphore_wait(free, 1)

    @pl.when(theirs)
    def _():
        for copy in cores:
            copy.start()

    @pl.when(step == 2)
    def _():
        for fold in folds:
            fold.advance(0)

    @pl.when(jnp.logical_not(theirs))
    def _():
        for copy in cores:
            copy.wait_send()

    @pl.when(step == 1)
    def _():
        pl.semaphore_signal(free, inc=1, device_id=peer_of("core"), device_id_type=MESH)
        for fold in folds:
            fold.begin()

    @pl.when(step == 3)
    def _():
        for store in stores_b:
            store.start()
        for fold in folds:
            fold.advance(2)
        for store in stores_a:
            store.start()
        for fold in folds:
            for stage in (1, 2):
                fold.copy(stage).wait_send()
        for store in stores_a + stores_b:
            store.wait()


def feed(normed, turned, c, gate, up, down):
    length, width = normed.shape
    part = gate.shape[1] // 8
    rows, down_rows = width // 16, part // 8
    whole = lambda a: pl.BlockSpec(a.shape, lambda t: (0, 0), pipeline_mode=pl.Buffered(1))
    total = pl.BlockSpec((length, width), lambda t: (0, 0), pipeline_mode=pl.Buffered(1))
    anywhere = pl.BlockSpec(memory_space=pl.ANY)
    low_type = jnp.bfloat16
    hidden = lambda left: (2,) * left + (rows, 2 * part)
    down_shape = lambda left: (2,) * left + (down_rows, width)
    return pl.pallas_call(
        feed_body,
        grid=(4,),
        in_specs=[whole(normed), whole(turned), whole(c)] + [anywhere] * 3,
        out_specs=[total, total] + [anywhere] * 6,
        out_shape=[
            jax.ShapeDtypeStruct((length, width), jnp.float32),
            jax.ShapeDtypeStruct((length, width), jnp.float32),
        ]
        + [
            jax.ShapeDtypeStruct(shape, low_type)
            for left in (1, 4)
            for shape in (hidden(left), hidden(left), down_shape(left))
        ],
        scratch_shapes=[
            pltpu.VMEM((2, width, 2 * part), low_type),
            pltpu.VMEM((2, width, 2 * part), low_type),
            pltpu.VMEM((2, 2 * part, width), low_type),
            pltpu.VMEM((2 * part, length), low_type),
            pltpu.VMEM((length, 2 * part), low_type),
            pltpu.VMEM((length, 2 * part), low_type),
        ]
        + [pltpu.VMEM(shape, low_type) for _ in range(3) for shape in ((2,) + hidden(4), down_shape(4))]
        + [pltpu.VMEM((2,) + hidden(left), low_type) for left in (3, 2, 1)]
        + [pltpu.VMEM(down_shape(left), low_type) for left in (3, 2, 1)]
        + [
            pltpu.SemaphoreType.DMA((2, 12)),
            pltpu.SemaphoreType.DMA((6,)),
            pltpu.SemaphoreType.DMA((2, 6)),
            pltpu.SemaphoreType.REGULAR,
        ],
        compiler_params=pltpu.CompilerParams(
            collective_id=5, has_side_effects=True, vmem_limit_bytes=VMEM_MOST
        ),
        cost_estimate=pl.CostEstimate(
            flops=18 * length * width * gate.shape[1],
            bytes_accessed=12 * width * gate.shape[1] + 16 * length * width,
            transcendentals=length * gate.shape[1],
        ),
        name="feed",
    )(normed, turned, c, gate, up, down)


def shortened(array):
    return jax.tree.map(lambda a: a.astype(jnp.bfloat16) if a.dtype == jnp.float32 else a, array)


def product(left, right):
    return jnp.dot(left, right, preferred_element_type=jnp.float32)


def product_tn(left, right):
    return lax.dot_general(
        left, right, (((0,), (0,)), ((), ())), preferred_element_type=jnp.float32
    )


def product_nt(left, right):
    return lax.dot_general(
        left, right, (((1,), (1,)), ((), ())), preferred_element_type=jnp.float32
    )


def rotary_tables(positions, width):
    half_width = width // 2
    freqs = jnp.exp(
        jnp.arange(half_width, dtype=jnp.float32) * (-2.0 * math.log(rope_base) / width)
    )
    angles = positions[:, None] * freqs[None, :]
    return (jnp.cos(angles), jnp.sin(angles))


def rotate(values, cosines, sines):
    half_width = values.shape[-1] // 2
    first = values[..., :half_width]
    second = values[..., half_width:]
    return jnp.concatenate(
        [first * cosines - second * sines, second * cosines + first * sines], axis=-1
    )


def unrotate(values, cosines, sines):
    half_width = values.shape[-1] // 2
    first = values[..., :half_width]
    second = values[..., half_width:]
    return jnp.concatenate(
        [first * cosines + second * sines, second * cosines - first * sines], axis=-1
    )


def norm_back(grad_rows, gain, scaled, inverse):
    weighted = grad_rows * gain
    return inverse * (weighted - scaled * jnp.mean(weighted * scaled, axis=-1, keepdims=True))


def plain_local(
    inputs,
    segments,
    out_grad,
    attention_gain,
    query_weight,
    key_weight,
    value_weight,
    output_weight,
    feedforward_gain,
    gate_weight,
    up_weight,
    down_weight,
):
    gathered = (
        lax.all_gather(attention_gain, "fsdp", axis=0, tiled=True),
        lax.all_gather(query_weight, "fsdp", axis=0, tiled=True),
        lax.all_gather(key_weight, "fsdp", axis=0, tiled=True),
        lax.all_gather(value_weight, "fsdp", axis=0, tiled=True),
        lax.all_gather(output_weight, "fsdp", axis=0, tiled=True),
        lax.all_gather(feedforward_gain, "fsdp", axis=0, tiled=True),
        lax.all_gather(gate_weight, "fsdp", axis=0, tiled=True),
        lax.all_gather(up_weight, "fsdp", axis=0, tiled=True),
        lax.all_gather(down_weight, "fsdp", axis=0, tiled=True),
    )
    full_query, full_key, full_value, full_output = (
        gathered[1],
        gathered[2],
        gathered[3],
        gathered[4],
    )
    full_gate, full_up, full_down = (gathered[6], gathered[7], gathered[8])
    gain_attention = gathered[0].astype(jnp.float32)
    gain_feed = gathered[5].astype(jnp.float32)
    span = inputs.shape[1]
    length = segments.shape[1]
    groups_q = HEADS // KV_HEADS
    key_width = KV_HEADS * HEAD
    start = lax.axis_index("fsdp") * span
    query_pos = start + jnp.arange(span, dtype=jnp.int32)
    key_pos = jnp.arange(length, dtype=jnp.int32)
    cosines, sines = rotary_tables(query_pos.astype(jnp.float32), HEAD)
    cos_four, sin_four = (cosines[:, None, None, :], sines[:, None, None, :])
    cos_three, sin_three = (cosines[:, None, :], sines[:, None, :])
    causal = query_pos[:, None] >= key_pos[None, :]
    scale = HEAD ** (-0.5)

    def micro_step(totals, sequence):
        tokens, segment_row, cotangent = sequence
        own_segment = lax.dynamic_slice_in_dim(segment_row, start, span)
        allowed = causal & (own_segment[:, None] == segment_row[None, :])
        values = tokens.astype(jnp.float32)
        inverse_a = lax.rsqrt(jnp.mean(values * values, axis=-1, keepdims=True) + epsilon)
        scaled_a = values * inverse_a
        normed_a = (scaled_a * gain_attention).astype(jnp.bfloat16)
        query_lin = product(normed_a, full_query).reshape(span, KV_HEADS, groups_q, HEAD)
        queries = rotate(query_lin, cos_four, sin_four).astype(jnp.bfloat16)
        key_lin = product(normed_a, full_key).reshape(span, KV_HEADS, HEAD)
        key_rows = (
            rotate(key_lin, cos_three, sin_three).astype(jnp.bfloat16).reshape(span, key_width)
        )
        value_rows = product(normed_a, full_value).astype(jnp.bfloat16)
        all_keys, all_values = (
            lax.all_gather(key_rows, "fsdp", axis=0, tiled=True),
            lax.all_gather(value_rows, "fsdp", axis=0, tiled=True),
        )
        all_keys = all_keys.reshape(length, KV_HEADS, HEAD)
        all_values = all_values.reshape(length, KV_HEADS, HEAD)
        scores = (
            jnp.einsum("qhgd,khd->hgqk", queries, all_keys, preferred_element_type=jnp.float32)
            * scale
        )
        scores = jnp.where(allowed, scores, -1e30)
        highest = jnp.max(scores, axis=-1, keepdims=True)
        expo_scores = jnp.exp(scores - highest)
        attention = expo_scores / jnp.sum(expo_scores, axis=-1, keepdims=True)
        attention_low = attention.astype(jnp.bfloat16)
        mixed = jnp.einsum(
            "hgqk,khd->qhgd", attention_low, all_values, preferred_element_type=jnp.float32
        )
        mixed = mixed.reshape(span, HEADS * HEAD).astype(jnp.bfloat16)
        residual = values + product(mixed, full_output)
        inverse_f = lax.rsqrt(jnp.mean(residual * residual, axis=-1, keepdims=True) + epsilon)
        scaled_f = residual * inverse_f
        normed_f = (scaled_f * gain_feed).astype(jnp.bfloat16)
        gate_sum = product(normed_f, full_gate)
        up_sum = product(normed_f, full_up)
        sigmoid_gate = jax.nn.sigmoid(gate_sum)
        activated = gate_sum * sigmoid_gate
        hidden = (activated * up_sum).astype(jnp.bfloat16)
        result = (residual + product(hidden, full_down)).astype(jnp.bfloat16)
        down_wgrad = product_tn(hidden, cotangent)
        hidden_grad = product_nt(cotangent, full_down)
        gate_grad = (
            hidden_grad * up_sum * sigmoid_gate * (1.0 + gate_sum * (1.0 - sigmoid_gate))
        ).astype(jnp.bfloat16)
        up_grad = (hidden_grad * activated).astype(jnp.bfloat16)
        gate_wgrad = product_tn(normed_f, gate_grad)
        up_wgrad = product_tn(normed_f, up_grad)
        normed_f_grad = product_nt(gate_grad, full_gate) + product_nt(up_grad, full_up)
        feed_gain_grad = jnp.sum(normed_f_grad * scaled_f, axis=0)
        residual_grad = cotangent.astype(jnp.float32) + norm_back(
            normed_f_grad, gain_feed, scaled_f, inverse_f
        )
        residual_low = residual_grad.astype(jnp.bfloat16)
        output_wgrad = product_tn(mixed, residual_low)
        mixed_grad = (
            product_nt(residual_low, full_output)
            .astype(jnp.bfloat16)
            .reshape(span, KV_HEADS, groups_q, HEAD)
        )
        attention_grad = jnp.einsum(
            "qhgd,khd->hgqk", mixed_grad, all_values, preferred_element_type=jnp.float32
        )
        row_totals = jnp.sum(attention * attention_grad, axis=-1, keepdims=True)
        score_grad = (attention * (attention_grad - row_totals) * scale).astype(jnp.bfloat16)
        value_grads = jnp.einsum(
            "hgqk,qhgd->khd", attention_low, mixed_grad, preferred_element_type=jnp.float32
        ).reshape(length, key_width)
        key_grads = jnp.einsum(
            "hgqk,qhgd->khd", score_grad, queries, preferred_element_type=jnp.float32
        ).reshape(length, key_width)
        query_grad = jnp.einsum(
            "hgqk,khd->qhgd", score_grad, all_keys, preferred_element_type=jnp.float32
        )
        key_back, value_back = (
            lax.psum_scatter(key_grads, "fsdp", scatter_dimension=0, tiled=True),
            lax.psum_scatter(value_grads, "fsdp", scatter_dimension=0, tiled=True),
        )
        query_low = (
            unrotate(query_grad, cos_four, sin_four)
            .reshape(span, HEADS * HEAD)
            .astype(jnp.bfloat16)
        )
        key_low = (
            unrotate(key_back.reshape(span, KV_HEADS, HEAD), cos_three, sin_three)
            .reshape(span, key_width)
            .astype(jnp.bfloat16)
        )
        value_low = value_back.astype(jnp.bfloat16)
        query_wgrad = product_tn(normed_a, query_low)
        key_wgrad = product_tn(normed_a, key_low)
        value_wgrad = product_tn(normed_a, value_low)
        normed_a_grad = (
            product_nt(query_low, full_query)
            + product_nt(key_low, full_key)
            + product_nt(value_low, full_value)
        )
        attention_gain_term = jnp.sum(normed_a_grad * scaled_a, axis=0)
        token_grad = (
            residual_grad + norm_back(normed_a_grad, gain_attention, scaled_a, inverse_a)
        ).astype(jnp.bfloat16)
        terms = (
            attention_gain_term,
            query_wgrad,
            key_wgrad,
            value_wgrad,
            output_wgrad,
            feed_gain_grad,
            gate_wgrad,
            up_wgrad,
            down_wgrad,
        )
        totals = tuple((left + right for left, right in zip(totals, terms)))
        return (totals, (result, token_grad))

    initial = tuple((jnp.zeros(weight.shape, jnp.float32) for weight in gathered))
    totals, (outputs, input_grads) = lax.scan(micro_step, initial, (inputs, segments, out_grad))
    shards = jax.tree.map(
        lambda part: part.astype(jnp.float32),
        lax.psum_scatter(shortened(totals), "fsdp", scatter_dimension=0, tiled=True),
    )
    summed = lax.psum(shards, "group")
    return (
        outputs,
        input_grads,
        summed[0],
        summed[1],
        summed[2],
        summed[3],
        summed[4],
        summed[5],
        summed[6],
        summed[7],
        summed[8],
    )


def paired_local(
    inputs,
    segments,
    out_grad,
    attention_gain,
    query_weight,
    key_weight,
    value_weight,
    output_weight,
    feedforward_gain,
    gate_weight,
    up_weight,
    down_weight,
):
    y = lax.axis_index("fsdp")
    span, length, width = inputs.shape[1], segments.shape[1], inputs.shape[2]
    q_width = query_weight.shape[1]

    gains = jnp.pad(
        jnp.stack([attention_gain, feedforward_gain]).astype(jnp.float32), ((0, 6), (0, 0))
    )
    tokens, qkv_weight, gains = fetch(inputs, query_weight, key_weight, value_weight, gains)
    gains = gains.transpose(1, 0, 2).reshape(8, width)
    gain_a, gain_f = gains[0:1], gains[1:2]

    segment = lax.dynamic_index_in_dim(segments, y, 0, False)
    seg_col, seg_row = segment[:, None], segment[None, :]
    cosines, sines = rope_tables(length)
    normed_a, qkv, mix_begun, gate_begun = project(
        tokens, gain_a, qkv_weight, cosines, sines, output_weight, gate_weight
    )
    mixed, lse, c, mix_weight, full_gate, full_up, full_down = attend(
        qkv, seg_col, seg_row, out_grad, output_weight, gate_weight, up_weight, down_weight,
        mix_begun, gate_begun,
    )

    residual, normed_f, turned_f = mix(tokens, mixed, mix_weight, gain_f)

    out, back, *chunks = feed(normed_f, turned_f, c, full_gate, full_up, full_down)
    result, residual_grad, mixed_grad, mix_term, feed_gain_term = turn(
        residual, out, back, c, mixed, mix_weight, gain_f
    )
    dq, dk, dv, *halves = attend_back(
        qkv, mixed_grad, mixed, lse, seg_col, seg_row, cosines, sines, *chunks[3:], *chunks[:3]
    )
    gate_sum, up_sum, down_sum, sums, outputs, input_grads, gain_sums = end(
        dq, dk, dv, normed_a, tokens, residual_grad, qkv_weight, gain_a, feed_gain_term,
        mix_term, result, *halves,
    )
    gain_grads = lax.dynamic_slice_in_dim(gain_sums, y * (width // 2), width // 2, 1)
    k_width = key_weight.shape[1]
    sums = sums.reshape(width // 2, -1).astype(jnp.float32)
    ends = (0, q_width, q_width + k_width, q_width + 2 * k_width, sums.shape[1])
    parts = [sums[:, a:b] for a, b in zip(ends[:-1], ends[1:])]
    return (
        outputs,
        input_grads,
        gain_grads[0],
        *parts,
        gain_grads[1],
        gate_sum.reshape(width // 2, -1).astype(jnp.float32),
        up_sum.reshape(width // 2, -1).astype(jnp.float32),
        down_sum.reshape(-1, width).astype(jnp.float32),
    )


def solution(mesh):
    placed = (
        P("group", "fsdp", None),
        P("group", None),
        P("group", "fsdp", None),
        P("fsdp"),
        P("fsdp", None),
        P("fsdp", None),
        P("fsdp", None),
        P("fsdp", None),
        P("fsdp"),
        P("fsdp", None),
        P("fsdp", None),
        P("fsdp", None),
    )
    group_size, fsdp_size = mesh.shape["group"], mesh.shape["fsdp"]

    def local(*arrays):
        if group_size == 16 and fsdp_size == 2 and arrays[0].shape[0] == 2:
            return paired_local(*arrays)
        return plain_local(*arrays)

    return jax.shard_map(
        local,
        mesh=mesh,
        in_specs=placed,
        out_specs=(
            P("group", "fsdp", None),
            P("group", "fsdp", None),
            P("fsdp"),
            P("fsdp", None),
            P("fsdp", None),
            P("fsdp", None),
            P("fsdp", None),
            P("fsdp"),
            P("fsdp", None),
            P("fsdp", None),
            P("fsdp", None),
        ),
        check_vma=False,
    )
```

```python
import functools
import math

import jax
import jax.numpy as jnp
from jax import lax
from jax.experimental import pallas as pl
from jax.experimental.pallas import tpu as pltpu
from jax.sharding import PartitionSpec as P

HEADS = 18
KV_HEADS = 6
HEAD = 64
epsilon = 1e-05
rope_base = 10000.0
BLOCK = 256
WIDE = 128
VMEM_MOST = 66 * 1024 * 1024 - 3 * 1024 * 1024


def mm(left, right):
    return jnp.dot(left, right, preferred_element_type=jnp.float32)


def mm_nt(left, right):
    return lax.dot_general(
        left, right, (((1,), (1,)), ((), ())), preferred_element_type=jnp.float32
    )


def mm_tn(left, right):
    return lax.dot_general(
        left, right, (((0,), (0,)), ((), ())), preferred_element_type=jnp.float32
    )


def low(values):
    return values.astype(jnp.bfloat16)


def lanes_below(rows, period, limit):
    lane = lax.broadcasted_iota(jnp.int32, (rows, WIDE), 1)
    return lane % period < limit


def swap_halves(tile):
    ahead = pltpu.roll(tile, WIDE - HEAD // 2, 1)
    behind = pltpu.roll(tile, HEAD // 2, 1)
    return jnp.where(lanes_below(tile.shape[0], HEAD, HEAD // 2), ahead, behind)


def rope_tables(length):
    half_width = HEAD // 2
    freqs = jnp.exp(
        jnp.arange(half_width, dtype=jnp.float32) * (-2.0 * math.log(rope_base) / HEAD)
    )
    angles = jnp.arange(length, dtype=jnp.float32)[:, None] * freqs[None, :]
    cosines, sines = jnp.cos(angles), jnp.sin(angles)
    return (
        jnp.concatenate([cosines] * 4, axis=1),
        jnp.concatenate([-sines, sines] * 2, axis=1),
    )


def project_body(x_ref, gain_ref, w_ref, cos_ref, sin_ref, mix_w, gate_w,
                 normed_ref, qkv_ref, mix_full, gate_full, sems):
    step = pl.program_id(0)
    spreads = (
        Spread(mix_w, mix_full, SPREADS["mix"], sems, 0),
        Spread(gate_w, gate_full, SPREADS["gate"], sems, 1),
    )

    @pl.when(step == 0)
    def _():
        greet(("y",))
        for spread in spreads:
            spread.copy(0).start()

    values = x_ref[...].astype(jnp.float32)
    inverse = lax.rsqrt(jnp.mean(values * values, axis=-1, keepdims=True) + epsilon)
    normed = low(values * inverse * gain_ref[...])
    normed_ref[...] = normed
    cosines, sines = cos_ref[...], sin_ref[...]
    width = qkv_ref.shape[1]
    q_width, k_width = HEADS * HEAD, KV_HEADS * HEAD
    chunk = 384
    for at in range(0, width, chunk):
        wide = mm(normed, w_ref[:, at : at + chunk])
        for part in range(0, chunk, WIDE):
            tile = wide[:, part : part + WIDE]
            if at + part < q_width + k_width:
                tile = tile * cosines + swap_halves(tile) * sines
            if at + part < q_width:
                tile = tile * HEAD ** (-0.5)
            qkv_ref[:, at + part : at + part + WIDE] = low(tile)

    @pl.when(step == pl.num_programs(0) - 1)
    def _():
        for spread in spreads:
            spread.copy(0).wait()


def eighths(w):
    return w.reshape(8, w.shape[0] // 8, w.shape[1])


def project(x, gain, w, cosines, sines, mix_w, gate_w):
    length, width = x.shape
    out = w.shape[1]
    rows = pl.BlockSpec((BLOCK, width), lambda i: (i, 0))
    table = pl.BlockSpec((BLOCK, WIDE), lambda i: (i, 0))
    anywhere = pl.BlockSpec(memory_space=pl.ANY)
    return pl.pallas_call(
        project_body,
        grid=(length // BLOCK,),
        in_specs=[
            rows,
            pl.BlockSpec((1, width), lambda i: (0, 0)),
            pl.BlockSpec((width, out), lambda i: (0, 0), pipeline_mode=pl.Buffered(1)),
            table,
            table,
            anywhere,
            anywhere,
        ],
        out_specs=[rows, pl.BlockSpec((BLOCK, out), lambda i: (i, 0)), anywhere, anywhere],
        out_shape=[
            jax.ShapeDtypeStruct((length, width), jnp.bfloat16),
            jax.ShapeDtypeStruct((length, out), jnp.bfloat16),
        ]
        + [jax.ShapeDtypeStruct((16,) + eighths(w).shape[1:], w.dtype) for w in (mix_w, gate_w)],
        scratch_shapes=[pltpu.SemaphoreType.DMA((2, 2))],
        compiler_params=pltpu.CompilerParams(collective_id=6, has_side_effects=True),
        cost_estimate=pl.CostEstimate(
            flops=2 * length * width * out,
            bytes_accessed=2 * (2 * length * width + length * out + width * out),
            transcendentals=0,
        ),
        name="project",
    )(x, gain, w, cosines, sines, eighths(mix_w), eighths(gate_w))


MESH = pl.DeviceIdType.MESH
MASKS = {"core": 1, "x": 2, "zlo": 4, "zhi": 8}


def bit_of(name):
    if name == "y":
        return lax.axis_index("fsdp")
    return (lax.axis_index("group") // MASKS[name]) % 2


def peer_of(name):
    if name == "y":
        return {"fsdp": 1 - lax.axis_index("fsdp")}
    return {"group": lax.axis_index("group") + MASKS[name] * (1 - 2 * bit_of(name))}


def greet(names):
    barrier = pltpu.get_barrier_semaphore()
    for name in names:
        pl.semaphore_signal(barrier, inc=1, device_id=peer_of(name), device_id_type=MESH)
    pl.semaphore_wait(barrier, len(names))


def across(source, target, sems, slot, name):
    return pltpu.make_async_remote_copy(
        src_ref=source,
        dst_ref=target,
        send_sem=sems.at[0, slot],
        recv_sem=sems.at[1, slot],
        device_id=peer_of(name),
        device_id_type=MESH,
    )


class Spread:
    def __init__(self, shard, full, order, sems, slot, columns=None):
        self.shard, self.full, self.order, self.sems, self.slot = shard, full, order, sems, slot
        self.columns = columns

    def copy(self, stage):
        y = lax.axis_index("fsdp")
        index = 0
        for at, name in enumerate(self.order):
            index = index + bit_of(name) * 2**at
        slot = self.slot + stage
        where = (slice(None), slice(None)) if self.columns is None else (slice(None), self.columns)
        if stage == 0:
            return across(
                self.shard.at[index], self.full.at[(y * 8 + index,) + where], self.sems, slot, "y"
            )
        count = 2 ** (stage - 1)
        block = self.full.at[(pl.ds((1 - y) * 8 + index // count * count, count),) + where]
        return across(block, block, self.sems, slot, self.order[stage - 1])

    def advance(self, stage):
        if stage >= 0:
            self.copy(stage).wait_recv()
        if stage < len(self.order):
            self.copy(stage + 1).start()

    def finish(self, first=0):
        for stage in range(first, len(self.order) + 1):
            self.copy(stage).wait_send()


SPREADS = {
    "mix": ("x", "zlo", "core"),
    "gate": ("zlo", "x", "core"),
    "up": ("x", "zlo", "core"),
    "down": ("zlo", "x", "core"),
}


def fetch_body(inputs, query, key, value, gains, tokens, weight, both_gains,
               held, held_weight, sems, near):
    y = lax.axis_index("fsdp")
    q_width, k_width = query.shape[2], key.shape[2]
    places = (
        slice(0, q_width),
        slice(q_width, q_width + k_width),
        slice(q_width + k_width, q_width + 2 * k_width),
    )
    shards = (query, key, value)
    loads = [pltpu.make_async_copy(inputs.at[y], held, near.at[0])] + [
        pltpu.make_async_copy(shard, held_weight.at[:, :, place], near.at[1 + at])
        for at, (shard, place) in enumerate(zip(shards, places))
    ]
    for load in loads:
        load.start()
    greet(("y", "x", "zlo", "core"))
    index = bit_of("x") + 2 * bit_of("zlo") + 4 * bit_of("core")
    first = [
        across(shard.at[index], weight.at[y * 8 + index, :, place], sems, at, "y")
        for at, (shard, place) in enumerate(zip(shards, places))
    ]
    span = held.shape[0]
    swap = across(
        inputs.at[1 - y], tokens.at[pl.ds(pl.multiple_of(y * span, span), span)], sems, 3, "y"
    )
    gain_swap = across(gains, both_gains.at[y], sems, 4, "y")
    for copy in first + [gain_swap, swap]:
        copy.start()
    for load in loads:
        load.wait()
    stores = [
        pltpu.make_async_copy(
            held, tokens.at[pl.ds(pl.multiple_of(y * span, span), span)], near.at[4]
        ),
        pltpu.make_async_copy(held_weight, weight.at[pl.ds(y * 8, 8)], near.at[5]),
        pltpu.make_async_copy(gains, both_gains.at[y], near.at[6]),
    ]
    for store in stores:
        store.start()
    for copy in first:
        copy.wait_recv()
    later = []
    for at, name in enumerate(("x", "zlo", "core")):
        count = 2**at
        block = weight.at[pl.ds((1 - y) * 8 + index // count * count, count)]
        copy = across(block, block, sems, 5 + at, name)
        copy.start()
        copy.wait_recv()
        later.append(copy)
    swap.wait_recv()
    gain_swap.wait_recv()
    for copy in first + [gain_swap, swap] + later:
        copy.wait_send()
    for store in stores:
        store.wait()


def fetch(inputs, query, key, value, gains):
    span, width = inputs.shape[1:]
    total = query.shape[1] + 2 * key.shape[1]
    eight = lambda shard: shard.reshape(8, shard.shape[0] // 8, shard.shape[1])
    rows = query.shape[0] // 8
    anywhere = pl.BlockSpec(memory_space=pl.ANY)
    tokens, weight, both_gains = pl.pallas_call(
        fetch_body,
        in_specs=[anywhere] * 5,
        out_specs=[anywhere] * 3,
        out_shape=[
            jax.ShapeDtypeStruct((2 * span, width), inputs.dtype),
            jax.ShapeDtypeStruct((16, rows, total), query.dtype),
            jax.ShapeDtypeStruct((2,) + gains.shape, gains.dtype),
        ],
        scratch_shapes=[
            pltpu.VMEM((span, width), inputs.dtype),
            pltpu.VMEM((8, rows, total), query.dtype),
            pltpu.SemaphoreType.DMA((2, 8)),
            pltpu.SemaphoreType.DMA((7,)),
        ],
        compiler_params=pltpu.CompilerParams(collective_id=1, has_side_effects=True),
        name="fetch",
    )(inputs, eight(query), eight(key), eight(value), gains)
    return tokens, weight.reshape(16 * rows, total), both_gains


AXES = ("y", "x", "zlo", "zhi")


class Fold:
    def __init__(self, source, kept, received, order, sems, slot, near, near_slot):
        self.source, self.kept, self.received = source, kept, received
        self.order, self.sems, self.slot = order, sems, slot
        self.near, self.near_slot = near, near_slot

    def pick(self, stage, bit):
        left = [name for name in AXES if name not in self.order[:stage]]
        return (slice(None),) * left.index(self.order[stage]) + (bit,)

    def held(self, stage):
        return self.source if stage == 0 else self.received[stage - 1]

    def copy(self, stage):
        name = self.order[stage]
        source = self.held(stage).at[self.pick(stage, 1 - bit_of(name))]
        return across(source, self.received[stage], self.sems, self.slot + stage, name)

    def load(self):
        source = self.source.at[self.pick(0, bit_of(self.order[0]))]
        return pltpu.make_async_copy(source, self.kept, self.near.at[self.near_slot])

    def begin(self):
        self.copy(0).start()
        if self.kept is not None:
            self.load().start()

    def advance(self, stage):
        self.copy(stage).wait_recv()
        target = self.received[stage]
        lead = target.ndim - 2
        if stage == 0 and self.kept is not None:
            self.load().wait()
            mine, at, bit = self.kept, 0, None
        else:
            bit = bit_of(self.order[stage])
            mine, at = self.held(stage), len(self.pick(stage, 0)) - 1

        @pl.loop(0, 2**lead)
        def _(n):
            index = tuple(n // 2 ** (lead - 1 - k) % 2 for k in range(lead))
            from_ = index if bit is None else index[:at] + (bit,) + index[at:]
            total = target[index].astype(jnp.float32) + mine[from_].astype(jnp.float32)
            target[index] = low(total)

        if stage + 1 < len(self.order):
            self.copy(stage + 1).start()

    def finish(self):
        for stage in range(len(self.order)):
            self.copy(stage).wait_send()


class Rise:
    def __init__(self, whole, order, columns, sems, slot):
        self.whole, self.order, self.columns, self.sems, self.slot = whole, order, columns, sems, slot

    def block(self, stage):
        index = tuple(
            slice(None) if name in self.order[:stage] + ("zhi",) else bit_of(name)
            for name in AXES[1:]
        )
        if self.whole.ndim == 7:
            return [self.whole.at[(bit_of("core"), self.columns) + index]]
        return [self.whole.at[index + (slice(None), columns)] for columns in self.columns]

    def copies(self, stage, first=None):
        blocks = self.block(stage)
        count = len(blocks)
        return [
            across(
                block if first is None else first[at],
                block,
                self.sems,
                self.slot + stage * count + at,
                self.order[stage],
            )
            for at, block in enumerate(blocks)
        ]

    def begin(self, first):
        for copy in self.copies(0, first):
            copy.start()

    def advance(self, stage):
        for copy in self.copies(stage):
            copy.wait_recv()
        if stage + 1 < len(self.order):
            for copy in self.copies(stage + 1):
                copy.start()

    def finish(self):
        for stage in range(len(self.order)):
            for copy in self.copies(stage):
                copy.wait_send()


ORDERS = (("y", "x", "zlo"), ("x", "zlo", "y"), ("zlo", "y", "x"))
BACKS = (("zlo", "x", "core"), ("x", "zlo", "core"), ("zlo", "x", "core"))
LATE_ORDERS = (("y", "x", "zlo"), ("x", "y", "zlo"), ("y", "x", "zlo"))
PART_ORDERS = (("x", "y", "zlo"), ("y", "x", "zlo"), ("x", "y", "zlo"))
PART_BACKS = (("zlo", "x", "core"), ("x", "zlo", "core"), ("zlo", "x", "core"))


class Sums:
    def __init__(self, wholes, held, chunk, sems, slot, near, near_slot):
        gate, up, down = wholes
        self.held, self.near, self.near_slot = held, near, near_slot
        self.part = gate.shape[-1] // 8
        columns = hidden_columns(self.part, chunk)
        self.rises = [
            Rise(gate, BACKS[0], columns, sems, slot),
            Rise(up, BACKS[1], columns, sems, slot + 6),
            Rise(down, BACKS[2], chunk, sems, slot + 12),
        ]

    def pieces(self, f):
        if f == 2:
            return [self.held[f]]
        part = self.part
        return [self.held[f].at[:, :, side * part : (side + 1) * part] for side in range(2)]

    def stores(self, f):
        return [
            pltpu.make_async_copy(piece, block, self.near.at[self.near_slot + 2 * f + n])
            for n, (piece, block) in enumerate(zip(self.pieces(f), self.rises[f].block(0)))
        ]

    def begin(self, f):
        for store in self.stores(f):
            store.start()
        self.rises[f].begin(self.pieces(f))

    def follow(self, f):
        for store in self.stores(f):
            store.wait()
        self.rises[f].advance(0)


def hidden_columns(part, chunk):
    at = (2 * bit_of("core") + chunk) * part
    return [pl.ds(pl.multiple_of(side * 4 * part + at, WIDE), part) for side in range(2)]


def place_heads(tile, variants_ref):
    wide = tile.astype(jnp.float32)
    turned = pltpu.roll(wide, HEAD, 1)
    low_lanes = lanes_below(tile.shape[0], WIDE, HEAD)
    variants_ref[0] = low(jnp.where(low_lanes, wide, 0.0))
    variants_ref[1] = low(jnp.where(low_lanes, 0.0, turned))
    variants_ref[2] = low(jnp.where(low_lanes, turned, 0.0))
    variants_ref[3] = low(jnp.where(low_lanes, 0.0, wide))


def allowed_block(seg_k, seg_q, diagonal):
    same = seg_k == seg_q
    if diagonal:
        rows = lax.broadcasted_iota(jnp.int32, same.shape, 0)
        lanes = lax.broadcasted_iota(jnp.int32, same.shape, 1)
        same = same & (rows <= lanes)
    return same


def attend_body(
    q_ref, k_ref, v_ref, seg_col_ref, seg_row_ref, out_grad, mix_w, gate_w, up_w, down_w,
    mix_begun, gate_begun, mixed_ref, lse_ref, whole_grad, mix_full, gate_full, up_full, down_full,
    ks, vt, acc, stats, sems, near, held_mix, held_gate, held_up, held_down, held_grad
):
    block = pl.program_id(1)
    now = pl.program_id(0) * pl.num_programs(1) + block
    most = pl.num_programs(0) * pl.num_programs(1) - 1
    y = lax.axis_index("fsdp")
    spreads = {
        "mix": Spread(mix_w, mix_full, SPREADS["mix"], sems, 0),
        "gate": Spread(gate_w, gate_full, SPREADS["gate"], sems, 4),
        "up": Spread(up_w, up_full, SPREADS["up"], sems, 8),
        "down": Spread(down_w, down_full, SPREADS["down"], sems, 12),
    }
    span = out_grad.shape[1]
    mine = whole_grad.at[pl.ds(pl.multiple_of(y * span, span), span)]
    grad_swap = across(out_grad.at[1 - y], mine, sems, 16, "y")
    half = pl.ds(y * 8, 8)
    own = (
        (mix_w, held_mix, mix_full.at[half]),
        (gate_w, held_gate, gate_full.at[half]),
        (up_w, held_up, up_full.at[half]),
        (down_w, held_down, down_full.at[half]),
        (out_grad.at[y], held_grad, mine),
    )
    loads = [pltpu.make_async_copy(a, b, near.at[0, at]) for at, (a, b, _) in enumerate(own)]
    stores = [pltpu.make_async_copy(b, c, near.at[1, at]) for at, (_, b, c) in enumerate(own)]
    plan = {
        3: (("mix", 1),),
        4: (("up", 0), ("gate", 1)),
        7: (("down", 0), ("up", 1), ("mix", 2)),
        11: (("down", 1),),
    }

    @pl.when(now == 0)
    def _():
        for load in loads:
            load.start()
        greet(("y", "x", "zlo", "core"))
        spreads["up"].advance(-1)
        spreads["down"].advance(-1)
        grad_swap.start()
        spreads["gate"].copy(1).start()
        spreads["mix"].copy(1).start()

    @pl.when(now == 1)
    def _():
        for load, store in zip(loads, stores):
            load.wait()
            store.start()

    for at, steps in plan.items():

        @pl.when(now == at)
        def _(steps=steps):
            for name, stage in steps:
                spreads[name].advance(stage)

    @pl.when(block == 0)
    def _():
        place_heads(k_ref[...], ks)
        vt[...] = low(v_ref[...].astype(jnp.float32).T)

    acc[...] = jnp.zeros_like(acc)
    stats[0] = jnp.full((8, BLOCK), -1e30, jnp.float32)
    stats[1] = jnp.zeros((8, BLOCK), jnp.float32)
    seg_q = seg_row_ref[...]

    def step(j, diagonal):
        rows = pl.ds(pl.multiple_of(j * BLOCK, BLOCK), BLOCK)
        seg_k = seg_col_ref[rows, :]
        allowed = allowed_block(seg_k, seg_q, diagonal)
        scores = []
        for head in range(6):
            part, side, kv = head // 2, head % 2, head // 3
            q_tile = q_ref[:, part * WIDE : (part + 1) * WIDE]
            scores.append(jnp.where(allowed, mm_nt(ks[kv * 2 + side, rows, :], q_tile), -1e30))
        before = stats[0]
        highest = [
            jnp.maximum(before[head : head + 1], jnp.max(scores[head], axis=0, keepdims=True))
            for head in range(6)
        ]
        chances = [jnp.exp(scores[head] - highest[head]) for head in range(6)]
        shrink = [jnp.exp(before[head : head + 1] - highest[head]) for head in range(6)]
        for head in range(6):
            kv = head // 3
            stats[0, head : head + 1, :] = highest[head]
            stats[1, head : head + 1, :] = stats[1, head : head + 1, :] * shrink[head] + jnp.sum(
                chances[head], axis=0, keepdims=True
            )
            values = vt[kv * HEAD : (kv + 1) * HEAD, rows]
            at = head * HEAD
            acc[at : at + HEAD, :] = acc[at : at + HEAD, :] * shrink[head] + mm(
                values, low(chances[head])
            )

    @pl.loop(0, block)
    def _(j):
        step(j, False)

    step(block, True)
    total = stats[1]
    for part in range(3):
        at = part * WIDE
        both = jnp.concatenate(
            [
                acc[at : at + HEAD, :] / total[2 * part : 2 * part + 1, :],
                acc[at + HEAD : at + WIDE, :] / total[2 * part + 1 : 2 * part + 2, :],
            ],
            axis=0,
        )
        mixed_ref[:, at : at + WIDE] = low(both.T)
    lse_ref[0] = stats[0] + jnp.log(jnp.maximum(total, 1e-30))

    @pl.when(now == most)
    def _():
        spreads["gate"].advance(2)
        spreads["up"].advance(2)
        spreads["down"].advance(2)
        for name, spread in spreads.items():
            spread.advance(3)
            spread.finish(1 if name in ("mix", "gate") else 0)
        grad_swap.wait()
        for store in stores:
            store.wait()


def attend(qkv, seg_col, seg_row, out_grad, mix_w, gate_w, up_w, down_w, mix_begun, gate_begun):
    length = qkv.shape[0]
    pairs = KV_HEADS // 2
    q_tiles = HEADS * HEAD // WIDE
    anywhere = pl.BlockSpec(memory_space=pl.ANY)
    shards = [eighths(w) for w in (mix_w, gate_w, up_w, down_w)]
    fulls = [jax.ShapeDtypeStruct((16,) + w.shape[1:], w.dtype) for w in shards]
    found = pl.pallas_call(
        attend_body,
        grid=(pairs, length // BLOCK),
        in_specs=[
            pl.BlockSpec((BLOCK, 3 * WIDE), lambda b, i: (i, b)),
            pl.BlockSpec((length, WIDE), lambda b, i: (0, q_tiles + b)),
            pl.BlockSpec((length, WIDE), lambda b, i: (0, q_tiles + pairs + b)),
            pl.BlockSpec((length, 1), lambda b, i: (0, 0)),
            pl.BlockSpec((1, BLOCK), lambda b, i: (0, i)),
        ]
        + [anywhere] * 7,
        out_specs=[
            pl.BlockSpec((BLOCK, 3 * WIDE), lambda b, i: (i, b)),
            pl.BlockSpec((1, 8, BLOCK), lambda b, i: (b, 0, i)),
        ]
        + [anywhere] * 5,
        out_shape=[
            jax.ShapeDtypeStruct((length, HEADS * HEAD), jnp.bfloat16),
            jax.ShapeDtypeStruct((pairs, 8, length), jnp.float32),
            jax.ShapeDtypeStruct((length, out_grad.shape[2]), out_grad.dtype),
        ]
        + fulls,
        input_output_aliases={10: 3, 11: 4},
        scratch_shapes=[
            pltpu.VMEM((4, length, WIDE), jnp.bfloat16),
            pltpu.VMEM((WIDE, length), jnp.bfloat16),
            pltpu.VMEM((6 * HEAD, BLOCK), jnp.float32),
            pltpu.VMEM((2, 8, BLOCK), jnp.float32),
            pltpu.SemaphoreType.DMA((2, 17)),
            pltpu.SemaphoreType.DMA((2, 5)),
        ]
        + [pltpu.VMEM(w.shape, w.dtype) for w in shards]
        + [pltpu.VMEM(out_grad.shape[1:], out_grad.dtype)],
        compiler_params=pltpu.CompilerParams(
            collective_id=2, has_side_effects=True, vmem_limit_bytes=VMEM_MOST
        ),
        cost_estimate=pl.CostEstimate(
            flops=16 * length * length * HEADS * HEAD // 2,
            bytes_accessed=6 * length * HEADS * HEAD,
            transcendentals=HEADS * length * length // 2,
        ),
        name="attend",
    )(qkv, qkv, qkv, seg_col, seg_row, out_grad, *shards, mix_begun, gate_begun)
    return tuple(found[:3]) + tuple(w.reshape(-1, w.shape[2]) for w in found[3:])


def attend_back_body(
    q_ref, k_ref, v_ref, grad_ref, mixed_ref, lse_ref, seg_col_ref, seg_row_ref, cos_ref, sin_ref,
    gate_term, up_term, down_term, gate_third, up_third, down_third,
    dq_ref, dk_ref, dv_ref, gate_left, up_left, down_left, gate_sum, up_sum, down_sum,
    ks, vs, kt, k_acc, v_acc, q_acc, sides, delta, sems, near,
    kept_h, r1_h, r2_h, r3_h, own_h, came_h, kept_d, r1_d, r2_d, r3_d, own_d, came_d
):
    block = pl.program_id(1)
    length = k_ref.shape[0]
    now = pl.program_id(0) * pl.num_programs(1) + block
    most = pl.num_programs(0) * pl.num_programs(1) - 1
    pick = lambda pair, single: [pair.at[0], pair.at[1], single]
    kept, owns, came = pick(kept_h, kept_d), pick(own_h, own_d), pick(came_h, came_d)
    ones, twos, threes = pick(r1_h, r1_d), pick(r2_h, r2_d), pick(r3_h, r3_d)
    folds = [
        Fold(term, kept[f], [ones[f], twos[f], threes[f]], LATE_ORDERS[f], sems, 3 * f, near, f)
        for f, term in enumerate((gate_term, up_term, down_term))
    ]
    loads = [
        pltpu.make_async_copy(third, owns[f], near.at[3 + f])
        for f, third in enumerate((gate_third, up_third, down_third))
    ]
    zs = [across(owns[f], came[f], sems, 9 + f, "zhi") for f in range(3)]
    stores = [
        pltpu.make_async_copy(threes[f], left, near.at[6 + f])
        for f, left in enumerate((gate_left, up_left, down_left))
    ]
    sums = Sums((gate_sum, up_sum, down_sum), came, 0, sems, 12, near, 9)

    def settle(f):
        zs[f].wait_recv()
        for n in range(2):
            came[f][n] = low(owns[f][n].astype(jnp.float32) + came[f][n].astype(jnp.float32))
        sums.begin(f)

    @pl.when(now == 0)
    def _():
        for load in loads:
            load.start()
        greet(("core",) + AXES)
        for fold in folds:
            fold.begin()
        for load, copy in zip(loads, zs):
            load.wait()
            copy.start()

    @pl.when(now == 5)
    def _():
        folds[0].advance(0)
        folds[1].advance(0)

    @pl.when(now == 7)
    def _():
        settle(0)
        settle(1)

    @pl.when(now == 8)
    def _():
        settle(2)
        folds[0].advance(1)

    @pl.when(now == 10)
    def _():
        folds[2].advance(0)
        sums.follow(0)
        sums.follow(1)

    @pl.when(now == 11)
    def _():
        sums.follow(2)

    @pl.when(block == 0)
    def _():
        place_heads(k_ref[...], ks)
        place_heads(v_ref[...], vs)
        kt[...] = low(k_ref[...].astype(jnp.float32).T)
        k_acc[...] = jnp.zeros_like(k_acc)
        v_acc[...] = jnp.zeros_like(v_acc)

    q_acc[...] = jnp.zeros_like(q_acc)
    seg_q = seg_row_ref[...]
    low_lanes = lanes_below(BLOCK, WIDE, HEAD)
    zero = jnp.zeros((BLOCK, WIDE), jnp.bfloat16)
    for part in range(3):
        at = part * WIDE
        tile, grad = q_ref[:, at : at + WIDE], grad_ref[:, at : at + WIDE]
        sides[0, part, 0:BLOCK, :] = jnp.where(low_lanes, tile, zero)
        sides[0, part, BLOCK : 2 * BLOCK, :] = jnp.where(low_lanes, zero, tile)
        sides[1, part, 0:BLOCK, :] = jnp.where(low_lanes, grad, zero)
        sides[1, part, BLOCK : 2 * BLOCK, :] = jnp.where(low_lanes, zero, grad)
        product = (grad.astype(jnp.float32) * mixed_ref[:, at : at + WIDE].astype(jnp.float32)).T
        delta[2 * part : 2 * part + 1, :] = jnp.sum(product[:HEAD], axis=0, keepdims=True)
        delta[2 * part + 1 : 2 * part + 2, :] = jnp.sum(product[HEAD:], axis=0, keepdims=True)

    def step(j, diagonal):
        rows = pl.ds(pl.multiple_of(j * BLOCK, BLOCK), BLOCK)
        allowed = allowed_block(seg_col_ref[rows, :], seg_q, diagonal)
        heads = range(6)
        tiles = [q_ref[:, p * WIDE : (p + 1) * WIDE] for p in range(3)]
        grads = [grad_ref[:, p * WIDE : (p + 1) * WIDE] for p in range(3)]
        scores = [mm_nt(ks[h // 3 * 2 + h % 2, rows, :], tiles[h // 2]) for h in heads]
        onto = [mm_nt(vs[h // 3 * 2 + h % 2, rows, :], grads[h // 2]) for h in heads]
        chances = [
            jnp.exp(jnp.where(allowed, scores[h], -1e30) - lse_ref[0, h : h + 1, :]) for h in heads
        ]
        score_grads = [low(chances[h] * (onto[h] - delta[h : h + 1, :])) for h in heads]
        chances = [low(chances[h]) for h in heads]
        for h in heads:
            to = h * HEAD
            q_acc[to : to + HEAD, :] += mm(kt[h // 3 * HEAD : (h // 3 + 1) * HEAD, rows], score_grads[h])
        for p in range(3):
            v_acc[p, rows, :] += mm(jnp.concatenate(chances[2 * p : 2 * p + 2], axis=1), sides[1, p])
            k_acc[p, rows, :] += mm(jnp.concatenate(score_grads[2 * p : 2 * p + 2], axis=1), sides[0, p])

    @pl.loop(0, block)
    def _(j):
        step(j, False)

    step(block, True)
    here = pl.ds(pl.multiple_of(block * BLOCK, BLOCK), BLOCK)
    for part in range(3):
        at = part * WIDE
        tile = q_acc[at : at + WIDE, :].T * HEAD ** (-0.5)
        tile = tile * cos_ref[here, :] - swap_halves(tile) * sin_ref[here, :]
        dq_ref[:, at : at + WIDE] = low(tile)

    @pl.when(block == length // BLOCK - 1)
    def _():
        for j in range(0, length, BLOCK):
            rows = slice(j, j + BLOCK)

            def gather(acc):
                first, middle, last = acc[0, rows, :], acc[1, rows, :], acc[2, rows, :]
                return middle + jnp.where(
                    low_lanes, first + pltpu.roll(first, HEAD, 1), last + pltpu.roll(last, HEAD, 1)
                )

            tile = gather(k_acc)
            tile = tile * cos_ref[rows, :] - swap_halves(tile) * sin_ref[rows, :]
            dk_ref[rows, :] = low(tile)
            dv_ref[rows, :] = low(gather(v_acc))

    @pl.when(now == most)
    def _():
        folds[1].advance(1)
        folds[2].advance(1)
        folds[0].advance(2)
        for f in range(3):
            sums.rises[f].advance(1)
        folds[1].advance(2)
        folds[2].advance(2)
        for store in stores:
            store.start()
        for f in range(3):
            sums.rises[f].advance(2)
        for fold in folds + sums.rises:
            fold.finish()
        for copy in zs:
            copy.wait_send()
        for store in stores:
            store.wait()


def attend_back(qkv, mixed_grad, mixed, lse, seg_col, seg_row, cosines, sines, *terms):
    length = qkv.shape[0]
    rows, wide = terms[0].shape[4:]
    down_rows, width = terms[2].shape[4:]
    anywhere = pl.BlockSpec(memory_space=pl.ANY)
    pairs = KV_HEADS // 2
    q_tiles = HEADS * HEAD // WIDE
    q_block = pl.BlockSpec((BLOCK, 3 * WIDE), lambda b, i: (i, b))
    kv_block = pl.BlockSpec((length, WIDE), lambda b, i: (0, b))
    table = pl.BlockSpec((length, WIDE), lambda b, i: (0, 0), pipeline_mode=pl.Buffered(1))
    return pl.pallas_call(
        attend_back_body,
        grid=(pairs, length // BLOCK),
        in_specs=[
            q_block,
            pl.BlockSpec((length, WIDE), lambda b, i: (0, q_tiles + b)),
            pl.BlockSpec((length, WIDE), lambda b, i: (0, q_tiles + pairs + b)),
            q_block,
            q_block,
            pl.BlockSpec((1, 8, BLOCK), lambda b, i: (b, 0, i)),
            pl.BlockSpec((length, 1), lambda b, i: (0, 0)),
            pl.BlockSpec((1, BLOCK), lambda b, i: (0, i)),
            table,
            table,
        ]
        + [anywhere] * 6,
        out_specs=[q_block, kv_block, kv_block] + [anywhere] * 6,
        out_shape=[
            jax.ShapeDtypeStruct((length, HEADS * HEAD), jnp.bfloat16),
            jax.ShapeDtypeStruct((length, KV_HEADS * HEAD), jnp.bfloat16),
            jax.ShapeDtypeStruct((length, KV_HEADS * HEAD), jnp.bfloat16),
        ]
        + [
            jax.ShapeDtypeStruct((2,) + shape, jnp.bfloat16)
            for shape in ((rows, wide), (rows, wide), (down_rows, width))
        ]
        + [
            jax.ShapeDtypeStruct((2, 2, 2, rows, 4 * wide), jnp.bfloat16),
            jax.ShapeDtypeStruct((2, 2, 2, rows, 4 * wide), jnp.bfloat16),
            jax.ShapeDtypeStruct((2, 2, 2, 2, 2, down_rows, width), jnp.bfloat16),
        ],
        scratch_shapes=[
            pltpu.VMEM((4, length, WIDE), jnp.bfloat16),
            pltpu.VMEM((4, length, WIDE), jnp.bfloat16),
            pltpu.VMEM((WIDE, length), jnp.bfloat16),
            pltpu.VMEM((3, length, WIDE), jnp.float32),
            pltpu.VMEM((3, length, WIDE), jnp.float32),
            pltpu.VMEM((6 * HEAD, BLOCK), jnp.float32),
            pltpu.VMEM((2, 3, 2 * BLOCK, WIDE), jnp.bfloat16),
            pltpu.VMEM((8, BLOCK), jnp.float32),
            pltpu.SemaphoreType.DMA((2, 27)),
            pltpu.SemaphoreType.DMA((14,)),
        ]
        + [pltpu.VMEM((2,) + (2,) * left + (rows, wide), jnp.bfloat16) for left in (3, 3, 2, 1, 1, 1)]
        + [pltpu.VMEM((2,) * left + (down_rows, width), jnp.bfloat16) for left in (3, 3, 2, 1, 1, 1)],
        compiler_params=pltpu.CompilerParams(
            collective_id=3, has_side_effects=True, vmem_limit_bytes=VMEM_MOST
        ),
        cost_estimate=pl.CostEstimate(
            flops=40 * length * length * HEADS * HEAD // 2,
            bytes_accessed=12 * length * HEADS * HEAD,
            transcendentals=HEADS * length * length // 2,
        ),
        name="attend_back",
    )(qkv, qkv, qkv, mixed_grad, mixed, lse, seg_col, seg_row, cosines, sines, *terms)


def mix_body(x_ref, mixed_ref, w_ref, gain_ref, residual_ref, normed_ref, turned_ref):
    residual = x_ref[...].astype(jnp.float32) + mm(mixed_ref[...], w_ref[...])
    residual_ref[...] = residual
    inverse = lax.rsqrt(jnp.mean(residual * residual, axis=-1, keepdims=True) + epsilon)
    normed = residual * inverse * gain_ref[...]
    normed_ref[...] = low(normed)
    turned_ref[...] = low(normed.T)


def mix(x, mixed, w, gain):
    length, width = x.shape
    rows = pl.BlockSpec((BLOCK, width), lambda i: (i, 0))
    return pl.pallas_call(
        mix_body,
        grid=(length // BLOCK,),
        in_specs=[
            rows,
            rows,
            pl.BlockSpec(w.shape, lambda i: (0, 0), pipeline_mode=pl.Buffered(1)),
            pl.BlockSpec((1, width), lambda i: (0, 0)),
        ],
        out_specs=[rows, rows, pl.BlockSpec((width, BLOCK), lambda i: (0, i))],
        out_shape=[
            jax.ShapeDtypeStruct((length, width), jnp.float32),
            jax.ShapeDtypeStruct((length, width), jnp.bfloat16),
            jax.ShapeDtypeStruct((width, length), jnp.bfloat16),
        ],
        cost_estimate=pl.CostEstimate(
            flops=2 * length * width * width, bytes_accessed=12 * length * width, transcendentals=0
        ),
        name="mix",
    )(x, mixed, w, gain)


def norm_grad(grad, gain, scaled, inverse):
    weighted = grad * gain
    return inverse * (weighted - scaled * jnp.mean(weighted * scaled, axis=-1, keepdims=True))


def turn_body(residual_ref, out_ref, back_ref, c_ref, mixed_ref, w_ref, gain_ref,
              result_ref, grad_ref, mixed_grad_ref, term_ref, gain_term_ref, total):
    step = pl.program_id(0)
    residual = residual_ref[...]
    result_ref[...] = low(residual + out_ref[...])
    inverse = lax.rsqrt(jnp.mean(residual * residual, axis=-1, keepdims=True) + epsilon)
    scaled = residual * inverse
    normed_grad = back_ref[...]
    gain_term = jnp.sum(normed_grad * scaled, axis=0, keepdims=True)
    grad = c_ref[...].astype(jnp.float32) + norm_grad(normed_grad, gain_ref[...], scaled, inverse)
    grad_ref[...] = grad
    grad_low = low(grad)
    mixed_grad_ref[...] = low(mm_nt(grad_low, w_ref[...]))
    term = mm_tn(mixed_ref[...], grad_low)

    @pl.when(step == 0)
    def _():
        total[...] = term
        gain_term_ref[...] = jnp.broadcast_to(gain_term, gain_term_ref.shape)

    @pl.when(step > 0)
    def _():
        total[...] += term
        gain_term_ref[...] += jnp.broadcast_to(gain_term, gain_term_ref.shape)

    @pl.when(step == pl.num_programs(0) - 1)
    def _():
        term_ref[...] = low(total[...])


def turn(residual, out, back, c, mixed, w, gain):
    length, width = residual.shape
    rows = pl.BlockSpec((BLOCK, width), lambda i: (i, 0))
    whole = lambda shape: pl.BlockSpec(shape, lambda i: (0, 0), pipeline_mode=pl.Buffered(1))
    return pl.pallas_call(
        turn_body,
        grid=(length // BLOCK,),
        in_specs=[rows] * 5 + [whole(w.shape), pl.BlockSpec((1, width), lambda i: (0, 0))],
        out_specs=[
            rows, rows, rows, whole((width, width)), pl.BlockSpec((8, width), lambda i: (0, 0)),
        ],
        out_shape=[
            jax.ShapeDtypeStruct((length, width), jnp.bfloat16),
            jax.ShapeDtypeStruct((length, width), jnp.float32),
            jax.ShapeDtypeStruct((length, width), jnp.bfloat16),
            jax.ShapeDtypeStruct((width, width), jnp.bfloat16),
            jax.ShapeDtypeStruct((8, width), jnp.float32),
        ],
        scratch_shapes=[pltpu.VMEM((width, width), jnp.float32)],
        compiler_params=pltpu.CompilerParams(vmem_limit_bytes=VMEM_MOST),
        cost_estimate=pl.CostEstimate(
            flops=4 * length * width * width, bytes_accessed=32 * length * width, transcendentals=0
        ),
        name="turn",
    )(residual, out, back, c, mixed, w, gain)


def end_body(dq_ref, dk_ref, dv_ref, normed_ref, x_ref, grad_ref, w_ref, gain_ref, feed_gain_ref,
             mix_term, result, gate_left, up_left, down_left, gate_begun, up_begun, down_begun,
             gate, up, down, sums, outputs, input_grads, gain_sums,
             turned, term, tokens, r0, r1, r2, r3, exchanged, hidden_b, hidden_came,
             down_b, down_came, gain_held, gain_came, rows_held, sems, near):
    step = pl.program_id(0)
    last = pl.num_programs(0) - 1
    rows_each = x_ref.shape[0]
    length = normed_ref.shape[0]
    q_width, k_width = dq_ref.shape[1], dk_ref.shape[1]
    core, y = bit_of("core"), lax.axis_index("fsdp")
    third = term.shape[-1] // 3
    wide = third // 2
    everything = (slice(None),) * 4 + (slice(None),)
    columns = [
        [pl.ds(pl.multiple_of(t * third + side * wide, WIDE), wide) for side in (core, 1 - core)]
        for t in range(3)
    ]
    span = outputs.shape[1]
    rows = [pl.ds(pl.multiple_of(at * span, span), span) for at in (y, 1 - y)]
    pick = lambda pair, single: [pair.at[0], pair.at[1], single]
    b_left, came = pick(hidden_b, down_b), pick(hidden_came, down_came)
    loads = [
        pltpu.make_async_copy(whole, held, near.at[f])
        for f, (whole, held) in enumerate(zip((gate_left, up_left, down_left), b_left))
    ]
    mix_load = pltpu.make_async_copy(
        mix_term, term.at[everything + (slice(q_width + 2 * k_width, term.shape[-1]),)], near.at[6]
    )
    result_load = pltpu.make_async_copy(result.at[rows[0]], rows_held, near.at[7])
    result_store = pltpu.make_async_copy(rows_held, outputs.at[y], near.at[8])
    token_store = pltpu.make_async_copy(tokens.at[rows[0]], input_grads.at[y], near.at[9])
    zs = [across(b_left[f], came[f], sems, f, "zhi") for f in range(3)]
    hidden = Sums((gate, up, down), came, 1, sems, 60, near, 10)
    cores = [
        across(term.at[everything + (columns[t][1],)], r0.at[t], sems, 27 + t, "core")
        for t in range(3)
    ]
    parts = [
        Fold(r0.at[t], None, [r1.at[t], r2.at[t], r3.at[t]], PART_ORDERS[t], sems, 30 + 3 * t, None, None)
        for t in range(3)
    ]
    part_zs = [across(r3.at[t], exchanged.at[t], sems, 39 + t, "zhi") for t in range(3)]
    tops = [Rise(sums, PART_BACKS[t], [columns[t][0]], sems, 42 + 3 * t) for t in range(3)]
    swaps = [
        across(result.at[rows[1]], outputs.at[y], sems, 51, "y"),
        across(tokens.at[rows[1]], input_grads.at[y], sems, 52, "y"),
    ]
    names = ("y", "core", "x", "zlo", "zhi")
    gain_copies = [
        across(gain_held.at[at], gain_came.at[at], sems, 53 + at, name)
        for at, name in enumerate(names)
    ]

    def part_store(t):
        return pltpu.make_async_copy(exchanged.at[t], tops[t].block(0)[0], near.at[20 + t])

    def settle(copy, mine, theirs):
        copy.wait_recv()
        for n in range(2):
            theirs[n] = low(mine[n].astype(jnp.float32) + theirs[n].astype(jnp.float32))

    def hidden_settle(f):
        settle(zs[f], b_left[f], came[f])
        hidden.begin(f)

    def part_settle(t):
        settle(part_zs[t], r3.at[t], exchanged.at[t])
        part_store(t).start()
        tops[t].begin([exchanged.at[t]])

    def core_sum(t):
        cores[t].wait_recv()

        @pl.loop(0, 16)
        def _(n):
            index = (n // 8, n // 4 % 2, n // 2 % 2, n % 2)
            mine = term[index + (slice(None), columns[t][0])]
            r0[(t,) + index] = low(r0[(t,) + index].astype(jnp.float32) + mine.astype(jnp.float32))

        parts[t].begin()

    def gain_step(at):
        gain_copies[at].wait_recv()
        gain_held[at + 1] = gain_held[at] + gain_came[at]
        if at + 1 < len(names):
            gain_copies[at + 1].start()

    @pl.when(step == 0)
    def _():
        for load in loads + [mix_load, result_load]:
            load.start()
        greet(names)
        for f in range(3):
            loads[f].wait()
            zs[f].start()
        mix_load.wait()
        cores[2].start()
        for at in range(0, length, BLOCK):
            turned[:, at : at + BLOCK] = normed_ref[at : at + BLOCK, :].T

    @pl.when(step == 1)
    def _():
        core_sum(2)
        result_load.wait()
        result_store.start()

    @pl.when(step == 3)
    def _():
        cores[0].start()

    @pl.when(step == 4)
    def _():
        core_sum(0)

    @pl.when(step == 5)
    def _():
        cores[1].start()
        hidden_settle(0)

    @pl.when(step == 6)
    def _():
        core_sum(1)
        parts[2].advance(0)

    @pl.when(step == 7)
    def _():
        hidden_settle(1)

    @pl.when(step == 8)
    def _():
        hidden.follow(0)
        parts[0].advance(0)

    def chunk(low_rows, at):
        wide_term = mm(turned[...], low_rows).reshape(16, turned.shape[0] // 16, k_width)
        for n in range(16):
            index = (n // 8, n // 4 % 2, n // 2 % 2, n % 2, slice(None), slice(at, at + k_width))
            term[index] = low(wide_term[n])

    for at in range(3):

        @pl.when(step == at)
        def _(at=at):
            chunk(dq_ref[:, at * k_width : (at + 1) * k_width], at * k_width)

    @pl.when(step == 3)
    def _():
        chunk(dk_ref[...], q_width)

    @pl.when(step == 4)
    def _():
        chunk(dv_ref[...], q_width + k_width)

    first = last + 1 - length // rows_each

    @pl.when(step >= first)
    def _():
        here = pl.ds(pl.multiple_of((step - first) * rows_each, rows_each), rows_each)
        normed_grad = (
            mm_nt(dq_ref[here, :], w_ref[:, :q_width])
            + mm_nt(dk_ref[here, :], w_ref[:, q_width : q_width + k_width])
            + mm_nt(dv_ref[here, :], w_ref[:, q_width + k_width :])
        )
        values = x_ref[...].astype(jnp.float32)
        inverse = lax.rsqrt(jnp.mean(values * values, axis=-1, keepdims=True) + epsilon)
        scaled = values * inverse
        gain_term = jnp.sum(normed_grad * scaled, axis=0, keepdims=True)
        tokens[here, :] = low(
            grad_ref[...] + norm_grad(normed_grad, gain_ref[...], scaled, inverse)
        )

        @pl.when(step == first)
        def _():
            gain_held[0, 0:1, :] = gain_term
            gain_held[0, 1:2, :] = feed_gain_ref[0:1, :]
            gain_held[0, 2:8, :] = jnp.zeros_like(gain_held[0, 2:8, :])

        @pl.when(step > first)
        def _():
            gain_held[0, 0:1, :] += gain_term

    @pl.when(step == last)
    def _():
        gain_copies[0].start()
        token_store.start()
        for copy in swaps:
            copy.start()
        hidden_settle(2)
        hidden.follow(1)
        gain_step(0)
        parts[1].advance(0)
        hidden.follow(2)
        gain_step(1)
        parts[2].advance(1)
        parts[1].advance(1)
        gain_step(2)
        parts[0].advance(1)
        hidden.rises[0].advance(1)
        for t in (2, 1, 0):
            parts[t].advance(2)
            part_zs[t].start()
        gain_step(3)
        hidden.rises[1].advance(1)
        hidden.rises[2].advance(1)
        for t in (2, 1, 0):
            part_settle(t)
        gain_step(4)
        for t in (2, 1, 0):
            part_store(t).wait()
            tops[t].advance(0)
        for t in (2, 1, 0):
            tops[t].advance(1)
        every = hidden.rises + tops
        for one in every:
            one.advance(2)
        for copy in cores + swaps + gain_copies + zs + part_zs:
            copy.wait_send()
        for one in every + parts:
            one.finish()
        for copy in swaps:
            copy.wait_recv()
        result_store.wait()
        token_store.wait()
        gain_sums[...] = gain_held[len(names)]


def end(dq, dk, dv, normed, x, grad, w, gain, feed_gain_term, mix_term, result, *sums):
    length, width = x.shape
    k_width = dk.shape[1]
    total = w.shape[1] + mix_term.shape[1]
    wide = total // 6
    mix_term = mix_term.reshape(2, 2, 2, 2, mix_term.shape[0] // 16, mix_term.shape[1])
    rows = mix_term.shape[4]
    hidden_rows, hidden = sums[0].shape[1:]
    down_rows = sums[2].shape[1]
    chunks, blocks = w.shape[1] // k_width, length // BLOCK
    block = pl.BlockSpec((BLOCK, width), lambda i: (jnp.maximum(i - chunks, 0), 0))
    whole = lambda a: pl.BlockSpec(a.shape, lambda i: (0,) * a.ndim, pipeline_mode=pl.Buffered(1))
    anywhere = pl.BlockSpec(memory_space=pl.ANY)
    both = jax.ShapeDtypeStruct((2, length // 2, width), result.dtype)
    low_type = jnp.bfloat16
    return pl.pallas_call(
        end_body,
        grid=(chunks + blocks,),
        in_specs=[whole(dq), whole(dk), whole(dv), whole(normed), block, block, whole(w), whole(gain),
                  whole(feed_gain_term)] + [anywhere] * 8,
        out_specs=[anywhere] * 6 + [pl.BlockSpec((8, width), lambda i: (0, 0))],
        out_shape=[
            jax.ShapeDtypeStruct((2, 2, 2, hidden_rows, 4 * hidden), low_type),
            jax.ShapeDtypeStruct((2, 2, 2, hidden_rows, 4 * hidden), low_type),
            jax.ShapeDtypeStruct((2, 2, 2, 2, 2, down_rows, width), low_type),
            jax.ShapeDtypeStruct((2, 2, 2, rows, total), low_type),
            both,
            both,
            jax.ShapeDtypeStruct((8, width), jnp.float32),
        ],
        input_output_aliases={14: 0, 15: 1, 16: 2},
        scratch_shapes=[
            pltpu.VMEM((width, length), low_type),
            pltpu.VMEM((2, 2, 2, 2, rows, total), low_type),
            pltpu.VMEM((length, width), low_type),
        ]
        + [pltpu.VMEM((3,) + (2,) * left + (rows, wide), low_type) for left in (4, 3, 2, 1, 1)]
        + [pltpu.VMEM((2, 2, hidden_rows, hidden), low_type)] * 2
        + [pltpu.VMEM((2, down_rows, width), low_type)] * 2
        + [
            pltpu.VMEM((6, 8, width), jnp.float32),
            pltpu.VMEM((5, 8, width), jnp.float32),
            pltpu.VMEM((length // 2, width), low_type),
            pltpu.SemaphoreType.DMA((2, 75)),
            pltpu.SemaphoreType.DMA((23,)),
        ],
        compiler_params=pltpu.CompilerParams(
            collective_id=4, has_side_effects=True, vmem_limit_bytes=VMEM_MOST
        ),
        name="end",
    )(dq, dk, dv, normed, x, grad, w, gain, feed_gain_term, mix_term, result, *sums)


def sixteenth(n):
    return (n // 8, n // 4 % 2, n // 2 % 2, n % 2)


def feed_body(normed_ref, turned_ref, c_ref, gate_w, up_w, down_w,
              out_ref, back_ref, gate_a, up_a, down_a, gate_b, up_b, down_b,
              gate_v, up_v, down_v, hidden_t, gate_low, up_low,
              hold_h, hold_d, came_h, came_d, own_h, own_d,
              r1_h, r2_h, r3_h, r1_d, r2_d, r3_d, sems, near, weight_sems, free):
    step = pl.program_id(0)
    length, width = normed_ref.shape
    core = bit_of("core")
    slot = step % 2
    part = gate_v.shape[2] // 2
    side_width = gate_w.shape[1] // 2

    def weights(of, into):
        owner = (core + 1 + of) % 2
        at = (2 * owner + of // 2) * part
        found = []
        for side in range(2):
            here = pl.ds(pl.multiple_of(side * side_width + at, WIDE), part)
            there = slice(side * part, (side + 1) * part)
            found += [
                (gate_w.at[:, here], gate_v.at[into, :, there]),
                (up_w.at[:, here], up_v.at[into, :, there]),
                (down_w.at[here], down_v.at[into, there]),
            ]
        return [
            pltpu.make_async_copy(a, b, weight_sems.at[into, n]) for n, (a, b) in enumerate(found)
        ]

    holds = (hold_h.at[0], hold_h.at[1], hold_d)
    arrived = (came_h.at[0], came_h.at[1], came_d)
    owns = (own_h.at[0], own_h.at[1], own_d)
    cores = [across(holds[f], arrived[f], sems, f, "core") for f in range(3)]
    received = (
        [r1_h.at[0], r2_h.at[0], r3_h.at[0]],
        [r1_h.at[1], r2_h.at[1], r3_h.at[1]],
        [r1_d, r2_d, r3_d],
    )
    folds = [
        Fold(owns[f], None, received[f], ORDERS[f], sems, 3 + 3 * f, None, None) for f in range(3)
    ]
    stores_a = [
        pltpu.make_async_copy(received[f][2], half, near.at[f])
        for f, half in enumerate((gate_a, up_a, down_a))
    ]
    stores_b = [
        pltpu.make_async_copy(owns[f], whole, near.at[3 + f])
        for f, whole in enumerate((gate_b, up_b, down_b))
    ]

    @pl.when(step == 0)
    def _():
        for load in weights(step, slot):
            load.start()
        out_ref[...] = jnp.zeros_like(out_ref)
        back_ref[...] = jnp.zeros_like(back_ref)
        greet(("core",) + AXES[:3])

    for load in weights(step, slot):
        load.wait()

    @pl.when(step < 3)
    def _():
        for load in weights(step + 1, 1 - slot):
            load.start()

    gate, up, down = gate_v.at[slot], up_v.at[slot], down_v.at[slot]
    for at in range(0, length, BLOCK):
        rows = slice(at, at + BLOCK)
        normed = normed_ref[rows, :]
        gate_sum = mm(normed, gate[...])
        up_sum = mm(normed, up[...])
        hidden_grad = mm_nt(c_ref[rows, :], down[...])
        sigmoid = jax.nn.sigmoid(gate_sum)
        activated = gate_sum * sigmoid
        hidden = low(activated * up_sum)
        gate_grad = low(hidden_grad * up_sum * (sigmoid + activated * (1.0 - sigmoid)))
        up_grad = low(hidden_grad * activated)
        hidden_t[:, rows] = hidden.T
        gate_low[rows, :] = gate_grad
        up_low[rows, :] = up_grad
        out_ref[rows, :] += mm(hidden, down[...])
        back_ref[rows, :] += mm_nt(gate_grad, gate[...]) + mm_nt(up_grad, up[...])

    theirs = slot == 0

    @pl.when(step == 3)
    def _():
        for fold in folds:
            fold.copy(0).wait_send()
            fold.advance(1)

    @pl.when(jnp.logical_not(theirs))
    def _():
        for copy in cores:
            copy.wait_recv()

    def put(blocks, hold, came, own):
        @pl.when(theirs)
        def _():
            for index, block in blocks:
                hold[index] = low(block)

        @pl.when(jnp.logical_not(theirs))
        def _():
            for index, block in blocks:
                own[index] = low(block + came[index].astype(jnp.float32))

    quarter = width // 4
    for n in range(4):
        rows = slice(n * quarter, (n + 1) * quarter)
        for f, grads in enumerate((gate_low, up_low)):
            value = mm(turned_ref[rows, :], grads[...]).reshape(4, quarter // 4, 2 * part)
            put(
                [((f,) + sixteenth(4 * n + k), value[k]) for k in range(4)], hold_h, came_h, own_h
            )
    third = width // 3
    for n in range(3):
        columns = slice(n * third, (n + 1) * third)
        value = mm(hidden_t[...], c_ref[:, columns]).reshape(16, part // 8, third)
        put(
            [(sixteenth(k) + (slice(None), columns), value[k]) for k in range(16)],
            hold_d, came_d, own_d,
        )

    @pl.when(step == 2)
    def _():
        pl.semaphore_wait(free, 1)

    @pl.when(theirs)
    def _():
        for copy in cores:
            copy.start()

    @pl.when(step == 2)
    def _():
        for fold in folds:
            fold.advance(0)

    @pl.when(jnp.logical_not(theirs))
    def _():
        for copy in cores:
            copy.wait_send()

    @pl.when(step == 1)
    def _():
        pl.semaphore_signal(free, inc=1, device_id=peer_of("core"), device_id_type=MESH)
        for fold in folds:
            fold.begin()

    @pl.when(step == 3)
    def _():
        for store in stores_b:
            store.start()
        for fold in folds:
            fold.advance(2)
        for store in stores_a:
            store.start()
        for fold in folds:
            for stage in (1, 2):
                fold.copy(stage).wait_send()
        for store in stores_a + stores_b:
            store.wait()


def feed(normed, turned, c, gate, up, down):
    length, width = normed.shape
    part = gate.shape[1] // 8
    rows, down_rows = width // 16, part // 8
    whole = lambda a: pl.BlockSpec(a.shape, lambda t: (0, 0), pipeline_mode=pl.Buffered(1))
    total = pl.BlockSpec((length, width), lambda t: (0, 0), pipeline_mode=pl.Buffered(1))
    anywhere = pl.BlockSpec(memory_space=pl.ANY)
    low_type = jnp.bfloat16
    hidden = lambda left: (2,) * left + (rows, 2 * part)
    down_shape = lambda left: (2,) * left + (down_rows, width)
    return pl.pallas_call(
        feed_body,
        grid=(4,),
        in_specs=[whole(normed), whole(turned), whole(c)] + [anywhere] * 3,
        out_specs=[total, total] + [anywhere] * 6,
        out_shape=[
            jax.ShapeDtypeStruct((length, width), jnp.float32),
            jax.ShapeDtypeStruct((length, width), jnp.float32),
        ]
        + [
            jax.ShapeDtypeStruct(shape, low_type)
            for left in (1, 4)
            for shape in (hidden(left), hidden(left), down_shape(left))
        ],
        scratch_shapes=[
            pltpu.VMEM((2, width, 2 * part), low_type),
            pltpu.VMEM((2, width, 2 * part), low_type),
            pltpu.VMEM((2, 2 * part, width), low_type),
            pltpu.VMEM((2 * part, length), low_type),
            pltpu.VMEM((length, 2 * part), low_type),
            pltpu.VMEM((length, 2 * part), low_type),
        ]
        + [pltpu.VMEM(shape, low_type) for _ in range(3) for shape in ((2,) + hidden(4), down_shape(4))]
        + [pltpu.VMEM((2,) + hidden(left), low_type) for left in (3, 2, 1)]
        + [pltpu.VMEM(down_shape(left), low_type) for left in (3, 2, 1)]
        + [
            pltpu.SemaphoreType.DMA((2, 12)),
            pltpu.SemaphoreType.DMA((6,)),
            pltpu.SemaphoreType.DMA((2, 6)),
            pltpu.SemaphoreType.REGULAR,
        ],
        compiler_params=pltpu.CompilerParams(
            collective_id=5, has_side_effects=True, vmem_limit_bytes=VMEM_MOST
        ),
        cost_estimate=pl.CostEstimate(
            flops=18 * length * width * gate.shape[1],
            bytes_accessed=12 * width * gate.shape[1] + 16 * length * width,
            transcendentals=length * gate.shape[1],
        ),
        name="feed",
    )(normed, turned, c, gate, up, down)


def shortened(array):
    return jax.tree.map(lambda a: a.astype(jnp.bfloat16) if a.dtype == jnp.float32 else a, array)


def product(left, right):
    return jnp.dot(left, right, preferred_element_type=jnp.float32)


def product_tn(left, right):
    return lax.dot_general(
        left, right, (((0,), (0,)), ((), ())), preferred_element_type=jnp.float32
    )


def product_nt(left, right):
    return lax.dot_general(
        left, right, (((1,), (1,)), ((), ())), preferred_element_type=jnp.float32
    )


def rotary_tables(positions, width):
    half_width = width // 2
    freqs = jnp.exp(
        jnp.arange(half_width, dtype=jnp.float32) * (-2.0 * math.log(rope_base) / width)
    )
    angles = positions[:, None] * freqs[None, :]
    return (jnp.cos(angles), jnp.sin(angles))


def rotate(values, cosines, sines):
    half_width = values.shape[-1] // 2
    first = values[..., :half_width]
    second = values[..., half_width:]
    return jnp.concatenate(
        [first * cosines - second * sines, second * cosines + first * sines], axis=-1
    )


def unrotate(values, cosines, sines):
    half_width = values.shape[-1] // 2
    first = values[..., :half_width]
    second = values[..., half_width:]
    return jnp.concatenate(
        [first * cosines + second * sines, second * cosines - first * sines], axis=-1
    )


def norm_back(grad_rows, gain, scaled, inverse):
    weighted = grad_rows * gain
    return inverse * (weighted - scaled * jnp.mean(weighted * scaled, axis=-1, keepdims=True))


def plain_local(
    inputs,
    segments,
    out_grad,
    attention_gain,
    query_weight,
    key_weight,
    value_weight,
    output_weight,
    feedforward_gain,
    gate_weight,
    up_weight,
    down_weight,
):
    gathered = (
        lax.all_gather(attention_gain, "fsdp", axis=0, tiled=True),
        lax.all_gather(query_weight, "fsdp", axis=0, tiled=True),
        lax.all_gather(key_weight, "fsdp", axis=0, tiled=True),
        lax.all_gather(value_weight, "fsdp", axis=0, tiled=True),
        lax.all_gather(output_weight, "fsdp", axis=0, tiled=True),
        lax.all_gather(feedforward_gain, "fsdp", axis=0, tiled=True),
        lax.all_gather(gate_weight, "fsdp", axis=0, tiled=True),
        lax.all_gather(up_weight, "fsdp", axis=0, tiled=True),
        lax.all_gather(down_weight, "fsdp", axis=0, tiled=True),
    )
    full_query, full_key, full_value, full_output = (
        gathered[1],
        gathered[2],
        gathered[3],
        gathered[4],
    )
    full_gate, full_up, full_down = (gathered[6], gathered[7], gathered[8])
    gain_attention = gathered[0].astype(jnp.float32)
    gain_feed = gathered[5].astype(jnp.float32)
    span = inputs.shape[1]
    length = segments.shape[1]
    groups_q = HEADS // KV_HEADS
    key_width = KV_HEADS * HEAD
    start = lax.axis_index("fsdp") * span
    query_pos = start + jnp.arange(span, dtype=jnp.int32)
    key_pos = jnp.arange(length, dtype=jnp.int32)
    cosines, sines = rotary_tables(query_pos.astype(jnp.float32), HEAD)
    cos_four, sin_four = (cosines[:, None, None, :], sines[:, None, None, :])
    cos_three, sin_three = (cosines[:, None, :], sines[:, None, :])
    causal = query_pos[:, None] >= key_pos[None, :]
    scale = HEAD ** (-0.5)

    def micro_step(totals, sequence):
        tokens, segment_row, cotangent = sequence
        own_segment = lax.dynamic_slice_in_dim(segment_row, start, span)
        allowed = causal & (own_segment[:, None] == segment_row[None, :])
        values = tokens.astype(jnp.float32)
        inverse_a = lax.rsqrt(jnp.mean(values * values, axis=-1, keepdims=True) + epsilon)
        scaled_a = values * inverse_a
        normed_a = (scaled_a * gain_attention).astype(jnp.bfloat16)
        query_lin = product(normed_a, full_query).reshape(span, KV_HEADS, groups_q, HEAD)
        queries = rotate(query_lin, cos_four, sin_four).astype(jnp.bfloat16)
        key_lin = product(normed_a, full_key).reshape(span, KV_HEADS, HEAD)
        key_rows = (
            rotate(key_lin, cos_three, sin_three).astype(jnp.bfloat16).reshape(span, key_width)
        )
        value_rows = product(normed_a, full_value).astype(jnp.bfloat16)
        all_keys, all_values = (
            lax.all_gather(key_rows, "fsdp", axis=0, tiled=True),
            lax.all_gather(value_rows, "fsdp", axis=0, tiled=True),
        )
        all_keys = all_keys.reshape(length, KV_HEADS, HEAD)
        all_values = all_values.reshape(length, KV_HEADS, HEAD)
        scores = (
            jnp.einsum("qhgd,khd->hgqk", queries, all_keys, preferred_element_type=jnp.float32)
            * scale
        )
        scores = jnp.where(allowed, scores, -1e30)
        highest = jnp.max(scores, axis=-1, keepdims=True)
        expo_scores = jnp.exp(scores - highest)
        attention = expo_scores / jnp.sum(expo_scores, axis=-1, keepdims=True)
        attention_low = attention.astype(jnp.bfloat16)
        mixed = jnp.einsum(
            "hgqk,khd->qhgd", attention_low, all_values, preferred_element_type=jnp.float32
        )
        mixed = mixed.reshape(span, HEADS * HEAD).astype(jnp.bfloat16)
        residual = values + product(mixed, full_output)
        inverse_f = lax.rsqrt(jnp.mean(residual * residual, axis=-1, keepdims=True) + epsilon)
        scaled_f = residual * inverse_f
        normed_f = (scaled_f * gain_feed).astype(jnp.bfloat16)
        gate_sum = product(normed_f, full_gate)
        up_sum = product(normed_f, full_up)
        sigmoid_gate = jax.nn.sigmoid(gate_sum)
        activated = gate_sum * sigmoid_gate
        hidden = (activated * up_sum).astype(jnp.bfloat16)
        result = (residual + product(hidden, full_down)).astype(jnp.bfloat16)
        down_wgrad = product_tn(hidden, cotangent)
        hidden_grad = product_nt(cotangent, full_down)
        gate_grad = (
            hidden_grad * up_sum * sigmoid_gate * (1.0 + gate_sum * (1.0 - sigmoid_gate))
        ).astype(jnp.bfloat16)
        up_grad = (hidden_grad * activated).astype(jnp.bfloat16)
        gate_wgrad = product_tn(normed_f, gate_grad)
        up_wgrad = product_tn(normed_f, up_grad)
        normed_f_grad = product_nt(gate_grad, full_gate) + product_nt(up_grad, full_up)
        feed_gain_grad = jnp.sum(normed_f_grad * scaled_f, axis=0)
        residual_grad = cotangent.astype(jnp.float32) + norm_back(
            normed_f_grad, gain_feed, scaled_f, inverse_f
        )
        residual_low = residual_grad.astype(jnp.bfloat16)
        output_wgrad = product_tn(mixed, residual_low)
        mixed_grad = (
            product_nt(residual_low, full_output)
            .astype(jnp.bfloat16)
            .reshape(span, KV_HEADS, groups_q, HEAD)
        )
        attention_grad = jnp.einsum(
            "qhgd,khd->hgqk", mixed_grad, all_values, preferred_element_type=jnp.float32
        )
        row_totals = jnp.sum(attention * attention_grad, axis=-1, keepdims=True)
        score_grad = (attention * (attention_grad - row_totals) * scale).astype(jnp.bfloat16)
        value_grads = jnp.einsum(
            "hgqk,qhgd->khd", attention_low, mixed_grad, preferred_element_type=jnp.float32
        ).reshape(length, key_width)
        key_grads = jnp.einsum(
            "hgqk,qhgd->khd", score_grad, queries, preferred_element_type=jnp.float32
        ).reshape(length, key_width)
        query_grad = jnp.einsum(
            "hgqk,khd->qhgd", score_grad, all_keys, preferred_element_type=jnp.float32
        )
        key_back, value_back = (
            lax.psum_scatter(key_grads, "fsdp", scatter_dimension=0, tiled=True),
            lax.psum_scatter(value_grads, "fsdp", scatter_dimension=0, tiled=True),
        )
        query_low = (
            unrotate(query_grad, cos_four, sin_four)
            .reshape(span, HEADS * HEAD)
            .astype(jnp.bfloat16)
        )
        key_low = (
            unrotate(key_back.reshape(span, KV_HEADS, HEAD), cos_three, sin_three)
            .reshape(span, key_width)
            .astype(jnp.bfloat16)
        )
        value_low = value_back.astype(jnp.bfloat16)
        query_wgrad = product_tn(normed_a, query_low)
        key_wgrad = product_tn(normed_a, key_low)
        value_wgrad = product_tn(normed_a, value_low)
        normed_a_grad = (
            product_nt(query_low, full_query)
            + product_nt(key_low, full_key)
            + product_nt(value_low, full_value)
        )
        attention_gain_term = jnp.sum(normed_a_grad * scaled_a, axis=0)
        token_grad = (
            residual_grad + norm_back(normed_a_grad, gain_attention, scaled_a, inverse_a)
        ).astype(jnp.bfloat16)
        terms = (
            attention_gain_term,
            query_wgrad,
            key_wgrad,
            value_wgrad,
            output_wgrad,
            feed_gain_grad,
            gate_wgrad,
            up_wgrad,
            down_wgrad,
        )
        totals = tuple((left + right for left, right in zip(totals, terms)))
        return (totals, (result, token_grad))

    initial = tuple((jnp.zeros(weight.shape, jnp.float32) for weight in gathered))
    totals, (outputs, input_grads) = lax.scan(micro_step, initial, (inputs, segments, out_grad))
    shards = jax.tree.map(
        lambda part: part.astype(jnp.float32),
        lax.psum_scatter(shortened(totals), "fsdp", scatter_dimension=0, tiled=True),
    )
    summed = lax.psum(shards, "group")
    return (
        outputs,
        input_grads,
        summed[0],
        summed[1],
        summed[2],
        summed[3],
        summed[4],
        summed[5],
        summed[6],
        summed[7],
        summed[8],
    )


def paired_local(
    inputs,
    segments,
    out_grad,
    attention_gain,
    query_weight,
    key_weight,
    value_weight,
    output_weight,
    feedforward_gain,
    gate_weight,
    up_weight,
    down_weight,
):
    y = lax.axis_index("fsdp")
    span, length, width = inputs.shape[1], segments.shape[1], inputs.shape[2]
    q_width = query_weight.shape[1]

    gains = jnp.pad(
        jnp.stack([attention_gain, feedforward_gain]).astype(jnp.float32), ((0, 6), (0, 0))
    )
    tokens, qkv_weight, gains = fetch(inputs, query_weight, key_weight, value_weight, gains)
    gains = gains.transpose(1, 0, 2).reshape(8, width)
    gain_a, gain_f = gains[0:1], gains[1:2]

    segment = lax.dynamic_index_in_dim(segments, y, 0, False)
    seg_col, seg_row = segment[:, None], segment[None, :]
    cosines, sines = rope_tables(length)
    normed_a, qkv, mix_begun, gate_begun = project(
        tokens, gain_a, qkv_weight, cosines, sines, output_weight, gate_weight
    )
    mixed, lse, c, mix_weight, full_gate, full_up, full_down = attend(
        qkv, seg_col, seg_row, out_grad, output_weight, gate_weight, up_weight, down_weight,
        mix_begun, gate_begun,
    )

    residual, normed_f, turned_f = mix(tokens, mixed, mix_weight, gain_f)

    out, back, *chunks = feed(normed_f, turned_f, c, full_gate, full_up, full_down)
    result, residual_grad, mixed_grad, mix_term, feed_gain_term = turn(
        residual, out, back, c, mixed, mix_weight, gain_f
    )
    dq, dk, dv, *halves = attend_back(
        qkv, mixed_grad, mixed, lse, seg_col, seg_row, cosines, sines, *chunks[3:], *chunks[:3]
    )
    gate_sum, up_sum, down_sum, sums, outputs, input_grads, gain_sums = end(
        dq, dk, dv, normed_a, tokens, residual_grad, qkv_weight, gain_a, feed_gain_term,
        mix_term, result, *halves,
    )
    gain_grads = lax.dynamic_slice_in_dim(gain_sums, y * (width // 2), width // 2, 1)
    k_width = key_weight.shape[1]
    sums = sums.reshape(width // 2, -1).astype(jnp.float32)
    ends = (0, q_width, q_width + k_width, q_width + 2 * k_width, sums.shape[1])
    parts = [sums[:, a:b] for a, b in zip(ends[:-1], ends[1:])]
    return (
        outputs,
        input_grads,
        gain_grads[0],
        *parts,
        gain_grads[1],
        gate_sum.reshape(width // 2, -1).astype(jnp.float32),
        up_sum.reshape(width // 2, -1).astype(jnp.float32),
        down_sum.reshape(-1, width).astype(jnp.float32),
    )


def solution(mesh):
    placed = (
        P("group", "fsdp", None),
        P("group", None),
        P("group", "fsdp", None),
        P("fsdp"),
        P("fsdp", None),
        P("fsdp", None),
        P("fsdp", None),
        P("fsdp", None),
        P("fsdp"),
        P("fsdp", None),
        P("fsdp", None),
        P("fsdp", None),
    )
    group_size, fsdp_size = mesh.shape["group"], mesh.shape["fsdp"]

    def local(*arrays):
        if group_size == 16 and fsdp_size == 2 and arrays[0].shape[0] == 2:
            return paired_local(*arrays)
        return plain_local(*arrays)

    return jax.shard_map(
        local,
        mesh=mesh,
        in_specs=placed,
        out_specs=(
            P("group", "fsdp", None),
            P("group", "fsdp", None),
            P("fsdp"),
            P("fsdp", None),
            P("fsdp", None),
            P("fsdp", None),
            P("fsdp", None),
            P("fsdp"),
            P("fsdp", None),
            P("fsdp", None),
            P("fsdp", None),
        ),
        check_vma=False,
    )
```

```python
import functools
import math

import jax
import jax.numpy as jnp
from jax import lax
from jax.experimental import pallas as pl
from jax.experimental.pallas import tpu as pltpu
from jax.sharding import PartitionSpec as P

HEADS = 18
KV_HEADS = 6
HEAD = 64
epsilon = 1e-05
rope_base = 10000.0
BLOCK = 256
WIDE = 128
VMEM_MOST = 66 * 1024 * 1024 - 3 * 1024 * 1024


def mm(left, right):
    return jnp.dot(left, right, preferred_element_type=jnp.float32)


def mm_nt(left, right):
    return lax.dot_general(
        left, right, (((1,), (1,)), ((), ())), preferred_element_type=jnp.float32
    )


def mm_tn(left, right):
    return lax.dot_general(
        left, right, (((0,), (0,)), ((), ())), preferred_element_type=jnp.float32
    )


def low(values):
    return values.astype(jnp.bfloat16)


def lanes_below(rows, period, limit):
    lane = lax.broadcasted_iota(jnp.int32, (rows, WIDE), 1)
    return lane % period < limit


def swap_halves(tile):
    ahead = pltpu.roll(tile, WIDE - HEAD // 2, 1)
    behind = pltpu.roll(tile, HEAD // 2, 1)
    return jnp.where(lanes_below(tile.shape[0], HEAD, HEAD // 2), ahead, behind)


def rope_tables(length):
    half_width = HEAD // 2
    freqs = jnp.exp(
        jnp.arange(half_width, dtype=jnp.float32) * (-2.0 * math.log(rope_base) / HEAD)
    )
    angles = jnp.arange(length, dtype=jnp.float32)[:, None] * freqs[None, :]
    cosines, sines = jnp.cos(angles), jnp.sin(angles)
    return (
        jnp.concatenate([cosines] * 4, axis=1),
        jnp.concatenate([-sines, sines] * 2, axis=1),
    )


def project_body(x_ref, gain_ref, w_ref, cos_ref, sin_ref, mix_w, gate_w,
                 normed_ref, qkv_ref, mix_full, gate_full, sems):
    step = pl.program_id(0)
    spreads = (
        Spread(mix_w, mix_full, SPREADS["mix"], sems, 0),
        Spread(gate_w, gate_full, SPREADS["gate"], sems, 1),
    )

    @pl.when(step == 0)
    def _():
        greet(("y",))
        for spread in spreads:
            spread.copy(0).start()

    values = x_ref[...].astype(jnp.float32)
    inverse = lax.rsqrt(jnp.mean(values * values, axis=-1, keepdims=True) + epsilon)
    normed = low(values * inverse * gain_ref[...])
    normed_ref[...] = normed
    cosines, sines = cos_ref[...], sin_ref[...]
    width = qkv_ref.shape[1]
    q_width, k_width = HEADS * HEAD, KV_HEADS * HEAD
    chunk = 384
    for at in range(0, width, chunk):
        wide = mm(normed, w_ref[:, at : at + chunk])
        for part in range(0, chunk, WIDE):
            tile = wide[:, part : part + WIDE]
            if at + part < q_width + k_width:
                tile = tile * cosines + swap_halves(tile) * sines
            if at + part < q_width:
                tile = tile * HEAD ** (-0.5)
            qkv_ref[:, at + part : at + part + WIDE] = low(tile)

    @pl.when(step == pl.num_programs(0) - 1)
    def _():
        for spread in spreads:
            spread.copy(0).wait()


def eighths(w):
    return w.reshape(8, w.shape[0] // 8, w.shape[1])


def project(x, gain, w, cosines, sines, mix_w, gate_w):
    length, width = x.shape
    out = w.shape[1]
    rows = pl.BlockSpec((BLOCK, width), lambda i: (i, 0))
    table = pl.BlockSpec((BLOCK, WIDE), lambda i: (i, 0))
    anywhere = pl.BlockSpec(memory_space=pl.ANY)
    return pl.pallas_call(
        project_body,
        grid=(length // BLOCK,),
        in_specs=[
            rows,
            pl.BlockSpec((1, width), lambda i: (0, 0)),
            pl.BlockSpec((width, out), lambda i: (0, 0), pipeline_mode=pl.Buffered(1)),
            table,
            table,
            anywhere,
            anywhere,
        ],
        out_specs=[rows, pl.BlockSpec((BLOCK, out), lambda i: (i, 0)), anywhere, anywhere],
        out_shape=[
            jax.ShapeDtypeStruct((length, width), jnp.bfloat16),
            jax.ShapeDtypeStruct((length, out), jnp.bfloat16),
        ]
        + [jax.ShapeDtypeStruct((16,) + eighths(w).shape[1:], w.dtype) for w in (mix_w, gate_w)],
        scratch_shapes=[pltpu.SemaphoreType.DMA((2, 2))],
        compiler_params=pltpu.CompilerParams(collective_id=6, has_side_effects=True),
        cost_estimate=pl.CostEstimate(
            flops=2 * length * width * out,
            bytes_accessed=2 * (2 * length * width + length * out + width * out),
            transcendentals=0,
        ),
        name="project",
    )(x, gain, w, cosines, sines, eighths(mix_w), eighths(gate_w))


MESH = pl.DeviceIdType.MESH
MASKS = {"core": 1, "x": 2, "zlo": 4, "zhi": 8}


def bit_of(name):
    if name == "y":
        return lax.axis_index("fsdp")
    return (lax.axis_index("group") // MASKS[name]) % 2


def peer_of(name):
    if name == "y":
        return {"fsdp": 1 - lax.axis_index("fsdp")}
    return {"group": lax.axis_index("group") + MASKS[name] * (1 - 2 * bit_of(name))}


def greet(names):
    barrier = pltpu.get_barrier_semaphore()
    for name in names:
        pl.semaphore_signal(barrier, inc=1, device_id=peer_of(name), device_id_type=MESH)
    pl.semaphore_wait(barrier, len(names))


def across(source, target, sems, slot, name):
    return pltpu.make_async_remote_copy(
        src_ref=source,
        dst_ref=target,
        send_sem=sems.at[0, slot],
        recv_sem=sems.at[1, slot],
        device_id=peer_of(name),
        device_id_type=MESH,
    )


class Spread:
    def __init__(self, shard, full, order, sems, slot, columns=None):
        self.shard, self.full, self.order, self.sems, self.slot = shard, full, order, sems, slot
        self.columns = columns

    def copy(self, stage):
        y = lax.axis_index("fsdp")
        index = 0
        for at, name in enumerate(self.order):
            index = index + bit_of(name) * 2**at
        slot = self.slot + stage
        where = (slice(None), slice(None)) if self.columns is None else (slice(None), self.columns)
        if stage == 0:
            return across(
                self.shard.at[index], self.full.at[(y * 8 + index,) + where], self.sems, slot, "y"
            )
        count = 2 ** (stage - 1)
        block = self.full.at[(pl.ds((1 - y) * 8 + index // count * count, count),) + where]
        return across(block, block, self.sems, slot, self.order[stage - 1])

    def advance(self, stage):
        if stage >= 0:
            self.copy(stage).wait_recv()
        if stage < len(self.order):
            self.copy(stage + 1).start()

    def finish(self, first=0):
        for stage in range(first, len(self.order) + 1):
            self.copy(stage).wait_send()


SPREADS = {
    "mix": ("x", "zlo", "core"),
    "gate": ("zlo", "x", "core"),
    "up": ("x", "zlo", "core"),
    "down": ("zlo", "x", "core"),
}


def fetch_body(inputs, query, key, value, gains, tokens, weight, both_gains,
               held, held_weight, sems, near):
    y = lax.axis_index("fsdp")
    q_width, k_width = query.shape[2], key.shape[2]
    places = (
        slice(0, q_width),
        slice(q_width, q_width + k_width),
        slice(q_width + k_width, q_width + 2 * k_width),
    )
    shards = (query, key, value)
    loads = [pltpu.make_async_copy(inputs.at[y], held, near.at[0])] + [
        pltpu.make_async_copy(shard, held_weight.at[:, :, place], near.at[1 + at])
        for at, (shard, place) in enumerate(zip(shards, places))
    ]
    for load in loads:
        load.start()
    greet(("y", "x", "zlo", "core"))
    index = bit_of("x") + 2 * bit_of("zlo") + 4 * bit_of("core")
    first = [
        across(shard.at[index], weight.at[y * 8 + index, :, place], sems, at, "y")
        for at, (shard, place) in enumerate(zip(shards, places))
    ]
    span = held.shape[0]
    swap = across(
        inputs.at[1 - y], tokens.at[pl.ds(pl.multiple_of(y * span, span), span)], sems, 3, "y"
    )
    gain_swap = across(gains, both_gains.at[y], sems, 4, "y")
    for copy in first + [gain_swap, swap]:
        copy.start()
    for load in loads:
        load.wait()
    stores = [
        pltpu.make_async_copy(
            held, tokens.at[pl.ds(pl.multiple_of(y * span, span), span)], near.at[4]
        ),
        pltpu.make_async_copy(held_weight, weight.at[pl.ds(y * 8, 8)], near.at[5]),
        pltpu.make_async_copy(gains, both_gains.at[y], near.at[6]),
    ]
    for store in stores:
        store.start()
    for copy in first:
        copy.wait_recv()
    later = []
    for at, name in enumerate(("x", "zlo", "core")):
        count = 2**at
        block = weight.at[pl.ds((1 - y) * 8 + index // count * count, count)]
        copy = across(block, block, sems, 5 + at, name)
        copy.start()
        copy.wait_recv()
        later.append(copy)
    swap.wait_recv()
    gain_swap.wait_recv()
    for copy in first + [gain_swap, swap] + later:
        copy.wait_send()
    for store in stores:
        store.wait()


def fetch(inputs, query, key, value, gains):
    span, width = inputs.shape[1:]
    total = query.shape[1] + 2 * key.shape[1]
    eight = lambda shard: shard.reshape(8, shard.shape[0] // 8, shard.shape[1])
    rows = query.shape[0] // 8
    anywhere = pl.BlockSpec(memory_space=pl.ANY)
    tokens, weight, both_gains = pl.pallas_call(
        fetch_body,
        in_specs=[anywhere] * 5,
        out_specs=[anywhere] * 3,
        out_shape=[
            jax.ShapeDtypeStruct((2 * span, width), inputs.dtype),
            jax.ShapeDtypeStruct((16, rows, total), query.dtype),
            jax.ShapeDtypeStruct((2,) + gains.shape, gains.dtype),
        ],
        scratch_shapes=[
            pltpu.VMEM((span, width), inputs.dtype),
            pltpu.VMEM((8, rows, total), query.dtype),
            pltpu.SemaphoreType.DMA((2, 8)),
            pltpu.SemaphoreType.DMA((7,)),
        ],
        compiler_params=pltpu.CompilerParams(collective_id=1, has_side_effects=True),
        name="fetch",
    )(inputs, eight(query), eight(key), eight(value), gains)
    return tokens, weight.reshape(16 * rows, total), both_gains


AXES = ("y", "x", "zlo", "zhi")


class Fold:
    def __init__(self, source, kept, received, order, sems, slot, near, near_slot):
        self.source, self.kept, self.received = source, kept, received
        self.order, self.sems, self.slot = order, sems, slot
        self.near, self.near_slot = near, near_slot

    def pick(self, stage, bit):
        left = [name for name in AXES if name not in self.order[:stage]]
        return (slice(None),) * left.index(self.order[stage]) + (bit,)

    def held(self, stage):
        return self.source if stage == 0 else self.received[stage - 1]

    def copy(self, stage):
        name = self.order[stage]
        source = self.held(stage).at[self.pick(stage, 1 - bit_of(name))]
        return across(source, self.received[stage], self.sems, self.slot + stage, name)

    def load(self):
        source = self.source.at[self.pick(0, bit_of(self.order[0]))]
        return pltpu.make_async_copy(source, self.kept, self.near.at[self.near_slot])

    def begin(self):
        self.copy(0).start()
        if self.kept is not None:
            self.load().start()

    def advance(self, stage):
        self.copy(stage).wait_recv()
        target = self.received[stage]
        lead = target.ndim - 2
        if stage == 0 and self.kept is not None:
            self.load().wait()
            mine, at, bit = self.kept, 0, None
        else:
            bit = bit_of(self.order[stage])
            mine, at = self.held(stage), len(self.pick(stage, 0)) - 1

        @pl.loop(0, 2**lead)
        def _(n):
            index = tuple(n // 2 ** (lead - 1 - k) % 2 for k in range(lead))
            from_ = index if bit is None else index[:at] + (bit,) + index[at:]
            total = target[index].astype(jnp.float32) + mine[from_].astype(jnp.float32)
            target[index] = low(total)

        if stage + 1 < len(self.order):
            self.copy(stage + 1).start()

    def finish(self):
        for stage in range(len(self.order)):
            self.copy(stage).wait_send()


class Rise:
    def __init__(self, whole, order, columns, sems, slot):
        self.whole, self.order, self.columns, self.sems, self.slot = whole, order, columns, sems, slot

    def block(self, stage):
        index = tuple(
            slice(None) if name in self.order[:stage] + ("zhi",) else bit_of(name)
            for name in AXES[1:]
        )
        if self.whole.ndim == 7:
            return [self.whole.at[(bit_of("core"), self.columns) + index]]
        return [self.whole.at[index + (slice(None), columns)] for columns in self.columns]

    def copies(self, stage, first=None):
        blocks = self.block(stage)
        count = len(blocks)
        return [
            across(
                block if first is None else first[at],
                block,
                self.sems,
                self.slot + stage * count + at,
                self.order[stage],
            )
            for at, block in enumerate(blocks)
        ]

    def begin(self, first):
        for copy in self.copies(0, first):
            copy.start()

    def advance(self, stage):
        for copy in self.copies(stage):
            copy.wait_recv()
        if stage + 1 < len(self.order):
            for copy in self.copies(stage + 1):
                copy.start()

    def finish(self):
        for stage in range(len(self.order)):
            for copy in self.copies(stage):
                copy.wait_send()


ORDERS = (("y", "x", "zlo"), ("x", "zlo", "y"), ("zlo", "y", "x"))
BACKS = (("zlo", "x", "core"), ("x", "zlo", "core"), ("zlo", "x", "core"))
LATE_ORDERS = (("y", "x", "zlo"), ("x", "y", "zlo"), ("y", "x", "zlo"))
PART_ORDERS = (("x", "y", "zlo"), ("y", "x", "zlo"), ("x", "y", "zlo"))
PART_BACKS = (("zlo", "x", "core"), ("x", "zlo", "core"), ("zlo", "x", "core"))


class Sums:
    def __init__(self, wholes, held, chunk, sems, slot, near, near_slot):
        gate, up, down = wholes
        self.held, self.near, self.near_slot = held, near, near_slot
        self.part = gate.shape[-1] // 8
        columns = hidden_columns(self.part, chunk)
        self.rises = [
            Rise(gate, BACKS[0], columns, sems, slot),
            Rise(up, BACKS[1], columns, sems, slot + 6),
            Rise(down, BACKS[2], chunk, sems, slot + 12),
        ]

    def pieces(self, f):
        if f == 2:
            return [self.held[f]]
        part = self.part
        return [self.held[f].at[:, :, side * part : (side + 1) * part] for side in range(2)]

    def stores(self, f):
        return [
            pltpu.make_async_copy(piece, block, self.near.at[self.near_slot + 2 * f + n])
            for n, (piece, block) in enumerate(zip(self.pieces(f), self.rises[f].block(0)))
        ]

    def begin(self, f):
        for store in self.stores(f):
            store.start()
        self.rises[f].begin(self.pieces(f))

    def follow(self, f):
        for store in self.stores(f):
            store.wait()
        self.rises[f].advance(0)


def hidden_columns(part, chunk):
    at = (2 * bit_of("core") + chunk) * part
    return [pl.ds(pl.multiple_of(side * 4 * part + at, WIDE), part) for side in range(2)]


def place_heads(tile, variants_ref):
    wide = tile.astype(jnp.float32)
    turned = pltpu.roll(wide, HEAD, 1)
    low_lanes = lanes_below(tile.shape[0], WIDE, HEAD)
    variants_ref[0] = low(jnp.where(low_lanes, wide, 0.0))
    variants_ref[1] = low(jnp.where(low_lanes, 0.0, turned))
    variants_ref[2] = low(jnp.where(low_lanes, turned, 0.0))
    variants_ref[3] = low(jnp.where(low_lanes, 0.0, wide))


def allowed_block(seg_k, seg_q, diagonal):
    same = seg_k == seg_q
    if diagonal:
        rows = lax.broadcasted_iota(jnp.int32, same.shape, 0)
        lanes = lax.broadcasted_iota(jnp.int32, same.shape, 1)
        same = same & (rows <= lanes)
    return same


def attend_body(
    q_ref, k_ref, v_ref, seg_col_ref, seg_row_ref, out_grad, mix_w, gate_w, up_w, down_w,
    mix_begun, gate_begun, mixed_ref, lse_ref, whole_grad, mix_full, gate_full, up_full, down_full,
    ks, vt, acc, stats, sems, near, held_mix, held_gate, held_up, held_down, held_grad
):
    block = pl.program_id(1)
    now = pl.program_id(0) * pl.num_programs(1) + block
    most = pl.num_programs(0) * pl.num_programs(1) - 1
    y = lax.axis_index("fsdp")
    spreads = {
        "mix": Spread(mix_w, mix_full, SPREADS["mix"], sems, 0),
        "gate": Spread(gate_w, gate_full, SPREADS["gate"], sems, 4),
        "up": Spread(up_w, up_full, SPREADS["up"], sems, 8),
        "down": Spread(down_w, down_full, SPREADS["down"], sems, 12),
    }
    span = out_grad.shape[1]
    mine = whole_grad.at[pl.ds(pl.multiple_of(y * span, span), span)]
    grad_swap = across(out_grad.at[1 - y], mine, sems, 16, "y")
    half = pl.ds(y * 8, 8)
    own = (
        (mix_w, held_mix, mix_full.at[half]),
        (gate_w, held_gate, gate_full.at[half]),
        (up_w, held_up, up_full.at[half]),
        (down_w, held_down, down_full.at[half]),
        (out_grad.at[y], held_grad, mine),
    )
    loads = [pltpu.make_async_copy(a, b, near.at[0, at]) for at, (a, b, _) in enumerate(own)]
    stores = [pltpu.make_async_copy(b, c, near.at[1, at]) for at, (_, b, c) in enumerate(own)]
    plan = {
        3: (("mix", 1),),
        4: (("up", 0), ("gate", 1)),
        7: (("down", 0), ("up", 1), ("mix", 2)),
        11: (("down", 1),),
    }

    @pl.when(now == 0)
    def _():
        for load in loads:
            load.start()
        greet(("y", "x", "zlo", "core"))
        spreads["up"].advance(-1)
        spreads["down"].advance(-1)
        grad_swap.start()
        spreads["gate"].copy(1).start()
        spreads["mix"].copy(1).start()

    @pl.when(now == 1)
    def _():
        for load, store in zip(loads, stores):
            load.wait()
            store.start()

    for at, steps in plan.items():

        @pl.when(now == at)
        def _(steps=steps):
            for name, stage in steps:
                spreads[name].advance(stage)

    @pl.when(block == 0)
    def _():
        place_heads(k_ref[...], ks)
        vt[...] = low(v_ref[...].astype(jnp.float32).T)

    acc[...] = jnp.zeros_like(acc)
    stats[0] = jnp.full((8, BLOCK), -1e30, jnp.float32)
    stats[1] = jnp.zeros((8, BLOCK), jnp.float32)
    seg_q = seg_row_ref[...]

    def step(j, diagonal):
        rows = pl.ds(pl.multiple_of(j * BLOCK, BLOCK), BLOCK)
        seg_k = seg_col_ref[rows, :]
        allowed = allowed_block(seg_k, seg_q, diagonal)
        scores = []
        for head in range(6):
            part, side, kv = head // 2, head % 2, head // 3
            q_tile = q_ref[:, part * WIDE : (part + 1) * WIDE]
            scores.append(jnp.where(allowed, mm_nt(ks[kv * 2 + side, rows, :], q_tile), -1e30))
        before = stats[0]
        highest = [
            jnp.maximum(before[head : head + 1], jnp.max(scores[head], axis=0, keepdims=True))
            for head in range(6)
        ]
        chances = [jnp.exp(scores[head] - highest[head]) for head in range(6)]
        shrink = [jnp.exp(before[head : head + 1] - highest[head]) for head in range(6)]
        for head in range(6):
            kv = head // 3
            stats[0, head : head + 1, :] = highest[head]
            stats[1, head : head + 1, :] = stats[1, head : head + 1, :] * shrink[head] + jnp.sum(
                chances[head], axis=0, keepdims=True
            )
            values = vt[kv * HEAD : (kv + 1) * HEAD, rows]
            at = head * HEAD
            acc[at : at + HEAD, :] = acc[at : at + HEAD, :] * shrink[head] + mm(
                values, low(chances[head])
            )

    @pl.loop(0, block)
    def _(j):
        step(j, False)

    step(block, True)
    total = stats[1]
    for part in range(3):
        at = part * WIDE
        both = jnp.concatenate(
            [
                acc[at : at + HEAD, :] / total[2 * part : 2 * part + 1, :],
                acc[at + HEAD : at + WIDE, :] / total[2 * part + 1 : 2 * part + 2, :],
            ],
            axis=0,
        )
        mixed_ref[:, at : at + WIDE] = low(both.T)
    lse_ref[0] = stats[0] + jnp.log(jnp.maximum(total, 1e-30))

    @pl.when(now == most)
    def _():
        spreads["gate"].advance(2)
        spreads["up"].advance(2)
        spreads["down"].advance(2)
        for name, spread in spreads.items():
            spread.advance(3)
            spread.finish(1 if name in ("mix", "gate") else 0)
        grad_swap.wait()
        for store in stores:
            store.wait()


def attend(qkv, seg_col, seg_row, out_grad, mix_w, gate_w, up_w, down_w, mix_begun, gate_begun):
    length = qkv.shape[0]
    pairs = KV_HEADS // 2
    q_tiles = HEADS * HEAD // WIDE
    anywhere = pl.BlockSpec(memory_space=pl.ANY)
    shards = [eighths(w) for w in (mix_w, gate_w, up_w, down_w)]
    fulls = [jax.ShapeDtypeStruct((16,) + w.shape[1:], w.dtype) for w in shards]
    found = pl.pallas_call(
        attend_body,
        grid=(pairs, length // BLOCK),
        in_specs=[
            pl.BlockSpec((BLOCK, 3 * WIDE), lambda b, i: (i, b)),
            pl.BlockSpec((length, WIDE), lambda b, i: (0, q_tiles + b)),
            pl.BlockSpec((length, WIDE), lambda b, i: (0, q_tiles + pairs + b)),
            pl.BlockSpec((length, 1), lambda b, i: (0, 0)),
            pl.BlockSpec((1, BLOCK), lambda b, i: (0, i)),
        ]
        + [anywhere] * 7,
        out_specs=[
            pl.BlockSpec((BLOCK, 3 * WIDE), lambda b, i: (i, b)),
            pl.BlockSpec((1, 8, BLOCK), lambda b, i: (b, 0, i)),
        ]
        + [anywhere] * 5,
        out_shape=[
            jax.ShapeDtypeStruct((length, HEADS * HEAD), jnp.bfloat16),
            jax.ShapeDtypeStruct((pairs, 8, length), jnp.float32),
            jax.ShapeDtypeStruct((length, out_grad.shape[2]), out_grad.dtype),
        ]
        + fulls,
        input_output_aliases={10: 3, 11: 4},
        scratch_shapes=[
            pltpu.VMEM((4, length, WIDE), jnp.bfloat16),
            pltpu.VMEM((WIDE, length), jnp.bfloat16),
            pltpu.VMEM((6 * HEAD, BLOCK), jnp.float32),
            pltpu.VMEM((2, 8, BLOCK), jnp.float32),
            pltpu.SemaphoreType.DMA((2, 17)),
            pltpu.SemaphoreType.DMA((2, 5)),
        ]
        + [pltpu.VMEM(w.shape, w.dtype) for w in shards]
        + [pltpu.VMEM(out_grad.shape[1:], out_grad.dtype)],
        compiler_params=pltpu.CompilerParams(
            collective_id=2, has_side_effects=True, vmem_limit_bytes=VMEM_MOST
        ),
        cost_estimate=pl.CostEstimate(
            flops=16 * length * length * HEADS * HEAD // 2,
            bytes_accessed=6 * length * HEADS * HEAD,
            transcendentals=HEADS * length * length // 2,
        ),
        name="attend",
    )(qkv, qkv, qkv, seg_col, seg_row, out_grad, *shards, mix_begun, gate_begun)
    return tuple(found[:3]) + tuple(w.reshape(-1, w.shape[2]) for w in found[3:])


def attend_back_body(
    q_ref, k_ref, v_ref, grad_ref, mixed_ref, lse_ref, seg_col_ref, seg_row_ref, cos_ref, sin_ref,
    gate_term, up_term, down_term, gate_third, up_third, down_third,
    dq_ref, dk_ref, dv_ref, gate_left, up_left, down_left, gate_sum, up_sum, down_sum,
    ks, vs, kt, k_acc, v_acc, q_acc, sides, delta, sems, near,
    kept_h, r1_h, r2_h, r3_h, own_h, came_h, kept_d, r1_d, r2_d, r3_d, own_d, came_d
):
    block = pl.program_id(1)
    length = k_ref.shape[0]
    now = pl.program_id(0) * pl.num_programs(1) + block
    most = pl.num_programs(0) * pl.num_programs(1) - 1
    pick = lambda pair, single: [pair.at[0], pair.at[1], single]
    kept, owns, came = pick(kept_h, kept_d), pick(own_h, own_d), pick(came_h, came_d)
    ones, twos, threes = pick(r1_h, r1_d), pick(r2_h, r2_d), pick(r3_h, r3_d)
    folds = [
        Fold(term, kept[f], [ones[f], twos[f], threes[f]], LATE_ORDERS[f], sems, 3 * f, near, f)
        for f, term in enumerate((gate_term, up_term, down_term))
    ]
    loads = [
        pltpu.make_async_copy(third, owns[f], near.at[3 + f])
        for f, third in enumerate((gate_third, up_third, down_third))
    ]
    zs = [across(owns[f], came[f], sems, 9 + f, "zhi") for f in range(3)]
    stores = [
        pltpu.make_async_copy(threes[f], left, near.at[6 + f])
        for f, left in enumerate((gate_left, up_left, down_left))
    ]
    sums = Sums((gate_sum, up_sum, down_sum), came, 0, sems, 12, near, 9)

    def settle(f):
        zs[f].wait_recv()
        for n in range(2):
            came[f][n] = low(owns[f][n].astype(jnp.float32) + came[f][n].astype(jnp.float32))
        sums.begin(f)

    @pl.when(now == 0)
    def _():
        for load in loads:
            load.start()
        greet(("core",) + AXES)
        for fold in folds:
            fold.begin()
        for load, copy in zip(loads, zs):
            load.wait()
            copy.start()

    @pl.when(now == 5)
    def _():
        folds[0].advance(0)
        folds[1].advance(0)

    @pl.when(now == 7)
    def _():
        settle(0)
        settle(1)

    @pl.when(now == 8)
    def _():
        settle(2)
        folds[0].advance(1)

    @pl.when(now == 9)
    def _():
        sums.follow(0)
        sums.follow(1)

    @pl.when(now == 10)
    def _():
        folds[2].advance(0)
        sums.follow(2)

    @pl.when(block == 0)
    def _():
        place_heads(k_ref[...], ks)
        place_heads(v_ref[...], vs)
        kt[...] = low(k_ref[...].astype(jnp.float32).T)
        k_acc[...] = jnp.zeros_like(k_acc)
        v_acc[...] = jnp.zeros_like(v_acc)

    q_acc[...] = jnp.zeros_like(q_acc)
    seg_q = seg_row_ref[...]
    low_lanes = lanes_below(BLOCK, WIDE, HEAD)
    zero = jnp.zeros((BLOCK, WIDE), jnp.bfloat16)
    for part in range(3):
        at = part * WIDE
        tile, grad = q_ref[:, at : at + WIDE], grad_ref[:, at : at + WIDE]
        sides[0, part, 0:BLOCK, :] = jnp.where(low_lanes, tile, zero)
        sides[0, part, BLOCK : 2 * BLOCK, :] = jnp.where(low_lanes, zero, tile)
        sides[1, part, 0:BLOCK, :] = jnp.where(low_lanes, grad, zero)
        sides[1, part, BLOCK : 2 * BLOCK, :] = jnp.where(low_lanes, zero, grad)
        product = (grad.astype(jnp.float32) * mixed_ref[:, at : at + WIDE].astype(jnp.float32)).T
        delta[2 * part : 2 * part + 1, :] = jnp.sum(product[:HEAD], axis=0, keepdims=True)
        delta[2 * part + 1 : 2 * part + 2, :] = jnp.sum(product[HEAD:], axis=0, keepdims=True)

    def step(j, diagonal):
        rows = pl.ds(pl.multiple_of(j * BLOCK, BLOCK), BLOCK)
        allowed = allowed_block(seg_col_ref[rows, :], seg_q, diagonal)
        heads = range(6)
        tiles = [q_ref[:, p * WIDE : (p + 1) * WIDE] for p in range(3)]
        grads = [grad_ref[:, p * WIDE : (p + 1) * WIDE] for p in range(3)]
        scores = [mm_nt(ks[h // 3 * 2 + h % 2, rows, :], tiles[h // 2]) for h in heads]
        onto = [mm_nt(vs[h // 3 * 2 + h % 2, rows, :], grads[h // 2]) for h in heads]
        chances = [
            jnp.exp(jnp.where(allowed, scores[h], -1e30) - lse_ref[0, h : h + 1, :]) for h in heads
        ]
        score_grads = [low(chances[h] * (onto[h] - delta[h : h + 1, :])) for h in heads]
        chances = [low(chances[h]) for h in heads]
        for h in heads:
            to = h * HEAD
            q_acc[to : to + HEAD, :] += mm(kt[h // 3 * HEAD : (h // 3 + 1) * HEAD, rows], score_grads[h])
        for p in range(3):
            v_acc[p, rows, :] += mm(jnp.concatenate(chances[2 * p : 2 * p + 2], axis=1), sides[1, p])
            k_acc[p, rows, :] += mm(jnp.concatenate(score_grads[2 * p : 2 * p + 2], axis=1), sides[0, p])

    @pl.loop(0, block)
    def _(j):
        step(j, False)

    step(block, True)
    here = pl.ds(pl.multiple_of(block * BLOCK, BLOCK), BLOCK)
    for part in range(3):
        at = part * WIDE
        tile = q_acc[at : at + WIDE, :].T * HEAD ** (-0.5)
        tile = tile * cos_ref[here, :] - swap_halves(tile) * sin_ref[here, :]
        dq_ref[:, at : at + WIDE] = low(tile)

    @pl.when(block == length // BLOCK - 1)
    def _():
        for j in range(0, length, BLOCK):
            rows = slice(j, j + BLOCK)

            def gather(acc):
                first, middle, last = acc[0, rows, :], acc[1, rows, :], acc[2, rows, :]
                return middle + jnp.where(
                    low_lanes, first + pltpu.roll(first, HEAD, 1), last + pltpu.roll(last, HEAD, 1)
                )

            tile = gather(k_acc)
            tile = tile * cos_ref[rows, :] - swap_halves(tile) * sin_ref[rows, :]
            dk_ref[rows, :] = low(tile)
            dv_ref[rows, :] = low(gather(v_acc))

    @pl.when(now == most)
    def _():
        folds[1].advance(1)
        folds[2].advance(1)
        folds[0].advance(2)
        for f in range(3):
            sums.rises[f].advance(1)
        folds[1].advance(2)
        folds[2].advance(2)
        for store in stores:
            store.start()
        for f in range(3):
            sums.rises[f].advance(2)
        for fold in folds + sums.rises:
            fold.finish()
        for copy in zs:
            copy.wait_send()
        for store in stores:
            store.wait()


def attend_back(qkv, mixed_grad, mixed, lse, seg_col, seg_row, cosines, sines, *terms):
    length = qkv.shape[0]
    rows, wide = terms[0].shape[4:]
    down_rows, width = terms[2].shape[4:]
    anywhere = pl.BlockSpec(memory_space=pl.ANY)
    pairs = KV_HEADS // 2
    q_tiles = HEADS * HEAD // WIDE
    q_block = pl.BlockSpec((BLOCK, 3 * WIDE), lambda b, i: (i, b))
    kv_block = pl.BlockSpec((length, WIDE), lambda b, i: (0, b))
    table = pl.BlockSpec((length, WIDE), lambda b, i: (0, 0), pipeline_mode=pl.Buffered(1))
    return pl.pallas_call(
        attend_back_body,
        grid=(pairs, length // BLOCK),
        in_specs=[
            q_block,
            pl.BlockSpec((length, WIDE), lambda b, i: (0, q_tiles + b)),
            pl.BlockSpec((length, WIDE), lambda b, i: (0, q_tiles + pairs + b)),
            q_block,
            q_block,
            pl.BlockSpec((1, 8, BLOCK), lambda b, i: (b, 0, i)),
            pl.BlockSpec((length, 1), lambda b, i: (0, 0)),
            pl.BlockSpec((1, BLOCK), lambda b, i: (0, i)),
            table,
            table,
        ]
        + [anywhere] * 6,
        out_specs=[q_block, kv_block, kv_block] + [anywhere] * 6,
        out_shape=[
            jax.ShapeDtypeStruct((length, HEADS * HEAD), jnp.bfloat16),
            jax.ShapeDtypeStruct((length, KV_HEADS * HEAD), jnp.bfloat16),
            jax.ShapeDtypeStruct((length, KV_HEADS * HEAD), jnp.bfloat16),
        ]
        + [
            jax.ShapeDtypeStruct((2,) + shape, jnp.bfloat16)
            for shape in ((rows, wide), (rows, wide), (down_rows, width))
        ]
        + [
            jax.ShapeDtypeStruct((2, 2, 2, rows, 4 * wide), jnp.bfloat16),
            jax.ShapeDtypeStruct((2, 2, 2, rows, 4 * wide), jnp.bfloat16),
            jax.ShapeDtypeStruct((2, 2, 2, 2, 2, down_rows, width), jnp.bfloat16),
        ],
        scratch_shapes=[
            pltpu.VMEM((4, length, WIDE), jnp.bfloat16),
            pltpu.VMEM((4, length, WIDE), jnp.bfloat16),
            pltpu.VMEM((WIDE, length), jnp.bfloat16),
            pltpu.VMEM((3, length, WIDE), jnp.float32),
            pltpu.VMEM((3, length, WIDE), jnp.float32),
            pltpu.VMEM((6 * HEAD, BLOCK), jnp.float32),
            pltpu.VMEM((2, 3, 2 * BLOCK, WIDE), jnp.bfloat16),
            pltpu.VMEM((8, BLOCK), jnp.float32),
            pltpu.SemaphoreType.DMA((2, 27)),
            pltpu.SemaphoreType.DMA((14,)),
        ]
        + [pltpu.VMEM((2,) + (2,) * left + (rows, wide), jnp.bfloat16) for left in (3, 3, 2, 1, 1, 1)]
        + [pltpu.VMEM((2,) * left + (down_rows, width), jnp.bfloat16) for left in (3, 3, 2, 1, 1, 1)],
        compiler_params=pltpu.CompilerParams(
            collective_id=3, has_side_effects=True, vmem_limit_bytes=VMEM_MOST
        ),
        cost_estimate=pl.CostEstimate(
            flops=40 * length * length * HEADS * HEAD // 2,
            bytes_accessed=12 * length * HEADS * HEAD,
            transcendentals=HEADS * length * length // 2,
        ),
        name="attend_back",
    )(qkv, qkv, qkv, mixed_grad, mixed, lse, seg_col, seg_row, cosines, sines, *terms)


def mix_body(x_ref, mixed_ref, w_ref, gain_ref, residual_ref, normed_ref, turned_ref):
    residual = x_ref[...].astype(jnp.float32) + mm(mixed_ref[...], w_ref[...])
    residual_ref[...] = residual
    inverse = lax.rsqrt(jnp.mean(residual * residual, axis=-1, keepdims=True) + epsilon)
    normed = residual * inverse * gain_ref[...]
    normed_ref[...] = low(normed)
    turned_ref[...] = low(normed.T)


def mix(x, mixed, w, gain):
    length, width = x.shape
    rows = pl.BlockSpec((BLOCK, width), lambda i: (i, 0))
    return pl.pallas_call(
        mix_body,
        grid=(length // BLOCK,),
        in_specs=[
            rows,
            rows,
            pl.BlockSpec(w.shape, lambda i: (0, 0), pipeline_mode=pl.Buffered(1)),
            pl.BlockSpec((1, width), lambda i: (0, 0)),
        ],
        out_specs=[rows, rows, pl.BlockSpec((width, BLOCK), lambda i: (0, i))],
        out_shape=[
            jax.ShapeDtypeStruct((length, width), jnp.float32),
            jax.ShapeDtypeStruct((length, width), jnp.bfloat16),
            jax.ShapeDtypeStruct((width, length), jnp.bfloat16),
        ],
        cost_estimate=pl.CostEstimate(
            flops=2 * length * width * width, bytes_accessed=12 * length * width, transcendentals=0
        ),
        name="mix",
    )(x, mixed, w, gain)


def norm_grad(grad, gain, scaled, inverse):
    weighted = grad * gain
    return inverse * (weighted - scaled * jnp.mean(weighted * scaled, axis=-1, keepdims=True))


def turn_body(residual_ref, out_ref, back_ref, c_ref, mixed_ref, w_ref, gain_ref,
              result_ref, grad_ref, mixed_grad_ref, term_ref, gain_term_ref, total):
    step = pl.program_id(0)
    residual = residual_ref[...]
    result_ref[...] = low(residual + out_ref[...])
    inverse = lax.rsqrt(jnp.mean(residual * residual, axis=-1, keepdims=True) + epsilon)
    scaled = residual * inverse
    normed_grad = back_ref[...]
    gain_term = jnp.sum(normed_grad * scaled, axis=0, keepdims=True)
    grad = c_ref[...].astype(jnp.float32) + norm_grad(normed_grad, gain_ref[...], scaled, inverse)
    grad_ref[...] = grad
    grad_low = low(grad)
    mixed_grad_ref[...] = low(mm_nt(grad_low, w_ref[...]))
    term = mm_tn(mixed_ref[...], grad_low)

    @pl.when(step == 0)
    def _():
        total[...] = term
        gain_term_ref[...] = jnp.broadcast_to(gain_term, gain_term_ref.shape)

    @pl.when(step > 0)
    def _():
        total[...] += term
        gain_term_ref[...] += jnp.broadcast_to(gain_term, gain_term_ref.shape)

    @pl.when(step == pl.num_programs(0) - 1)
    def _():
        term_ref[...] = low(total[...])


def turn(residual, out, back, c, mixed, w, gain):
    length, width = residual.shape
    rows = pl.BlockSpec((BLOCK, width), lambda i: (i, 0))
    whole = lambda shape: pl.BlockSpec(shape, lambda i: (0, 0), pipeline_mode=pl.Buffered(1))
    return pl.pallas_call(
        turn_body,
        grid=(length // BLOCK,),
        in_specs=[rows] * 5 + [whole(w.shape), pl.BlockSpec((1, width), lambda i: (0, 0))],
        out_specs=[
            rows, rows, rows, whole((width, width)), pl.BlockSpec((8, width), lambda i: (0, 0)),
        ],
        out_shape=[
            jax.ShapeDtypeStruct((length, width), jnp.bfloat16),
            jax.ShapeDtypeStruct((length, width), jnp.float32),
            jax.ShapeDtypeStruct((length, width), jnp.bfloat16),
            jax.ShapeDtypeStruct((width, width), jnp.bfloat16),
            jax.ShapeDtypeStruct((8, width), jnp.float32),
        ],
        scratch_shapes=[pltpu.VMEM((width, width), jnp.float32)],
        compiler_params=pltpu.CompilerParams(vmem_limit_bytes=VMEM_MOST),
        cost_estimate=pl.CostEstimate(
            flops=4 * length * width * width, bytes_accessed=32 * length * width, transcendentals=0
        ),
        name="turn",
    )(residual, out, back, c, mixed, w, gain)


def end_body(dq_ref, dk_ref, dv_ref, normed_ref, x_ref, grad_ref, w_ref, gain_ref, feed_gain_ref,
             mix_term, result, gate_left, up_left, down_left, gate_begun, up_begun, down_begun,
             gate, up, down, sums, outputs, input_grads, gain_sums,
             turned, term, tokens, r0, r1, r2, r3, exchanged, hidden_b, hidden_came,
             down_b, down_came, gain_held, gain_came, rows_held, sems, near):
    step = pl.program_id(0)
    last = pl.num_programs(0) - 1
    rows_each = x_ref.shape[0]
    length = normed_ref.shape[0]
    q_width, k_width = dq_ref.shape[1], dk_ref.shape[1]
    core, y = bit_of("core"), lax.axis_index("fsdp")
    third = term.shape[-1] // 3
    wide = third // 2
    everything = (slice(None),) * 4 + (slice(None),)
    columns = [
        [pl.ds(pl.multiple_of(t * third + side * wide, WIDE), wide) for side in (core, 1 - core)]
        for t in range(3)
    ]
    span = outputs.shape[1]
    rows = [pl.ds(pl.multiple_of(at * span, span), span) for at in (y, 1 - y)]
    pick = lambda pair, single: [pair.at[0], pair.at[1], single]
    b_left, came = pick(hidden_b, down_b), pick(hidden_came, down_came)
    loads = [
        pltpu.make_async_copy(whole, held, near.at[f])
        for f, (whole, held) in enumerate(zip((gate_left, up_left, down_left), b_left))
    ]
    mix_load = pltpu.make_async_copy(
        mix_term, term.at[everything + (slice(q_width + 2 * k_width, term.shape[-1]),)], near.at[6]
    )
    result_load = pltpu.make_async_copy(result.at[rows[0]], rows_held, near.at[7])
    result_store = pltpu.make_async_copy(rows_held, outputs.at[y], near.at[8])
    token_store = pltpu.make_async_copy(tokens.at[rows[0]], input_grads.at[y], near.at[9])
    zs = [across(b_left[f], came[f], sems, f, "zhi") for f in range(3)]
    hidden = Sums((gate, up, down), came, 1, sems, 60, near, 10)
    cores = [
        across(term.at[everything + (columns[t][1],)], r0.at[t], sems, 27 + t, "core")
        for t in range(3)
    ]
    parts = [
        Fold(r0.at[t], None, [r1.at[t], r2.at[t], r3.at[t]], PART_ORDERS[t], sems, 30 + 3 * t, None, None)
        for t in range(3)
    ]
    part_zs = [across(r3.at[t], exchanged.at[t], sems, 39 + t, "zhi") for t in range(3)]
    tops = [Rise(sums, PART_BACKS[t], [columns[t][0]], sems, 42 + 3 * t) for t in range(3)]
    swaps = [
        across(result.at[rows[1]], outputs.at[y], sems, 51, "y"),
        across(tokens.at[rows[1]], input_grads.at[y], sems, 52, "y"),
    ]
    names = ("y", "core", "x", "zlo", "zhi")
    gain_copies = [
        across(gain_held.at[at], gain_came.at[at], sems, 53 + at, name)
        for at, name in enumerate(names)
    ]

    def part_store(t):
        return pltpu.make_async_copy(exchanged.at[t], tops[t].block(0)[0], near.at[20 + t])

    def settle(copy, mine, theirs):
        copy.wait_recv()
        for n in range(2):
            theirs[n] = low(mine[n].astype(jnp.float32) + theirs[n].astype(jnp.float32))

    def hidden_settle(f):
        settle(zs[f], b_left[f], came[f])
        hidden.begin(f)

    def part_settle(t):
        settle(part_zs[t], r3.at[t], exchanged.at[t])
        part_store(t).start()
        tops[t].begin([exchanged.at[t]])

    def core_sum(t):
        cores[t].wait_recv()

        @pl.loop(0, 16)
        def _(n):
            index = (n // 8, n // 4 % 2, n // 2 % 2, n % 2)
            mine = term[index + (slice(None), columns[t][0])]
            r0[(t,) + index] = low(r0[(t,) + index].astype(jnp.float32) + mine.astype(jnp.float32))

        parts[t].begin()

    def gain_step(at):
        gain_copies[at].wait_recv()
        gain_held[at + 1] = gain_held[at] + gain_came[at]
        if at + 1 < len(names):
            gain_copies[at + 1].start()

    @pl.when(step == 0)
    def _():
        for load in [mix_load] + loads + [result_load]:
            load.start()
        greet(names)
        mix_load.wait()
        cores[2].start()
        for f in range(3):
            loads[f].wait()
            zs[f].start()
        for at in range(0, length, BLOCK):
            turned[:, at : at + BLOCK] = normed_ref[at : at + BLOCK, :].T

    @pl.when(step == 1)
    def _():
        core_sum(2)
        result_load.wait()
        result_store.start()

    @pl.when(step == 3)
    def _():
        cores[0].start()

    @pl.when(step == 4)
    def _():
        core_sum(0)

    @pl.when(step == 5)
    def _():
        cores[1].start()
        parts[2].advance(0)

    @pl.when(step == 6)
    def _():
        core_sum(1)
        hidden_settle(0)

    @pl.when(step == 7)
    def _():
        parts[0].advance(0)
        hidden_settle(1)

    @pl.when(step == 8)
    def _():
        hidden.follow(0)

    def chunk(low_rows, at):
        wide_term = mm(turned[...], low_rows).reshape(16, turned.shape[0] // 16, k_width)
        for n in range(16):
            index = (n // 8, n // 4 % 2, n // 2 % 2, n % 2, slice(None), slice(at, at + k_width))
            term[index] = low(wide_term[n])

    for at in range(3):

        @pl.when(step == at)
        def _(at=at):
            chunk(dq_ref[:, at * k_width : (at + 1) * k_width], at * k_width)

    @pl.when(step == 3)
    def _():
        chunk(dk_ref[...], q_width)

    @pl.when(step == 4)
    def _():
        chunk(dv_ref[...], q_width + k_width)

    first = last + 1 - length // rows_each

    @pl.when(step >= first)
    def _():
        here = pl.ds(pl.multiple_of((step - first) * rows_each, rows_each), rows_each)
        normed_grad = (
            mm_nt(dq_ref[here, :], w_ref[:, :q_width])
            + mm_nt(dk_ref[here, :], w_ref[:, q_width : q_width + k_width])
            + mm_nt(dv_ref[here, :], w_ref[:, q_width + k_width :])
        )
        values = x_ref[...].astype(jnp.float32)
        inverse = lax.rsqrt(jnp.mean(values * values, axis=-1, keepdims=True) + epsilon)
        scaled = values * inverse
        gain_term = jnp.sum(normed_grad * scaled, axis=0, keepdims=True)
        tokens[here, :] = low(
            grad_ref[...] + norm_grad(normed_grad, gain_ref[...], scaled, inverse)
        )

        @pl.when(step == first)
        def _():
            gain_held[0, 0:1, :] = gain_term
            gain_held[0, 1:2, :] = feed_gain_ref[0:1, :]
            gain_held[0, 2:8, :] = jnp.zeros_like(gain_held[0, 2:8, :])

        @pl.when(step > first)
        def _():
            gain_held[0, 0:1, :] += gain_term

    @pl.when(step == last)
    def _():
        gain_copies[0].start()
        token_store.start()
        for copy in swaps:
            copy.start()
        hidden_settle(2)
        hidden.follow(1)
        gain_step(0)
        parts[1].advance(0)
        hidden.follow(2)
        gain_step(1)
        parts[2].advance(1)
        parts[1].advance(1)
        gain_step(2)
        parts[0].advance(1)
        hidden.rises[0].advance(1)
        for t in (2, 1, 0):
            parts[t].advance(2)
            part_zs[t].start()
        gain_step(3)
        hidden.rises[1].advance(1)
        hidden.rises[2].advance(1)
        for t in (2, 1, 0):
            part_settle(t)
        gain_step(4)
        for t in (2, 1, 0):
            part_store(t).wait()
            tops[t].advance(0)
        for t in (2, 1, 0):
            tops[t].advance(1)
        every = hidden.rises + tops
        for one in every:
            one.advance(2)
        for copy in cores + swaps + gain_copies + zs + part_zs:
            copy.wait_send()
        for one in every + parts:
            one.finish()
        for copy in swaps:
            copy.wait_recv()
        result_store.wait()
        token_store.wait()
        gain_sums[...] = gain_held[len(names)]


def end(dq, dk, dv, normed, x, grad, w, gain, feed_gain_term, mix_term, result, *sums):
    length, width = x.shape
    k_width = dk.shape[1]
    total = w.shape[1] + mix_term.shape[1]
    wide = total // 6
    mix_term = mix_term.reshape(2, 2, 2, 2, mix_term.shape[0] // 16, mix_term.shape[1])
    rows = mix_term.shape[4]
    hidden_rows, hidden = sums[0].shape[1:]
    down_rows = sums[2].shape[1]
    chunks, blocks = w.shape[1] // k_width, length // BLOCK
    block = pl.BlockSpec((BLOCK, width), lambda i: (jnp.maximum(i - chunks, 0), 0))
    whole = lambda a: pl.BlockSpec(a.shape, lambda i: (0,) * a.ndim, pipeline_mode=pl.Buffered(1))
    anywhere = pl.BlockSpec(memory_space=pl.ANY)
    both = jax.ShapeDtypeStruct((2, length // 2, width), result.dtype)
    low_type = jnp.bfloat16
    return pl.pallas_call(
        end_body,
        grid=(chunks + blocks,),
        in_specs=[whole(dq), whole(dk), whole(dv), whole(normed), block, block, whole(w), whole(gain),
                  whole(feed_gain_term)] + [anywhere] * 8,
        out_specs=[anywhere] * 6 + [pl.BlockSpec((8, width), lambda i: (0, 0))],
        out_shape=[
            jax.ShapeDtypeStruct((2, 2, 2, hidden_rows, 4 * hidden), low_type),
            jax.ShapeDtypeStruct((2, 2, 2, hidden_rows, 4 * hidden), low_type),
            jax.ShapeDtypeStruct((2, 2, 2, 2, 2, down_rows, width), low_type),
            jax.ShapeDtypeStruct((2, 2, 2, rows, total), low_type),
            both,
            both,
            jax.ShapeDtypeStruct((8, width), jnp.float32),
        ],
        input_output_aliases={14: 0, 15: 1, 16: 2},
        scratch_shapes=[
            pltpu.VMEM((width, length), low_type),
            pltpu.VMEM((2, 2, 2, 2, rows, total), low_type),
            pltpu.VMEM((length, width), low_type),
        ]
        + [pltpu.VMEM((3,) + (2,) * left + (rows, wide), low_type) for left in (4, 3, 2, 1, 1)]
        + [pltpu.VMEM((2, 2, hidden_rows, hidden), low_type)] * 2
        + [pltpu.VMEM((2, down_rows, width), low_type)] * 2
        + [
            pltpu.VMEM((6, 8, width), jnp.float32),
            pltpu.VMEM((5, 8, width), jnp.float32),
            pltpu.VMEM((length // 2, width), low_type),
            pltpu.SemaphoreType.DMA((2, 75)),
            pltpu.SemaphoreType.DMA((23,)),
        ],
        compiler_params=pltpu.CompilerParams(
            collective_id=4, has_side_effects=True, vmem_limit_bytes=VMEM_MOST
        ),
        name="end",
    )(dq, dk, dv, normed, x, grad, w, gain, feed_gain_term, mix_term, result, *sums)


def sixteenth(n):
    return (n // 8, n // 4 % 2, n // 2 % 2, n % 2)


def feed_body(normed_ref, turned_ref, c_ref, gate_w, up_w, down_w,
              out_ref, back_ref, gate_a, up_a, down_a, gate_b, up_b, down_b,
              gate_v, up_v, down_v, hidden_t, gate_low, up_low,
              hold_h, hold_d, came_h, came_d, own_h, own_d,
              r1_h, r2_h, r3_h, r1_d, r2_d, r3_d, sems, near, weight_sems, free):
    step = pl.program_id(0)
    length, width = normed_ref.shape
    core = bit_of("core")
    slot = step % 2
    part = gate_v.shape[2] // 2
    side_width = gate_w.shape[1] // 2

    def weights(of, into):
        owner = (core + 1 + of) % 2
        at = (2 * owner + of // 2) * part
        found = []
        for side in range(2):
            here = pl.ds(pl.multiple_of(side * side_width + at, WIDE), part)
            there = slice(side * part, (side + 1) * part)
            found += [
                (gate_w.at[:, here], gate_v.at[into, :, there]),
                (up_w.at[:, here], up_v.at[into, :, there]),
                (down_w.at[here], down_v.at[into, there]),
            ]
        return [
            pltpu.make_async_copy(a, b, weight_sems.at[into, n]) for n, (a, b) in enumerate(found)
        ]

    holds = (hold_h.at[0], hold_h.at[1], hold_d)
    arrived = (came_h.at[0], came_h.at[1], came_d)
    owns = (own_h.at[0], own_h.at[1], own_d)
    cores = [across(holds[f], arrived[f], sems, f, "core") for f in range(3)]
    received = (
        [r1_h.at[0], r2_h.at[0], r3_h.at[0]],
        [r1_h.at[1], r2_h.at[1], r3_h.at[1]],
        [r1_d, r2_d, r3_d],
    )
    folds = [
        Fold(owns[f], None, received[f], ORDERS[f], sems, 3 + 3 * f, None, None) for f in range(3)
    ]
    stores_a = [
        pltpu.make_async_copy(received[f][2], half, near.at[f])
        for f, half in enumerate((gate_a, up_a, down_a))
    ]
    stores_b = [
        pltpu.make_async_copy(owns[f], whole, near.at[3 + f])
        for f, whole in enumerate((gate_b, up_b, down_b))
    ]

    @pl.when(step == 0)
    def _():
        for load in weights(step, slot):
            load.start()
        out_ref[...] = jnp.zeros_like(out_ref)
        back_ref[...] = jnp.zeros_like(back_ref)
        greet(("core",) + AXES[:3])

    for load in weights(step, slot):
        load.wait()

    @pl.when(step < 3)
    def _():
        for load in weights(step + 1, 1 - slot):
            load.start()

    gate, up, down = gate_v.at[slot], up_v.at[slot], down_v.at[slot]
    for at in range(0, length, BLOCK):
        rows = slice(at, at + BLOCK)
        normed = normed_ref[rows, :]
        gate_sum = mm(normed, gate[...])
        up_sum = mm(normed, up[...])
        hidden_grad = mm_nt(c_ref[rows, :], down[...])
        sigmoid = jax.nn.sigmoid(gate_sum)
        activated = gate_sum * sigmoid
        hidden = low(activated * up_sum)
        gate_grad = low(hidden_grad * up_sum * (sigmoid + activated * (1.0 - sigmoid)))
        up_grad = low(hidden_grad * activated)
        hidden_t[:, rows] = hidden.T
        gate_low[rows, :] = gate_grad
        up_low[rows, :] = up_grad
        out_ref[rows, :] += mm(hidden, down[...])
        back_ref[rows, :] += mm_nt(gate_grad, gate[...]) + mm_nt(up_grad, up[...])

    theirs = slot == 0

    @pl.when(step == 3)
    def _():
        for fold in folds:
            fold.copy(0).wait_send()
            fold.advance(1)

    @pl.when(jnp.logical_not(theirs))
    def _():
        for copy in cores:
            copy.wait_recv()

    def weight_grads(store):
        quarter = width // 4
        for n in range(4):
            rows = slice(n * quarter, (n + 1) * quarter)
            for f, grads in enumerate((gate_low, up_low)):
                value = mm(turned_ref[rows, :], grads[...]).reshape(4, quarter // 4, 2 * part)
                for k in range(4):
                    store(f, sixteenth(4 * n + k), value[k])
        third = width // 3
        for n in range(3):
            columns = slice(n * third, (n + 1) * third)
            value = mm(hidden_t[...], c_ref[:, columns]).reshape(16, part // 8, third)
            for k in range(16):
                store(2, sixteenth(k) + (slice(None), columns), value[k])

    def keep(f, index, value):
        holds[f][index] = low(value)

    def add(f, index, value):
        owns[f][index] = low(value + arrived[f][index].astype(jnp.float32))

    @pl.when(theirs)
    def _():
        weight_grads(keep)

    @pl.when(jnp.logical_not(theirs))
    def _():
        weight_grads(add)

    @pl.when(step == 2)
    def _():
        pl.semaphore_wait(free, 1)

    @pl.when(theirs)
    def _():
        for copy in cores:
            copy.start()

    @pl.when(step == 2)
    def _():
        for fold in folds:
            fold.advance(0)

    @pl.when(jnp.logical_not(theirs))
    def _():
        for copy in cores:
            copy.wait_send()

    @pl.when(step == 1)
    def _():
        pl.semaphore_signal(free, inc=1, device_id=peer_of("core"), device_id_type=MESH)
        for fold in folds:
            fold.begin()

    @pl.when(step == 3)
    def _():
        for store in stores_b:
            store.start()
        for fold in folds:
            fold.advance(2)
        for store in stores_a:
            store.start()
        for fold in folds:
            for stage in (1, 2):
                fold.copy(stage).wait_send()
        for store in stores_a + stores_b:
            store.wait()


def feed(normed, turned, c, gate, up, down):
    length, width = normed.shape
    part = gate.shape[1] // 8
    rows, down_rows = width // 16, part // 8
    whole = lambda a: pl.BlockSpec(a.shape, lambda t: (0, 0), pipeline_mode=pl.Buffered(1))
    total = pl.BlockSpec((length, width), lambda t: (0, 0), pipeline_mode=pl.Buffered(1))
    anywhere = pl.BlockSpec(memory_space=pl.ANY)
    low_type = jnp.bfloat16
    hidden = lambda left: (2,) * left + (rows, 2 * part)
    down_shape = lambda left: (2,) * left + (down_rows, width)
    return pl.pallas_call(
        feed_body,
        grid=(4,),
        in_specs=[whole(normed), whole(turned), whole(c)] + [anywhere] * 3,
        out_specs=[total, total] + [anywhere] * 6,
        out_shape=[
            jax.ShapeDtypeStruct((length, width), jnp.float32),
            jax.ShapeDtypeStruct((length, width), jnp.float32),
        ]
        + [
            jax.ShapeDtypeStruct(shape, low_type)
            for left in (1, 4)
            for shape in (hidden(left), hidden(left), down_shape(left))
        ],
        scratch_shapes=[
            pltpu.VMEM((2, width, 2 * part), low_type),
            pltpu.VMEM((2, width, 2 * part), low_type),
            pltpu.VMEM((2, 2 * part, width), low_type),
            pltpu.VMEM((2 * part, length), low_type),
            pltpu.VMEM((length, 2 * part), low_type),
            pltpu.VMEM((length, 2 * part), low_type),
        ]
        + [pltpu.VMEM(shape, low_type) for _ in range(3) for shape in ((2,) + hidden(4), down_shape(4))]
        + [pltpu.VMEM((2,) + hidden(left), low_type) for left in (3, 2, 1)]
        + [pltpu.VMEM(down_shape(left), low_type) for left in (3, 2, 1)]
        + [
            pltpu.SemaphoreType.DMA((2, 12)),
            pltpu.SemaphoreType.DMA((6,)),
            pltpu.SemaphoreType.DMA((2, 6)),
            pltpu.SemaphoreType.REGULAR,
        ],
        compiler_params=pltpu.CompilerParams(
            collective_id=5, has_side_effects=True, vmem_limit_bytes=VMEM_MOST
        ),
        cost_estimate=pl.CostEstimate(
            flops=18 * length * width * gate.shape[1],
            bytes_accessed=12 * width * gate.shape[1] + 16 * length * width,
            transcendentals=length * gate.shape[1],
        ),
        name="feed",
    )(normed, turned, c, gate, up, down)


def shortened(array):
    return jax.tree.map(lambda a: a.astype(jnp.bfloat16) if a.dtype == jnp.float32 else a, array)


def product(left, right):
    return jnp.dot(left, right, preferred_element_type=jnp.float32)


def product_tn(left, right):
    return lax.dot_general(
        left, right, (((0,), (0,)), ((), ())), preferred_element_type=jnp.float32
    )


def product_nt(left, right):
    return lax.dot_general(
        left, right, (((1,), (1,)), ((), ())), preferred_element_type=jnp.float32
    )


def rotary_tables(positions, width):
    half_width = width // 2
    freqs = jnp.exp(
        jnp.arange(half_width, dtype=jnp.float32) * (-2.0 * math.log(rope_base) / width)
    )
    angles = positions[:, None] * freqs[None, :]
    return (jnp.cos(angles), jnp.sin(angles))


def rotate(values, cosines, sines):
    half_width = values.shape[-1] // 2
    first = values[..., :half_width]
    second = values[..., half_width:]
    return jnp.concatenate(
        [first * cosines - second * sines, second * cosines + first * sines], axis=-1
    )


def unrotate(values, cosines, sines):
    half_width = values.shape[-1] // 2
    first = values[..., :half_width]
    second = values[..., half_width:]
    return jnp.concatenate(
        [first * cosines + second * sines, second * cosines - first * sines], axis=-1
    )


def norm_back(grad_rows, gain, scaled, inverse):
    weighted = grad_rows * gain
    return inverse * (weighted - scaled * jnp.mean(weighted * scaled, axis=-1, keepdims=True))


def plain_local(
    inputs,
    segments,
    out_grad,
    attention_gain,
    query_weight,
    key_weight,
    value_weight,
    output_weight,
    feedforward_gain,
    gate_weight,
    up_weight,
    down_weight,
):
    gathered = (
        lax.all_gather(attention_gain, "fsdp", axis=0, tiled=True),
        lax.all_gather(query_weight, "fsdp", axis=0, tiled=True),
        lax.all_gather(key_weight, "fsdp", axis=0, tiled=True),
        lax.all_gather(value_weight, "fsdp", axis=0, tiled=True),
        lax.all_gather(output_weight, "fsdp", axis=0, tiled=True),
        lax.all_gather(feedforward_gain, "fsdp", axis=0, tiled=True),
        lax.all_gather(gate_weight, "fsdp", axis=0, tiled=True),
        lax.all_gather(up_weight, "fsdp", axis=0, tiled=True),
        lax.all_gather(down_weight, "fsdp", axis=0, tiled=True),
    )
    full_query, full_key, full_value, full_output = (
        gathered[1],
        gathered[2],
        gathered[3],
        gathered[4],
    )
    full_gate, full_up, full_down = (gathered[6], gathered[7], gathered[8])
    gain_attention = gathered[0].astype(jnp.float32)
    gain_feed = gathered[5].astype(jnp.float32)
    span = inputs.shape[1]
    length = segments.shape[1]
    groups_q = HEADS // KV_HEADS
    key_width = KV_HEADS * HEAD
    start = lax.axis_index("fsdp") * span
    query_pos = start + jnp.arange(span, dtype=jnp.int32)
    key_pos = jnp.arange(length, dtype=jnp.int32)
    cosines, sines = rotary_tables(query_pos.astype(jnp.float32), HEAD)
    cos_four, sin_four = (cosines[:, None, None, :], sines[:, None, None, :])
    cos_three, sin_three = (cosines[:, None, :], sines[:, None, :])
    causal = query_pos[:, None] >= key_pos[None, :]
    scale = HEAD ** (-0.5)

    def micro_step(totals, sequence):
        tokens, segment_row, cotangent = sequence
        own_segment = lax.dynamic_slice_in_dim(segment_row, start, span)
        allowed = causal & (own_segment[:, None] == segment_row[None, :])
        values = tokens.astype(jnp.float32)
        inverse_a = lax.rsqrt(jnp.mean(values * values, axis=-1, keepdims=True) + epsilon)
        scaled_a = values * inverse_a
        normed_a = (scaled_a * gain_attention).astype(jnp.bfloat16)
        query_lin = product(normed_a, full_query).reshape(span, KV_HEADS, groups_q, HEAD)
        queries = rotate(query_lin, cos_four, sin_four).astype(jnp.bfloat16)
        key_lin = product(normed_a, full_key).reshape(span, KV_HEADS, HEAD)
        key_rows = (
            rotate(key_lin, cos_three, sin_three).astype(jnp.bfloat16).reshape(span, key_width)
        )
        value_rows = product(normed_a, full_value).astype(jnp.bfloat16)
        all_keys, all_values = (
            lax.all_gather(key_rows, "fsdp", axis=0, tiled=True),
            lax.all_gather(value_rows, "fsdp", axis=0, tiled=True),
        )
        all_keys = all_keys.reshape(length, KV_HEADS, HEAD)
        all_values = all_values.reshape(length, KV_HEADS, HEAD)
        scores = (
            jnp.einsum("qhgd,khd->hgqk", queries, all_keys, preferred_element_type=jnp.float32)
            * scale
        )
        scores = jnp.where(allowed, scores, -1e30)
        highest = jnp.max(scores, axis=-1, keepdims=True)
        expo_scores = jnp.exp(scores - highest)
        attention = expo_scores / jnp.sum(expo_scores, axis=-1, keepdims=True)
        attention_low = attention.astype(jnp.bfloat16)
        mixed = jnp.einsum(
            "hgqk,khd->qhgd", attention_low, all_values, preferred_element_type=jnp.float32
        )
        mixed = mixed.reshape(span, HEADS * HEAD).astype(jnp.bfloat16)
        residual = values + product(mixed, full_output)
        inverse_f = lax.rsqrt(jnp.mean(residual * residual, axis=-1, keepdims=True) + epsilon)
        scaled_f = residual * inverse_f
        normed_f = (scaled_f * gain_feed).astype(jnp.bfloat16)
        gate_sum = product(normed_f, full_gate)
        up_sum = product(normed_f, full_up)
        sigmoid_gate = jax.nn.sigmoid(gate_sum)
        activated = gate_sum * sigmoid_gate
        hidden = (activated * up_sum).astype(jnp.bfloat16)
        result = (residual + product(hidden, full_down)).astype(jnp.bfloat16)
        down_wgrad = product_tn(hidden, cotangent)
        hidden_grad = product_nt(cotangent, full_down)
        gate_grad = (
            hidden_grad * up_sum * sigmoid_gate * (1.0 + gate_sum * (1.0 - sigmoid_gate))
        ).astype(jnp.bfloat16)
        up_grad = (hidden_grad * activated).astype(jnp.bfloat16)
        gate_wgrad = product_tn(normed_f, gate_grad)
        up_wgrad = product_tn(normed_f, up_grad)
        normed_f_grad = product_nt(gate_grad, full_gate) + product_nt(up_grad, full_up)
        feed_gain_grad = jnp.sum(normed_f_grad * scaled_f, axis=0)
        residual_grad = cotangent.astype(jnp.float32) + norm_back(
            normed_f_grad, gain_feed, scaled_f, inverse_f
        )
        residual_low = residual_grad.astype(jnp.bfloat16)
        output_wgrad = product_tn(mixed, residual_low)
        mixed_grad = (
            product_nt(residual_low, full_output)
            .astype(jnp.bfloat16)
            .reshape(span, KV_HEADS, groups_q, HEAD)
        )
        attention_grad = jnp.einsum(
            "qhgd,khd->hgqk", mixed_grad, all_values, preferred_element_type=jnp.float32
        )
        row_totals = jnp.sum(attention * attention_grad, axis=-1, keepdims=True)
        score_grad = (attention * (attention_grad - row_totals) * scale).astype(jnp.bfloat16)
        value_grads = jnp.einsum(
            "hgqk,qhgd->khd", attention_low, mixed_grad, preferred_element_type=jnp.float32
        ).reshape(length, key_width)
        key_grads = jnp.einsum(
            "hgqk,qhgd->khd", score_grad, queries, preferred_element_type=jnp.float32
        ).reshape(length, key_width)
        query_grad = jnp.einsum(
            "hgqk,khd->qhgd", score_grad, all_keys, preferred_element_type=jnp.float32
        )
        key_back, value_back = (
            lax.psum_scatter(key_grads, "fsdp", scatter_dimension=0, tiled=True),
            lax.psum_scatter(value_grads, "fsdp", scatter_dimension=0, tiled=True),
        )
        query_low = (
            unrotate(query_grad, cos_four, sin_four)
            .reshape(span, HEADS * HEAD)
            .astype(jnp.bfloat16)
        )
        key_low = (
            unrotate(key_back.reshape(span, KV_HEADS, HEAD), cos_three, sin_three)
            .reshape(span, key_width)
            .astype(jnp.bfloat16)
        )
        value_low = value_back.astype(jnp.bfloat16)
        query_wgrad = product_tn(normed_a, query_low)
        key_wgrad = product_tn(normed_a, key_low)
        value_wgrad = product_tn(normed_a, value_low)
        normed_a_grad = (
            product_nt(query_low, full_query)
            + product_nt(key_low, full_key)
            + product_nt(value_low, full_value)
        )
        attention_gain_term = jnp.sum(normed_a_grad * scaled_a, axis=0)
        token_grad = (
            residual_grad + norm_back(normed_a_grad, gain_attention, scaled_a, inverse_a)
        ).astype(jnp.bfloat16)
        terms = (
            attention_gain_term,
            query_wgrad,
            key_wgrad,
            value_wgrad,
            output_wgrad,
            feed_gain_grad,
            gate_wgrad,
            up_wgrad,
            down_wgrad,
        )
        totals = tuple((left + right for left, right in zip(totals, terms)))
        return (totals, (result, token_grad))

    initial = tuple((jnp.zeros(weight.shape, jnp.float32) for weight in gathered))
    totals, (outputs, input_grads) = lax.scan(micro_step, initial, (inputs, segments, out_grad))
    shards = jax.tree.map(
        lambda part: part.astype(jnp.float32),
        lax.psum_scatter(shortened(totals), "fsdp", scatter_dimension=0, tiled=True),
    )
    summed = lax.psum(shards, "group")
    return (
        outputs,
        input_grads,
        summed[0],
        summed[1],
        summed[2],
        summed[3],
        summed[4],
        summed[5],
        summed[6],
        summed[7],
        summed[8],
    )


def paired_local(
    inputs,
    segments,
    out_grad,
    attention_gain,
    query_weight,
    key_weight,
    value_weight,
    output_weight,
    feedforward_gain,
    gate_weight,
    up_weight,
    down_weight,
):
    y = lax.axis_index("fsdp")
    span, length, width = inputs.shape[1], segments.shape[1], inputs.shape[2]
    q_width = query_weight.shape[1]

    gains = jnp.pad(
        jnp.stack([attention_gain, feedforward_gain]).astype(jnp.float32), ((0, 6), (0, 0))
    )
    tokens, qkv_weight, gains = fetch(inputs, query_weight, key_weight, value_weight, gains)
    gains = gains.transpose(1, 0, 2).reshape(8, width)
    gain_a, gain_f = gains[0:1], gains[1:2]

    segment = lax.dynamic_index_in_dim(segments, y, 0, False)
    seg_col, seg_row = segment[:, None], segment[None, :]
    cosines, sines = rope_tables(length)
    normed_a, qkv, mix_begun, gate_begun = project(
        tokens, gain_a, qkv_weight, cosines, sines, output_weight, gate_weight
    )
    mixed, lse, c, mix_weight, full_gate, full_up, full_down = attend(
        qkv, seg_col, seg_row, out_grad, output_weight, gate_weight, up_weight, down_weight,
        mix_begun, gate_begun,
    )

    residual, normed_f, turned_f = mix(tokens, mixed, mix_weight, gain_f)

    out, back, *chunks = feed(normed_f, turned_f, c, full_gate, full_up, full_down)
    result, residual_grad, mixed_grad, mix_term, feed_gain_term = turn(
        residual, out, back, c, mixed, mix_weight, gain_f
    )
    dq, dk, dv, *halves = attend_back(
        qkv, mixed_grad, mixed, lse, seg_col, seg_row, cosines, sines, *chunks[3:], *chunks[:3]
    )
    gate_sum, up_sum, down_sum, sums, outputs, input_grads, gain_sums = end(
        dq, dk, dv, normed_a, tokens, residual_grad, qkv_weight, gain_a, feed_gain_term,
        mix_term, result, *halves,
    )
    gain_grads = lax.dynamic_slice_in_dim(gain_sums, y * (width // 2), width // 2, 1)
    k_width = key_weight.shape[1]
    sums = sums.reshape(width // 2, -1).astype(jnp.float32)
    ends = (0, q_width, q_width + k_width, q_width + 2 * k_width, sums.shape[1])
    parts = [sums[:, a:b] for a, b in zip(ends[:-1], ends[1:])]
    return (
        outputs,
        input_grads,
        gain_grads[0],
        *parts,
        gain_grads[1],
        gate_sum.reshape(width // 2, -1).astype(jnp.float32),
        up_sum.reshape(width // 2, -1).astype(jnp.float32),
        down_sum.reshape(-1, width).astype(jnp.float32),
    )


def solution(mesh):
    placed = (
        P("group", "fsdp", None),
        P("group", None),
        P("group", "fsdp", None),
        P("fsdp"),
        P("fsdp", None),
        P("fsdp", None),
        P("fsdp", None),
        P("fsdp", None),
        P("fsdp"),
        P("fsdp", None),
        P("fsdp", None),
        P("fsdp", None),
    )
    group_size, fsdp_size = mesh.shape["group"], mesh.shape["fsdp"]

    def local(*arrays):
        if group_size == 16 and fsdp_size == 2 and arrays[0].shape[0] == 2:
            return paired_local(*arrays)
        return plain_local(*arrays)

    return jax.shard_map(
        local,
        mesh=mesh,
        in_specs=placed,
        out_specs=(
            P("group", "fsdp", None),
            P("group", "fsdp", None),
            P("fsdp"),
            P("fsdp", None),
            P("fsdp", None),
            P("fsdp", None),
            P("fsdp", None),
            P("fsdp"),
            P("fsdp", None),
            P("fsdp", None),
            P("fsdp", None),
        ),
        check_vma=False,
    )
```
